32 devices in a mesh: dp: 2 (over core), head: 2 (over x), blk: 8 (over z, y).
Axes of the slice: x: 2, y: 2, z: 4, core: 2. Of those that a mesh axis runs over, the one named last changes fastest.
Arguments:
- tokens: bfloat16 [2, 2048, 2304], P('dp', ('head', 'blk')), may hold values from -6 to 6
- cotangent: bfloat16 [2, 2048, 2304], P('dp', ('head', 'blk')), may hold values from -6 to 6
- segments: int32 [2, 2048], P('dp'), may hold values from 0 to 3, never falling along the last dimension, each value on 1 to 1024 neighbouring positions
- norm_gains: bfloat16 [2304, 4], P(('dp', 'head', 'blk')), may hold values from 0.25 to 1.75
- qkv_weight: bfloat16 [4096, 2304], P(('dp', 'head', 'blk')), may hold values from -4 to 4
- out_weight: bfloat16 [2304, 2048], P(('dp', 'head', 'blk')), may hold values from -0.125 to 0.125
- gate_up_weight: bfloat16 [9216, 4608], P(('dp', 'head', 'blk')), may hold values from -0.125 to 0.125
- down_weight: bfloat16 [9216, 2304], P(('dp', 'head', 'blk')), may hold values from -0.0625 to 0.0625
Outputs:
- layer_out: bfloat16 [2, 2048, 2304], P('dp', ('head', 'blk'))
- tokens_grad: bfloat16 [2, 2048, 2304], P('dp', ('head', 'blk'))
- norm_gains_grad: float32 [2304, 4], P(('dp', 'head', 'blk'))
- qkv_grad: float32 [4096, 2304], P(('dp', 'head', 'blk'))
- out_grad: float32 [2304, 2048], P(('dp', 'head', 'blk'))
- gate_up_grad: float32 [9216, 4608], P(('dp', 'head', 'blk'))
- down_grad: float32 [9216, 2304], P(('dp', 'head', 'blk'))
The draws below stay inside these ranges and needn't reach their ends.
Inputs may be any that keep to these rules, and one draw needn't show every extreme that they name: `segments`: document ids never fall along a sequence; every id appears, and one document has exactly 1024 tokens.
All inputs are finite; a program needn't handle non-finite values.
Results may differ from the reference program's by a relative error of at most 0.024.
Values may be sent and summed in bfloat16 or wider, within the bound.
A program may use at most 256 MiB of HBM per device.

```python
import math
import jax
import jax.numpy as jnp
import numpy as np
from jax import lax

MODEL_DIMENSION = 2304
HEADS = 8
KV_HEADS = 4
HEAD_DIM = 256
FF = 9216
DOCS = 4
SEQS = 2
SEQ_LEN = 2048
DOC_MOST = 1024


def draw_qkv_weight(key, part):
    group_rows = HEADS // KV_HEADS + 2
    level_key = jax.random.fold_in(key, 11)
    entry_key = jax.random.fold_in(key, 23)
    ranking = jax.random.permutation(level_key, KV_HEADS)
    levels = jnp.exp(ranking.astype(jnp.float32) * (0.5 / max(KV_HEADS - 1, 1)))
    is_value = jnp.arange(group_rows) == group_rows - 1
    row_scale = jnp.where(is_value[None, :], 1.0, levels[:, None])
    draw_shape = (KV_HEADS, group_rows, HEAD_DIM, MODEL_DIMENSION)
    entries = jnp.clip(jax.random.normal(entry_key, draw_shape, jnp.float32), -6.0, 6.0)
    values = entries * row_scale[:, :, None, None] * MODEL_DIMENSION ** (-0.5)
    return values.reshape(KV_HEADS * group_rows * HEAD_DIM, MODEL_DIMENSION).astype(jnp.bfloat16)


def shard_levels(rng, extent, cuts, least, top_value):
    def one(dim, parts):
        heights = jax.random.uniform(jax.random.fold_in(jax.random.fold_in(rng, 6), dim), (parts,), jnp.float32, least / len(cuts), top_value / len(cuts))
        return jnp.repeat(jnp.exp(heights), extent[dim] // parts).reshape((-1,) + (1,) * (len(extent) - dim - 1))

    loudness = one(*cuts[0])
    for cut in cuts[1:]:
        loudness = loudness * one(*cut)
    return loudness


def split_up(amount, total, most, slope):
    loads = [(1 << 20) // math.isqrt(standing ** slope) + 1 for standing in range(2, amount + 1)]
    surplus, counts = total - most - (amount - 1), [1] * (amount - 1)
    while surplus > 0:
        free = [i for i in range(amount - 1) if counts[i] < most]
        whole, left = sum([loads[i] for i in free]), surplus
        for i in free:
            extra = min(most - counts[i], max(1, left * loads[i] // whole), surplus)
            counts[i] = counts[i] + extra
            surplus = surplus - extra
    return np.array([most] + counts)


def uneven_parts(stream_key, number_of, total, reach, skew):
    if number_of == 2:
        one = jax.random.randint(stream_key, (), max(1, total - reach), min(reach, total - 1) + 1)
        return jnp.stack([one, total - one])
    tallies = jnp.asarray(split_up(number_of, total, reach, skew), jnp.int32)
    twos = (number_of - 1) // 2
    donor, sink = tallies[1:1 + 2 * twos:2], tallies[2:2 + 2 * twos:2]
    slack = jnp.minimum(donor - 1, reach - sink)
    passed = jax.random.randint(jax.random.fold_in(stream_key, 1), (twos,), 0, 1 << 20) % (slack + 1)
    tallies = tallies.at[1:1 + 2 * twos:2].set(donor - passed).at[2:2 + 2 * twos:2].set(sink + passed)
    return tallies[jax.random.permutation(jax.random.fold_in(stream_key, 2), number_of)]


def bell_draw(rng, shape, deviation, most, split=(), kind=jnp.bfloat16):
    factor_of = shard_levels(rng, shape, split, -0.22, 0.18) if split else 1.0
    values = jax.random.normal(rng, shape, jnp.float32) * deviation * factor_of
    return jnp.minimum(jnp.maximum(values, -most), most).astype(kind)


def setup_inputs(seed: int = 0) -> dict:
    streams_of = jax.random.split(jax.random.key(seed), 9)
    tokens = bell_draw(streams_of[0], (SEQS, SEQ_LEN, MODEL_DIMENSION), 1.0, 6.0, ((0, 2), (1, 16)))
    cotangent = bell_draw(streams_of[1], (SEQS, SEQ_LEN, MODEL_DIMENSION), 1.0, 6.0, ((0, 2), (1, 16)))
    segments = jax.vmap(lambda own: jnp.searchsorted(jnp.cumsum(uneven_parts(own, DOCS, SEQ_LEN, DOC_MOST, 2)), jnp.arange(SEQ_LEN), side="right"))(jax.random.split(streams_of[2], SEQS)).reshape((SEQS, SEQ_LEN)).astype(jnp.int32)
    norm_gains = jnp.clip(1.0 + 0.15 * jax.random.normal(streams_of[3], (MODEL_DIMENSION, 4), jnp.float32), 0.25, 1.75).astype(jnp.bfloat16)
    qkv_weight = draw_qkv_weight(jax.random.fold_in(streams_of[8], 71), 0)
    out_weight = bell_draw(streams_of[5], (MODEL_DIMENSION, HEADS * HEAD_DIM), (HEADS * HEAD_DIM) ** -0.5, 0.125, ((0, 32),))
    gate_up_weight = bell_draw(streams_of[6], (FF, 2 * MODEL_DIMENSION), MODEL_DIMENSION ** -0.5, 0.125, ((0, 32),))
    down_weight = bell_draw(streams_of[7], (FF, MODEL_DIMENSION), FF ** -0.5, 0.0625, ((0, 32),))
    return {"tokens": tokens, "cotangent": cotangent, "segments": segments, "norm_gains": norm_gains, "qkv_weight": qkv_weight, "out_weight": out_weight, "gate_up_weight": gate_up_weight, "down_weight": down_weight}


SOFT_CAP = 50.0
NORM_EPS = 1e-06
ROPE_BASE = 10000.0

@jax.custom_vjp
def low(v):
    return lax.optimization_barrier(v.astype(jnp.bfloat16)).astype(jnp.float32)

@jax.custom_vjp
def low_back(v):
    return v

def low_keep(v):
    return (low(v), None)

def low_pass(kept, grad):
    return (grad,)

def back_keep(v):
    return (v, None)

def back_low(kept, grad):
    return (low(grad),)
low.defvjp(low_keep, low_pass)
low_back.defvjp(back_keep, back_low)

def rms_scale(values, gain_row):
    return values * lax.rsqrt(lax.optimization_barrier(jnp.mean(values * values, axis=-1, keepdims=True)) + NORM_EPS) * gain_row

def gelu_tanh(values):
    return jax.nn.gelu(values, approximate=True)

def rope_tables(positions, head_width):
    half_width = head_width // 2
    frequency = jnp.exp(jnp.arange(half_width, dtype=jnp.float32) * (-2.0 * math.log(ROPE_BASE) / head_width))
    angles = positions.astype(jnp.float32)[:, None] * frequency[None, :]
    cosine = jnp.concatenate([jnp.cos(angles), jnp.cos(angles)], axis=-1)
    sine_table = jnp.concatenate([jnp.sin(angles), jnp.sin(angles)], axis=-1)
    return (cosine[:, None, None, :], sine_table[:, None, None, :])

def rotate(values, cosine, sine_table):
    half_width = values.shape[-1] // 2
    turned = jnp.concatenate([-values[..., half_width:], values[..., :half_width]], axis=-1)
    return values * cosine + turned * sine_table

def attend_sequence(operands):
    queries, key_rows, value_rows, doc_ids = operands
    score_scale = HEAD_DIM ** (-0.5)
    block_rows = math.gcd(512, SEQ_LEN)
    key_pos = jnp.arange(SEQ_LEN, dtype=jnp.int32)

    def one_block(first_row):
        query_block = lax.dynamic_slice_in_dim(queries, first_row, block_rows, 0)
        raw_score = low_back(jnp.einsum('qgjd,kgd->gjqk', query_block, key_rows, precision=lax.Precision.HIGHEST))
        capped = jnp.tanh(raw_score * (score_scale / SOFT_CAP))
        query_pos = first_row + jnp.arange(block_rows, dtype=jnp.int32)
        query_doc = lax.dynamic_slice_in_dim(doc_ids, first_row, block_rows, 0)
        visible = (key_pos[None, :] <= query_pos[:, None]) & (doc_ids[None, :] == query_doc[:, None])
        exp_weights = jnp.where(visible, jnp.exp(SOFT_CAP * capped), 0.0)
        row_total = jnp.transpose(lax.optimization_barrier(jnp.sum(exp_weights, axis=-1)), (2, 0, 1))
        row_sums = low_back(jnp.einsum('gjqk,kgd->qgjd', low(exp_weights), value_rows, precision=lax.Precision.HIGHEST))
        inverse_total = jnp.exp(-jnp.log(row_total))
        return row_sums * inverse_total[..., None]
    firsts = (jnp.arange(SEQ_LEN // block_rows) * block_rows).astype(jnp.int32)
    blocks = lax.map(jax.checkpoint(one_block), firsts)
    return blocks.reshape(queries.shape)

def layer_forward(inputs, gain_table, query_key_value_weight, output_projection, gate_up_projection, down_projection_weight, segments):
    rep_count = HEADS // KV_HEADS
    first_normalized = low(rms_scale(inputs, gain_table[:, 0]))
    projected_rows = low_back(jnp.einsum('oxa,za->oxz', first_normalized, query_key_value_weight, precision=lax.Precision.HIGHEST))
    projected_rows = projected_rows.reshape(SEQS, SEQ_LEN, KV_HEADS, rep_count + 2, HEAD_DIM)
    cosine, sine_table = rope_tables(jnp.arange(SEQ_LEN, dtype=jnp.int32), HEAD_DIM)
    turned = rotate(projected_rows[:, :, :, :rep_count + 1], cosine, sine_table)
    sent_rows = low(low_back(jnp.concatenate([turned, projected_rows[:, :, :, rep_count + 1:]], axis=3)))
    attended = lax.map(jax.checkpoint(attend_sequence), (sent_rows[:, :, :, :rep_count], sent_rows[:, :, :, rep_count], sent_rows[:, :, :, rep_count + 1], segments))
    attention_result = low(low_back(attended)).reshape(SEQS, SEQ_LEN, HEADS * HEAD_DIM)
    residual_branch = low_back(jnp.einsum('jhv,iv->jhi', attention_result, output_projection, precision=lax.Precision.HIGHEST))
    middle = inputs + rms_scale(residual_branch, gain_table[:, 1])
    third_normalized = low(rms_scale(middle, gain_table[:, 2]))
    gate_activation = low_back(jnp.einsum('ita,ha->ith', third_normalized, gate_up_projection[:, :MODEL_DIMENSION], precision=lax.Precision.HIGHEST))
    up_activation = low_back(jnp.einsum('ita,ha->ith', third_normalized, gate_up_projection[:, MODEL_DIMENSION:], precision=lax.Precision.HIGHEST))
    hidden_state = low(gelu_tanh(gate_activation) * up_activation)
    feedforward_result = low_back(jnp.einsum('gbo,om->gbm', hidden_state, down_projection_weight, precision=lax.Precision.HIGHEST))
    return middle + rms_scale(feedforward_result, gain_table[:, 3])

def reference(tokens, cotangent, segments, norm_gains, qkv_weight, out_weight, gate_up_weight, down_weight):

    def forward(inputs, gain_table, query_key_value_weight, output_projection, gate_up_projection, down_projection_weight):
        return layer_forward(inputs, gain_table, query_key_value_weight, output_projection, gate_up_projection, down_projection_weight, segments)
    result, backward = jax.vjp(forward, tokens.astype(jnp.float32), norm_gains.astype(jnp.float32), qkv_weight.astype(jnp.float32), out_weight.astype(jnp.float32), gate_up_weight.astype(jnp.float32), down_weight.astype(jnp.float32))
    gradients = backward(cotangent.astype(jnp.float32))
    return (result.astype(jnp.bfloat16), gradients[0].astype(jnp.bfloat16), gradients[1], gradients[2], gradients[3], gradients[4], gradients[5])
```

```python
import functools
import math

import jax
import jax.numpy as jnp
from jax import lax
from jax.experimental import pallas as pl
from jax.experimental.pallas import tpu as pltpu
from jax.sharding import PartitionSpec as P

HEADS = 8
KV_HEADS = 4
HEAD_DIM = 256
REPS = HEADS // KV_HEADS
GROUPS = 4
SOFT_CAP = 50.0
NORM_EPS = 1e-06
ROPE_BASE = 10000.0
SCORE_SCALE = HEAD_DIM ** (-0.5)

MESH = pl.DeviceIdType.MESH
VMEM_LIMIT = 60 * 1024 * 1024


class Place:
    def __init__(self, count):
        self.count = count
        self.inner = 4 if count >= 32 else 2
        self.outer = count // self.inner
        self.here = lax.axis_index("blk")
        self.line = self.here // self.inner
        self.side = lax.rem(self.here, self.inner)
        self.core = lax.axis_index("dp")
        self.half = lax.axis_index("head")
        self.group = 2 * self.core + self.half

    def at(self, line, side):
        return {"blk": line * self.inner + side}

    def beside(self, step):
        return lax.rem(self.side + step, self.inner)

    def partner(self):
        return {"dp": 1 - self.core}

    def across(self):
        return {"head": 1 - self.half}

    def corner(self):
        return {"dp": 1 - self.core, "head": 1 - self.half}


def remote(src, dst, sent, came, device):
    return pltpu.make_async_remote_copy(
        src_ref=src, dst_ref=dst, send_sem=sent, recv_sem=came, device_id=device, device_id_type=MESH
    )


def greet(place, blk=False, core=False, half=False, corner=False):
    sem = pltpu.get_barrier_semaphore()
    amount = jnp.int32(0)

    def hello(device):
        pl.semaphore_signal(sem, inc=1, device_id=device, device_id_type=MESH)

    if blk:
        up, down = place.line < place.outer - 1, place.line > 0
        pl.when(up)(lambda: hello(place.at(place.line + 1, place.side)))
        pl.when(down)(lambda: hello(place.at(place.line - 1, place.side)))
        amount = amount + up.astype(jnp.int32) + down.astype(jnp.int32) + (place.inner - 1)
        for step in range(1, place.inner):
            hello(place.at(place.line, place.beside(step)))
    for wanted, device in (
        (core, place.partner()),
        (half, place.across()),
        (corner, place.corner()),
    ):
        if wanted:
            hello(device)
            amount = amount + 1
    pl.semaphore_wait(sem, amount)


def together(*tasks):
    tasks = list(tasks)
    while tasks:
        for task in list(tasks):
            try:
                next(task)
            except StopIteration:
                tasks.remove(task)


def gather_blk_sems(place_count):
    inner = 4 if place_count >= 32 else 2
    return [
        pltpu.SemaphoreType.DMA((1 + inner, place_count)),
        pltpu.SemaphoreType.DMA((place_count,)),
        pltpu.SemaphoreType.DMA,
    ]


def gather_blk(place, src, out, sent, came, own):
    outer, inner, line, side = place.outer, place.inner, place.line, place.side
    copy = pltpu.make_async_copy(src, out.at[place.here], own)
    copy.start()
    finishing = []
    is_below, is_above = line < outer - 1, line > 0

    def spread(what, piece, up, down):
        def send(kind, device):
            return remote(what, out.at[piece], sent.at[kind, piece], came.at[piece], device)

        if up is not None:
            pl.when(up)(lambda: send(0, place.at(line + 1, side)).start())
            finishing.append((up, lambda: send(0, place.at(line + 1, side)).wait_send()))
        if down is not None:
            pl.when(down)(lambda: send(1, place.at(line - 1, side)).start())
            finishing.append((down, lambda: send(1, place.at(line - 1, side)).wait_send()))
        for step in range(1, inner):
            send(1 + step, place.at(line, place.beside(step))).start()
            finishing.append(
                (None, lambda step=step: send(1 + step, place.at(line, place.beside(step))).wait_send())
            )

    def arrived(piece):
        remote(
            src, out.at[piece], sent.at[0, piece], came.at[piece], place.at(line, place.beside(1))
        ).wait_recv()

    spread(src, place.here, is_below, is_above)
    yield
    ends = []
    for away in range(1, outer):
        for sign in (-1, 1):
            there = line + sign * away
            fits = (there >= 0) if sign < 0 else (there < outer)
            piece = there * inner + side

            @pl.when(fits)
            def _(piece=piece, sign=sign):
                arrived(piece)
                mark = len(finishing)
                if sign < 0:
                    spread(out.at[piece], piece, is_below, None)
                else:
                    spread(out.at[piece], piece, None, is_above)
                later = finishing[mark:]
                del finishing[mark:]
                ends.append(later)

        yield

    for there in range(outer):
        for step in range(1, inner):
            arrived(there * inner + place.beside(step))
    for needed, finish in finishing:
        if needed is None:
            finish()
        else:
            pl.when(needed)(finish)
    index = 0
    for away in range(1, outer):
        for sign in (-1, 1):
            there = line + sign * away
            fits = (there >= 0) if sign < 0 else (there < outer)
            later = ends[index]
            index += 1

            @pl.when(fits)
            def _(later=later):
                for needed, finish in later:
                    if needed is None:
                        finish()
                    else:
                        pl.when(needed)(finish)

    copy.wait()


def add_into(out, *terms):
    def one(i, carry):
        total = terms[0][i].astype(jnp.float32)
        for term in terms[1:]:
            total = total + term[i].astype(jnp.float32)
        out[i] = total.astype(out.dtype)
        return carry

    lax.fori_loop(0, out.shape[0], one, 0)


def reduce_blk_scratch(place_count, piece, dtype):
    inner = 4 if place_count >= 32 else 2
    outer = place_count // inner
    return [
        pltpu.VMEM((outer, inner - 1) + piece, dtype),
        pltpu.VMEM((outer + 1,) + piece, dtype),
        pltpu.VMEM((outer,) + piece, dtype),
        pltpu.SemaphoreType.DMA((outer, inner - 1)),
        pltpu.SemaphoreType.DMA((outer, inner - 1)),
        pltpu.SemaphoreType.DMA((outer,)),
        pltpu.SemaphoreType.DMA((outer + 1,)),
    ]


def reduce_blk(place, part, out, beside, along, held, side_sent, side_came, line_sent, line_came):
    outer, inner, line, side = place.outer, place.inner, place.line, place.side

    def side_copy(there, step):
        to = place.beside(step)
        return remote(
            part.at[there * inner + to],
            beside.at[there, inner - step - 1],
            side_sent.at[there, step - 1],
            side_came.at[there, inner - step - 1],
            place.at(line, to),
        )

    def line_copy(there, slot, to):
        return remote(
            held.at[there], along.at[slot], line_sent.at[there], line_came.at[slot], place.at(to, side)
        )

    def each(away, act):
        for sign in (-1, 1) if away else (0,):
            there = line + sign * away
            if away == 0:
                act(there, 0)
            else:
                fits = (there >= 0) if sign < 0 else (there < outer)
                pl.when(fits)(functools.partial(act, there, sign))

    def send_aside(there, sign):
        for step in range(1, inner):
            side_copy(there, step).start()

    def side_terms(there):
        for step in range(1, inner):
            side_copy(there, step).wait_recv()
        return [part.at[there * inner + side]] + [beside.at[there, k] for k in range(inner - 1)]

    def pass_on(there, sign):
        terms = side_terms(there)
        starts = (line == outer - 1) if sign < 0 else (line == 0)

        @pl.when(starts)
        def _():
            add_into(held.at[there], *terms)

        @pl.when(jnp.logical_not(starts))
        def _():
            line_copy(there, there, line + sign).wait_recv()
            add_into(held.at[there], along.at[there], *terms)

        slot = there if sign < 0 else jnp.where(there == line + 1, outer, there)
        line_copy(there, slot, line + sign).start()

    for away in range(outer - 1, -1, -1):
        each(away, send_aside)
    yield
    for away in range(outer - 1, 0, -1):
        each(away, pass_on)
        yield
    terms = side_terms(line)
    below, above = line > 0, line < outer - 1
    from_above, from_below = along.at[line], along.at[outer]

    @pl.when(above)
    def _():
        line_copy(line, line, line + 1).wait_recv()

    @pl.when(below)
    def _():
        line_copy(line, outer, line - 1).wait_recv()

    @pl.when(above & below)
    def _():
        add_into(out, from_above, from_below, *terms)

    @pl.when(above & jnp.logical_not(below))
    def _():
        add_into(out, from_above, *terms)

    @pl.when(jnp.logical_not(above) & below)
    def _():
        add_into(out, from_below, *terms)

    yield

    def end_line(there, sign):
        line_copy(there, there, line + sign).wait_send()

    for away in range(outer - 1, 0, -1):
        each(away, end_line)
    for there in range(outer):
        for step in range(1, inner):
            side_copy(there, step).wait_send()


def gather_group_sems():
    return [pltpu.SemaphoreType.DMA((3,)), pltpu.SemaphoreType.DMA((4,)), pltpu.SemaphoreType.DMA]


def gather_group(place, src, out, sent, came, own):
    copy = pltpu.make_async_copy(src, out.at[place.group], own)
    copy.start()
    mine, other = place.group, 2 * place.core + (1 - place.half)
    to_half = remote(src, out.at[mine], sent.at[0], came.at[mine], place.across())
    to_core = remote(src, out.at[mine], sent.at[1], came.at[mine], place.partner())
    to_half.start()
    to_core.start()
    yield
    remote(src, out.at[other], sent.at[0], came.at[other], place.across()).wait_recv()
    relay = remote(out.at[other], out.at[other], sent.at[2], came.at[other], place.partner())
    relay.start()
    yield
    for half in (0, 1):
        slot = 2 * (1 - place.core) + half
        remote(src, out.at[slot], sent.at[0], came.at[slot], place.partner()).wait_recv()
    to_half.wait_send()
    to_core.wait_send()
    relay.wait_send()
    copy.wait()


def reduce_group_scratch(piece, dtype):
    return [
        pltpu.VMEM((2,) + piece, dtype),
        pltpu.VMEM(piece, dtype),
        pltpu.VMEM(piece, dtype),
        pltpu.SemaphoreType.DMA((3,)),
        pltpu.SemaphoreType.DMA((3,)),
    ]


def reduce_group(place, part, out, from_core, from_half, held, sent, came):
    far = 2 * (1 - place.core) + (1 - place.half)
    near = 2 * (1 - place.core) + place.half
    first = remote(part.at[far], from_core.at[1], sent.at[0], came.at[0], place.partner())
    second = remote(part.at[near], from_core.at[0], sent.at[1], came.at[1], place.partner())
    first.start()
    second.start()
    yield
    first.wait_recv()
    add_into(held, part.at[2 * place.core + (1 - place.half)], from_core.at[1])
    third = remote(held, from_half, sent.at[2], came.at[2], place.across())
    third.start()
    yield
    second.wait_recv()
    third.wait_recv()
    add_into(out, part.at[place.group], from_core.at[0], from_half)
    first.wait_send()
    second.wait_send()
    third.wait_send()


def exchange_group_sems():
    return [pltpu.SemaphoreType.DMA((3,)), pltpu.SemaphoreType.DMA((4,)), pltpu.SemaphoreType.DMA]


def exchange_group(place, src, out, sent, came, own):
    mine = place.group
    copy = pltpu.make_async_copy(src.at[mine], out.at[mine], own)
    copy.start()
    core, half = place.core, place.half
    links = (
        (2 * (1 - core) + (1 - half), place.corner()),
        (2 * core + (1 - half), place.across()),
        (2 * (1 - core) + half, place.partner()),
    )
    copies = [
        remote(src.at[to], out.at[mine], sent.at[k], came.at[mine], device)
        for k, (to, device) in enumerate(links)
    ]
    for one in copies:
        one.start()
    yield
    for k, (peer, device) in enumerate(links):
        remote(src.at[peer], out.at[peer], sent.at[k], came.at[peer], device).wait_recv()
    for one in copies:
        one.wait_send()
    copy.wait()


def transfer(name, number, body, ins, outs, scratch, moved, out_spaces=None):
    spaces = out_spaces or [pl.ANY] * len(outs)
    return pl.pallas_call(
        body,
        name=name,
        out_shape=outs,
        in_specs=[pl.BlockSpec(memory_space=pltpu.VMEM)] * len(ins),
        out_specs=[pl.BlockSpec(memory_space=space) for space in spaces],
        scratch_shapes=scratch,
        compiler_params=pltpu.CompilerParams(
            collective_id=number, has_side_effects=True, vmem_limit_bytes=VMEM_LIMIT
        ),
        cost_estimate=pl.CostEstimate(flops=0, bytes_accessed=moved * 40, transcendentals=0),
    )(*ins)


def shape(dims, dtype):
    return jax.ShapeDtypeStruct(tuple(dims), dtype)


def slabs(rows):
    return math.gcd(rows, 16)


def all_gather_blk(value, count, number):
    def body(src, out, *sems):
        place = Place(count)
        greet(place, blk=True)
        together(gather_blk(place, src, out, *sems))

    return transfer(
        f"gather{number}",
        number,
        body,
        [value],
        [shape((count,) + value.shape, value.dtype)],
        gather_blk_sems(count),
        value.size * 2 * count,
    )[0]


def reduce_scatter_blk(value, count, number):
    piece = value.shape[1:]

    def body(part, out, *scratch):
        place = Place(count)
        greet(place, blk=True)
        together(reduce_blk(place, part, out, *scratch))

    return transfer(
        f"reduce{number}",
        number,
        body,
        [value],
        [shape(piece, jnp.float32)],
        reduce_blk_scratch(count, piece, value.dtype),
        value.size * 2,
        [pltpu.VMEM],
    )[0]


def gather_first(qkv, out_parts, tokens, gains, docs, count, number):
    names = 5

    def body(*refs):
        qkv_ref, out_ref, tok_ref, gain_ref, doc_ref = refs[:names]
        qkv_all, out_all, tok_all, gain_all, doc_all = refs[names : 2 * names]
        out_mine, gain_mine = refs[2 * names : 2 * names + 2]
        sems = list(refs[2 * names + 2 :])

        def take(amount):
            taken = sems[:amount]
            del sems[:amount]
            return taken

        place = Place(count)
        greet(place, blk=True, core=True, half=True, corner=True)

        def gain_task(near, far):
            yield from gather_blk(place, gain_ref, gain_mine, *near)
            yield from gather_group(place, gain_mine, gain_all, *far)

        def out_task(near, far):
            yield from exchange_group(place, out_ref, out_mine, *near)
            yield from gather_blk(place, out_mine, out_all, *far)

        def doc_task(sent, came, own):
            copy = pltpu.make_async_copy(doc_ref, doc_all.at[place.core], own)
            copy.start()
            send = remote(doc_ref, doc_all.at[place.core], sent, came, place.partner())
            send.start()
            yield
            remote(doc_ref, doc_all.at[1 - place.core], sent, came, place.partner()).wait_recv()
            send.wait_send()
            copy.wait()

        together(
            gain_task(take(3), take(3)),
            doc_task(*take(3)),
            gather_group(place, tok_ref, tok_all, *take(3)),
            gather_blk(place, qkv_ref, qkv_all, *take(3)),
            out_task(take(3), take(3)),
        )

    ins = [qkv, out_parts, tokens, gains, docs]
    return transfer(
        f"first{number}",
        number,
        body,
        ins,
        [
            shape((count,) + qkv.shape, qkv.dtype),
            shape((count,) + out_parts.shape, out_parts.dtype),
            shape((GROUPS,) + tokens.shape, tokens.dtype),
            shape((GROUPS, count) + gains.shape, gains.dtype),
            shape((2,) + docs.shape, docs.dtype),
        ],
        [
            pltpu.VMEM(out_parts.shape, out_parts.dtype),
            pltpu.VMEM((count,) + gains.shape, gains.dtype),
        ]
        + gather_blk_sems(count)
        + gather_group_sems()
        + [pltpu.SemaphoreType.DMA] * 3
        + gather_group_sems()
        + gather_blk_sems(count)
        + exchange_group_sems()
        + gather_blk_sems(count),
        (qkv.size + out_parts.size) * 2 * count,
    )


def reduce_last(qkv_part, out_part, norm_part, gain_part, count, number):
    out_piece, gain_piece = out_part.shape[1:], gain_part.shape[1:]
    qkv_piece, norm_piece = qkv_part.shape[1:], norm_part.shape[1:]

    def body(*refs):
        qkv_ref, out_ref, norm_ref, gain_ref = refs[:4]
        qkv_sum, out_sum, norm_sum, gain_sum = refs[4:8]
        out_mine, gain_mine = refs[8:10]
        rest = list(refs[10:])

        def take(amount):
            taken = rest[:amount]
            del rest[:amount]
            return taken

        place = Place(count)
        greet(place, blk=True, core=True, half=True, corner=True)

        def out_task(near, far):
            yield from reduce_blk(place, out_ref, out_mine, *near)
            yield from exchange_group(place, out_mine, out_sum, *far)

        def gain_task(near, far):
            yield from reduce_blk(place, gain_ref, gain_mine, *near)
            yield from reduce_group(place, gain_mine, gain_sum, *far)

        together(
            gain_task(take(7), take(5)),
            reduce_group(place, norm_ref, norm_sum, *take(5)),
            out_task(take(7), take(3)),
            reduce_blk(place, qkv_ref, qkv_sum, *take(7)),
        )

    return transfer(
        f"last{number}",
        number,
        body,
        [qkv_part, out_part, norm_part, gain_part],
        [
            shape(qkv_piece, jnp.float32),
            shape(out_piece, jnp.bfloat16),
            shape(norm_piece, jnp.float32),
            shape(gain_piece[1:], jnp.float32),
        ],
        [pltpu.VMEM(out_piece, jnp.bfloat16), pltpu.VMEM(gain_piece, jnp.float32)]
        + reduce_blk_scratch(count, gain_piece, jnp.float32)
        + reduce_group_scratch(gain_piece[1:], jnp.float32)
        + reduce_group_scratch(norm_piece, jnp.bfloat16)
        + reduce_blk_scratch(count, out_piece, jnp.bfloat16)
        + exchange_group_sems()
        + reduce_blk_scratch(count, qkv_piece, jnp.bfloat16),
        (qkv_part.size + out_part.size) * 2,
        [pltpu.VMEM] * 4,
    )


def all_gather_group(value, number):
    def body(src, out, *sems):
        place = Place(lax.axis_size("blk"))
        greet(place, core=True, half=True)
        together(gather_group(place, src, out, *sems))

    return transfer(
        f"group{number}",
        number,
        body,
        [value],
        [shape((GROUPS,) + value.shape, value.dtype)],
        gather_group_sems(),
        value.size * 8,
    )[0]


def reduce_scatter_group(value, number):
    piece = value.shape[1:]

    def body(part, out, *scratch):
        place = Place(lax.axis_size("blk"))
        greet(place, core=True, half=True)
        together(reduce_group(place, part, out, *scratch))

    return transfer(
        f"fold{number}",
        number,
        body,
        [value],
        [shape(piece, jnp.float32)],
        reduce_group_scratch(piece, value.dtype),
        value.size * 2,
        [pltpu.VMEM],
    )[0]


def attention_scores(q2, k, query_pos, query_doc, key_block, key_doc, rows):
    raw = lax.dot_general(q2, k, (((1,), (1,)), ((), ())), preferred_element_type=jnp.float32)
    capped = jnp.tanh(raw * (SCORE_SCALE / SOFT_CAP))
    key_pos = key_block * rows + lax.broadcasted_iota(jnp.int32, (1, rows), 1)
    visible = (key_pos <= query_pos) & (key_doc == query_doc)
    return capped, jnp.where(visible, jnp.exp(SOFT_CAP * capped), 0.0)


def attention_query(q_ref, doc_ref, here, count, rows):
    half = pl.program_id(1)
    block = half * count + here
    q2 = jnp.concatenate([q_ref[0, :, :HEAD_DIM], q_ref[0, :, HEAD_DIM:]], axis=0)
    inside = lax.broadcasted_iota(jnp.int32, (rows, 1), 0)
    position = block * rows + jnp.concatenate([inside, inside], axis=0)
    doc = jnp.concatenate([doc_ref[0], doc_ref[0]], axis=0)
    return block, q2, position, doc


def attention_forward_kernel(
    count, here_ref, q_ref, kv_ref, doc_ref, key_doc_ref, attn_ref, full_ref, total_ref, acc, tot
):
    rows = q_ref.shape[1]
    block, q2, position, doc = attention_query(q_ref, doc_ref, here_ref[0], count, rows)
    acc[...] = jnp.zeros_like(acc)
    tot[...] = jnp.zeros_like(tot)

    def one(key_block, carry):
        key_half = (key_block >= count).astype(jnp.int32)
        kv = kv_ref.at[key_block - key_half * count, key_half]
        _, weights = attention_scores(
            q2, kv[:, :HEAD_DIM], position, doc, key_block, key_doc_ref[0, key_block], rows
        )
        tot[...] += jnp.sum(weights, axis=-1, keepdims=True)
        acc[...] += jnp.dot(
            weights.astype(jnp.bfloat16), kv[:, HEAD_DIM:], preferred_element_type=jnp.float32
        )
        return carry

    lax.fori_loop(jnp.maximum(block - count, 0), block + 1, one, 0)
    attended = acc[...] / tot[...]
    attended = jnp.concatenate([attended[:rows], attended[rows:]], axis=1)
    full_ref[0] = attended
    attn_ref[0] = attended.astype(jnp.bfloat16)
    total_ref[0] = tot[...]


def attention_backward_kernel(
    count,
    here_ref,
    q_ref,
    kv_ref,
    doc_ref,
    key_doc_ref,
    grad_ref,
    full_ref,
    total_ref,
    dq_ref,
    dkv_ref,
    acc,
    key_acc,
):
    rows = q_ref.shape[1]
    half = pl.program_id(1)
    block, q2, position, doc = attention_query(q_ref, doc_ref, here_ref[0], count, rows)
    total = total_ref[0]
    grad = grad_ref[0].astype(jnp.float32)
    grad2 = jnp.concatenate([grad[:, :HEAD_DIM], grad[:, HEAD_DIM:]], axis=0)
    full2 = jnp.concatenate([full_ref[0, :, :HEAD_DIM], full_ref[0, :, HEAD_DIM:]], axis=0)
    total_grad = -jnp.sum(grad2 * full2, axis=-1, keepdims=True) / total
    sums_grad = (grad2 / total).astype(jnp.bfloat16)
    acc[...] = jnp.zeros_like(acc)

    @pl.when(half == 0)
    def _():
        def clear(i, carry):
            key_acc[i] = jnp.zeros(key_acc.shape[1:], jnp.float32)
            return carry

        lax.fori_loop(0, key_acc.shape[0], clear, 0)

    def one(key_block, carry):
        key_half = (key_block >= count).astype(jnp.int32)
        inner = key_block - key_half * count
        kv = kv_ref.at[inner, key_half]
        keys = kv[:, :HEAD_DIM]
        capped, weights = attention_scores(
            q2, keys, position, doc, key_block, key_doc_ref[0, key_block], rows
        )
        exp_grad = lax.dot_general(
            sums_grad, kv[:, HEAD_DIM:], (((1,), (1,)), ((), ())), preferred_element_type=jnp.float32
        )
        raw_grad = (
            weights * (exp_grad + total_grad) * (1.0 - capped * capped) * SCORE_SCALE
        ).astype(jnp.bfloat16)
        acc[...] += jnp.dot(raw_grad, keys, preferred_element_type=jnp.float32)
        over_rows = (((0,), (0,)), ((), ()))
        slot = inner * 2 + key_half
        key_acc[slot, :, :HEAD_DIM] += lax.dot_general(
            raw_grad, q2, over_rows, preferred_element_type=jnp.float32
        )
        key_acc[slot, :, HEAD_DIM:] += lax.dot_general(
            weights.astype(jnp.bfloat16), sums_grad, over_rows, preferred_element_type=jnp.float32
        )
        return carry

    lax.fori_loop(jnp.maximum(block - count, 0), block + 1, one, 0)
    dq = acc[...]
    dq_ref[0] = jnp.concatenate([dq[:rows], dq[rows:]], axis=1).astype(jnp.bfloat16)

    @pl.when(half == 1)
    def _():
        def put(i, carry):
            for k in (0, 1):
                dkv_ref[i, k] = key_acc[i * 2 + k].astype(jnp.bfloat16)
            return carry

        lax.fori_loop(0, count, put, 0)


def attention_specs(count, rows, width):
    query = pl.BlockSpec((1, rows, width), lambda s, h, here: (2 * s + h, 0, 0))
    keys = pl.BlockSpec((count, 2, rows, 2 * HEAD_DIM), lambda s, h, here: (0, s, 0, 0))
    doc = pl.BlockSpec((1, rows, 1), lambda s, h, here: (2 * s + h, 0, 0))
    key_doc = pl.BlockSpec((1, 2 * count, 1, rows), lambda s, h, here: (s, 0, 0, 0))
    total = pl.BlockSpec((1, REPS * rows, 1), lambda s, h, here: (2 * s + h, 0, 0))
    return query, keys, doc, key_doc, total


def attention_forward(here, q, kv, doc, key_doc):
    count, _, rows, _ = kv.shape
    width = REPS * HEAD_DIM
    query, keys, doc_spec, key_doc_spec, total = attention_specs(count, rows, width)
    return pl.pallas_call(
        functools.partial(attention_forward_kernel, count),
        name="attend",
        grid_spec=pltpu.PrefetchScalarGridSpec(
            num_scalar_prefetch=1,
            grid=(2, 2),
            in_specs=[query, keys, doc_spec, key_doc_spec],
            out_specs=[query, query, total],
            scratch_shapes=[
                pltpu.VMEM((REPS * rows, HEAD_DIM), jnp.float32),
                pltpu.VMEM((REPS * rows, 1), jnp.float32),
            ],
        ),
        out_shape=[
            shape((GROUPS, rows, width), jnp.bfloat16),
            shape((GROUPS, rows, width), jnp.float32),
            shape((GROUPS, REPS * rows, 1), jnp.float32),
        ],
        compiler_params=pltpu.CompilerParams(vmem_limit_bytes=VMEM_LIMIT),
        cost_estimate=pl.CostEstimate(flops=10**9, bytes_accessed=40 * 2**20, transcendentals=0),
    )(here, q, kv, doc, key_doc)


def attention_backward(here, q, kv, doc, key_doc, grad, full, totals):
    count, _, rows, _ = kv.shape
    width = REPS * HEAD_DIM
    query, keys, doc_spec, key_doc_spec, total = attention_specs(count, rows, width)
    return pl.pallas_call(
        functools.partial(attention_backward_kernel, count),
        name="attend_back",
        grid_spec=pltpu.PrefetchScalarGridSpec(
            num_scalar_prefetch=1,
            grid=(2, 2),
            in_specs=[query, keys, doc_spec, key_doc_spec, query, query, total],
            out_specs=[query, keys],
            scratch_shapes=[
                pltpu.VMEM((REPS * rows, HEAD_DIM), jnp.float32),
                pltpu.VMEM((2 * count, rows, 2 * HEAD_DIM), jnp.float32),
            ],
        ),
        out_shape=[shape((GROUPS, rows, width), jnp.bfloat16), shape(kv.shape, jnp.bfloat16)],
        compiler_params=pltpu.CompilerParams(vmem_limit_bytes=VMEM_LIMIT),
        cost_estimate=pl.CostEstimate(flops=2 * 10**9, bytes_accessed=80 * 2**20, transcendentals=0),
    )(here, q, kv, doc, key_doc, grad, full, totals)


def rms_scale(values, gain_row):
    return (
        values * lax.rsqrt(jnp.mean(values * values, axis=-1, keepdims=True) + NORM_EPS) * gain_row
    )


def gelu_tanh(values):
    return jax.nn.gelu(values, approximate=True)


def rope_tables(positions):
    half_width = HEAD_DIM // 2
    frequency = jnp.exp(
        jnp.arange(half_width, dtype=jnp.float32) * (-2.0 * math.log(ROPE_BASE) / HEAD_DIM)
    )
    angles = positions.astype(jnp.float32)[:, None] * frequency[None, :]
    cosine = jnp.concatenate([jnp.cos(angles), jnp.cos(angles)], axis=-1)
    sine = jnp.concatenate([jnp.sin(angles), jnp.sin(angles)], axis=-1)
    return cosine[:, None, :], sine[:, None, :]


def rotate(values, cosine, sine):
    half_width = HEAD_DIM // 2
    turned = jnp.concatenate([-values[..., half_width:], values[..., :half_width]], axis=-1)
    return values * cosine + turned * sine


def dot(left, right, contract):
    return lax.dot_general(left, right, (contract, ((), ())), preferred_element_type=jnp.float32)


LAST = ((1,), (1,))
PLAIN = ((1,), (0,))
FIRST = ((0,), (0,))


def shards(
    tokens, cotangent, segments, norm_gains, qkv_weight, out_weight, gate_up_weight, down_weight
):
    _, rows, width = tokens.shape
    count = lax.axis_size("blk")
    here = lax.axis_index("blk")
    mine = 2 * lax.axis_index("dp") + lax.axis_index("head")
    group_rows = GROUPS * rows
    head_width = REPS * HEAD_DIM
    bf16 = jnp.bfloat16
    slab = slabs(rows)
    piece = (rows // slab, slab, width)

    gate_up_all = lax.all_gather(gate_up_weight, ("dp", "head"), axis=0, tiled=True)
    down_all = lax.all_gather(down_weight, ("dp", "head"), axis=0, tiled=True)

    gain_rows = norm_gains.shape[0]
    gain_lanes = -(-gain_rows // 128) * 128
    gains_sent = jnp.pad(
        jnp.transpose(norm_gains).astype(jnp.float32), ((0, 4), (0, gain_lanes - gain_rows))
    )
    out_rows = out_weight.shape[0]
    out_sent = jnp.transpose(out_weight.reshape(out_rows, GROUPS, head_width), (1, 0, 2))
    qkv_rows = qkv_weight.shape[0]
    qkv_slab = slabs(qkv_rows)
    qkv_piece = (qkv_rows // qkv_slab, qkv_slab, width)
    qkv_all, out_all, tokens_all, gains_all, docs_all = gather_first(
        qkv_weight, out_sent, tokens[0], gains_sent, segments.reshape(-1, 128), count, 1
    )
    gains = jnp.transpose(gains_all[:, :, :4, :gain_rows], (2, 0, 1, 3)).reshape(4, width)
    qkv_head = qkv_all.reshape(count * qkv_rows, width)
    out_head = out_all.reshape(count, GROUPS, out_rows, head_width)
    out_head = jnp.transpose(out_head, (1, 0, 2, 3)).reshape(width, head_width)
    docs = docs_all.reshape(2, 2, count, rows)
    key_doc = docs.reshape(2, 2 * count, 1, rows)
    own_doc = lax.dynamic_index_in_dim(docs, here, 2, keepdims=False).reshape(GROUPS, rows, 1)
    here_one = here.reshape(1)

    group_tokens = tokens_all.reshape(group_rows, width).astype(jnp.float32)
    norm_one = rms_scale(group_tokens, gains[0]).astype(bf16)
    proj = dot(norm_one, qkv_head, LAST)
    inside = jnp.arange(rows, dtype=jnp.int32)
    position = jnp.concatenate([here * rows + inside, (count + here) * rows + inside])
    cosine, sine = rope_tables(jnp.concatenate([position, position]))
    proj = proj.reshape(group_rows, REPS + 2, HEAD_DIM)
    turned = rotate(proj[:, : REPS + 1], cosine, sine)
    sent = jnp.concatenate([turned, proj[:, REPS + 1 :]], axis=1).astype(bf16)
    queries = sent[:, :REPS].reshape(GROUPS, rows, head_width)
    own_kv = sent[:, REPS:].reshape(group_rows, 2 * HEAD_DIM)
    kv_slab = slabs(group_rows)
    kv_piece = (group_rows // kv_slab, kv_slab, 2 * HEAD_DIM)
    kv = all_gather_blk(own_kv, count, 2).reshape(count, GROUPS, rows, 2 * HEAD_DIM)
    attn, attended, totals = attention_forward(here_one, queries, kv, own_doc, key_doc)
    attn = attn.reshape(group_rows, head_width)
    branch_part = dot(attn, out_head, LAST).astype(bf16)
    branch = reduce_scatter_group(branch_part.reshape((GROUPS,) + piece), 3).reshape(rows, width)
    inputs = tokens[0].astype(jnp.float32)
    middle = inputs + rms_scale(branch, gains[1])
    norm_three = rms_scale(middle, gains[2]).astype(bf16)

    gate_all = gate_up_all[:, :width]
    up_all = gate_up_all[:, width:]
    norm_all = all_gather_blk(norm_three, count, 4).reshape(count * rows, width)
    gate = dot(norm_all, gate_all, LAST)
    up = dot(norm_all, up_all, LAST)
    hidden = (gelu_tanh(gate) * up).astype(bf16)
    ffn_part = dot(hidden, down_all, PLAIN).astype(bf16)
    ffn_out = reduce_scatter_blk(ffn_part.reshape((count,) + piece), count, 5).reshape(rows, width)
    output = (middle + rms_scale(ffn_out, gains[3])).astype(bf16)[None]

    out_cotangent = cotangent[0].astype(jnp.float32)
    _, post_ffn_back = jax.vjp(rms_scale, ffn_out, gains[3])
    ffn_grad, gain_grad_four = post_ffn_back(out_cotangent)
    grad_all = all_gather_blk(ffn_grad.astype(bf16), count, 6).reshape(count * rows, width)
    activated, gelu_back = jax.vjp(gelu_tanh, gate)
    hidden_grad = dot(grad_all, down_all, LAST)
    gate_grad = gelu_back(hidden_grad * up)[0].astype(bf16)
    up_grad = (hidden_grad * activated).astype(bf16)
    norm_part = dot(gate_grad, gate_all, PLAIN) + dot(up_grad, up_all, PLAIN)
    norm_three_grad = reduce_scatter_blk(
        norm_part.astype(bf16).reshape((count,) + piece), count, 7
    ).reshape(rows, width)
    down_part = dot(hidden, grad_all, FIRST).astype(bf16)
    gate_up_part = jnp.concatenate(
        [dot(gate_grad, norm_all, FIRST), dot(up_grad, norm_all, FIRST)], axis=1
    ).astype(bf16)
    gate_up_grad = lax.psum_scatter(
        gate_up_part, ("dp", "head"), scatter_dimension=0, tiled=True
    ).astype(jnp.float32)
    down_grad = lax.psum_scatter(
        down_part, ("dp", "head"), scatter_dimension=0, tiled=True
    ).astype(jnp.float32)

    _, pre_ffn_back = jax.vjp(rms_scale, middle, gains[2])
    middle_part, gain_grad_three = pre_ffn_back(norm_three_grad)
    middle_grad = out_cotangent + middle_part
    _, post_attn_back = jax.vjp(rms_scale, branch, gains[1])
    branch_grad, gain_grad_two = post_attn_back(middle_grad)
    branch_all = all_gather_group(branch_grad.astype(bf16), 8).reshape(group_rows, width)
    attn_grad = dot(branch_all, out_head, PLAIN).astype(bf16).reshape(GROUPS, rows, head_width)
    out_part = dot(branch_all, attn, FIRST).astype(bf16)
    out_part = jnp.transpose(out_part.reshape(GROUPS, count, out_rows, head_width), (1, 0, 2, 3))
    dq, dkv_part = attention_backward(
        here_one, queries, kv, own_doc, key_doc, attn_grad, attended, totals
    )
    dkv = reduce_scatter_blk(dkv_part.reshape((count,) + kv_piece), count, 9)
    sent_grad = jnp.concatenate(
        [
            dq.reshape(group_rows, REPS, HEAD_DIM),
            dkv.astype(bf16).reshape(group_rows, 2, HEAD_DIM),
        ],
        axis=1,
    ).astype(jnp.float32)
    unturned = rotate(sent_grad[:, : REPS + 1], cosine, -sine)
    proj_grad = (
        jnp.concatenate([unturned, sent_grad[:, REPS + 1 :]], axis=1)
        .astype(bf16)
        .reshape(group_rows, (REPS + 2) * HEAD_DIM)
    )
    qkv_part = dot(proj_grad, norm_one, FIRST).astype(bf16)
    norm_one_part = dot(proj_grad, qkv_head, PLAIN)
    _, gain_back = jax.vjp(lambda gain: rms_scale(group_tokens, gain), gains[0])
    (gain_grad_one,) = gain_back(norm_one_part)
    gain_part = jnp.stack([gain_grad_one, gain_grad_two, gain_grad_three, gain_grad_four])
    gain_part = jnp.transpose(gain_part.reshape(4, GROUPS, count, gain_rows), (2, 1, 0, 3))
    gain_part = jnp.pad(gain_part, ((0, 0), (0, 0), (0, 4), (0, gain_lanes - gain_rows)))
    qkv_grad, out_grad, norm_one_grad, gain_grad = reduce_last(
        qkv_part.reshape((count,) + qkv_piece),
        out_part,
        norm_one_part.astype(bf16).reshape((GROUPS,) + piece),
        gain_part[:, :, None],
        count,
        10,
    )
    qkv_grad = qkv_grad.reshape(qkv_rows, width)
    out_grad = (
        jnp.transpose(out_grad, (1, 0, 2)).reshape(out_rows, GROUPS * head_width).astype(jnp.float32)
    )
    gain_grad = jnp.transpose(gain_grad.reshape(8, gain_lanes)[:4, :gain_rows])
    _, pre_attn_back = jax.vjp(lambda values: rms_scale(values, gains[0]), inputs)
    (input_part,) = pre_attn_back(norm_one_grad.reshape(rows, width))
    tokens_grad = (middle_grad + input_part).astype(bf16)[None]
    return (output, tokens_grad, gain_grad, qkv_grad, out_grad, gate_up_grad, down_grad)


def solution(mesh):
    whole = ("dp", "head", "blk")
    return jax.shard_map(
        shards,
        mesh=mesh,
        in_specs=(
            P("dp", ("head", "blk"), None),
            P("dp", ("head", "blk"), None),
            P("dp", None),
            P(whole, None),
            P(whole, None),
            P(whole, None),
            P(whole, None),
            P(whole, None),
        ),
        out_specs=(
            P("dp", ("head", "blk"), None),
            P("dp", ("head", "blk"), None),
            P(whole, None),
            P(whole, None),
            P(whole, None),
            P(whole, None),
            P(whole, None),
        ),
        check_vma=False,
    )
```

```python
import functools
import math

import jax
import jax.numpy as jnp
from jax import lax
from jax.experimental import pallas as pl
from jax.experimental.pallas import tpu as pltpu
from jax.sharding import PartitionSpec as P

HEADS = 8
KV_HEADS = 4
HEAD_DIM = 256
REPS = HEADS // KV_HEADS
GROUPS = 4
SOFT_CAP = 50.0
NORM_EPS = 1e-06
ROPE_BASE = 10000.0
SCORE_SCALE = HEAD_DIM ** (-0.5)

MESH = pl.DeviceIdType.MESH
VMEM_LIMIT = 60 * 1024 * 1024


class Place:
    def __init__(self, count):
        self.count = count
        self.inner = 4 if count >= 32 else 2
        self.outer = count // self.inner
        self.here = lax.axis_index("blk")
        self.line = self.here // self.inner
        self.side = lax.rem(self.here, self.inner)
        self.core = lax.axis_index("dp")
        self.half = lax.axis_index("head")
        self.group = 2 * self.core + self.half

    def near(self, k):
        orders = [near_order(self.outer, line)[k] for line in range(self.outer)]
        found = jnp.int32(orders[0])
        for line in range(1, self.outer):
            found = jnp.where(self.line == line, jnp.int32(orders[line]), found)
        return found

    def at(self, line, side):
        return {"blk": line * self.inner + side}

    def beside(self, step):
        return lax.rem(self.side + step, self.inner)

    def partner(self):
        return {"dp": 1 - self.core}

    def across(self):
        return {"head": 1 - self.half}

    def corner(self):
        return {"dp": 1 - self.core, "head": 1 - self.half}


def remote(src, dst, sent, came, device):
    return pltpu.make_async_remote_copy(
        src_ref=src, dst_ref=dst, send_sem=sent, recv_sem=came, device_id=device, device_id_type=MESH
    )


def greet(place, blk=False, core=False, half=False, corner=False):
    sem = pltpu.get_barrier_semaphore()
    amount = jnp.int32(0)

    def hello(device):
        pl.semaphore_signal(sem, inc=1, device_id=device, device_id_type=MESH)

    if blk:
        up, down = place.line < place.outer - 1, place.line > 0
        pl.when(up)(lambda: hello(place.at(place.line + 1, place.side)))
        pl.when(down)(lambda: hello(place.at(place.line - 1, place.side)))
        amount = amount + up.astype(jnp.int32) + down.astype(jnp.int32) + (place.inner - 1)
        for step in range(1, place.inner):
            hello(place.at(place.line, place.beside(step)))
    for wanted, device in (
        (core, place.partner()),
        (half, place.across()),
        (corner, place.corner()),
    ):
        if wanted:
            hello(device)
            amount = amount + 1
    pl.semaphore_wait(sem, amount)


def together(*tasks):
    tasks = list(tasks)
    while tasks:
        for task in list(tasks):
            try:
                next(task)
            except StopIteration:
                tasks.remove(task)


def near_order(outer, line):
    return sorted(range(outer), key=lambda other: (abs(other - line), other))


def gather_blk_sems(place_count):
    inner = 4 if place_count >= 32 else 2
    return [
        pltpu.SemaphoreType.DMA((1 + inner, place_count)),
        pltpu.SemaphoreType.DMA((place_count,)),
        pltpu.SemaphoreType.DMA,
    ]


class GatherBlk:
    def __init__(self, place, src, view, sent, came, own):
        self.place, self.src, self.view, self.sent, self.came = place, src, view, sent, came
        self.copy = pltpu.make_async_copy(src, view(place.here), own)

    def sends(self, k):
        place = self.place
        there = place.near(k)
        piece = there * place.inner + place.side
        src = self.src if k == 0 else self.view(piece)

        def send(kind, device):
            return remote(
                src, self.view(piece), self.sent.at[kind, piece], self.came.at[piece], device
            )

        line, side = place.line, place.side
        up = (there <= line) & (line < place.outer - 1)
        down = (there >= line) & (line > 0)
        return (
            [
                (up, lambda: send(0, place.at(line + 1, side))),
                (down, lambda: send(1, place.at(line - 1, side))),
            ],
            [send(1 + step, place.at(line, place.beside(step))) for step in range(1, place.inner)],
        )

    def forward(self, k):
        along, aside = self.sends(k)
        for needed, make in along:
            pl.when(needed)(lambda make=make: make().start())
        for one in aside:
            one.start()

    def start(self):
        self.copy.start()
        self.forward(0)

    def arrived(self, piece):
        place = self.place
        remote(
            self.src,
            self.view(piece),
            self.sent.at[0, piece],
            self.came.at[piece],
            place.at(place.line, place.beside(1)),
        ).wait_recv()

    def pass_on(self, k):
        self.arrived(self.place.near(k) * self.place.inner + self.place.side)
        self.forward(k)

    def beside_arrived(self, k):
        for step in range(1, self.place.inner):
            self.arrived(self.place.near(k) * self.place.inner + self.place.beside(step))

    def finish(self):
        for k in range(self.place.outer):
            along, aside = self.sends(k)
            for needed, make in along:
                pl.when(needed)(lambda make=make: make().wait_send())
            for one in aside:
                one.wait_send()


def gather_blk(place, src, view, sent, came, own):
    if not callable(view):
        out = view
        view = lambda piece: out.at[piece]
    work = GatherBlk(place, src, view, sent, came, own)
    work.start()
    yield
    for k in range(1, place.outer):
        work.pass_on(k)
        yield
    for k in range(place.outer):
        work.beside_arrived(k)
    work.finish()
    work.copy.wait()


def add_into(out, *terms):
    def one(i, carry):
        total = terms[0][i].astype(jnp.float32)
        for term in terms[1:]:
            total = total + term[i].astype(jnp.float32)
        out[i] = total.astype(out.dtype)
        return carry

    lax.fori_loop(0, out.shape[0], one, 0)


def reduce_blk_scratch(place_count, piece, dtype):
    inner = 4 if place_count >= 32 else 2
    outer = place_count // inner
    return [
        pltpu.VMEM((outer, inner - 1) + piece, dtype),
        pltpu.VMEM((outer + 1,) + piece, dtype),
        pltpu.VMEM((outer,) + piece, dtype),
        pltpu.SemaphoreType.DMA((outer, inner - 1)),
        pltpu.SemaphoreType.DMA((outer, inner - 1)),
        pltpu.SemaphoreType.DMA((outer,)),
        pltpu.SemaphoreType.DMA((outer + 1,)),
    ]


class ReduceBlk:
    def __init__(
        self, place, view, out, beside, along, held, side_sent, side_came, line_sent, line_came
    ):
        self.place, self.view, self.out = place, view, out
        self.beside, self.along, self.held = beside, along, held
        self.side_sems, self.line_sems = (side_sent, side_came), (line_sent, line_came)

    def far(self, k):
        return self.place.near(self.place.outer - 1 - k)

    def side_copy(self, there, step):
        place = self.place
        to = place.beside(step)
        return remote(
            self.view(there * place.inner + to),
            self.beside.at[there, place.inner - step - 1],
            self.side_sems[0].at[there, step - 1],
            self.side_sems[1].at[there, place.inner - step - 1],
            place.at(place.line, to),
        )

    def line_copy(self, there, slot, to):
        return remote(
            self.held.at[there],
            self.along.at[slot],
            self.line_sems[0].at[there],
            self.line_sems[1].at[slot],
            self.place.at(to, self.place.side),
        )

    def send(self, k):
        for step in range(1, self.place.inner):
            self.side_copy(self.far(k), step).start()

    def terms(self, there):
        place = self.place
        for step in range(1, place.inner):
            self.side_copy(there, step).wait_recv()
        own = self.view(there * place.inner + place.side)
        return [own] + [self.beside.at[there, k] for k in range(place.inner - 1)]

    def onward(self, there):
        line, outer = self.place.line, self.place.outer
        to = jnp.where(there < line, line - 1, line + 1)
        slot = jnp.where(there == line + 1, outer, there)
        return self.line_copy(there, slot, to)

    def pass_on(self, k):
        place = self.place
        line, outer = place.line, place.outer
        there = self.far(k)
        terms = self.terms(there)
        starts = ((there < line) & (line == outer - 1)) | ((there > line) & (line == 0))

        @pl.when(starts)
        def _():
            add_into(self.held.at[there], *terms)

        @pl.when(jnp.logical_not(starts))
        def _():
            back = jnp.where(there < line, line + 1, line - 1)
            self.line_copy(there, there, back).wait_recv()
            add_into(self.held.at[there], self.along.at[there], *terms)

        self.onward(there).start()

    def last(self):
        place = self.place
        line, outer = place.line, place.outer
        terms = self.terms(line)
        below, above = line > 0, line < outer - 1
        from_above, from_below = self.along.at[line], self.along.at[outer]

        @pl.when(above)
        def _():
            self.line_copy(line, line, line + 1).wait_recv()

        @pl.when(below)
        def _():
            self.line_copy(line, outer, line - 1).wait_recv()

        @pl.when(above & below)
        def _():
            add_into(self.out, from_above, from_below, *terms)

        @pl.when(above & jnp.logical_not(below))
        def _():
            add_into(self.out, from_above, *terms)

        @pl.when(jnp.logical_not(above) & below)
        def _():
            add_into(self.out, from_below, *terms)

    def finish(self):
        for k in range(self.place.outer):
            if k < self.place.outer - 1:
                self.onward(self.far(k)).wait_send()
            for step in range(1, self.place.inner):
                self.side_copy(self.far(k), step).wait_send()


def reduce_blk(place, view, out, *scratch):
    if not callable(view):
        part = view
        view = lambda piece: part.at[piece]
    work = ReduceBlk(place, view, out, *scratch)
    for k in range(place.outer):
        work.send(k)
    yield
    for k in range(place.outer - 1):
        work.pass_on(k)
        yield
    work.last()
    yield
    work.finish()


def gather_group_sems():
    return [pltpu.SemaphoreType.DMA((3,)), pltpu.SemaphoreType.DMA((4,)), pltpu.SemaphoreType.DMA]


def gather_group(place, src, out, sent, came, own):
    copy = pltpu.make_async_copy(src, out.at[place.group], own)
    copy.start()
    mine, other = place.group, 2 * place.core + (1 - place.half)
    to_half = remote(src, out.at[mine], sent.at[0], came.at[mine], place.across())
    to_core = remote(src, out.at[mine], sent.at[1], came.at[mine], place.partner())
    to_half.start()
    to_core.start()
    yield
    remote(src, out.at[other], sent.at[0], came.at[other], place.across()).wait_recv()
    relay = remote(out.at[other], out.at[other], sent.at[2], came.at[other], place.partner())
    relay.start()
    yield
    for half in (0, 1):
        slot = 2 * (1 - place.core) + half
        remote(src, out.at[slot], sent.at[0], came.at[slot], place.partner()).wait_recv()
    to_half.wait_send()
    to_core.wait_send()
    relay.wait_send()
    copy.wait()


def reduce_group_scratch(piece, dtype):
    return [
        pltpu.VMEM((2,) + piece, dtype),
        pltpu.VMEM(piece, dtype),
        pltpu.VMEM(piece, dtype),
        pltpu.SemaphoreType.DMA((3,)),
        pltpu.SemaphoreType.DMA((3,)),
    ]


def reduce_group(place, part, out, from_core, from_half, held, sent, came):
    far = 2 * (1 - place.core) + (1 - place.half)
    near = 2 * (1 - place.core) + place.half
    first = remote(part.at[far], from_core.at[1], sent.at[0], came.at[0], place.partner())
    second = remote(part.at[near], from_core.at[0], sent.at[1], came.at[1], place.partner())
    first.start()
    second.start()
    yield
    first.wait_recv()
    add_into(held, part.at[2 * place.core + (1 - place.half)], from_core.at[1])
    third = remote(held, from_half, sent.at[2], came.at[2], place.across())
    third.start()
    yield
    second.wait_recv()
    third.wait_recv()
    add_into(out, part.at[place.group], from_core.at[0], from_half)
    first.wait_send()
    second.wait_send()
    third.wait_send()


def exchange_group_sems():
    return [pltpu.SemaphoreType.DMA((3,)), pltpu.SemaphoreType.DMA((4,)), pltpu.SemaphoreType.DMA]


def exchange_group(place, src, out, sent, came, own):
    mine = place.group
    copy = pltpu.make_async_copy(src.at[mine], out.at[mine], own)
    copy.start()
    core, half = place.core, place.half
    links = (
        (2 * (1 - core) + (1 - half), place.corner()),
        (2 * core + (1 - half), place.across()),
        (2 * (1 - core) + half, place.partner()),
    )
    copies = [
        remote(src.at[to], out.at[mine], sent.at[k], came.at[mine], device)
        for k, (to, device) in enumerate(links)
    ]
    for one in copies:
        one.start()
    yield
    for k, (peer, device) in enumerate(links):
        remote(src.at[peer], out.at[peer], sent.at[k], came.at[peer], device).wait_recv()
    for one in copies:
        one.wait_send()
    copy.wait()


def transfer(name, number, body, ins, outs, scratch, moved, out_spaces=None):
    spaces = out_spaces or [pl.ANY] * len(outs)
    return pl.pallas_call(
        body,
        name=name,
        out_shape=outs,
        in_specs=[pl.BlockSpec(memory_space=pltpu.VMEM)] * len(ins),
        out_specs=[pl.BlockSpec(memory_space=space) for space in spaces],
        scratch_shapes=scratch,
        compiler_params=pltpu.CompilerParams(
            collective_id=number, has_side_effects=True, vmem_limit_bytes=VMEM_LIMIT
        ),
        cost_estimate=pl.CostEstimate(flops=0, bytes_accessed=moved * 40, transcendentals=0),
    )(*ins)


def shape(dims, dtype):
    return jax.ShapeDtypeStruct(tuple(dims), dtype)


def slabs(rows):
    return math.gcd(rows, 16)


def all_gather_blk(value, count, number):
    def body(src, out, *sems):
        place = Place(count)
        greet(place, blk=True)
        together(gather_blk(place, src, out, *sems))

    return transfer(
        f"gather{number}",
        number,
        body,
        [value],
        [shape((count,) + value.shape, value.dtype)],
        gather_blk_sems(count),
        value.size * 2 * count,
    )[0]


def reduce_scatter_blk(value, count, number):
    piece = value.shape[1:]

    def body(part, out, *scratch):
        place = Place(count)
        greet(place, blk=True)
        together(reduce_blk(place, part, out, *scratch))

    return transfer(
        f"reduce{number}",
        number,
        body,
        [value],
        [shape(piece, jnp.float32)],
        reduce_blk_scratch(count, piece, value.dtype),
        value.size * 2,
        [pltpu.VMEM],
    )[0]


def gather_first(qkv, out_parts, tokens, gains, docs, count, number):
    names = 5

    def body(*refs):
        qkv_ref, out_ref, tok_ref, gain_ref, doc_ref = refs[:names]
        qkv_all, out_all, tok_all, gain_all, doc_all = refs[names : 2 * names]
        out_mine, gain_mine = refs[2 * names : 2 * names + 2]
        sems = list(refs[2 * names + 2 :])

        def take(amount):
            taken = sems[:amount]
            del sems[:amount]
            return taken

        place = Place(count)
        greet(place, blk=True, core=True, half=True, corner=True)

        def gain_task(near, far):
            yield from gather_blk(place, gain_ref, gain_mine, *near)
            yield from gather_group(place, gain_mine, gain_all, *far)

        def out_task(near, far):
            yield from exchange_group(place, out_ref, out_mine, *near)
            yield from gather_blk(place, out_mine, out_all, *far)

        def doc_task(sent, came, own):
            copy = pltpu.make_async_copy(doc_ref, doc_all.at[place.core], own)
            copy.start()
            send = remote(doc_ref, doc_all.at[place.core], sent, came, place.partner())
            send.start()
            yield
            remote(doc_ref, doc_all.at[1 - place.core], sent, came, place.partner()).wait_recv()
            send.wait_send()
            copy.wait()

        together(
            gain_task(take(3), take(3)),
            doc_task(*take(3)),
            gather_group(place, tok_ref, tok_all, *take(3)),
            gather_blk(place, qkv_ref, qkv_all, *take(3)),
            out_task(take(3), take(3)),
        )

    ins = [qkv, out_parts, tokens, gains, docs]
    return transfer(
        f"first{number}",
        number,
        body,
        ins,
        [
            shape((count,) + qkv.shape, qkv.dtype),
            shape((count,) + out_parts.shape, out_parts.dtype),
            shape((GROUPS,) + tokens.shape, tokens.dtype),
            shape((GROUPS, count) + gains.shape, gains.dtype),
            shape((2,) + docs.shape, docs.dtype),
        ],
        [
            pltpu.VMEM(out_parts.shape, out_parts.dtype),
            pltpu.VMEM((count,) + gains.shape, gains.dtype),
        ]
        + gather_blk_sems(count)
        + gather_group_sems()
        + [pltpu.SemaphoreType.DMA] * 3
        + gather_group_sems()
        + gather_blk_sems(count)
        + exchange_group_sems()
        + gather_blk_sems(count),
        (qkv.size + out_parts.size) * 2 * count,
    )


def reduce_last(qkv_part, out_part, norm_part, gain_part, count, number):
    out_piece, gain_piece = out_part.shape[1:], gain_part.shape[1:]
    qkv_piece, norm_piece = qkv_part.shape[1:], norm_part.shape[1:]

    def body(*refs):
        qkv_ref, out_ref, norm_ref, gain_ref = refs[:4]
        qkv_sum, out_sum, norm_sum, gain_sum = refs[4:8]
        out_mine, gain_mine = refs[8:10]
        rest = list(refs[10:])

        def take(amount):
            taken = rest[:amount]
            del rest[:amount]
            return taken

        place = Place(count)
        greet(place, blk=True, core=True, half=True, corner=True)

        def out_task(near, far):
            yield from reduce_blk(place, out_ref, out_mine, *near)
            yield from exchange_group(place, out_mine, out_sum, *far)

        def gain_task(near, far):
            yield from reduce_blk(place, gain_ref, gain_mine, *near)
            yield from reduce_group(place, gain_mine, gain_sum, *far)

        together(
            gain_task(take(7), take(5)),
            reduce_group(place, norm_ref, norm_sum, *take(5)),
            out_task(take(7), take(3)),
            reduce_blk(place, qkv_ref, qkv_sum, *take(7)),
        )

    return transfer(
        f"last{number}",
        number,
        body,
        [qkv_part, out_part, norm_part, gain_part],
        [
            shape(qkv_piece, jnp.float32),
            shape(out_piece, jnp.bfloat16),
            shape(norm_piece, jnp.float32),
            shape(gain_piece[1:], jnp.float32),
        ],
        [pltpu.VMEM(out_piece, jnp.bfloat16), pltpu.VMEM(gain_piece, jnp.float32)]
        + reduce_blk_scratch(count, gain_piece, jnp.float32)
        + reduce_group_scratch(gain_piece[1:], jnp.float32)
        + reduce_group_scratch(norm_piece, jnp.bfloat16)
        + reduce_blk_scratch(count, out_piece, jnp.bfloat16)
        + exchange_group_sems()
        + reduce_blk_scratch(count, qkv_piece, jnp.bfloat16),
        (qkv_part.size + out_part.size) * 2,
        [pltpu.VMEM] * 4,
    )


def all_gather_group(value, number):
    def body(src, out, *sems):
        place = Place(lax.axis_size("blk"))
        greet(place, core=True, half=True)
        together(gather_group(place, src, out, *sems))

    return transfer(
        f"group{number}",
        number,
        body,
        [value],
        [shape((GROUPS,) + value.shape, value.dtype)],
        gather_group_sems(),
        value.size * 8,
    )[0]


def reduce_scatter_group(value, number):
    piece = value.shape[1:]

    def body(part, out, *scratch):
        place = Place(lax.axis_size("blk"))
        greet(place, core=True, half=True)
        together(reduce_group(place, part, out, *scratch))

    return transfer(
        f"fold{number}",
        number,
        body,
        [value],
        [shape(piece, jnp.float32)],
        reduce_group_scratch(piece, value.dtype),
        value.size * 2,
        [pltpu.VMEM],
    )[0]


def dot(left, right, contract):
    return lax.dot_general(left, right, (contract, ((), ())), preferred_element_type=jnp.float32)


LAST = ((1,), (1,))
PLAIN = ((1,), (0,))
FIRST = ((0,), (0,))


LANES = 128
GELU_A = math.sqrt(2.0 / math.pi)
GELU_B = 0.044715


def feed_forward_fits(count, rows, width, hidden):
    inner = 4 if count >= 32 else 2
    outer = count // inner
    tile = rows * width * 2
    weights = 3 * hidden * width * 2
    kept = count * rows * 3 * hidden * 2
    total = weights + kept + tile * (3 * count + outer * (inner - 1) + 2 * outer + 1) + 9 * tile
    total += 3 * LANES * (count * rows + 2 * width) * 2
    return total < 58 * 2**20 and hidden % (3 * LANES) == 0 and width % 256 == 0


def feed_forward_kernel(
    count,
    branch_ref,
    token_ref,
    cot_ref,
    gain_ref,
    gate_up_hbm,
    down_hbm,
    out_ref,
    middle_grad_ref,
    branch_grad_ref,
    gain_grad_ref,
    gate_up_grad_hbm,
    down_grad_hbm,
    w_gate_up,
    w_down,
    norm_all,
    grad_all,
    act,
    hidden,
    part,
    middle,
    norm_own,
    grad_own,
    total,
    turned,
    staged,
    beside,
    along,
    held,
    w_sems,
    out_sems,
    *sems,
):
    place = Place(count)
    rows, width = norm_all.shape[1:]
    units = hidden.shape[1]
    chunks = units // LANES
    inner, outer = place.inner, place.outer
    slab = branch_ref.shape[1]
    steps = rows // slab
    columns = width // 256
    pair = inner * rows
    sems = list(sems)

    def take(amount):
        taken = sems[:amount]
        del sems[:amount]
        return taken

    def weight_copies(i):
        units_at = pl.ds(pl.multiple_of(i * LANES, LANES), LANES)
        return [
            pltpu.make_async_copy(
                gate_up_hbm.at[units_at, pl.ds(0, width)],
                w_gate_up.at[i, pl.ds(0, LANES)],
                w_sems.at[3 * i],
            ),
            pltpu.make_async_copy(
                gate_up_hbm.at[units_at, pl.ds(width, width)],
                w_gate_up.at[i, pl.ds(LANES, LANES)],
                w_sems.at[3 * i + 1],
            ),
            pltpu.make_async_copy(down_hbm.at[units_at], w_down.at[units_at], w_sems.at[3 * i + 2]),
        ]

    def start_weights(i, carry):
        for copy in weight_copies(i):
            copy.start()
        return carry

    def wait_weights(i, carry):
        for copy in weight_copies(i):
            copy.wait()
        return carry

    lax.fori_loop(0, chunks, start_weights, 0)

    def scale_of(values):
        return lax.rsqrt(jnp.mean(values * values, axis=-1, keepdims=True) + NORM_EPS)

    def slab_rows(i):
        return pl.ds(pl.multiple_of(i * slab, slab), slab)

    def before(i, carry):
        value = branch_ref[i]
        mid = token_ref[i].astype(jnp.float32) + value * scale_of(value) * gain_ref[1:2]
        middle[i] = mid
        norm_own[slab_rows(i)] = (mid * scale_of(mid) * gain_ref[2:3]).astype(jnp.bfloat16)
        return carry

    lax.fori_loop(0, steps, before, 0)
    greet(place, blk=True)

    def pair_rows(k):
        return pl.ds(pl.multiple_of(place.near(k) * pair, pair), pair)

    def pair_pieces(k):
        return pl.ds(place.near(k) * inner, inner)

    def column(n):
        return pl.ds(pl.multiple_of(n * 256, 256), 256)

    def put_part(k, n, value):
        split = value.astype(jnp.bfloat16).reshape((inner, steps, slab, 256))
        part[pair_pieces(k), :, :, column(n)] = split

    gather = GatherBlk(place, norm_own, lambda i: norm_all.at[i], *take(3))
    gather.start()
    lax.fori_loop(0, chunks, wait_weights, 0)
    for k in range(outer):
        if k == 0:
            gather.copy.wait()
        if k + 1 < outer:
            gather.pass_on(k + 1)
        gather.beside_arrived(k)
        at = pair_rows(k)

        def up_chunk(j, carry, k=k, at=at):
            x = norm_all[pair_pieces(k)].reshape(pair, width)
            both = dot(x, w_gate_up[j], LAST)
            act[at, column(j)] = both.astype(jnp.bfloat16)
            gate, up = both[:, :LANES], both[:, LANES:]
            bent = 0.5 * gate * (1.0 + jnp.tanh(GELU_A * (gate + GELU_B * (gate * gate * gate))))
            hidden[at, pl.ds(pl.multiple_of(j * LANES, LANES), LANES)] = (bent * up).astype(
                jnp.bfloat16
            )
            return carry

        lax.fori_loop(0, chunks, up_chunk, 0)

        def down_chunk(n, carry, k=k, at=at):
            put_part(k, n, dot(hidden[at, :], w_down[:, column(n)], PLAIN))
            return carry

        lax.fori_loop(0, columns, down_chunk, 0)
    gather.finish()
    reduce = ReduceBlk(place, lambda i: part.at[i], total, beside, along, held, *take(4))
    for k in range(outer):
        reduce.send(k)
    for k in range(outer - 1):
        reduce.pass_on(k)
    reduce.last()

    gain_grad_ref[...] = jnp.zeros_like(gain_grad_ref)

    def norm_back(value, gain, incoming):
        scale = scale_of(value)
        lifted = incoming * gain
        pull = jnp.mean(lifted * value, axis=-1, keepdims=True)
        gain_grad = jnp.sum(incoming * value * scale, axis=0, keepdims=True)
        return scale * lifted - value * (scale * scale * scale) * pull, gain_grad

    def between(i, carry):
        value, cot = total[i], cot_ref[i].astype(jnp.float32)
        gain = gain_ref[3:4]
        out_ref[i] = (middle[i] + value * scale_of(value) * gain).astype(jnp.bfloat16)
        grad, gain_grad = norm_back(value, gain, cot)
        gain_grad_ref[3:4] += gain_grad
        grad_own[slab_rows(i)] = grad.astype(jnp.bfloat16)
        return carry

    lax.fori_loop(0, steps, between, 0)
    reduce.finish()

    gather = GatherBlk(place, grad_own, lambda i: grad_all.at[i], *take(3))
    gather.start()
    for k in range(outer):
        if k == 0:
            gather.copy.wait()
        if k + 1 < outer:
            gather.pass_on(k + 1)
        gather.beside_arrived(k)
        at = pair_rows(k)

        def back_chunk(j, carry, k=k, at=at):
            g = grad_all[pair_pieces(k)].reshape(pair, width)
            units_at = pl.ds(pl.multiple_of(j * LANES, LANES), LANES)
            grad = dot(g, w_down[units_at], LAST)
            both = act[at, column(j)].astype(jnp.float32)
            gate, up = both[:, :LANES], both[:, LANES:]
            bend = jnp.tanh(GELU_A * (gate + GELU_B * (gate * gate * gate)))
            bent = 0.5 * gate * (1.0 + bend)
            slope = 0.5 * (1.0 + bend) + (0.5 * GELU_A) * gate * (1.0 - bend * bend) * (
                1.0 + (3.0 * GELU_B) * gate * gate
            )
            pulled = jnp.concatenate([grad * up * slope, grad * bent], axis=1)
            act[at, column(j)] = pulled.astype(jnp.bfloat16)
            return carry

        lax.fori_loop(0, chunks, back_chunk, 0)

        def input_chunk(n, carry, k=k, at=at):
            w = w_gate_up[:, :, column(n)].reshape(2 * units, 256)
            put_part(k, n, dot(act[at, :], w, PLAIN))
            return carry

        lax.fori_loop(0, columns, input_chunk, 0)
    gather.finish()
    reduce = ReduceBlk(place, lambda i: part.at[i], total, beside, along, held, *take(4))
    for k in range(outer):
        reduce.send(k)

    tokens = count * rows
    slots = staged.shape[0]

    def up_store(i):
        slot = lax.rem(i, slots)
        units_at = pl.ds(pl.multiple_of(i * LANES, LANES), LANES)
        return [
            pltpu.make_async_copy(
                staged.at[slot, pl.ds(h * LANES, LANES)],
                gate_up_grad_hbm.at[units_at, pl.ds(h * width, width)],
                out_sems.at[slot, h],
            )
            for h in (0, 1)
        ]

    def up_grad(i, carry):
        @pl.when(i >= slots)
        def _():
            for copy in up_store(i - slots):
                copy.wait()

        turned[pl.ds(0, 256)] = jnp.transpose(act[:, column(i)])

        def one(n, c):
            x = norm_all[:, :, column(n)].reshape(tokens, 256)
            staged[lax.rem(i, slots), pl.ds(0, 256), column(n)] = dot(
                turned[pl.ds(0, 256)], x, PLAIN
            ).astype(jnp.bfloat16)
            return c

        lax.fori_loop(0, columns, one, 0)
        for copy in up_store(i):
            copy.start()
        return carry

    three = 3 * LANES

    def down_store(i):
        slot = lax.rem(i, slots)
        return pltpu.make_async_copy(
            staged.at[slot],
            down_grad_hbm.at[pl.ds(pl.multiple_of(i * three, three), three)],
            out_sems.at[slot, 2],
        )

    def down_grad(i, carry):
        @pl.when(i >= slots)
        def _():
            down_store(i - slots).wait()

        turned[...] = jnp.transpose(hidden[:, pl.ds(pl.multiple_of(i * three, three), three)])

        def one(n, c):
            x = grad_all[:, :, column(n)].reshape(tokens, 256)
            staged[lax.rem(i, slots), :, column(n)] = dot(turned[...], x, PLAIN).astype(jnp.bfloat16)
            return c

        lax.fori_loop(0, columns, one, 0)
        down_store(i).start()
        return carry

    bounds = [chunks * k // (outer - 1) for k in range(outer)]
    for k in range(outer - 1):
        lax.fori_loop(bounds[k], bounds[k + 1], up_grad, 0)
        reduce.pass_on(k)
    for i in range(max(0, chunks - slots), chunks):
        for copy in up_store(i):
            copy.wait()
    thirds = units // three
    lax.fori_loop(0, thirds, down_grad, 0)
    reduce.last()

    def after(i, carry):
        value, mid, cot = branch_ref[i], middle[i], cot_ref[i].astype(jnp.float32)
        grad, gain_grad = norm_back(mid, gain_ref[2:3], total[i])
        gain_grad_ref[2:3] += gain_grad
        middle_grad = cot + grad
        middle_grad_ref[i] = middle_grad
        grad, gain_grad = norm_back(value, gain_ref[1:2], middle_grad)
        gain_grad_ref[1:2] += gain_grad
        branch_grad_ref[i] = grad.astype(jnp.bfloat16)
        return carry

    lax.fori_loop(0, steps, after, 0)
    reduce.finish()
    for i in range(max(0, thirds - slots), thirds):
        down_store(i).wait()


def feed_forward(branch, tokens, cotangent, gains, gate_up_all, down_all, count, number):
    steps, slab, width = branch.shape
    rows = steps * slab
    units = down_all.shape[0]
    inner = 4 if count >= 32 else 2
    outer = count // inner
    piece = branch.shape
    bf16, f32 = jnp.bfloat16, jnp.float32
    vmem = pl.BlockSpec(memory_space=pltpu.VMEM)
    anywhere = pl.BlockSpec(memory_space=pl.ANY)
    slots = 2
    line_scratch = reduce_blk_scratch(count, piece, bf16)
    return pl.pallas_call(
        functools.partial(feed_forward_kernel, count),
        name="feed_forward",
        out_shape=[
            shape(piece, bf16),
            shape(piece, f32),
            shape(piece, bf16),
            shape((4, width), f32),
            shape(gate_up_all.shape, bf16),
            shape(down_all.shape, bf16),
        ],
        in_specs=[vmem] * 4 + [anywhere] * 2,
        out_specs=[vmem] * 4 + [anywhere] * 2,
        scratch_shapes=[
            pltpu.VMEM((units // LANES, 2 * LANES, width), bf16),
            pltpu.VMEM((units, width), bf16),
            pltpu.VMEM((count, rows, width), bf16),
            pltpu.VMEM((count, rows, width), bf16),
            pltpu.VMEM((count * rows, 2 * units), bf16),
            pltpu.VMEM((count * rows, units), bf16),
            pltpu.VMEM((count,) + piece, bf16),
            pltpu.VMEM(piece, f32),
            pltpu.VMEM((rows, width), bf16),
            pltpu.VMEM((rows, width), bf16),
            pltpu.VMEM(piece, f32),
            pltpu.VMEM((3 * LANES, count * rows), bf16),
            pltpu.VMEM((slots, 3 * LANES, width), bf16),
        ]
        + line_scratch[:3]
        + [
            pltpu.SemaphoreType.DMA((3 * units // LANES,)),
            pltpu.SemaphoreType.DMA((slots, 3)),
        ]
        + gather_blk_sems(count)
        + line_scratch[3:]
        + gather_blk_sems(count)
        + line_scratch[3:],
        compiler_params=pltpu.CompilerParams(
            collective_id=number, has_side_effects=True, vmem_limit_bytes=67043328
        ),
        cost_estimate=pl.CostEstimate(
            flops=18 * count * rows * units * width,
            bytes_accessed=500 * 2**20,
            transcendentals=0,
        ),
    )(branch, tokens, cotangent, gains, gate_up_all, down_all)


def attention_scores(q2, k, query_pos, query_doc, key_block, key_doc, rows):
    raw = lax.dot_general(q2, k, (((1,), (1,)), ((), ())), preferred_element_type=jnp.float32)
    capped = jnp.tanh(raw * (SCORE_SCALE / SOFT_CAP))
    key_pos = key_block * rows + lax.broadcasted_iota(jnp.int32, (1, rows), 1)
    visible = (key_pos <= query_pos) & (key_doc == query_doc)
    return capped, jnp.where(visible, jnp.exp(SOFT_CAP * capped), 0.0)


def attention_query(q_ref, doc_ref, here, count, rows):
    half = pl.program_id(1)
    block = half * count + here
    q2 = jnp.concatenate([q_ref[0, :, :HEAD_DIM], q_ref[0, :, HEAD_DIM:]], axis=0)
    inside = lax.broadcasted_iota(jnp.int32, (rows, 1), 0)
    position = block * rows + jnp.concatenate([inside, inside], axis=0)
    doc = jnp.concatenate([doc_ref[0], doc_ref[0]], axis=0)
    return block, q2, position, doc


def attention_forward_kernel(
    count, here_ref, q_ref, kv_ref, doc_ref, key_doc_ref, attn_ref, full_ref, total_ref, acc, tot
):
    rows = q_ref.shape[1]
    block, q2, position, doc = attention_query(q_ref, doc_ref, here_ref[0], count, rows)
    acc[...] = jnp.zeros_like(acc)
    tot[...] = jnp.zeros_like(tot)

    def one(key_block, carry):
        key_half = (key_block >= count).astype(jnp.int32)
        kv = kv_ref.at[key_block - key_half * count, key_half]
        _, weights = attention_scores(
            q2, kv[:, :HEAD_DIM], position, doc, key_block, key_doc_ref[0, key_block], rows
        )
        tot[...] += jnp.sum(weights, axis=-1, keepdims=True)
        acc[...] += jnp.dot(
            weights.astype(jnp.bfloat16), kv[:, HEAD_DIM:], preferred_element_type=jnp.float32
        )
        return carry

    lax.fori_loop(jnp.maximum(block - count, 0), block + 1, one, 0)
    attended = acc[...] / tot[...]
    attended = jnp.concatenate([attended[:rows], attended[rows:]], axis=1)
    full_ref[0] = attended
    attn_ref[0] = attended.astype(jnp.bfloat16)
    total_ref[0] = tot[...]


def attention_backward_kernel(
    count,
    here_ref,
    q_ref,
    kv_ref,
    doc_ref,
    key_doc_ref,
    grad_ref,
    full_ref,
    total_ref,
    dq_ref,
    dkv_ref,
    acc,
    key_acc,
):
    rows = q_ref.shape[1]
    half = pl.program_id(1)
    block, q2, position, doc = attention_query(q_ref, doc_ref, here_ref[0], count, rows)
    total = total_ref[0]
    grad = grad_ref[0].astype(jnp.float32)
    grad2 = jnp.concatenate([grad[:, :HEAD_DIM], grad[:, HEAD_DIM:]], axis=0)
    full2 = jnp.concatenate([full_ref[0, :, :HEAD_DIM], full_ref[0, :, HEAD_DIM:]], axis=0)
    total_grad = -jnp.sum(grad2 * full2, axis=-1, keepdims=True) / total
    sums_grad = (grad2 / total).astype(jnp.bfloat16)
    acc[...] = jnp.zeros_like(acc)

    @pl.when(half == 0)
    def _():
        def clear(i, carry):
            key_acc[i] = jnp.zeros(key_acc.shape[1:], jnp.float32)
            return carry

        lax.fori_loop(0, key_acc.shape[0], clear, 0)

    def one(key_block, carry):
        key_half = (key_block >= count).astype(jnp.int32)
        inner = key_block - key_half * count
        kv = kv_ref.at[inner, key_half]
        keys = kv[:, :HEAD_DIM]
        capped, weights = attention_scores(
            q2, keys, position, doc, key_block, key_doc_ref[0, key_block], rows
        )
        exp_grad = lax.dot_general(
            sums_grad, kv[:, HEAD_DIM:], (((1,), (1,)), ((), ())), preferred_element_type=jnp.float32
        )
        raw_grad = (
            weights * (exp_grad + total_grad) * (1.0 - capped * capped) * SCORE_SCALE
        ).astype(jnp.bfloat16)
        acc[...] += jnp.dot(raw_grad, keys, preferred_element_type=jnp.float32)
        over_rows = (((0,), (0,)), ((), ()))
        slot = inner * 2 + key_half
        key_acc[slot, :, :HEAD_DIM] += lax.dot_general(
            raw_grad, q2, over_rows, preferred_element_type=jnp.float32
        )
        key_acc[slot, :, HEAD_DIM:] += lax.dot_general(
            weights.astype(jnp.bfloat16), sums_grad, over_rows, preferred_element_type=jnp.float32
        )
        return carry

    lax.fori_loop(jnp.maximum(block - count, 0), block + 1, one, 0)
    dq = acc[...]
    dq_ref[0] = jnp.concatenate([dq[:rows], dq[rows:]], axis=1).astype(jnp.bfloat16)

    @pl.when(half == 1)
    def _():
        def put(i, carry):
            for k in (0, 1):
                dkv_ref[i, k] = key_acc[i * 2 + k].astype(jnp.bfloat16)
            return carry

        lax.fori_loop(0, count, put, 0)


def attention_specs(count, rows, width):
    query = pl.BlockSpec((1, rows, width), lambda s, h, here: (2 * s + h, 0, 0))
    keys = pl.BlockSpec((count, 2, rows, 2 * HEAD_DIM), lambda s, h, here: (0, s, 0, 0))
    doc = pl.BlockSpec((1, rows, 1), lambda s, h, here: (2 * s + h, 0, 0))
    key_doc = pl.BlockSpec((1, 2 * count, 1, rows), lambda s, h, here: (s, 0, 0, 0))
    total = pl.BlockSpec((1, REPS * rows, 1), lambda s, h, here: (2 * s + h, 0, 0))
    return query, keys, doc, key_doc, total


def attention_forward(here, q, kv, doc, key_doc):
    count, _, rows, _ = kv.shape
    width = REPS * HEAD_DIM
    query, keys, doc_spec, key_doc_spec, total = attention_specs(count, rows, width)
    return pl.pallas_call(
        functools.partial(attention_forward_kernel, count),
        name="attend",
        grid_spec=pltpu.PrefetchScalarGridSpec(
            num_scalar_prefetch=1,
            grid=(2, 2),
            in_specs=[query, keys, doc_spec, key_doc_spec],
            out_specs=[query, query, total],
            scratch_shapes=[
                pltpu.VMEM((REPS * rows, HEAD_DIM), jnp.float32),
                pltpu.VMEM((REPS * rows, 1), jnp.float32),
            ],
        ),
        out_shape=[
            shape((GROUPS, rows, width), jnp.bfloat16),
            shape((GROUPS, rows, width), jnp.float32),
            shape((GROUPS, REPS * rows, 1), jnp.float32),
        ],
        compiler_params=pltpu.CompilerParams(vmem_limit_bytes=VMEM_LIMIT),
        cost_estimate=pl.CostEstimate(flops=10**9, bytes_accessed=40 * 2**20, transcendentals=0),
    )(here, q, kv, doc, key_doc)


def attention_backward(here, q, kv, doc, key_doc, grad, full, totals):
    count, _, rows, _ = kv.shape
    width = REPS * HEAD_DIM
    query, keys, doc_spec, key_doc_spec, total = attention_specs(count, rows, width)
    return pl.pallas_call(
        functools.partial(attention_backward_kernel, count),
        name="attend_back",
        grid_spec=pltpu.PrefetchScalarGridSpec(
            num_scalar_prefetch=1,
            grid=(2, 2),
            in_specs=[query, keys, doc_spec, key_doc_spec, query, query, total],
            out_specs=[query, keys],
            scratch_shapes=[
                pltpu.VMEM((REPS * rows, HEAD_DIM), jnp.float32),
                pltpu.VMEM((2 * count, rows, 2 * HEAD_DIM), jnp.float32),
            ],
        ),
        out_shape=[shape((GROUPS, rows, width), jnp.bfloat16), shape(kv.shape, jnp.bfloat16)],
        compiler_params=pltpu.CompilerParams(vmem_limit_bytes=VMEM_LIMIT),
        cost_estimate=pl.CostEstimate(flops=2 * 10**9, bytes_accessed=80 * 2**20, transcendentals=0),
    )(here, q, kv, doc, key_doc, grad, full, totals)


def rms_scale(values, gain_row):
    return (
        values * lax.rsqrt(jnp.mean(values * values, axis=-1, keepdims=True) + NORM_EPS) * gain_row
    )


def gelu_tanh(values):
    return jax.nn.gelu(values, approximate=True)


def rope_tables(positions):
    half_width = HEAD_DIM // 2
    frequency = jnp.exp(
        jnp.arange(half_width, dtype=jnp.float32) * (-2.0 * math.log(ROPE_BASE) / HEAD_DIM)
    )
    angles = positions.astype(jnp.float32)[:, None] * frequency[None, :]
    cosine = jnp.concatenate([jnp.cos(angles), jnp.cos(angles)], axis=-1)
    sine = jnp.concatenate([jnp.sin(angles), jnp.sin(angles)], axis=-1)
    return cosine[:, None, :], sine[:, None, :]


def rotate(values, cosine, sine):
    half_width = HEAD_DIM // 2
    turned = jnp.concatenate([-values[..., half_width:], values[..., :half_width]], axis=-1)
    return values * cosine + turned * sine


def feed_forward_apart(
    branch_slabs, inputs, cotangent, gains, gate_up_all, down_all, count, piece
):
    rows, width = inputs.shape
    bf16 = jnp.bfloat16
    branch = branch_slabs.reshape(rows, width)
    middle = inputs + rms_scale(branch, gains[1])
    norm_three = rms_scale(middle, gains[2]).astype(bf16)
    gate_all = gate_up_all[:, :width]
    up_all = gate_up_all[:, width:]
    norm_all = all_gather_blk(norm_three, count, 4).reshape(count * rows, width)
    gate = dot(norm_all, gate_all, LAST)
    up = dot(norm_all, up_all, LAST)
    hidden = (gelu_tanh(gate) * up).astype(bf16)
    ffn_part = dot(hidden, down_all, PLAIN).astype(bf16)
    ffn_out = reduce_scatter_blk(ffn_part.reshape((count,) + piece), count, 5).reshape(rows, width)
    output = (middle + rms_scale(ffn_out, gains[3])).astype(bf16)[None]

    out_cotangent = cotangent[0].astype(jnp.float32)
    _, post_ffn_back = jax.vjp(rms_scale, ffn_out, gains[3])
    ffn_grad, gain_grad_four = post_ffn_back(out_cotangent)
    grad_all = all_gather_blk(ffn_grad.astype(bf16), count, 6).reshape(count * rows, width)
    activated, gelu_back = jax.vjp(gelu_tanh, gate)
    hidden_grad = dot(grad_all, down_all, LAST)
    gate_grad = gelu_back(hidden_grad * up)[0].astype(bf16)
    up_grad = (hidden_grad * activated).astype(bf16)
    norm_part = dot(gate_grad, gate_all, PLAIN) + dot(up_grad, up_all, PLAIN)
    norm_three_grad = reduce_scatter_blk(
        norm_part.astype(bf16).reshape((count,) + piece), count, 7
    ).reshape(rows, width)
    down_part = dot(hidden, grad_all, FIRST).astype(bf16)
    gate_up_part = jnp.concatenate(
        [dot(gate_grad, norm_all, FIRST), dot(up_grad, norm_all, FIRST)], axis=1
    ).astype(bf16)
    _, pre_ffn_back = jax.vjp(rms_scale, middle, gains[2])
    middle_part, gain_grad_three = pre_ffn_back(norm_three_grad)
    middle_grad = out_cotangent + middle_part
    _, post_attn_back = jax.vjp(rms_scale, branch, gains[1])
    branch_grad, gain_grad_two = post_attn_back(middle_grad)
    return (
        output,
        middle_grad,
        branch_grad.astype(bf16),
        gain_grad_two,
        gain_grad_three,
        gain_grad_four,
        gate_up_part,
        down_part,
    )


def shards(
    tokens, cotangent, segments, norm_gains, qkv_weight, out_weight, gate_up_weight, down_weight
):
    _, rows, width = tokens.shape
    count = lax.axis_size("blk")
    here = lax.axis_index("blk")
    mine = 2 * lax.axis_index("dp") + lax.axis_index("head")
    group_rows = GROUPS * rows
    head_width = REPS * HEAD_DIM
    bf16 = jnp.bfloat16
    slab = slabs(rows)
    piece = (rows // slab, slab, width)

    gate_up_all = lax.all_gather(gate_up_weight, ("dp", "head"), axis=0, tiled=True)
    down_all = lax.all_gather(down_weight, ("dp", "head"), axis=0, tiled=True)

    gain_rows = norm_gains.shape[0]
    gain_lanes = -(-gain_rows // 128) * 128
    gains_sent = jnp.pad(
        jnp.transpose(norm_gains).astype(jnp.float32), ((0, 4), (0, gain_lanes - gain_rows))
    )
    out_rows = out_weight.shape[0]
    out_sent = jnp.transpose(out_weight.reshape(out_rows, GROUPS, head_width), (1, 0, 2))
    qkv_rows = qkv_weight.shape[0]
    qkv_slab = slabs(qkv_rows)
    qkv_piece = (qkv_rows // qkv_slab, qkv_slab, width)
    qkv_all, out_all, tokens_all, gains_all, docs_all = gather_first(
        qkv_weight, out_sent, tokens[0], gains_sent, segments.reshape(-1, 128), count, 1
    )
    gains = jnp.transpose(gains_all[:, :, :4, :gain_rows], (2, 0, 1, 3)).reshape(4, width)
    qkv_head = qkv_all.reshape(count * qkv_rows, width)
    out_head = out_all.reshape(count, GROUPS, out_rows, head_width)
    out_head = jnp.transpose(out_head, (1, 0, 2, 3)).reshape(width, head_width)
    docs = docs_all.reshape(2, 2, count, rows)
    key_doc = docs.reshape(2, 2 * count, 1, rows)
    own_doc = lax.dynamic_index_in_dim(docs, here, 2, keepdims=False).reshape(GROUPS, rows, 1)
    here_one = here.reshape(1)

    group_tokens = tokens_all.reshape(group_rows, width).astype(jnp.float32)
    norm_one = rms_scale(group_tokens, gains[0]).astype(bf16)
    proj = dot(norm_one, qkv_head, LAST)
    inside = jnp.arange(rows, dtype=jnp.int32)
    position = jnp.concatenate([here * rows + inside, (count + here) * rows + inside])
    cosine, sine = rope_tables(jnp.concatenate([position, position]))
    proj = proj.reshape(group_rows, REPS + 2, HEAD_DIM)
    turned = rotate(proj[:, : REPS + 1], cosine, sine)
    sent = jnp.concatenate([turned, proj[:, REPS + 1 :]], axis=1).astype(bf16)
    queries = sent[:, :REPS].reshape(GROUPS, rows, head_width)
    own_kv = sent[:, REPS:].reshape(group_rows, 2 * HEAD_DIM)
    kv_slab = slabs(group_rows)
    kv_piece = (group_rows // kv_slab, kv_slab, 2 * HEAD_DIM)
    kv = all_gather_blk(own_kv, count, 2).reshape(count, GROUPS, rows, 2 * HEAD_DIM)
    attn, attended, totals = attention_forward(here_one, queries, kv, own_doc, key_doc)
    attn = attn.reshape(group_rows, head_width)
    branch_part = dot(attn, out_head, LAST).astype(bf16)
    branch_slabs = reduce_scatter_group(branch_part.reshape((GROUPS,) + piece), 3)
    inputs = tokens[0].astype(jnp.float32)
    if feed_forward_fits(count, rows, width, down_all.shape[0]):
        output, middle_grad, branch_grad, gain_rest, gate_up_part, down_part = feed_forward(
            branch_slabs,
            tokens.reshape(piece),
            cotangent.reshape(piece),
            gains,
            gate_up_all,
            down_all,
            count,
            4,
        )
        output = output.reshape(tokens.shape)
        middle_grad = middle_grad.reshape(rows, width)
        branch_grad = branch_grad.reshape(rows, width)
        gain_grad_two, gain_grad_three, gain_grad_four = gain_rest[1], gain_rest[2], gain_rest[3]
    else:
        (
            output,
            middle_grad,
            branch_grad,
            gain_grad_two,
            gain_grad_three,
            gain_grad_four,
            gate_up_part,
            down_part,
        ) = feed_forward_apart(
            branch_slabs, inputs, cotangent, gains, gate_up_all, down_all, count, piece
        )
    gate_up_grad = lax.psum_scatter(
        gate_up_part, ("dp", "head"), scatter_dimension=0, tiled=True
    ).astype(jnp.float32)
    down_grad = lax.psum_scatter(
        down_part, ("dp", "head"), scatter_dimension=0, tiled=True
    ).astype(jnp.float32)
    branch_all = all_gather_group(branch_grad, 8).reshape(group_rows, width)
    attn_grad = dot(branch_all, out_head, PLAIN).astype(bf16).reshape(GROUPS, rows, head_width)
    out_part = dot(branch_all, attn, FIRST).astype(bf16)
    out_part = jnp.transpose(out_part.reshape(GROUPS, count, out_rows, head_width), (1, 0, 2, 3))
    dq, dkv_part = attention_backward(
        here_one, queries, kv, own_doc, key_doc, attn_grad, attended, totals
    )
    dkv = reduce_scatter_blk(dkv_part.reshape((count,) + kv_piece), count, 9)
    sent_grad = jnp.concatenate(
        [
            dq.reshape(group_rows, REPS, HEAD_DIM),
            dkv.astype(bf16).reshape(group_rows, 2, HEAD_DIM),
        ],
        axis=1,
    ).astype(jnp.float32)
    unturned = rotate(sent_grad[:, : REPS + 1], cosine, -sine)
    proj_grad = (
        jnp.concatenate([unturned, sent_grad[:, REPS + 1 :]], axis=1)
        .astype(bf16)
        .reshape(group_rows, (REPS + 2) * HEAD_DIM)
    )
    qkv_part = dot(proj_grad, norm_one, FIRST).astype(bf16)
    norm_one_part = dot(proj_grad, qkv_head, PLAIN)
    _, gain_back = jax.vjp(lambda gain: rms_scale(group_tokens, gain), gains[0])
    (gain_grad_one,) = gain_back(norm_one_part)
    gain_part = jnp.stack([gain_grad_one, gain_grad_two, gain_grad_three, gain_grad_four])
    gain_part = jnp.transpose(gain_part.reshape(4, GROUPS, count, gain_rows), (2, 1, 0, 3))
    gain_part = jnp.pad(gain_part, ((0, 0), (0, 0), (0, 4), (0, gain_lanes - gain_rows)))
    qkv_grad, out_grad, norm_one_grad, gain_grad = reduce_last(
        qkv_part.reshape((count,) + qkv_piece),
        out_part,
        norm_one_part.astype(bf16).reshape((GROUPS,) + piece),
        gain_part[:, :, None],
        count,
        10,
    )
    qkv_grad = qkv_grad.reshape(qkv_rows, width)
    out_grad = (
        jnp.transpose(out_grad, (1, 0, 2)).reshape(out_rows, GROUPS * head_width).astype(jnp.float32)
    )
    gain_grad = jnp.transpose(gain_grad.reshape(8, gain_lanes)[:4, :gain_rows])
    _, pre_attn_back = jax.vjp(lambda values: rms_scale(values, gains[0]), inputs)
    (input_part,) = pre_attn_back(norm_one_grad.reshape(rows, width))
    tokens_grad = (middle_grad + input_part).astype(bf16)[None]
    return (output, tokens_grad, gain_grad, qkv_grad, out_grad, gate_up_grad, down_grad)


def solution(mesh):
    whole = ("dp", "head", "blk")
    return jax.shard_map(
        shards,
        mesh=mesh,
        in_specs=(
            P("dp", ("head", "blk"), None),
            P("dp", ("head", "blk"), None),
            P("dp", None),
            P(whole, None),
            P(whole, None),
            P(whole, None),
            P(whole, None),
            P(whole, None),
        ),
        out_specs=(
            P("dp", ("head", "blk"), None),
            P("dp", ("head", "blk"), None),
            P(whole, None),
            P(whole, None),
            P(whole, None),
            P(whole, None),
            P(whole, None),
        ),
        check_vma=False,
    )
```

```python
import functools
import math

import jax
import jax.numpy as jnp
from jax import lax
from jax.experimental import pallas as pl
from jax.experimental.pallas import tpu as pltpu
from jax.sharding import PartitionSpec as P

HEADS = 8
KV_HEADS = 4
HEAD_DIM = 256
REPS = HEADS // KV_HEADS
GROUPS = 4
SOFT_CAP = 50.0
NORM_EPS = 1e-06
ROPE_BASE = 10000.0
SCORE_SCALE = HEAD_DIM ** (-0.5)

MESH = pl.DeviceIdType.MESH
VMEM_LIMIT = 60 * 1024 * 1024


class Place:
    def __init__(self, count):
        self.count = count
        self.inner = 4 if count >= 32 else 2
        self.outer = count // self.inner
        self.here = lax.axis_index("blk")
        self.line = self.here // self.inner
        self.side = lax.rem(self.here, self.inner)
        self.core = lax.axis_index("dp")
        self.half = lax.axis_index("head")
        self.group = 2 * self.core + self.half

    def near(self, k):
        orders = [near_order(self.outer, line)[k] for line in range(self.outer)]
        found = jnp.int32(orders[0])
        for line in range(1, self.outer):
            found = jnp.where(self.line == line, jnp.int32(orders[line]), found)
        return found

    def at(self, line, side):
        return {"blk": line * self.inner + side}

    def beside(self, step):
        return lax.rem(self.side + step, self.inner)

    def partner(self):
        return {"dp": 1 - self.core}

    def across(self):
        return {"head": 1 - self.half}

    def corner(self):
        return {"dp": 1 - self.core, "head": 1 - self.half}


def remote(src, dst, sent, came, device):
    return pltpu.make_async_remote_copy(
        src_ref=src, dst_ref=dst, send_sem=sent, recv_sem=came, device_id=device, device_id_type=MESH
    )


def greet(place, blk=False, core=False, half=False, corner=False):
    sem = pltpu.get_barrier_semaphore()
    amount = jnp.int32(0)

    def hello(device):
        pl.semaphore_signal(sem, inc=1, device_id=device, device_id_type=MESH)

    if blk:
        up, down = place.line < place.outer - 1, place.line > 0
        pl.when(up)(lambda: hello(place.at(place.line + 1, place.side)))
        pl.when(down)(lambda: hello(place.at(place.line - 1, place.side)))
        amount = amount + up.astype(jnp.int32) + down.astype(jnp.int32) + (place.inner - 1)
        for step in range(1, place.inner):
            hello(place.at(place.line, place.beside(step)))
    for wanted, device in (
        (core, place.partner()),
        (half, place.across()),
        (corner, place.corner()),
    ):
        if wanted:
            hello(device)
            amount = amount + 1
    pl.semaphore_wait(sem, amount)


def together(*tasks):
    tasks = list(tasks)
    while tasks:
        for task in list(tasks):
            try:
                next(task)
            except StopIteration:
                tasks.remove(task)


def near_order(outer, line):
    ends = outer == 4
    return sorted(
        range(outer),
        key=lambda other: (abs(other - line), ends and other not in (0, outer - 1), other),
    )


def evened(place, parts):
    return parts == 2 and place.inner == 2 and place.outer == 4


def part_of(ref, h, parts):
    if parts == 1:
        return ref
    size = ref.shape[0] // parts
    return ref.at[pl.ds(h * size, size)]


def gather_blk_sems(place_count, parts=2):
    inner = 4 if place_count >= 32 else 2
    return [
        pltpu.SemaphoreType.DMA((2 + inner, place_count, parts)),
        pltpu.SemaphoreType.DMA((place_count, parts)),
        pltpu.SemaphoreType.DMA,
    ]


class GatherBlk:
    def __init__(self, place, src, view, sent, came, own):
        self.place, self.src, self.view, self.sent, self.came = place, src, view, sent, came
        self.parts = came.shape[1]
        self.evened = evened(place, self.parts)
        self.middle = (place.line > 0) & (place.line < place.outer - 1)
        self.copy = pltpu.make_async_copy(src, view(place.here), own)

    def sends(self, k, h):
        place = self.place
        there = place.near(k)
        piece = there * place.inner + place.side
        there_view = part_of(self.view(piece), h, self.parts)
        src = part_of(self.src, h, self.parts) if k == 0 else there_view

        def send(kind, device):
            return remote(
                src, there_view, self.sent.at[kind, piece, h], self.came.at[piece, h], device
            )

        line, side = place.line, place.side
        up = (there <= line) & (line < place.outer - 1)
        down = (there >= line) & (line > 0)
        aside = range(1, place.inner)
        if self.evened and h == 1 and k == place.outer - 1:
            aside = ()
        return (
            [
                (up, lambda: send(0, place.at(line + 1, side))),
                (down, lambda: send(1, place.at(line - 1, side))),
            ],
            [send(1 + step, place.at(line, place.beside(step))) for step in aside],
        )

    def forward(self, k, h):
        along, aside = self.sends(k, h)
        for needed, make in along:
            pl.when(needed)(lambda make=make: make().start())
        for one in aside:
            one.start()

    def start(self):
        self.copy.start()
        for h in range(self.parts):
            self.forward(0, h)

    def arrived(self, piece, h):
        place = self.place
        remote(
            part_of(self.src, h, self.parts),
            part_of(self.view(piece), h, self.parts),
            self.sent.at[0, piece, h],
            self.came.at[piece, h],
            place.at(place.line, place.beside(1)),
        ).wait_recv()

    def pass_on(self, k):
        for h in range(self.parts):
            self.arrived(self.place.near(k) * self.place.inner + self.place.side, h)
            self.forward(k, h)

    def extra(self, k):
        place = self.place
        piece = place.near(k) * place.inner + place.beside(1)
        to = place.near(2 if k == 1 else 1)
        half = part_of(self.view(piece), 1, 2)
        return remote(
            half,
            half,
            self.sent.at[place.inner + 1, piece, 1],
            self.came.at[piece, 1],
            place.at(to, place.side),
        )

    def pass_extra(self, k):
        if self.evened:

            @pl.when(self.middle)
            def _():
                self.arrived(self.place.near(k) * self.place.inner + self.place.beside(1), 1)
                self.extra(k).start()

    def beside_arrived(self, k):
        for step in range(1, self.place.inner):
            piece = self.place.near(k) * self.place.inner + self.place.beside(step)
            for h in range(self.parts):
                if self.evened and h == 1 and k in (1, self.place.outer - 1):
                    pl.when(jnp.logical_not(self.middle))(lambda: self.arrived(piece, 1))
                else:
                    self.arrived(piece, h)

    def finish(self):
        for k in range(self.place.outer):
            for h in range(self.parts):
                along, aside = self.sends(k, h)
                for needed, make in along:
                    pl.when(needed)(lambda make=make: make().wait_send())
                for one in aside:
                    one.wait_send()
        if self.evened:

            @pl.when(self.middle)
            def _():
                self.extra(1).wait_send()
                self.extra(self.place.outer - 1).wait_send()


def gather_blk(place, src, view, sent, came, own):
    if not callable(view):
        out = view
        view = lambda piece: out.at[piece]
    work = GatherBlk(place, src, view, sent, came, own)
    work.start()
    yield
    for k in range(1, place.outer):
        work.pass_on(k)
        if k == place.outer - 2:
            work.pass_extra(1)
        yield
    work.pass_extra(place.outer - 1)
    yield
    for k in range(place.outer):
        work.beside_arrived(k)
    work.finish()
    work.copy.wait()


def add_into(out, *terms):
    def one(i, carry):
        total = terms[0][i].astype(jnp.float32)
        for term in terms[1:]:
            total = total + term[i].astype(jnp.float32)
        out[i] = total.astype(out.dtype)
        return carry

    lax.fori_loop(0, out.shape[0], one, 0)


def reduce_blk_scratch(place_count, piece, dtype, parts=2):
    inner = 4 if place_count >= 32 else 2
    outer = place_count // inner
    half = (piece[0] // 2,) + tuple(piece[1:]) if parts == 2 and inner == 2 and outer == 4 else (1, 8, 128)
    return [
        pltpu.VMEM((outer, inner - 1) + piece, dtype),
        pltpu.VMEM((outer + 1,) + piece, dtype),
        pltpu.VMEM((outer,) + piece, dtype),
        pltpu.VMEM((4,) + half, dtype),
        pltpu.SemaphoreType.DMA((outer, inner - 1, parts)),
        pltpu.SemaphoreType.DMA((outer, inner - 1, parts)),
        pltpu.SemaphoreType.DMA((outer, parts)),
        pltpu.SemaphoreType.DMA((outer + 1, parts)),
        pltpu.SemaphoreType.DMA((2,)),
        pltpu.SemaphoreType.DMA((2,)),
    ]


REDUCE_REFS = 10


class ReduceBlk:
    def __init__(
        self,
        place,
        view,
        out,
        beside,
        along,
        held,
        spare,
        side_sent,
        side_came,
        line_sent,
        line_came,
        spare_sent,
        spare_came,
    ):
        self.place, self.view, self.out = place, view, out
        self.beside, self.along, self.held, self.spare = beside, along, held, spare
        self.side_sems, self.line_sems = (side_sent, side_came), (line_sent, line_came)
        self.spare_sems = (spare_sent, spare_came)
        self.parts = line_sent.shape[1]
        self.evened = evened(place, self.parts)
        self.middle = (place.line > 0) & (place.line < place.outer - 1)

    def part(self, ref, h):
        return part_of(ref, h, self.parts)

    def far(self, k):
        return self.place.near(self.place.outer - 1 - k)

    def alone(self, k, h):
        return self.evened and k == 0 and h == 1

    def side_copy(self, there, step, h, src=None):
        place = self.place
        to = place.beside(step)
        if src is None:
            src = self.part(self.view(there * place.inner + to), h)
        return remote(
            src,
            self.part(self.beside.at[there, place.inner - step - 1], h),
            self.side_sems[0].at[there, step - 1, h],
            self.side_sems[1].at[there, place.inner - step - 1, h],
            place.at(place.line, to),
        )

    def line_copy(self, there, slot, to, h, src=None):
        return remote(
            self.part(self.held.at[there], h) if src is None else src,
            self.part(self.along.at[slot], h),
            self.line_sems[0].at[there, h],
            self.line_sems[1].at[slot, h],
            self.place.at(to, self.place.side),
        )

    def send(self, k, h):
        for step in range(1, self.place.inner):
            self.side_copy(self.far(k), step, h).start()

    def terms(self, k, h):
        place = self.place
        there = self.far(k)
        own = [self.part(self.view(there * place.inner + place.side), h)]
        if self.alone(k, h):
            return own
        for step in range(1, place.inner):
            self.side_copy(there, step, h).wait_recv()
        return own + [self.part(self.beside.at[there, j], h) for j in range(place.inner - 1)]

    def onward(self, there, h, src=None):
        line, outer = self.place.line, self.place.outer
        to = jnp.where(there < line, line - 1, line + 1)
        slot = jnp.where(there == line + 1, outer, there)
        return self.line_copy(there, slot, to, h, src)

    def starts(self, there):
        line, outer = self.place.line, self.place.outer
        return ((there < line) & (line == outer - 1)) | ((there > line) & (line == 0))

    def pass_on(self, k, h):
        place = self.place
        line = place.line
        there = self.far(k)
        terms = self.terms(k, h)
        held = self.part(self.held.at[there], h)
        starts = self.starts(there)

        @pl.when(starts)
        def _():
            add_into(held, *terms)

        @pl.when(jnp.logical_not(starts))
        def _():
            back = jnp.where(there < line, line + 1, line - 1)
            self.line_copy(there, there, back, h).wait_recv()
            add_into(held, self.part(self.along.at[there], h), *terms)

        self.onward(there, h).start()

    def last(self, h):
        place = self.place
        line, outer = place.line, place.outer
        terms = self.terms(outer - 1, h)
        below, above = line > 0, line < outer - 1
        from_above = self.part(self.along.at[line], h)
        from_below = self.part(self.along.at[outer], h)
        out = self.part(self.out, h)

        @pl.when(above)
        def _():
            self.line_copy(line, line, line + 1, h).wait_recv()

        @pl.when(below)
        def _():
            self.line_copy(line, outer, line - 1, h).wait_recv()

        @pl.when(above & below)
        def _():
            add_into(out, from_above, from_below, *terms)

        @pl.when(above & jnp.logical_not(below))
        def _():
            add_into(out, from_above, *terms)

        @pl.when(jnp.logical_not(above) & below)
        def _():
            add_into(out, from_below, *terms)


    def spare_view(self, k):
        place = self.place
        return self.part(self.view(place.near(k) * place.inner + place.beside(1)), 1)

    def spare_first(self):
        return remote(
            self.spare_view(3),
            self.spare.at[0],
            self.spare_sems[0].at[0],
            self.spare_sems[1].at[0],
            self.place.at(self.place.near(1), self.place.side),
        )

    def spare_second(self):
        return remote(
            self.spare.at[2],
            self.spare.at[1],
            self.spare_sems[0].at[1],
            self.spare_sems[1].at[1],
            self.place.at(self.place.near(2), self.place.side),
        )

    def spare_side(self):
        return self.side_copy(self.far(2), 1, 1, self.spare.at[3])

    def start(self):
        outer = self.place.outer
        if not self.evened:
            for k in range(outer):
                for h in range(self.parts):
                    self.send(k, h)
            return
        self.send(0, 0)
        for k, h in ((1, 0), (1, 1), (2, 0)):
            self.send(k, h)

        @pl.when(jnp.logical_not(self.middle))
        def _():
            self.spare_first().start()
            there = self.far(0)
            self.onward(
                there, 1, self.part(self.view(there * self.place.inner + self.place.side), 1)
            ).start()
            for k, h in ((2, 1), (3, 0), (3, 1)):
                self.send(k, h)

    def turn(self):
        @pl.when(self.middle)
        def _():
            self.spare_first().wait_recv()
            add_into(self.spare.at[2], self.spare.at[0], self.spare_view(3))
            self.spare_second().start()
            self.pass_on(0, 1)
            self.spare_second().wait_recv()
            add_into(self.spare.at[3], self.spare.at[1], self.spare_view(1))
            self.spare_side().start()
            for h in (0, 1):
                self.send(3, h)

    def events(self):
        outer, parts = self.place.outer, self.parts
        todo = []
        if self.evened:
            todo.append(self.turn)
            todo.append(lambda: self.pass_on(0, 0))
        else:
            for h in range(parts):
                todo.append(lambda h=h: self.pass_on(0, h))
        for k in range(1, outer - 1):
            for h in range(parts):
                todo.append(lambda k=k, h=h: self.pass_on(k, h))
        for h in range(parts):
            todo.append(lambda h=h: self.last(h))
        return todo

    def finish(self):
        for k in range(self.place.outer):
            for h in range(self.parts):
                if k < self.place.outer - 1:
                    self.onward(self.far(k), h).wait_send()
                if not self.alone(k, h):
                    for step in range(1, self.place.inner):
                        self.side_copy(self.far(k), step, h).wait_send()
        if self.evened:

            @pl.when(self.middle)
            def _():
                self.spare_second().wait_send()

            @pl.when(jnp.logical_not(self.middle))
            def _():
                self.spare_first().wait_send()


def reduce_blk(place, view, out, *scratch):
    if not callable(view):
        part = view
        view = lambda piece: part.at[piece]
    work = ReduceBlk(place, view, out, *scratch)
    work.start()
    yield
    for event in work.events():
        event()
        yield
    work.finish()


def gather_group_sems():
    return [pltpu.SemaphoreType.DMA((3,)), pltpu.SemaphoreType.DMA((4,)), pltpu.SemaphoreType.DMA]


def gather_group(place, src, out, sent, came, own):
    copy = pltpu.make_async_copy(src, out.at[place.group], own)
    copy.start()
    mine, other = place.group, 2 * place.core + (1 - place.half)
    to_half = remote(src, out.at[mine], sent.at[0], came.at[mine], place.across())
    to_core = remote(src, out.at[mine], sent.at[1], came.at[mine], place.partner())
    to_half.start()
    to_core.start()
    yield
    remote(src, out.at[other], sent.at[0], came.at[other], place.across()).wait_recv()
    relay = remote(out.at[other], out.at[other], sent.at[2], came.at[other], place.partner())
    relay.start()
    yield
    for half in (0, 1):
        slot = 2 * (1 - place.core) + half
        remote(src, out.at[slot], sent.at[0], came.at[slot], place.partner()).wait_recv()
    to_half.wait_send()
    to_core.wait_send()
    relay.wait_send()
    copy.wait()


def reduce_group_scratch(piece, dtype):
    return [
        pltpu.VMEM((2,) + piece, dtype),
        pltpu.VMEM(piece, dtype),
        pltpu.VMEM(piece, dtype),
        pltpu.SemaphoreType.DMA((3,)),
        pltpu.SemaphoreType.DMA((3,)),
    ]


def reduce_group(place, part, out, from_core, from_half, held, sent, came):
    far = 2 * (1 - place.core) + (1 - place.half)
    near = 2 * (1 - place.core) + place.half
    first = remote(part.at[far], from_core.at[1], sent.at[0], came.at[0], place.partner())
    second = remote(part.at[near], from_core.at[0], sent.at[1], came.at[1], place.partner())
    first.start()
    second.start()
    yield
    first.wait_recv()
    add_into(held, part.at[2 * place.core + (1 - place.half)], from_core.at[1])
    third = remote(held, from_half, sent.at[2], came.at[2], place.across())
    third.start()
    yield
    second.wait_recv()
    third.wait_recv()
    add_into(out, part.at[place.group], from_core.at[0], from_half)
    first.wait_send()
    second.wait_send()
    third.wait_send()


def exchange_group_sems():
    return [pltpu.SemaphoreType.DMA((3,)), pltpu.SemaphoreType.DMA((4,)), pltpu.SemaphoreType.DMA]


def exchange_group(place, src, out, sent, came, own):
    mine = place.group
    copy = pltpu.make_async_copy(src.at[mine], out.at[mine], own)
    copy.start()
    core, half = place.core, place.half
    links = (
        (2 * (1 - core) + (1 - half), place.corner()),
        (2 * core + (1 - half), place.across()),
        (2 * (1 - core) + half, place.partner()),
    )
    copies = [
        remote(src.at[to], out.at[mine], sent.at[k], came.at[mine], device)
        for k, (to, device) in enumerate(links)
    ]
    for one in copies:
        one.start()
    yield
    for k, (peer, device) in enumerate(links):
        remote(src.at[peer], out.at[peer], sent.at[k], came.at[peer], device).wait_recv()
    for one in copies:
        one.wait_send()
    copy.wait()


def transfer(name, number, body, ins, outs, scratch, moved, out_spaces=None):
    spaces = out_spaces or [pl.ANY] * len(outs)
    return pl.pallas_call(
        body,
        name=name,
        out_shape=outs,
        in_specs=[pl.BlockSpec(memory_space=pltpu.VMEM)] * len(ins),
        out_specs=[pl.BlockSpec(memory_space=space) for space in spaces],
        scratch_shapes=scratch,
        compiler_params=pltpu.CompilerParams(
            collective_id=number, has_side_effects=True, vmem_limit_bytes=VMEM_LIMIT
        ),
        cost_estimate=pl.CostEstimate(flops=0, bytes_accessed=moved * 40, transcendentals=0),
    )(*ins)


def shape(dims, dtype):
    return jax.ShapeDtypeStruct(tuple(dims), dtype)


def slabs(rows):
    return math.gcd(rows, 16)


def all_gather_blk(value, count, number):
    def body(src, out, *sems):
        place = Place(count)
        greet(place, blk=True)
        together(gather_blk(place, src, out, *sems))

    return transfer(
        f"gather{number}",
        number,
        body,
        [value],
        [shape((count,) + value.shape, value.dtype)],
        gather_blk_sems(count),
        value.size * 2 * count,
    )[0]


def reduce_scatter_blk(value, count, number):
    piece = value.shape[1:]

    def body(part, out, *scratch):
        place = Place(count)
        greet(place, blk=True)
        together(reduce_blk(place, part, out, *scratch))

    return transfer(
        f"reduce{number}",
        number,
        body,
        [value],
        [shape(piece, jnp.float32)],
        reduce_blk_scratch(count, piece, value.dtype),
        value.size * 2,
        [pltpu.VMEM],
    )[0]


class Taker:
    def __init__(self, refs):
        self.refs = list(refs)

    def __call__(self, amount):
        taken = self.refs[:amount]
        del self.refs[:amount]
        return taken


def gather_first(qkv, out_parts, tokens, gains, docs, count, number):
    names = 5

    def body(*refs):
        qkv_ref, out_ref, tok_ref, gain_ref, doc_ref = refs[:names]
        qkv_all, out_mine, tok_all, gain_all, doc_all = refs[names : 2 * names]
        gain_mine = refs[2 * names]
        take = Taker(refs[2 * names + 1 :])
        place = Place(count)
        greet(place, blk=True, core=True, half=True, corner=True)

        def gain_task(near, far):
            yield from gather_blk(place, gain_ref, gain_mine, *near)
            yield from gather_group(place, gain_mine, gain_all, *far)

        def doc_task(sent, came, own):
            copy = pltpu.make_async_copy(doc_ref, doc_all.at[place.core], own)
            copy.start()
            send = remote(doc_ref, doc_all.at[place.core], sent, came, place.partner())
            send.start()
            yield
            remote(doc_ref, doc_all.at[1 - place.core], sent, came, place.partner()).wait_recv()
            send.wait_send()
            copy.wait()

        together(
            gain_task(take(3), take(3)),
            gather_blk(place, qkv_ref, qkv_all, *take(3)),
            doc_task(*take(3)),
            gather_group(place, tok_ref, tok_all, *take(3)),
            exchange_group(place, out_ref, out_mine, *take(3)),
        )

    ins = [qkv, out_parts, tokens, gains, docs]
    return transfer(
        f"first{number}",
        number,
        body,
        ins,
        [
            shape((count,) + qkv.shape, qkv.dtype),
            shape(out_parts.shape, out_parts.dtype),
            shape((GROUPS,) + tokens.shape, tokens.dtype),
            shape((GROUPS, count) + gains.shape, gains.dtype),
            shape((2,) + docs.shape, docs.dtype),
        ],
        [pltpu.VMEM((count,) + gains.shape, gains.dtype)]
        + gather_blk_sems(count, 1)
        + gather_group_sems()
        + gather_blk_sems(count)
        + [pltpu.SemaphoreType.DMA] * 3
        + gather_group_sems()
        + exchange_group_sems(),
        (qkv.size + out_parts.size) * 2 * count,
    )


def gather_second(kv, out_mine, count, number):
    def body(kv_ref, out_ref, kv_all, out_all, *sems):
        take = Taker(sems)
        place = Place(count)
        greet(place, blk=True)
        together(
            gather_blk(place, kv_ref, kv_all, *take(3)),
            gather_blk(place, out_ref, lambda i: out_all.at[:, i], *take(3)),
        )

    groups, rows, width = out_mine.shape
    return transfer(
        f"gather{number}",
        number,
        body,
        [kv, out_mine],
        [
            shape((count,) + kv.shape, kv.dtype),
            shape((groups, count, rows, width), out_mine.dtype),
        ],
        gather_blk_sems(count) + gather_blk_sems(count),
        (kv.size + out_mine.size) * 2 * count,
    )


def reduce_middle(dkv_part, out_part, count, number):
    dkv_piece = dkv_part.shape[1:]
    out_piece = out_part.shape[:1] + out_part.shape[2:]

    def body(dkv_ref, out_ref, dkv_sum, out_sum, out_mine, *scratch):
        take = Taker(scratch)
        place = Place(count)
        greet(place, blk=True, core=True, half=True, corner=True)
        far = take(3)

        def out_task(near):
            yield from reduce_blk(place, lambda i: out_ref.at[:, i], out_mine, *near)
            yield from exchange_group(place, out_mine, out_sum, *far)

        together(
            reduce_blk(place, dkv_ref, dkv_sum, *take(REDUCE_REFS)),
            out_task(take(REDUCE_REFS)),
        )

    return transfer(
        f"reduce{number}",
        number,
        body,
        [dkv_part, out_part],
        [shape(dkv_piece, jnp.bfloat16), shape(out_piece, jnp.bfloat16)],
        [pltpu.VMEM(out_piece, jnp.bfloat16)]
        + exchange_group_sems()
        + reduce_blk_scratch(count, dkv_piece, jnp.bfloat16)
        + reduce_blk_scratch(count, out_piece, jnp.bfloat16),
        (dkv_part.size + out_part.size) * 2,
        [pltpu.VMEM] * 2,
    )


def reduce_last(qkv_part, norm_part, gain_part, count, number):
    gain_piece = gain_part.shape[1:]
    qkv_piece, norm_piece = qkv_part.shape[1:], norm_part.shape[1:]

    def body(*refs):
        qkv_ref, norm_ref, gain_ref = refs[:3]
        qkv_sum, norm_sum, gain_sum = refs[3:6]
        gain_mine = refs[6]
        take = Taker(refs[7:])
        place = Place(count)
        greet(place, blk=True, core=True, half=True, corner=True)

        def gain_task(near, far):
            yield from reduce_blk(place, gain_ref, gain_mine, *near)
            yield from reduce_group(place, gain_mine, gain_sum, *far)

        together(
            gain_task(take(REDUCE_REFS), take(5)),
            reduce_blk(place, qkv_ref, qkv_sum, *take(REDUCE_REFS)),
            reduce_group(place, norm_ref, norm_sum, *take(5)),
        )

    return transfer(
        f"last{number}",
        number,
        body,
        [qkv_part, norm_part, gain_part],
        [
            shape(qkv_piece, jnp.float32),
            shape(norm_piece, jnp.float32),
            shape(gain_piece[1:], jnp.float32),
        ],
        [pltpu.VMEM(gain_piece, jnp.float32)]
        + reduce_blk_scratch(count, gain_piece, jnp.float32, 1)
        + reduce_group_scratch(gain_piece[1:], jnp.float32)
        + reduce_blk_scratch(count, qkv_piece, jnp.bfloat16)
        + reduce_group_scratch(norm_piece, jnp.bfloat16),
        qkv_part.size * 2,
        [pltpu.VMEM] * 3,
    )


def all_gather_group(value, number):
    def body(src, out, *sems):
        place = Place(lax.axis_size("blk"))
        greet(place, core=True, half=True)
        together(gather_group(place, src, out, *sems))

    return transfer(
        f"group{number}",
        number,
        body,
        [value],
        [shape((GROUPS,) + value.shape, value.dtype)],
        gather_group_sems(),
        value.size * 8,
    )[0]


def reduce_scatter_group(value, number):
    piece = value.shape[1:]

    def body(part, out, *scratch):
        place = Place(lax.axis_size("blk"))
        greet(place, core=True, half=True)
        together(reduce_group(place, part, out, *scratch))

    return transfer(
        f"fold{number}",
        number,
        body,
        [value],
        [shape(piece, jnp.float32)],
        reduce_group_scratch(piece, value.dtype),
        value.size * 2,
        [pltpu.VMEM],
    )[0]


def dot(left, right, contract):
    return lax.dot_general(left, right, (contract, ((), ())), preferred_element_type=jnp.float32)


LAST = ((1,), (1,))
PLAIN = ((1,), (0,))
FIRST = ((0,), (0,))


LANES = 128
GELU_A = math.sqrt(2.0 / math.pi)
GELU_B = 0.044715


def feed_forward_fits(count, rows, width, hidden):
    inner = 4 if count >= 32 else 2
    outer = count // inner
    tile = rows * width * 2
    weights = 3 * hidden * width * 2
    kept = count * rows * 3 * hidden * 2
    total = weights + kept + tile * (3 * count + outer * (inner - 1) + 2 * outer + 3) + 9 * tile
    total += 3 * LANES * (count * rows + 2 * width) * 2
    return total < 58 * 2**20 and hidden % (3 * LANES) == 0 and width % 256 == 0


def feed_forward_kernel(
    count,
    branch_ref,
    token_ref,
    cot_ref,
    gain_ref,
    gate_up_hbm,
    down_hbm,
    out_ref,
    middle_grad_ref,
    branch_grad_ref,
    gain_grad_ref,
    gate_up_grad_hbm,
    down_grad_hbm,
    w_gate_up,
    w_down,
    norm_all,
    grad_all,
    act,
    hidden,
    part,
    middle,
    norm_own,
    grad_own,
    total,
    turned,
    staged,
    beside,
    along,
    held,
    spare,
    w_sems,
    out_sems,
    *sems,
):
    place = Place(count)
    rows, width = norm_all.shape[1:]
    units = hidden.shape[1]
    chunks = units // LANES
    inner, outer = place.inner, place.outer
    slab = branch_ref.shape[1]
    steps = rows // slab
    columns = width // 256
    pair = inner * rows
    take = Taker(sems)

    def weight_copies(i):
        units_at = pl.ds(pl.multiple_of(i * LANES, LANES), LANES)
        return [
            pltpu.make_async_copy(
                gate_up_hbm.at[units_at, pl.ds(0, width)],
                w_gate_up.at[i, pl.ds(0, LANES)],
                w_sems.at[3 * i],
            ),
            pltpu.make_async_copy(
                gate_up_hbm.at[units_at, pl.ds(width, width)],
                w_gate_up.at[i, pl.ds(LANES, LANES)],
                w_sems.at[3 * i + 1],
            ),
            pltpu.make_async_copy(down_hbm.at[units_at], w_down.at[units_at], w_sems.at[3 * i + 2]),
        ]

    def start_weights(i, carry):
        for copy in weight_copies(i):
            copy.start()
        return carry

    def wait_weights(i, carry):
        for copy in weight_copies(i):
            copy.wait()
        return carry

    lax.fori_loop(0, chunks, start_weights, 0)

    def scale_of(values):
        return lax.rsqrt(jnp.mean(values * values, axis=-1, keepdims=True) + NORM_EPS)

    def slab_rows(i):
        return pl.ds(pl.multiple_of(i * slab, slab), slab)

    def before(i, carry):
        value = branch_ref[i]
        mid = token_ref[i].astype(jnp.float32) + value * scale_of(value) * gain_ref[1:2]
        middle[i] = mid
        norm_own[slab_rows(i)] = (mid * scale_of(mid) * gain_ref[2:3]).astype(jnp.bfloat16)
        return carry

    lax.fori_loop(0, steps, before, 0)
    greet(place, blk=True)

    def pair_rows(k):
        return pl.ds(pl.multiple_of(place.near(k) * pair, pair), pair)

    def pair_pieces(k):
        return pl.ds(place.near(k) * inner, inner)

    def column(n):
        return pl.ds(pl.multiple_of(n * 256, 256), 256)

    def put_part(k, n, value):
        split = value.astype(jnp.bfloat16).reshape((inner, steps, slab, 256))
        part[pair_pieces(k), :, :, column(n)] = split

    def receive(gather, k):
        if k == 0:
            gather.copy.wait()
        if not gather.evened:
            if k + 1 < outer:
                gather.pass_on(k + 1)
            gather.beside_arrived(k)
            return
        ends = jnp.logical_not(gather.middle)
        if k == 0:
            gather.pass_on(1)
            pl.when(gather.middle)(lambda: gather.pass_on(2))
        elif k == 1:
            pl.when(ends)(lambda: gather.pass_on(2))
            gather.pass_extra(1)
            pl.when(gather.middle)(lambda: gather.pass_on(3))
        elif k == 2:
            pl.when(ends)(lambda: gather.pass_on(3))
            gather.pass_extra(3)
        gather.beside_arrived(k)

    gather = GatherBlk(place, norm_own, lambda i: norm_all.at[i], *take(3))
    gather.start()
    lax.fori_loop(0, chunks, wait_weights, 0)
    for k in range(outer):
        receive(gather, k)
        at = pair_rows(k)

        def up_chunk(j, carry, k=k, at=at):
            x = norm_all[pair_pieces(k)].reshape(pair, width)
            both = dot(x, w_gate_up[j], LAST)
            act[at, column(j)] = both.astype(jnp.bfloat16)
            gate, up = both[:, :LANES], both[:, LANES:]
            bent = 0.5 * gate * (1.0 + jnp.tanh(GELU_A * (gate + GELU_B * (gate * gate * gate))))
            hidden[at, pl.ds(pl.multiple_of(j * LANES, LANES), LANES)] = (bent * up).astype(
                jnp.bfloat16
            )
            return carry

        lax.fori_loop(0, chunks, up_chunk, 0)

        def down_chunk(n, carry, k=k, at=at):
            put_part(k, n, dot(hidden[at, :], w_down[:, column(n)], PLAIN))
            return carry

        lax.fori_loop(0, columns, down_chunk, 0)
    gather.finish()
    reduce = ReduceBlk(place, lambda i: part.at[i], total, beside, along, held, spare, *take(6))
    reduce.start()
    for event in reduce.events():
        event()

    gain_grad_ref[...] = jnp.zeros_like(gain_grad_ref)

    def norm_back(value, gain, incoming):
        scale = scale_of(value)
        lifted = incoming * gain
        pull = jnp.mean(lifted * value, axis=-1, keepdims=True)
        gain_grad = jnp.sum(incoming * value * scale, axis=0, keepdims=True)
        return scale * lifted - value * (scale * scale * scale) * pull, gain_grad

    def between(i, carry):
        value, cot = total[i], cot_ref[i].astype(jnp.float32)
        gain = gain_ref[3:4]
        out_ref[i] = (middle[i] + value * scale_of(value) * gain).astype(jnp.bfloat16)
        grad, gain_grad = norm_back(value, gain, cot)
        gain_grad_ref[3:4] += gain_grad
        grad_own[slab_rows(i)] = grad.astype(jnp.bfloat16)
        return carry

    lax.fori_loop(0, steps, between, 0)
    reduce.finish()

    gather = GatherBlk(place, grad_own, lambda i: grad_all.at[i], *take(3))
    gather.start()
    for k in range(outer):
        receive(gather, k)
        at = pair_rows(k)

        def back_chunk(j, carry, k=k, at=at):
            g = grad_all[pair_pieces(k)].reshape(pair, width)
            units_at = pl.ds(pl.multiple_of(j * LANES, LANES), LANES)
            grad = dot(g, w_down[units_at], LAST)
            both = act[at, column(j)].astype(jnp.float32)
            gate, up = both[:, :LANES], both[:, LANES:]
            bend = jnp.tanh(GELU_A * (gate + GELU_B * (gate * gate * gate)))
            bent = 0.5 * gate * (1.0 + bend)
            slope = 0.5 * (1.0 + bend) + (0.5 * GELU_A) * gate * (1.0 - bend * bend) * (
                1.0 + (3.0 * GELU_B) * gate * gate
            )
            pulled = jnp.concatenate([grad * up * slope, grad * bent], axis=1)
            act[at, column(j)] = pulled.astype(jnp.bfloat16)
            return carry

        lax.fori_loop(0, chunks, back_chunk, 0)

        def input_chunk(n, carry, k=k, at=at):
            w = w_gate_up[:, :, column(n)].reshape(2 * units, 256)
            put_part(k, n, dot(act[at, :], w, PLAIN))
            return carry

        lax.fori_loop(0, columns, input_chunk, 0)
    gather.finish()
    reduce = ReduceBlk(place, lambda i: part.at[i], total, beside, along, held, spare, *take(6))
    reduce.start()

    tokens = count * rows
    slots = staged.shape[0]

    def up_store(i):
        slot = lax.rem(i, slots)
        units_at = pl.ds(pl.multiple_of(i * LANES, LANES), LANES)
        return [
            pltpu.make_async_copy(
                staged.at[slot, pl.ds(h * LANES, LANES)],
                gate_up_grad_hbm.at[units_at, pl.ds(h * width, width)],
                out_sems.at[slot, h],
            )
            for h in (0, 1)
        ]

    def up_grad(i, carry):
        @pl.when(i >= slots)
        def _():
            for copy in up_store(i - slots):
                copy.wait()

        turned[pl.ds(0, 256)] = jnp.transpose(act[:, column(i)])

        def one(n, c):
            x = norm_all[:, :, column(n)].reshape(tokens, 256)
            staged[lax.rem(i, slots), pl.ds(0, 256), column(n)] = dot(
                turned[pl.ds(0, 256)], x, PLAIN
            ).astype(jnp.bfloat16)
            return c

        lax.fori_loop(0, columns, one, 0)
        for copy in up_store(i):
            copy.start()
        return carry

    three = 3 * LANES

    def down_store(i):
        slot = lax.rem(i, slots)
        return pltpu.make_async_copy(
            staged.at[slot],
            down_grad_hbm.at[pl.ds(pl.multiple_of(i * three, three), three)],
            out_sems.at[slot, 2],
        )

    def down_grad(i, carry):
        @pl.when(i >= slots)
        def _():
            down_store(i - slots).wait()

        turned[...] = jnp.transpose(hidden[:, pl.ds(pl.multiple_of(i * three, three), three)])

        def one(n, c):
            x = grad_all[:, :, column(n)].reshape(tokens, 256)
            staged[lax.rem(i, slots), :, column(n)] = dot(turned[...], x, PLAIN).astype(jnp.bfloat16)
            return c

        lax.fori_loop(0, columns, one, 0)
        down_store(i).start()
        return carry

    events = reduce.events()
    early = len(events) - 3
    bounds = [chunks * k // early for k in range(early + 1)]
    for k in range(early):
        lax.fori_loop(bounds[k], bounds[k + 1], up_grad, 0)
        events[k]()
    for i in range(max(0, chunks - slots), chunks):
        for copy in up_store(i):
            copy.wait()
    thirds = units // three
    bounds = [thirds * k // 3 for k in range(4)]
    for k in range(3):
        lax.fori_loop(bounds[k], bounds[k + 1], down_grad, 0)
        events[early + k]()

    def after(i, carry):
        value, mid, cot = branch_ref[i], middle[i], cot_ref[i].astype(jnp.float32)
        grad, gain_grad = norm_back(mid, gain_ref[2:3], total[i])
        gain_grad_ref[2:3] += gain_grad
        middle_grad = cot + grad
        middle_grad_ref[i] = middle_grad
        grad, gain_grad = norm_back(value, gain_ref[1:2], middle_grad)
        gain_grad_ref[1:2] += gain_grad
        branch_grad_ref[i] = grad.astype(jnp.bfloat16)
        return carry

    lax.fori_loop(0, steps, after, 0)
    reduce.finish()
    for i in range(max(0, thirds - slots), thirds):
        down_store(i).wait()


def feed_forward(branch, tokens, cotangent, gains, gate_up_all, down_all, count, number):
    steps, slab, width = branch.shape
    rows = steps * slab
    units = down_all.shape[0]
    inner = 4 if count >= 32 else 2
    outer = count // inner
    piece = branch.shape
    bf16, f32 = jnp.bfloat16, jnp.float32
    vmem = pl.BlockSpec(memory_space=pltpu.VMEM)
    anywhere = pl.BlockSpec(memory_space=pl.ANY)
    slots = 2
    line_scratch = reduce_blk_scratch(count, piece, bf16)
    return pl.pallas_call(
        functools.partial(feed_forward_kernel, count),
        name="feed_forward",
        out_shape=[
            shape(piece, bf16),
            shape(piece, f32),
            shape(piece, bf16),
            shape((4, width), f32),
            shape(gate_up_all.shape, bf16),
            shape(down_all.shape, bf16),
        ],
        in_specs=[vmem] * 4 + [anywhere] * 2,
        out_specs=[vmem] * 4 + [anywhere] * 2,
        scratch_shapes=[
            pltpu.VMEM((units // LANES, 2 * LANES, width), bf16),
            pltpu.VMEM((units, width), bf16),
            pltpu.VMEM((count, rows, width), bf16),
            pltpu.VMEM((count, rows, width), bf16),
            pltpu.VMEM((count * rows, 2 * units), bf16),
            pltpu.VMEM((count * rows, units), bf16),
            pltpu.VMEM((count,) + piece, bf16),
            pltpu.VMEM(piece, f32),
            pltpu.VMEM((rows, width), bf16),
            pltpu.VMEM((rows, width), bf16),
            pltpu.VMEM(piece, f32),
            pltpu.VMEM((3 * LANES, count * rows), bf16),
            pltpu.VMEM((slots, 3 * LANES, width), bf16),
        ]
        + line_scratch[:4]
        + [
            pltpu.SemaphoreType.DMA((3 * units // LANES,)),
            pltpu.SemaphoreType.DMA((slots, 3)),
        ]
        + gather_blk_sems(count)
        + line_scratch[4:]
        + gather_blk_sems(count)
        + line_scratch[4:],
        compiler_params=pltpu.CompilerParams(
            collective_id=number, has_side_effects=True, vmem_limit_bytes=67043328
        ),
        cost_estimate=pl.CostEstimate(
            flops=18 * count * rows * units * width,
            bytes_accessed=500 * 2**20,
            transcendentals=0,
        ),
    )(branch, tokens, cotangent, gains, gate_up_all, down_all)


def attention_scores(q2, k, query_pos, query_doc, key_block, key_doc, rows):
    raw = lax.dot_general(q2, k, (((1,), (1,)), ((), ())), preferred_element_type=jnp.float32)
    capped = jnp.tanh(raw * (SCORE_SCALE / SOFT_CAP))
    key_pos = key_block * rows + lax.broadcasted_iota(jnp.int32, (1, rows), 1)
    visible = (key_pos <= query_pos) & (key_doc == query_doc)
    return capped, jnp.where(visible, jnp.exp(SOFT_CAP * capped), 0.0)


def attention_query(q_ref, doc_ref, here, count, rows):
    half = pl.program_id(1)
    block = half * count + here
    q2 = jnp.concatenate([q_ref[0, :, :HEAD_DIM], q_ref[0, :, HEAD_DIM:]], axis=0)
    inside = lax.broadcasted_iota(jnp.int32, (rows, 1), 0)
    position = block * rows + jnp.concatenate([inside, inside], axis=0)
    doc = jnp.concatenate([doc_ref[0], doc_ref[0]], axis=0)
    return block, q2, position, doc


def attention_forward_kernel(
    count, here_ref, q_ref, kv_ref, doc_ref, key_doc_ref, attn_ref, full_ref, total_ref, acc, tot
):
    rows = q_ref.shape[1]
    block, q2, position, doc = attention_query(q_ref, doc_ref, here_ref[0], count, rows)
    acc[...] = jnp.zeros_like(acc)
    tot[...] = jnp.zeros_like(tot)

    def one(key_block, carry):
        key_half = (key_block >= count).astype(jnp.int32)
        kv = kv_ref.at[key_block - key_half * count, key_half]
        _, weights = attention_scores(
            q2, kv[:, :HEAD_DIM], position, doc, key_block, key_doc_ref[0, key_block], rows
        )
        tot[...] += jnp.sum(weights, axis=-1, keepdims=True)
        acc[...] += jnp.dot(
            weights.astype(jnp.bfloat16), kv[:, HEAD_DIM:], preferred_element_type=jnp.float32
        )
        return carry

    lax.fori_loop(jnp.maximum(block - count, 0), block + 1, one, 0)
    attended = acc[...] / tot[...]
    attended = jnp.concatenate([attended[:rows], attended[rows:]], axis=1)
    full_ref[0] = attended
    attn_ref[0] = attended.astype(jnp.bfloat16)
    total_ref[0] = tot[...]


def attention_backward_kernel(
    count,
    here_ref,
    q_ref,
    kv_ref,
    doc_ref,
    key_doc_ref,
    grad_ref,
    full_ref,
    total_ref,
    dq_ref,
    dkv_ref,
    acc,
    key_acc,
):
    rows = q_ref.shape[1]
    half = pl.program_id(1)
    block, q2, position, doc = attention_query(q_ref, doc_ref, here_ref[0], count, rows)
    total = total_ref[0]
    grad = grad_ref[0].astype(jnp.float32)
    grad2 = jnp.concatenate([grad[:, :HEAD_DIM], grad[:, HEAD_DIM:]], axis=0)
    full2 = jnp.concatenate([full_ref[0, :, :HEAD_DIM], full_ref[0, :, HEAD_DIM:]], axis=0)
    total_grad = -jnp.sum(grad2 * full2, axis=-1, keepdims=True) / total
    sums_grad = (grad2 / total).astype(jnp.bfloat16)
    acc[...] = jnp.zeros_like(acc)

    @pl.when(half == 0)
    def _():
        def clear(i, carry):
            key_acc[i] = jnp.zeros(key_acc.shape[1:], jnp.float32)
            return carry

        lax.fori_loop(0, key_acc.shape[0], clear, 0)

    def one(key_block, carry):
        key_half = (key_block >= count).astype(jnp.int32)
        inner = key_block - key_half * count
        kv = kv_ref.at[inner, key_half]
        keys = kv[:, :HEAD_DIM]
        capped, weights = attention_scores(
            q2, keys, position, doc, key_block, key_doc_ref[0, key_block], rows
        )
        exp_grad = lax.dot_general(
            sums_grad, kv[:, HEAD_DIM:], (((1,), (1,)), ((), ())), preferred_element_type=jnp.float32
        )
        raw_grad = (
            weights * (exp_grad + total_grad) * (1.0 - capped * capped) * SCORE_SCALE
        ).astype(jnp.bfloat16)
        acc[...] += jnp.dot(raw_grad, keys, preferred_element_type=jnp.float32)
        over_rows = (((0,), (0,)), ((), ()))
        slot = inner * 2 + key_half
        key_acc[slot, :, :HEAD_DIM] += lax.dot_general(
            raw_grad, q2, over_rows, preferred_element_type=jnp.float32
        )
        key_acc[slot, :, HEAD_DIM:] += lax.dot_general(
            weights.astype(jnp.bfloat16), sums_grad, over_rows, preferred_element_type=jnp.float32
        )
        return carry

    lax.fori_loop(jnp.maximum(block - count, 0), block + 1, one, 0)
    dq = acc[...]
    dq_ref[0] = jnp.concatenate([dq[:rows], dq[rows:]], axis=1).astype(jnp.bfloat16)

    @pl.when(half == 1)
    def _():
        def put(i, carry):
            for k in (0, 1):
                dkv_ref[i, k] = key_acc[i * 2 + k].astype(jnp.bfloat16)
            return carry

        lax.fori_loop(0, count, put, 0)


def attention_specs(count, rows, width):
    query = pl.BlockSpec((1, rows, width), lambda s, h, here: (2 * s + h, 0, 0))
    keys = pl.BlockSpec((count, 2, rows, 2 * HEAD_DIM), lambda s, h, here: (0, s, 0, 0))
    doc = pl.BlockSpec((1, rows, 1), lambda s, h, here: (2 * s + h, 0, 0))
    key_doc = pl.BlockSpec((1, 2 * count, 1, rows), lambda s, h, here: (s, 0, 0, 0))
    total = pl.BlockSpec((1, REPS * rows, 1), lambda s, h, here: (2 * s + h, 0, 0))
    return query, keys, doc, key_doc, total


def attention_forward(here, q, kv, doc, key_doc):
    count, _, rows, _ = kv.shape
    width = REPS * HEAD_DIM
    query, keys, doc_spec, key_doc_spec, total = attention_specs(count, rows, width)
    return pl.pallas_call(
        functools.partial(attention_forward_kernel, count),
        name="attend",
        grid_spec=pltpu.PrefetchScalarGridSpec(
            num_scalar_prefetch=1,
            grid=(2, 2),
            in_specs=[query, keys, doc_spec, key_doc_spec],
            out_specs=[query, query, total],
            scratch_shapes=[
                pltpu.VMEM((REPS * rows, HEAD_DIM), jnp.float32),
                pltpu.VMEM((REPS * rows, 1), jnp.float32),
            ],
        ),
        out_shape=[
            shape((GROUPS, rows, width), jnp.bfloat16),
            shape((GROUPS, rows, width), jnp.float32),
            shape((GROUPS, REPS * rows, 1), jnp.float32),
        ],
        compiler_params=pltpu.CompilerParams(vmem_limit_bytes=VMEM_LIMIT),
        cost_estimate=pl.CostEstimate(flops=10**9, bytes_accessed=40 * 2**20, transcendentals=0),
    )(here, q, kv, doc, key_doc)


def attention_backward(here, q, kv, doc, key_doc, grad, full, totals):
    count, _, rows, _ = kv.shape
    width = REPS * HEAD_DIM
    query, keys, doc_spec, key_doc_spec, total = attention_specs(count, rows, width)
    return pl.pallas_call(
        functools.partial(attention_backward_kernel, count),
        name="attend_back",
        grid_spec=pltpu.PrefetchScalarGridSpec(
            num_scalar_prefetch=1,
            grid=(2, 2),
            in_specs=[query, keys, doc_spec, key_doc_spec, query, query, total],
            out_specs=[query, keys],
            scratch_shapes=[
                pltpu.VMEM((REPS * rows, HEAD_DIM), jnp.float32),
                pltpu.VMEM((2 * count, rows, 2 * HEAD_DIM), jnp.float32),
            ],
        ),
        out_shape=[shape((GROUPS, rows, width), jnp.bfloat16), shape(kv.shape, jnp.bfloat16)],
        compiler_params=pltpu.CompilerParams(vmem_limit_bytes=VMEM_LIMIT),
        cost_estimate=pl.CostEstimate(flops=2 * 10**9, bytes_accessed=80 * 2**20, transcendentals=0),
    )(here, q, kv, doc, key_doc, grad, full, totals)


def rms_scale(values, gain_row):
    return (
        values * lax.rsqrt(jnp.mean(values * values, axis=-1, keepdims=True) + NORM_EPS) * gain_row
    )


def gelu_tanh(values):
    return jax.nn.gelu(values, approximate=True)


def rope_tables(positions):
    half_width = HEAD_DIM // 2
    frequency = jnp.exp(
        jnp.arange(half_width, dtype=jnp.float32) * (-2.0 * math.log(ROPE_BASE) / HEAD_DIM)
    )
    angles = positions.astype(jnp.float32)[:, None] * frequency[None, :]
    cosine = jnp.concatenate([jnp.cos(angles), jnp.cos(angles)], axis=-1)
    sine = jnp.concatenate([jnp.sin(angles), jnp.sin(angles)], axis=-1)
    return cosine[:, None, :], sine[:, None, :]


def rotate(values, cosine, sine):
    half_width = HEAD_DIM // 2
    turned = jnp.concatenate([-values[..., half_width:], values[..., :half_width]], axis=-1)
    return values * cosine + turned * sine


def feed_forward_apart(
    branch_slabs, inputs, cotangent, gains, gate_up_all, down_all, count, piece
):
    rows, width = inputs.shape
    bf16 = jnp.bfloat16
    branch = branch_slabs.reshape(rows, width)
    middle = inputs + rms_scale(branch, gains[1])
    norm_three = rms_scale(middle, gains[2]).astype(bf16)
    gate_all = gate_up_all[:, :width]
    up_all = gate_up_all[:, width:]
    norm_all = all_gather_blk(norm_three, count, 4).reshape(count * rows, width)
    gate = dot(norm_all, gate_all, LAST)
    up = dot(norm_all, up_all, LAST)
    hidden = (gelu_tanh(gate) * up).astype(bf16)
    ffn_part = dot(hidden, down_all, PLAIN).astype(bf16)
    ffn_out = reduce_scatter_blk(ffn_part.reshape((count,) + piece), count, 5).reshape(rows, width)
    output = (middle + rms_scale(ffn_out, gains[3])).astype(bf16)[None]

    out_cotangent = cotangent[0].astype(jnp.float32)
    _, post_ffn_back = jax.vjp(rms_scale, ffn_out, gains[3])
    ffn_grad, gain_grad_four = post_ffn_back(out_cotangent)
    grad_all = all_gather_blk(ffn_grad.astype(bf16), count, 6).reshape(count * rows, width)
    activated, gelu_back = jax.vjp(gelu_tanh, gate)
    hidden_grad = dot(grad_all, down_all, LAST)
    gate_grad = gelu_back(hidden_grad * up)[0].astype(bf16)
    up_grad = (hidden_grad * activated).astype(bf16)
    norm_part = dot(gate_grad, gate_all, PLAIN) + dot(up_grad, up_all, PLAIN)
    norm_three_grad = reduce_scatter_blk(
        norm_part.astype(bf16).reshape((count,) + piece), count, 7
    ).reshape(rows, width)
    down_part = dot(hidden, grad_all, FIRST).astype(bf16)
    gate_up_part = jnp.concatenate(
        [dot(gate_grad, norm_all, FIRST), dot(up_grad, norm_all, FIRST)], axis=1
    ).astype(bf16)
    _, pre_ffn_back = jax.vjp(rms_scale, middle, gains[2])
    middle_part, gain_grad_three = pre_ffn_back(norm_three_grad)
    middle_grad = out_cotangent + middle_part
    _, post_attn_back = jax.vjp(rms_scale, branch, gains[1])
    branch_grad, gain_grad_two = post_attn_back(middle_grad)
    return (
        output,
        middle_grad,
        branch_grad.astype(bf16),
        gain_grad_two,
        gain_grad_three,
        gain_grad_four,
        gate_up_part,
        down_part,
    )


def shards(
    tokens, cotangent, segments, norm_gains, qkv_weight, out_weight, gate_up_weight, down_weight
):
    _, rows, width = tokens.shape
    count = lax.axis_size("blk")
    here = lax.axis_index("blk")
    mine = 2 * lax.axis_index("dp") + lax.axis_index("head")
    group_rows = GROUPS * rows
    head_width = REPS * HEAD_DIM
    bf16 = jnp.bfloat16
    slab = slabs(rows)
    piece = (rows // slab, slab, width)

    gate_up_all = lax.all_gather(gate_up_weight, ("dp", "head"), axis=0, tiled=True)
    down_all = lax.all_gather(down_weight, ("dp", "head"), axis=0, tiled=True)

    gain_rows = norm_gains.shape[0]
    gain_lanes = -(-gain_rows // 128) * 128
    gains_sent = jnp.pad(
        jnp.transpose(norm_gains).astype(jnp.float32), ((0, 4), (0, gain_lanes - gain_rows))
    )
    out_rows = out_weight.shape[0]
    out_sent = jnp.transpose(out_weight.reshape(out_rows, GROUPS, head_width), (1, 0, 2))
    qkv_rows = qkv_weight.shape[0]
    qkv_slab = slabs(qkv_rows)
    qkv_piece = (qkv_rows // qkv_slab, qkv_slab, width)
    qkv_all, out_mine, tokens_all, gains_all, docs_all = gather_first(
        qkv_weight, out_sent, tokens[0], gains_sent, segments.reshape(-1, 128), count, 1
    )
    gains = jnp.transpose(gains_all[:, :, :4, :gain_rows], (2, 0, 1, 3)).reshape(4, width)
    qkv_head = qkv_all.reshape(count * qkv_rows, width)
    docs = docs_all.reshape(2, 2, count, rows)
    key_doc = docs.reshape(2, 2 * count, 1, rows)
    own_doc = lax.dynamic_index_in_dim(docs, here, 2, keepdims=False).reshape(GROUPS, rows, 1)
    here_one = here.reshape(1)

    group_tokens = tokens_all.reshape(group_rows, width).astype(jnp.float32)
    norm_one = rms_scale(group_tokens, gains[0]).astype(bf16)
    proj = dot(norm_one, qkv_head, LAST)
    inside = jnp.arange(rows, dtype=jnp.int32)
    position = jnp.concatenate([here * rows + inside, (count + here) * rows + inside])
    cosine, sine = rope_tables(jnp.concatenate([position, position]))
    proj = proj.reshape(group_rows, REPS + 2, HEAD_DIM)
    turned = rotate(proj[:, : REPS + 1], cosine, sine)
    sent = jnp.concatenate([turned, proj[:, REPS + 1 :]], axis=1).astype(bf16)
    queries = sent[:, :REPS].reshape(GROUPS, rows, head_width)
    own_kv = sent[:, REPS:].reshape(group_rows, 2 * HEAD_DIM)
    kv_slab = slabs(group_rows)
    kv_piece = (group_rows // kv_slab, kv_slab, 2 * HEAD_DIM)
    kv, out_all = gather_second(own_kv, out_mine, count, 2)
    kv = kv.reshape(count, GROUPS, rows, 2 * HEAD_DIM)
    out_head = out_all.reshape(width, head_width)
    attn, attended, totals = attention_forward(here_one, queries, kv, own_doc, key_doc)
    attn = attn.reshape(group_rows, head_width)
    branch_part = dot(attn, out_head, LAST).astype(bf16)
    branch_slabs = reduce_scatter_group(branch_part.reshape((GROUPS,) + piece), 3)
    inputs = tokens[0].astype(jnp.float32)
    if feed_forward_fits(count, rows, width, down_all.shape[0]):
        output, middle_grad, branch_grad, gain_rest, gate_up_part, down_part = feed_forward(
            branch_slabs,
            tokens.reshape(piece),
            cotangent.reshape(piece),
            gains,
            gate_up_all,
            down_all,
            count,
            4,
        )
        output = output.reshape(tokens.shape)
        middle_grad = middle_grad.reshape(rows, width)
        branch_grad = branch_grad.reshape(rows, width)
        gain_grad_two, gain_grad_three, gain_grad_four = gain_rest[1], gain_rest[2], gain_rest[3]
    else:
        (
            output,
            middle_grad,
            branch_grad,
            gain_grad_two,
            gain_grad_three,
            gain_grad_four,
            gate_up_part,
            down_part,
        ) = feed_forward_apart(
            branch_slabs, inputs, cotangent, gains, gate_up_all, down_all, count, piece
        )
    gate_up_grad = lax.psum_scatter(
        gate_up_part, ("dp", "head"), scatter_dimension=0, tiled=True
    ).astype(jnp.float32)
    down_grad = lax.psum_scatter(
        down_part, ("dp", "head"), scatter_dimension=0, tiled=True
    ).astype(jnp.float32)
    branch_all = all_gather_group(branch_grad, 8).reshape(group_rows, width)
    attn_grad = dot(branch_all, out_head, PLAIN).astype(bf16).reshape(GROUPS, rows, head_width)
    out_part = dot(branch_all, attn, FIRST).astype(bf16)
    out_part = out_part.reshape(GROUPS, count, out_rows, head_width)
    dq, dkv_part = attention_backward(
        here_one, queries, kv, own_doc, key_doc, attn_grad, attended, totals
    )
    dkv, out_grad = reduce_middle(dkv_part.reshape((count,) + kv_piece), out_part, count, 9)
    sent_grad = jnp.concatenate(
        [
            dq.reshape(group_rows, REPS, HEAD_DIM),
            dkv.reshape(group_rows, 2, HEAD_DIM),
        ],
        axis=1,
    ).astype(jnp.float32)
    unturned = rotate(sent_grad[:, : REPS + 1], cosine, -sine)
    proj_grad = (
        jnp.concatenate([unturned, sent_grad[:, REPS + 1 :]], axis=1)
        .astype(bf16)
        .reshape(group_rows, (REPS + 2) * HEAD_DIM)
    )
    qkv_part = dot(proj_grad, norm_one, FIRST).astype(bf16)
    norm_one_part = dot(proj_grad, qkv_head, PLAIN)
    _, gain_back = jax.vjp(lambda gain: rms_scale(group_tokens, gain), gains[0])
    (gain_grad_one,) = gain_back(norm_one_part)
    gain_part = jnp.stack([gain_grad_one, gain_grad_two, gain_grad_three, gain_grad_four])
    gain_part = jnp.transpose(gain_part.reshape(4, GROUPS, count, gain_rows), (2, 1, 0, 3))
    gain_part = jnp.pad(gain_part, ((0, 0), (0, 0), (0, 4), (0, gain_lanes - gain_rows)))
    qkv_grad, norm_one_grad, gain_grad = reduce_last(
        qkv_part.reshape((count,) + qkv_piece),
        norm_one_part.astype(bf16).reshape((GROUPS,) + piece),
        gain_part[:, :, None],
        count,
        10,
    )
    qkv_grad = qkv_grad.reshape(qkv_rows, width)
    out_grad = (
        jnp.transpose(out_grad, (1, 0, 2)).reshape(out_rows, GROUPS * head_width).astype(jnp.float32)
    )
    gain_grad = jnp.transpose(gain_grad.reshape(8, gain_lanes)[:4, :gain_rows])
    _, pre_attn_back = jax.vjp(lambda values: rms_scale(values, gains[0]), inputs)
    (input_part,) = pre_attn_back(norm_one_grad.reshape(rows, width))
    tokens_grad = (middle_grad + input_part).astype(bf16)[None]
    return (output, tokens_grad, gain_grad, qkv_grad, out_grad, gate_up_grad, down_grad)


def solution(mesh):
    whole = ("dp", "head", "blk")
    return jax.shard_map(
        shards,
        mesh=mesh,
        in_specs=(
            P("dp", ("head", "blk"), None),
            P("dp", ("head", "blk"), None),
            P("dp", None),
            P(whole, None),
            P(whole, None),
            P(whole, None),
            P(whole, None),
            P(whole, None),
        ),
        out_specs=(
            P("dp", ("head", "blk"), None),
            P("dp", ("head", "blk"), None),
            P(whole, None),
            P(whole, None),
            P(whole, None),
            P(whole, None),
            P(whole, None),
        ),
        check_vma=False,
    )
```

```python
import functools
import math

import jax
import jax.numpy as jnp
from jax import lax
from jax.experimental import pallas as pl
from jax.experimental.pallas import tpu as pltpu
from jax.sharding import PartitionSpec as P

HEADS = 8
KV_HEADS = 4
HEAD_DIM = 256
REPS = HEADS // KV_HEADS
GROUPS = 4
SOFT_CAP = 50.0
NORM_EPS = 1e-06
ROPE_BASE = 10000.0
SCORE_SCALE = HEAD_DIM ** (-0.5)

MESH = pl.DeviceIdType.MESH
VMEM_LIMIT = 60 * 1024 * 1024


class Place:
    def __init__(self, count):
        self.count = count
        self.inner = 4 if count >= 32 else 2
        self.outer = count // self.inner
        self.here = lax.axis_index("blk")
        self.line = self.here // self.inner
        self.side = lax.rem(self.here, self.inner)
        self.core = lax.axis_index("dp")
        self.half = lax.axis_index("head")
        self.group = 2 * self.core + self.half

    def near(self, k):
        orders = [near_order(self.outer, line)[k] for line in range(self.outer)]
        found = jnp.int32(orders[0])
        for line in range(1, self.outer):
            found = jnp.where(self.line == line, jnp.int32(orders[line]), found)
        return found

    def at(self, line, side):
        return {"blk": line * self.inner + side}

    def beside(self, step):
        return lax.rem(self.side + step, self.inner)

    def partner(self):
        return {"dp": 1 - self.core}

    def across(self):
        return {"head": 1 - self.half}

    def corner(self):
        return {"dp": 1 - self.core, "head": 1 - self.half}


def remote(src, dst, sent, came, device):
    return pltpu.make_async_remote_copy(
        src_ref=src, dst_ref=dst, send_sem=sent, recv_sem=came, device_id=device, device_id_type=MESH
    )


def greet(place, blk=False, core=False, half=False, corner=False):
    sem = pltpu.get_barrier_semaphore()
    amount = jnp.int32(0)

    def hello(device):
        pl.semaphore_signal(sem, inc=1, device_id=device, device_id_type=MESH)

    if blk:
        up, down = place.line < place.outer - 1, place.line > 0
        pl.when(up)(lambda: hello(place.at(place.line + 1, place.side)))
        pl.when(down)(lambda: hello(place.at(place.line - 1, place.side)))
        amount = amount + up.astype(jnp.int32) + down.astype(jnp.int32) + (place.inner - 1)
        for step in range(1, place.inner):
            hello(place.at(place.line, place.beside(step)))
    for wanted, device in (
        (core, place.partner()),
        (half, place.across()),
        (corner, place.corner()),
    ):
        if wanted:
            hello(device)
            amount = amount + 1
    pl.semaphore_wait(sem, amount)


def together(*tasks):
    tasks = list(tasks)
    while tasks:
        for task in list(tasks):
            try:
                next(task)
            except StopIteration:
                tasks.remove(task)


def waiting(task, *rounds):
    for step, _ in enumerate(task):
        yield
        if step < len(rounds):
            for _ in range(rounds[step]):
                yield


def near_order(outer, line):
    ends = outer == 4
    return sorted(
        range(outer),
        key=lambda other: (abs(other - line), ends and other not in (0, outer - 1), other),
    )


def evened(place, parts):
    return parts == 2 and place.inner == 2 and place.outer == 4


def part_of(ref, h, parts):
    if parts == 1:
        return ref
    size = ref.shape[0] // parts
    return ref.at[pl.ds(h * size, size)]


def gather_blk_sems(place_count, parts=2):
    inner = 4 if place_count >= 32 else 2
    return [
        pltpu.SemaphoreType.DMA((2 + inner, place_count, parts)),
        pltpu.SemaphoreType.DMA((place_count, parts)),
        pltpu.SemaphoreType.DMA,
    ]


class GatherBlk:
    def __init__(self, place, src, view, sent, came, own):
        self.place, self.src, self.view, self.sent, self.came = place, src, view, sent, came
        self.parts = came.shape[1]
        self.evened = evened(place, self.parts)
        self.middle = (place.line > 0) & (place.line < place.outer - 1)
        self.copy = pltpu.make_async_copy(src, view(place.here), own)

    def sends(self, k, h):
        place = self.place
        there = place.near(k)
        piece = there * place.inner + place.side
        there_view = part_of(self.view(piece), h, self.parts)
        src = part_of(self.src, h, self.parts) if k == 0 else there_view

        def send(kind, device):
            return remote(
                src, there_view, self.sent.at[kind, piece, h], self.came.at[piece, h], device
            )

        line, side = place.line, place.side
        up = (there <= line) & (line < place.outer - 1)
        down = (there >= line) & (line > 0)
        aside = range(1, place.inner)
        if self.evened and h == 1 and k == place.outer - 1:
            aside = ()
        return (
            [
                (up, lambda: send(0, place.at(line + 1, side))),
                (down, lambda: send(1, place.at(line - 1, side))),
            ],
            [send(1 + step, place.at(line, place.beside(step))) for step in aside],
        )

    def forward(self, k, h):
        along, aside = self.sends(k, h)
        for needed, make in along:
            pl.when(needed)(lambda make=make: make().start())
        for one in aside:
            one.start()

    def start(self):
        self.copy.start()
        for h in range(self.parts):
            self.forward(0, h)

    def arrived(self, piece, h):
        place = self.place
        remote(
            part_of(self.src, h, self.parts),
            part_of(self.view(piece), h, self.parts),
            self.sent.at[0, piece, h],
            self.came.at[piece, h],
            place.at(place.line, place.beside(1)),
        ).wait_recv()

    def pass_on(self, k):
        for h in range(self.parts):
            self.arrived(self.place.near(k) * self.place.inner + self.place.side, h)
            self.forward(k, h)

    def extra(self, k):
        place = self.place
        piece = place.near(k) * place.inner + place.beside(1)
        to = place.near(2 if k == 1 else 1)
        half = part_of(self.view(piece), 1, 2)
        return remote(
            half,
            half,
            self.sent.at[place.inner + 1, piece, 1],
            self.came.at[piece, 1],
            place.at(to, place.side),
        )

    def pass_extra(self, k):
        if self.evened:

            @pl.when(self.middle)
            def _():
                self.arrived(self.place.near(k) * self.place.inner + self.place.beside(1), 1)
                self.extra(k).start()

    def beside_arrived(self, k):
        for step in range(1, self.place.inner):
            piece = self.place.near(k) * self.place.inner + self.place.beside(step)
            for h in range(self.parts):
                if self.evened and h == 1 and k in (1, self.place.outer - 1):
                    pl.when(jnp.logical_not(self.middle))(lambda: self.arrived(piece, 1))
                else:
                    self.arrived(piece, h)

    def finish(self):
        for k in range(self.place.outer):
            for h in range(self.parts):
                along, aside = self.sends(k, h)
                for needed, make in along:
                    pl.when(needed)(lambda make=make: make().wait_send())
                for one in aside:
                    one.wait_send()
        if self.evened:

            @pl.when(self.middle)
            def _():
                self.extra(1).wait_send()
                self.extra(self.place.outer - 1).wait_send()


def gather_blk(place, src, view, sent, came, own):
    if not callable(view):
        out = view
        view = lambda piece: out.at[piece]
    work = GatherBlk(place, src, view, sent, came, own)
    work.start()
    yield
    for k in range(1, place.outer):
        work.pass_on(k)
        if k == place.outer - 2:
            work.pass_extra(1)
        yield
    work.pass_extra(place.outer - 1)
    yield
    for k in range(place.outer):
        work.beside_arrived(k)
    work.finish()
    work.copy.wait()


def add_into(out, *terms):
    def one(i, carry):
        total = terms[0][i].astype(jnp.float32)
        for term in terms[1:]:
            total = total + term[i].astype(jnp.float32)
        out[i] = total.astype(out.dtype)
        return carry

    lax.fori_loop(0, out.shape[0], one, 0)


def reduce_blk_scratch(place_count, piece, dtype, parts=2):
    inner = 4 if place_count >= 32 else 2
    outer = place_count // inner
    half = (piece[0] // 2,) + tuple(piece[1:]) if parts == 2 and inner == 2 and outer == 4 else (1, 8, 128)
    return [
        pltpu.VMEM((outer, inner - 1) + piece, dtype),
        pltpu.VMEM((outer + 1,) + piece, dtype),
        pltpu.VMEM((outer,) + piece, dtype),
        pltpu.VMEM((4,) + half, dtype),
        pltpu.SemaphoreType.DMA((outer, inner - 1, parts)),
        pltpu.SemaphoreType.DMA((outer, inner - 1, parts)),
        pltpu.SemaphoreType.DMA((outer, parts)),
        pltpu.SemaphoreType.DMA((outer + 1, parts)),
        pltpu.SemaphoreType.DMA((2,)),
        pltpu.SemaphoreType.DMA((2,)),
    ]


REDUCE_REFS = 10


class ReduceBlk:
    def __init__(
        self,
        place,
        view,
        out,
        beside,
        along,
        held,
        spare,
        side_sent,
        side_came,
        line_sent,
        line_came,
        spare_sent,
        spare_came,
    ):
        self.place, self.view, self.out = place, view, out
        self.beside, self.along, self.held, self.spare = beside, along, held, spare
        self.side_sems, self.line_sems = (side_sent, side_came), (line_sent, line_came)
        self.spare_sems = (spare_sent, spare_came)
        self.parts = line_sent.shape[1]
        self.evened = evened(place, self.parts)
        self.middle = (place.line > 0) & (place.line < place.outer - 1)

    def part(self, ref, h):
        return part_of(ref, h, self.parts)

    def far(self, k):
        return self.place.near(self.place.outer - 1 - k)

    def alone(self, k, h):
        return self.evened and k == 0 and h == 1

    def side_copy(self, there, step, h, src=None):
        place = self.place
        to = place.beside(step)
        if src is None:
            src = self.part(self.view(there * place.inner + to), h)
        return remote(
            src,
            self.part(self.beside.at[there, place.inner - step - 1], h),
            self.side_sems[0].at[there, step - 1, h],
            self.side_sems[1].at[there, place.inner - step - 1, h],
            place.at(place.line, to),
        )

    def line_copy(self, there, slot, to, h, src=None):
        return remote(
            self.part(self.held.at[there], h) if src is None else src,
            self.part(self.along.at[slot], h),
            self.line_sems[0].at[there, h],
            self.line_sems[1].at[slot, h],
            self.place.at(to, self.place.side),
        )

    def send(self, k, h):
        for step in range(1, self.place.inner):
            self.side_copy(self.far(k), step, h).start()

    def terms(self, k, h):
        place = self.place
        there = self.far(k)
        own = [self.part(self.view(there * place.inner + place.side), h)]
        if self.alone(k, h):
            return own
        for step in range(1, place.inner):
            self.side_copy(there, step, h).wait_recv()
        return own + [self.part(self.beside.at[there, j], h) for j in range(place.inner - 1)]

    def onward(self, there, h, src=None):
        line, outer = self.place.line, self.place.outer
        to = jnp.where(there < line, line - 1, line + 1)
        slot = jnp.where(there == line + 1, outer, there)
        return self.line_copy(there, slot, to, h, src)

    def starts(self, there):
        line, outer = self.place.line, self.place.outer
        return ((there < line) & (line == outer - 1)) | ((there > line) & (line == 0))

    def pass_on(self, k, h):
        place = self.place
        line = place.line
        there = self.far(k)
        terms = self.terms(k, h)
        held = self.part(self.held.at[there], h)
        starts = self.starts(there)

        @pl.when(starts)
        def _():
            add_into(held, *terms)

        @pl.when(jnp.logical_not(starts))
        def _():
            back = jnp.where(there < line, line + 1, line - 1)
            self.line_copy(there, there, back, h).wait_recv()
            add_into(held, self.part(self.along.at[there], h), *terms)

        self.onward(there, h).start()

    def last(self, h):
        place = self.place
        line, outer = place.line, place.outer
        terms = self.terms(outer - 1, h)
        below, above = line > 0, line < outer - 1
        from_above = self.part(self.along.at[line], h)
        from_below = self.part(self.along.at[outer], h)
        out = self.part(self.out, h)

        @pl.when(above)
        def _():
            self.line_copy(line, line, line + 1, h).wait_recv()

        @pl.when(below)
        def _():
            self.line_copy(line, outer, line - 1, h).wait_recv()

        @pl.when(above & below)
        def _():
            add_into(out, from_above, from_below, *terms)

        @pl.when(above & jnp.logical_not(below))
        def _():
            add_into(out, from_above, *terms)

        @pl.when(jnp.logical_not(above) & below)
        def _():
            add_into(out, from_below, *terms)


    def spare_view(self, k):
        place = self.place
        return self.part(self.view(place.near(k) * place.inner + place.beside(1)), 1)

    def spare_first(self):
        return remote(
            self.spare_view(3),
            self.spare.at[0],
            self.spare_sems[0].at[0],
            self.spare_sems[1].at[0],
            self.place.at(self.place.near(1), self.place.side),
        )

    def spare_second(self):
        return remote(
            self.spare.at[2],
            self.spare.at[1],
            self.spare_sems[0].at[1],
            self.spare_sems[1].at[1],
            self.place.at(self.place.near(2), self.place.side),
        )

    def spare_side(self):
        return self.side_copy(self.far(2), 1, 1, self.spare.at[3])

    def opening(self):
        outer = self.place.outer
        if not self.evened:

            def every():
                for k in range(outer):
                    for h in range(self.parts):
                        self.send(k, h)

            return [every]
        ends = jnp.logical_not(self.middle)

        def along():
            self.spare_first().start()
            there = self.far(0)
            self.onward(
                there, 1, self.part(self.view(there * self.place.inner + self.place.side), 1)
            ).start()

        todo = [lambda: self.send(0, 0), lambda: pl.when(ends)(along)]
        todo += [lambda k=k, h=h: self.send(k, h) for k, h in ((1, 0), (1, 1), (2, 0))]
        todo += [
            lambda k=k, h=h: pl.when(ends)(lambda: self.send(k, h))
            for k, h in ((2, 1), (3, 0), (3, 1))
        ]
        return todo

    def start(self):
        for step in self.opening():
            step()

    def turning(self):
        def first():
            self.spare_first().wait_recv()
            add_into(self.spare.at[2], self.spare.at[0], self.spare_view(3))
            self.spare_second().start()

        def second():
            self.spare_second().wait_recv()
            add_into(self.spare.at[3], self.spare.at[1], self.spare_view(1))
            self.spare_side().start()
            for h in (0, 1):
                self.send(3, h)

        steps = (first, lambda: self.pass_on(0, 1), second)
        return [lambda step=step: pl.when(self.middle)(step) for step in steps]

    def events(self):
        outer, parts = self.place.outer, self.parts
        if self.evened:
            todo = self.turning() + [lambda: self.pass_on(0, 0)]
        else:
            todo = [lambda h=h: self.pass_on(0, h) for h in range(parts)]
        for k in range(1, outer - 1):
            for h in range(parts):
                todo.append(lambda k=k, h=h: self.pass_on(k, h))
        for h in range(parts):
            todo.append(lambda h=h: self.last(h))
        return todo

    def finish(self):
        for k in range(self.place.outer):
            for h in range(self.parts):
                if k < self.place.outer - 1:
                    self.onward(self.far(k), h).wait_send()
                if not self.alone(k, h):
                    for step in range(1, self.place.inner):
                        self.side_copy(self.far(k), step, h).wait_send()
        if self.evened:

            @pl.when(self.middle)
            def _():
                self.spare_second().wait_send()

            @pl.when(jnp.logical_not(self.middle))
            def _():
                self.spare_first().wait_send()


def reduce_blk(place, view, out, *scratch):
    if not callable(view):
        part = view
        view = lambda piece: part.at[piece]
    work = ReduceBlk(place, view, out, *scratch)
    for step in work.opening() + work.events():
        step()
        yield
    work.finish()


def gather_group_sems():
    return [pltpu.SemaphoreType.DMA((3,)), pltpu.SemaphoreType.DMA((4,)), pltpu.SemaphoreType.DMA]


def gather_group(place, src, out, sent, came, own):
    copy = pltpu.make_async_copy(src, out.at[place.group], own)
    copy.start()
    mine, other = place.group, 2 * place.core + (1 - place.half)
    to_half = remote(src, out.at[mine], sent.at[0], came.at[mine], place.across())
    to_core = remote(src, out.at[mine], sent.at[1], came.at[mine], place.partner())
    to_half.start()
    to_core.start()
    yield
    remote(src, out.at[other], sent.at[0], came.at[other], place.across()).wait_recv()
    relay = remote(out.at[other], out.at[other], sent.at[2], came.at[other], place.partner())
    relay.start()
    yield
    for half in (0, 1):
        slot = 2 * (1 - place.core) + half
        remote(src, out.at[slot], sent.at[0], came.at[slot], place.partner()).wait_recv()
    to_half.wait_send()
    to_core.wait_send()
    relay.wait_send()
    copy.wait()


def reduce_group_scratch(piece, dtype):
    return [
        pltpu.VMEM((2,) + piece, dtype),
        pltpu.VMEM(piece, dtype),
        pltpu.VMEM(piece, dtype),
        pltpu.SemaphoreType.DMA((3,)),
        pltpu.SemaphoreType.DMA((3,)),
    ]


def reduce_group(place, part, out, from_core, from_half, held, sent, came):
    far = 2 * (1 - place.core) + (1 - place.half)
    near = 2 * (1 - place.core) + place.half
    first = remote(part.at[far], from_core.at[1], sent.at[0], came.at[0], place.partner())
    second = remote(part.at[near], from_core.at[0], sent.at[1], came.at[1], place.partner())
    first.start()
    second.start()
    yield
    first.wait_recv()
    add_into(held, part.at[2 * place.core + (1 - place.half)], from_core.at[1])
    third = remote(held, from_half, sent.at[2], came.at[2], place.across())
    third.start()
    yield
    second.wait_recv()
    third.wait_recv()
    add_into(out, part.at[place.group], from_core.at[0], from_half)
    first.wait_send()
    second.wait_send()
    third.wait_send()


def exchange_group_sems():
    return [pltpu.SemaphoreType.DMA((3,)), pltpu.SemaphoreType.DMA((4,)), pltpu.SemaphoreType.DMA]


def exchange_group(place, src, out, sent, came, own):
    mine = place.group
    copy = pltpu.make_async_copy(src.at[mine], out.at[mine], own)
    copy.start()
    core, half = place.core, place.half
    links = (
        (2 * (1 - core) + (1 - half), place.corner()),
        (2 * core + (1 - half), place.across()),
        (2 * (1 - core) + half, place.partner()),
    )
    copies = [
        remote(src.at[to], out.at[mine], sent.at[k], came.at[mine], device)
        for k, (to, device) in enumerate(links)
    ]
    for one in copies:
        one.start()
    yield
    for k, (peer, device) in enumerate(links):
        remote(src.at[peer], out.at[peer], sent.at[k], came.at[peer], device).wait_recv()
    for one in copies:
        one.wait_send()
    copy.wait()


def transfer(name, number, body, ins, outs, scratch, moved, out_spaces=None):
    spaces = out_spaces or [pl.ANY] * len(outs)
    return pl.pallas_call(
        body,
        name=name,
        out_shape=outs,
        in_specs=[pl.BlockSpec(memory_space=pltpu.VMEM)] * len(ins),
        out_specs=[pl.BlockSpec(memory_space=space) for space in spaces],
        scratch_shapes=scratch,
        compiler_params=pltpu.CompilerParams(
            collective_id=number, has_side_effects=True, vmem_limit_bytes=VMEM_LIMIT
        ),
        cost_estimate=pl.CostEstimate(flops=0, bytes_accessed=moved * 40, transcendentals=0),
    )(*ins)


def shape(dims, dtype):
    return jax.ShapeDtypeStruct(tuple(dims), dtype)


def slabs(rows):
    return math.gcd(rows, 16)


def all_gather_blk(value, count, number):
    def body(src, out, *sems):
        place = Place(count)
        greet(place, blk=True)
        together(gather_blk(place, src, out, *sems))

    return transfer(
        f"gather{number}",
        number,
        body,
        [value],
        [shape((count,) + value.shape, value.dtype)],
        gather_blk_sems(count),
        value.size * 2 * count,
    )[0]


def reduce_scatter_blk(value, count, number):
    piece = value.shape[1:]

    def body(part, out, *scratch):
        place = Place(count)
        greet(place, blk=True)
        together(reduce_blk(place, part, out, *scratch))

    return transfer(
        f"reduce{number}",
        number,
        body,
        [value],
        [shape(piece, jnp.float32)],
        reduce_blk_scratch(count, piece, value.dtype),
        value.size * 2,
        [pltpu.VMEM],
    )[0]


class Taker:
    def __init__(self, refs):
        self.refs = list(refs)

    def __call__(self, amount):
        taken = self.refs[:amount]
        del self.refs[:amount]
        return taken


def gather_first(qkv, out_parts, tokens, gains, docs, count, number):
    names = 5

    def body(*refs):
        qkv_ref, out_ref, tok_ref, gain_ref, doc_ref = refs[:names]
        qkv_all, out_mine, tok_all, gain_all, doc_all = refs[names : 2 * names]
        gain_mine = refs[2 * names]
        take = Taker(refs[2 * names + 1 :])
        place = Place(count)
        greet(place, blk=True, core=True, half=True, corner=True)

        def gain_task(near, far):
            yield from gather_blk(place, gain_ref, gain_mine, *near)
            yield from gather_group(place, gain_mine, gain_all, *far)

        def doc_task(sent, came, own):
            copy = pltpu.make_async_copy(doc_ref, doc_all.at[place.core], own)
            copy.start()
            send = remote(doc_ref, doc_all.at[place.core], sent, came, place.partner())
            send.start()
            yield
            remote(doc_ref, doc_all.at[1 - place.core], sent, came, place.partner()).wait_recv()
            send.wait_send()
            copy.wait()

        together(
            gain_task(take(3), take(3)),
            gather_blk(place, qkv_ref, qkv_all, *take(3)),
            doc_task(*take(3)),
            waiting(gather_group(place, tok_ref, tok_all, *take(3)), 2),
            waiting(exchange_group(place, out_ref, out_mine, *take(3)), 3),
        )

    ins = [qkv, out_parts, tokens, gains, docs]
    return transfer(
        f"first{number}",
        number,
        body,
        ins,
        [
            shape((count,) + qkv.shape, qkv.dtype),
            shape(out_parts.shape, out_parts.dtype),
            shape((GROUPS,) + tokens.shape, tokens.dtype),
            shape((GROUPS, count) + gains.shape, gains.dtype),
            shape((2,) + docs.shape, docs.dtype),
        ],
        [pltpu.VMEM((count,) + gains.shape, gains.dtype)]
        + gather_blk_sems(count, 1)
        + gather_group_sems()
        + gather_blk_sems(count)
        + [pltpu.SemaphoreType.DMA] * 3
        + gather_group_sems()
        + exchange_group_sems(),
        (qkv.size + out_parts.size) * 2 * count,
    )


def gather_second(kv, out_mine, count, number):
    def body(kv_ref, out_ref, kv_all, out_all, *sems):
        take = Taker(sems)
        place = Place(count)
        greet(place, blk=True)
        together(
            gather_blk(place, kv_ref, kv_all, *take(3)),
            gather_blk(place, out_ref, lambda i: out_all.at[:, i], *take(3)),
        )

    groups, rows, width = out_mine.shape
    return transfer(
        f"gather{number}",
        number,
        body,
        [kv, out_mine],
        [
            shape((count,) + kv.shape, kv.dtype),
            shape((groups, count, rows, width), out_mine.dtype),
        ],
        gather_blk_sems(count) + gather_blk_sems(count),
        (kv.size + out_mine.size) * 2 * count,
    )


def reduce_middle(dkv_part, out_part, count, number):
    dkv_piece = dkv_part.shape[1:]
    out_piece = out_part.shape[:1] + out_part.shape[2:]

    def body(dkv_ref, out_ref, dkv_sum, out_sum, *scratch):
        take = Taker(scratch)
        place = Place(count)
        greet(place, blk=True)
        together(
            reduce_blk(place, dkv_ref, dkv_sum, *take(REDUCE_REFS)),
            reduce_blk(place, lambda i: out_ref.at[:, i], out_sum, *take(REDUCE_REFS)),
        )

    return transfer(
        f"reduce{number}",
        number,
        body,
        [dkv_part, out_part],
        [shape(dkv_piece, jnp.bfloat16), shape(out_piece, jnp.bfloat16)],
        reduce_blk_scratch(count, dkv_piece, jnp.bfloat16)
        + reduce_blk_scratch(count, out_piece, jnp.bfloat16),
        (dkv_part.size + out_part.size) * 2,
        [pltpu.VMEM] * 2,
    )


def reduce_last(qkv_part, norm_part, gain_part, out_sum, count, number):
    gain_piece = gain_part.shape[1:]
    qkv_piece, norm_piece = qkv_part.shape[1:], norm_part.shape[1:]

    def body(*refs):
        qkv_ref, norm_ref, gain_ref, out_ref = refs[:4]
        qkv_sum, norm_sum, gain_sum, out_all = refs[4:8]
        gain_mine = refs[8]
        take = Taker(refs[9:])
        place = Place(count)
        greet(place, blk=True, core=True, half=True, corner=True)

        def gain_task(near, far):
            yield from reduce_blk(place, gain_ref, gain_mine, *near)
            yield from reduce_group(place, gain_mine, gain_sum, *far)

        main = reduce_blk(place, qkv_ref, qkv_sum, *take(REDUCE_REFS))
        gain = gain_task(take(REDUCE_REFS), take(5))
        together(
            waiting(gain, 11),
            main,
            waiting(exchange_group(place, out_ref, out_all, *take(3)), 16),
            waiting(reduce_group(place, norm_ref, norm_sum, *take(5)), 7, 9),
        )

    return transfer(
        f"last{number}",
        number,
        body,
        [qkv_part, norm_part, gain_part, out_sum],
        [
            shape(qkv_piece, jnp.float32),
            shape(norm_piece, jnp.float32),
            shape(gain_piece[1:], jnp.float32),
            shape(out_sum.shape, jnp.bfloat16),
        ],
        [pltpu.VMEM(gain_piece, jnp.float32)]
        + reduce_blk_scratch(count, qkv_piece, jnp.bfloat16)
        + reduce_blk_scratch(count, gain_piece, jnp.float32, 1)
        + reduce_group_scratch(gain_piece[1:], jnp.float32)
        + exchange_group_sems()
        + reduce_group_scratch(norm_piece, jnp.bfloat16),
        qkv_part.size * 2,
        [pltpu.VMEM] * 4,
    )


def all_gather_group(value, number):
    def body(src, out, *sems):
        place = Place(lax.axis_size("blk"))
        greet(place, core=True, half=True)
        together(gather_group(place, src, out, *sems))

    return transfer(
        f"group{number}",
        number,
        body,
        [value],
        [shape((GROUPS,) + value.shape, value.dtype)],
        gather_group_sems(),
        value.size * 8,
    )[0]


def reduce_scatter_group(value, number):
    piece = value.shape[1:]

    def body(part, out, *scratch):
        place = Place(lax.axis_size("blk"))
        greet(place, core=True, half=True)
        together(reduce_group(place, part, out, *scratch))

    return transfer(
        f"fold{number}",
        number,
        body,
        [value],
        [shape(piece, jnp.float32)],
        reduce_group_scratch(piece, value.dtype),
        value.size * 2,
        [pltpu.VMEM],
    )[0]


def dot(left, right, contract):
    return lax.dot_general(left, right, (contract, ((), ())), preferred_element_type=jnp.float32)


LAST = ((1,), (1,))
PLAIN = ((1,), (0,))
FIRST = ((0,), (0,))


LANES = 128
GELU_A = math.sqrt(2.0 / math.pi)
GELU_B = 0.044715


def feed_forward_fits(count, rows, width, hidden):
    inner = 4 if count >= 32 else 2
    outer = count // inner
    tile = rows * width * 2
    weights = 3 * hidden * width * 2
    kept = count * rows * 3 * hidden * 2
    total = weights + kept + tile * (3 * count + outer * (inner - 1) + 2 * outer + 3) + 9 * tile
    total += 3 * LANES * (count * rows + 2 * width) * 2
    return total < 58 * 2**20 and hidden % (3 * LANES) == 0 and width % 256 == 0


def feed_forward_kernel(
    count,
    branch_ref,
    token_ref,
    cot_ref,
    gain_ref,
    gate_up_hbm,
    down_hbm,
    out_ref,
    middle_grad_ref,
    branch_grad_ref,
    gain_grad_ref,
    gate_up_grad_hbm,
    down_grad_hbm,
    w_gate_up,
    w_down,
    norm_all,
    grad_all,
    act,
    hidden,
    part,
    middle,
    norm_own,
    grad_own,
    total,
    turned,
    staged,
    beside,
    along,
    held,
    spare,
    w_sems,
    out_sems,
    *sems,
):
    place = Place(count)
    rows, width = norm_all.shape[1:]
    units = hidden.shape[1]
    chunks = units // LANES
    inner, outer = place.inner, place.outer
    slab = branch_ref.shape[1]
    steps = rows // slab
    columns = width // 256
    pair = inner * rows
    take = Taker(sems)

    def weight_copies(i):
        units_at = pl.ds(pl.multiple_of(i * LANES, LANES), LANES)
        return [
            pltpu.make_async_copy(
                gate_up_hbm.at[units_at, pl.ds(0, width)],
                w_gate_up.at[i, pl.ds(0, LANES)],
                w_sems.at[3 * i],
            ),
            pltpu.make_async_copy(
                gate_up_hbm.at[units_at, pl.ds(width, width)],
                w_gate_up.at[i, pl.ds(LANES, LANES)],
                w_sems.at[3 * i + 1],
            ),
            pltpu.make_async_copy(down_hbm.at[units_at], w_down.at[units_at], w_sems.at[3 * i + 2]),
        ]

    def start_weights(i, carry):
        for copy in weight_copies(i):
            copy.start()
        return carry

    def wait_weights(i, carry):
        for copy in weight_copies(i):
            copy.wait()
        return carry

    lax.fori_loop(0, chunks, start_weights, 0)

    def scale_of(values):
        return lax.rsqrt(jnp.mean(values * values, axis=-1, keepdims=True) + NORM_EPS)

    def slab_rows(i):
        return pl.ds(pl.multiple_of(i * slab, slab), slab)

    def before(i, carry):
        value = branch_ref[i]
        mid = token_ref[i].astype(jnp.float32) + value * scale_of(value) * gain_ref[1:2]
        middle[i] = mid
        norm_own[slab_rows(i)] = (mid * scale_of(mid) * gain_ref[2:3]).astype(jnp.bfloat16)
        return carry

    lax.fori_loop(0, steps, before, 0)
    greet(place, blk=True)

    def pair_rows(k):
        return pl.ds(pl.multiple_of(place.near(k) * pair, pair), pair)

    def pair_pieces(k):
        return pl.ds(place.near(k) * inner, inner)

    def column(n):
        return pl.ds(pl.multiple_of(n * 256, 256), 256)

    def put_part(k, n, value):
        split = value.astype(jnp.bfloat16).reshape((inner, steps, slab, 256))
        part[pair_pieces(k), :, :, column(n)] = split

    def receive(gather, k):
        if k == 0:
            gather.copy.wait()
        if not gather.evened:
            if k + 1 < outer:
                gather.pass_on(k + 1)
            gather.beside_arrived(k)
            return
        ends = jnp.logical_not(gather.middle)
        if k == 0:
            gather.pass_on(1)
            pl.when(gather.middle)(lambda: gather.pass_on(2))
        elif k == 1:
            pl.when(ends)(lambda: gather.pass_on(2))
            gather.pass_extra(1)
            pl.when(gather.middle)(lambda: gather.pass_on(3))
        elif k == 2:
            pl.when(ends)(lambda: gather.pass_on(3))
            gather.pass_extra(3)
        gather.beside_arrived(k)

    gather = GatherBlk(place, norm_own, lambda i: norm_all.at[i], *take(3))
    gather.start()
    lax.fori_loop(0, chunks, wait_weights, 0)
    for k in range(outer):
        receive(gather, k)
        at = pair_rows(k)

        def up_chunk(j, carry, k=k, at=at):
            x = norm_all[pair_pieces(k)].reshape(pair, width)
            both = dot(x, w_gate_up[j], LAST)
            act[at, column(j)] = both.astype(jnp.bfloat16)
            gate, up = both[:, :LANES], both[:, LANES:]
            bent = 0.5 * gate * (1.0 + jnp.tanh(GELU_A * (gate + GELU_B * (gate * gate * gate))))
            hidden[at, pl.ds(pl.multiple_of(j * LANES, LANES), LANES)] = (bent * up).astype(
                jnp.bfloat16
            )
            return carry

        lax.fori_loop(0, chunks, up_chunk, 0)

        def down_chunk(n, carry, k=k, at=at):
            put_part(k, n, dot(hidden[at, :], w_down[:, column(n)], PLAIN))
            return carry

        lax.fori_loop(0, columns, down_chunk, 0)
    gather.finish()
    reduce = ReduceBlk(place, lambda i: part.at[i], total, beside, along, held, spare, *take(6))
    reduce.start()
    for event in reduce.events():
        event()

    gain_grad_ref[...] = jnp.zeros_like(gain_grad_ref)

    def norm_back(value, gain, incoming):
        scale = scale_of(value)
        lifted = incoming * gain
        pull = jnp.mean(lifted * value, axis=-1, keepdims=True)
        gain_grad = jnp.sum(incoming * value * scale, axis=0, keepdims=True)
        return scale * lifted - value * (scale * scale * scale) * pull, gain_grad

    def between(i, carry):
        value, cot = total[i], cot_ref[i].astype(jnp.float32)
        gain = gain_ref[3:4]
        out_ref[i] = (middle[i] + value * scale_of(value) * gain).astype(jnp.bfloat16)
        grad, gain_grad = norm_back(value, gain, cot)
        gain_grad_ref[3:4] += gain_grad
        grad_own[slab_rows(i)] = grad.astype(jnp.bfloat16)
        return carry

    lax.fori_loop(0, steps, between, 0)
    reduce.finish()

    gather = GatherBlk(place, grad_own, lambda i: grad_all.at[i], *take(3))
    gather.start()
    for k in range(outer):
        receive(gather, k)
        at = pair_rows(k)

        def back_chunk(j, carry, k=k, at=at):
            g = grad_all[pair_pieces(k)].reshape(pair, width)
            units_at = pl.ds(pl.multiple_of(j * LANES, LANES), LANES)
            grad = dot(g, w_down[units_at], LAST)
            both = act[at, column(j)].astype(jnp.float32)
            gate, up = both[:, :LANES], both[:, LANES:]
            bend = jnp.tanh(GELU_A * (gate + GELU_B * (gate * gate * gate)))
            bent = 0.5 * gate * (1.0 + bend)
            slope = 0.5 * (1.0 + bend) + (0.5 * GELU_A) * gate * (1.0 - bend * bend) * (
                1.0 + (3.0 * GELU_B) * gate * gate
            )
            pulled = jnp.concatenate([grad * up * slope, grad * bent], axis=1)
            act[at, column(j)] = pulled.astype(jnp.bfloat16)
            return carry

        lax.fori_loop(0, chunks, back_chunk, 0)

        def input_chunk(n, carry, k=k, at=at):
            w = w_gate_up[:, :, column(n)].reshape(2 * units, 256)
            put_part(k, n, dot(act[at, :], w, PLAIN))
            return carry

        lax.fori_loop(0, columns, input_chunk, 0)
    gather.finish()
    reduce = ReduceBlk(place, lambda i: part.at[i], total, beside, along, held, spare, *take(6))
    reduce.start()

    tokens = count * rows
    slots = staged.shape[0]

    def up_store(i):
        slot = lax.rem(i, slots)
        units_at = pl.ds(pl.multiple_of(i * LANES, LANES), LANES)
        return [
            pltpu.make_async_copy(
                staged.at[slot, pl.ds(h * LANES, LANES)],
                gate_up_grad_hbm.at[units_at, pl.ds(h * width, width)],
                out_sems.at[slot, h],
            )
            for h in (0, 1)
        ]

    def up_grad(i, carry):
        @pl.when(i >= slots)
        def _():
            for copy in up_store(i - slots):
                copy.wait()

        turned[pl.ds(0, 256)] = jnp.transpose(act[:, column(i)])

        def one(n, c):
            x = norm_all[:, :, column(n)].reshape(tokens, 256)
            staged[lax.rem(i, slots), pl.ds(0, 256), column(n)] = dot(
                turned[pl.ds(0, 256)], x, PLAIN
            ).astype(jnp.bfloat16)
            return c

        lax.fori_loop(0, columns, one, 0)
        for copy in up_store(i):
            copy.start()
        return carry

    three = 3 * LANES

    def down_store(i):
        slot = lax.rem(i, slots)
        return pltpu.make_async_copy(
            staged.at[slot],
            down_grad_hbm.at[pl.ds(pl.multiple_of(i * three, three), three)],
            out_sems.at[slot, 2],
        )

    def down_grad(i, carry):
        @pl.when(i >= slots)
        def _():
            down_store(i - slots).wait()

        turned[...] = jnp.transpose(hidden[:, pl.ds(pl.multiple_of(i * three, three), three)])

        def one(n, c):
            x = grad_all[:, :, column(n)].reshape(tokens, 256)
            staged[lax.rem(i, slots), :, column(n)] = dot(turned[...], x, PLAIN).astype(jnp.bfloat16)
            return c

        lax.fori_loop(0, columns, one, 0)
        down_store(i).start()
        return carry

    events = reduce.events()
    early = len(events) - 3
    bounds = [chunks * k // early for k in range(early + 1)]
    for k in range(early):
        lax.fori_loop(bounds[k], bounds[k + 1], up_grad, 0)
        events[k]()
    for i in range(max(0, chunks - slots), chunks):
        for copy in up_store(i):
            copy.wait()
    thirds = units // three
    bounds = [thirds * k // 3 for k in range(4)]
    for k in range(3):
        lax.fori_loop(bounds[k], bounds[k + 1], down_grad, 0)
        events[early + k]()

    def after(i, carry):
        value, mid, cot = branch_ref[i], middle[i], cot_ref[i].astype(jnp.float32)
        grad, gain_grad = norm_back(mid, gain_ref[2:3], total[i])
        gain_grad_ref[2:3] += gain_grad
        middle_grad = cot + grad
        middle_grad_ref[i] = middle_grad
        grad, gain_grad = norm_back(value, gain_ref[1:2], middle_grad)
        gain_grad_ref[1:2] += gain_grad
        branch_grad_ref[i] = grad.astype(jnp.bfloat16)
        return carry

    lax.fori_loop(0, steps, after, 0)
    reduce.finish()
    for i in range(max(0, thirds - slots), thirds):
        down_store(i).wait()


def feed_forward(branch, tokens, cotangent, gains, gate_up_all, down_all, count, number):
    steps, slab, width = branch.shape
    rows = steps * slab
    units = down_all.shape[0]
    inner = 4 if count >= 32 else 2
    outer = count // inner
    piece = branch.shape
    bf16, f32 = jnp.bfloat16, jnp.float32
    vmem = pl.BlockSpec(memory_space=pltpu.VMEM)
    anywhere = pl.BlockSpec(memory_space=pl.ANY)
    slots = 2
    line_scratch = reduce_blk_scratch(count, piece, bf16)
    return pl.pallas_call(
        functools.partial(feed_forward_kernel, count),
        name="feed_forward",
        out_shape=[
            shape(piece, bf16),
            shape(piece, f32),
            shape(piece, bf16),
            shape((4, width), f32),
            shape(gate_up_all.shape, bf16),
            shape(down_all.shape, bf16),
        ],
        in_specs=[vmem] * 4 + [anywhere] * 2,
        out_specs=[vmem] * 4 + [anywhere] * 2,
        scratch_shapes=[
            pltpu.VMEM((units // LANES, 2 * LANES, width), bf16),
            pltpu.VMEM((units, width), bf16),
            pltpu.VMEM((count, rows, width), bf16),
            pltpu.VMEM((count, rows, width), bf16),
            pltpu.VMEM((count * rows, 2 * units), bf16),
            pltpu.VMEM((count * rows, units), bf16),
            pltpu.VMEM((count,) + piece, bf16),
            pltpu.VMEM(piece, f32),
            pltpu.VMEM((rows, width), bf16),
            pltpu.VMEM((rows, width), bf16),
            pltpu.VMEM(piece, f32),
            pltpu.VMEM((3 * LANES, count * rows), bf16),
            pltpu.VMEM((slots, 3 * LANES, width), bf16),
        ]
        + line_scratch[:4]
        + [
            pltpu.SemaphoreType.DMA((3 * units // LANES,)),
            pltpu.SemaphoreType.DMA((slots, 3)),
        ]
        + gather_blk_sems(count)
        + line_scratch[4:]
        + gather_blk_sems(count)
        + line_scratch[4:],
        compiler_params=pltpu.CompilerParams(
            collective_id=number, has_side_effects=True, vmem_limit_bytes=67043328
        ),
        cost_estimate=pl.CostEstimate(
            flops=18 * count * rows * units * width,
            bytes_accessed=500 * 2**20,
            transcendentals=0,
        ),
    )(branch, tokens, cotangent, gains, gate_up_all, down_all)


def attention_scores(q2, k, query_pos, query_doc, key_block, key_doc, rows):
    raw = lax.dot_general(q2, k, (((1,), (1,)), ((), ())), preferred_element_type=jnp.float32)
    capped = jnp.tanh(raw * (SCORE_SCALE / SOFT_CAP))
    key_pos = key_block * rows + lax.broadcasted_iota(jnp.int32, (1, rows), 1)
    visible = (key_pos <= query_pos) & (key_doc == query_doc)
    return capped, jnp.where(visible, jnp.exp(SOFT_CAP * capped), 0.0)


def attention_query(q_ref, doc_ref, here, count, rows):
    half = pl.program_id(1)
    block = half * count + here
    q2 = jnp.concatenate([q_ref[0, :, :HEAD_DIM], q_ref[0, :, HEAD_DIM:]], axis=0)
    inside = lax.broadcasted_iota(jnp.int32, (rows, 1), 0)
    position = block * rows + jnp.concatenate([inside, inside], axis=0)
    doc = jnp.concatenate([doc_ref[0], doc_ref[0]], axis=0)
    return block, q2, position, doc


def attention_forward_kernel(
    count, here_ref, q_ref, kv_ref, doc_ref, key_doc_ref, attn_ref, full_ref, total_ref, acc, tot
):
    rows = q_ref.shape[1]
    block, q2, position, doc = attention_query(q_ref, doc_ref, here_ref[0], count, rows)
    acc[...] = jnp.zeros_like(acc)
    tot[...] = jnp.zeros_like(tot)

    def one(key_block, carry):
        key_half = (key_block >= count).astype(jnp.int32)
        kv = kv_ref.at[key_block - key_half * count, key_half]
        _, weights = attention_scores(
            q2, kv[:, :HEAD_DIM], position, doc, key_block, key_doc_ref[0, key_block], rows
        )
        tot[...] += jnp.sum(weights, axis=-1, keepdims=True)
        acc[...] += jnp.dot(
            weights.astype(jnp.bfloat16), kv[:, HEAD_DIM:], preferred_element_type=jnp.float32
        )
        return carry

    lax.fori_loop(jnp.maximum(block - count, 0), block + 1, one, 0)
    attended = acc[...] / tot[...]
    attended = jnp.concatenate([attended[:rows], attended[rows:]], axis=1)
    full_ref[0] = attended
    attn_ref[0] = attended.astype(jnp.bfloat16)
    total_ref[0] = tot[...]


def attention_backward_kernel(
    count,
    here_ref,
    q_ref,
    kv_ref,
    doc_ref,
    key_doc_ref,
    grad_ref,
    full_ref,
    total_ref,
    dq_ref,
    dkv_ref,
    acc,
    key_acc,
):
    rows = q_ref.shape[1]
    half = pl.program_id(1)
    block, q2, position, doc = attention_query(q_ref, doc_ref, here_ref[0], count, rows)
    total = total_ref[0]
    grad = grad_ref[0].astype(jnp.float32)
    grad2 = jnp.concatenate([grad[:, :HEAD_DIM], grad[:, HEAD_DIM:]], axis=0)
    full2 = jnp.concatenate([full_ref[0, :, :HEAD_DIM], full_ref[0, :, HEAD_DIM:]], axis=0)
    total_grad = -jnp.sum(grad2 * full2, axis=-1, keepdims=True) / total
    sums_grad = (grad2 / total).astype(jnp.bfloat16)
    acc[...] = jnp.zeros_like(acc)

    @pl.when(half == 0)
    def _():
        def clear(i, carry):
            key_acc[i] = jnp.zeros(key_acc.shape[1:], jnp.float32)
            return carry

        lax.fori_loop(0, key_acc.shape[0], clear, 0)

    def one(key_block, carry):
        key_half = (key_block >= count).astype(jnp.int32)
        inner = key_block - key_half * count
        kv = kv_ref.at[inner, key_half]
        keys = kv[:, :HEAD_DIM]
        capped, weights = attention_scores(
            q2, keys, position, doc, key_block, key_doc_ref[0, key_block], rows
        )
        exp_grad = lax.dot_general(
            sums_grad, kv[:, HEAD_DIM:], (((1,), (1,)), ((), ())), preferred_element_type=jnp.float32
        )
        raw_grad = (
            weights * (exp_grad + total_grad) * (1.0 - capped * capped) * SCORE_SCALE
        ).astype(jnp.bfloat16)
        acc[...] += jnp.dot(raw_grad, keys, preferred_element_type=jnp.float32)
        over_rows = (((0,), (0,)), ((), ()))
        slot = inner * 2 + key_half
        key_acc[slot, :, :HEAD_DIM] += lax.dot_general(
            raw_grad, q2, over_rows, preferred_element_type=jnp.float32
        )
        key_acc[slot, :, HEAD_DIM:] += lax.dot_general(
            weights.astype(jnp.bfloat16), sums_grad, over_rows, preferred_element_type=jnp.float32
        )
        return carry

    lax.fori_loop(jnp.maximum(block - count, 0), block + 1, one, 0)
    dq = acc[...]
    dq_ref[0] = jnp.concatenate([dq[:rows], dq[rows:]], axis=1).astype(jnp.bfloat16)

    @pl.when(half == 1)
    def _():
        def put(i, carry):
            for k in (0, 1):
                dkv_ref[i, k] = key_acc[i * 2 + k].astype(jnp.bfloat16)
            return carry

        lax.fori_loop(0, count, put, 0)


def attention_specs(count, rows, width):
    query = pl.BlockSpec((1, rows, width), lambda s, h, here: (2 * s + h, 0, 0))
    keys = pl.BlockSpec((count, 2, rows, 2 * HEAD_DIM), lambda s, h, here: (0, s, 0, 0))
    doc = pl.BlockSpec((1, rows, 1), lambda s, h, here: (2 * s + h, 0, 0))
    key_doc = pl.BlockSpec((1, 2 * count, 1, rows), lambda s, h, here: (s, 0, 0, 0))
    total = pl.BlockSpec((1, REPS * rows, 1), lambda s, h, here: (2 * s + h, 0, 0))
    return query, keys, doc, key_doc, total


def attention_forward(here, q, kv, doc, key_doc):
    count, _, rows, _ = kv.shape
    width = REPS * HEAD_DIM
    query, keys, doc_spec, key_doc_spec, total = attention_specs(count, rows, width)
    return pl.pallas_call(
        functools.partial(attention_forward_kernel, count),
        name="attend",
        grid_spec=pltpu.PrefetchScalarGridSpec(
            num_scalar_prefetch=1,
            grid=(2, 2),
            in_specs=[query, keys, doc_spec, key_doc_spec],
            out_specs=[query, query, total],
            scratch_shapes=[
                pltpu.VMEM((REPS * rows, HEAD_DIM), jnp.float32),
                pltpu.VMEM((REPS * rows, 1), jnp.float32),
            ],
        ),
        out_shape=[
            shape((GROUPS, rows, width), jnp.bfloat16),
            shape((GROUPS, rows, width), jnp.float32),
            shape((GROUPS, REPS * rows, 1), jnp.float32),
        ],
        compiler_params=pltpu.CompilerParams(vmem_limit_bytes=VMEM_LIMIT),
        cost_estimate=pl.CostEstimate(flops=10**9, bytes_accessed=40 * 2**20, transcendentals=0),
    )(here, q, kv, doc, key_doc)


def attention_backward(here, q, kv, doc, key_doc, grad, full, totals):
    count, _, rows, _ = kv.shape
    width = REPS * HEAD_DIM
    query, keys, doc_spec, key_doc_spec, total = attention_specs(count, rows, width)
    return pl.pallas_call(
        functools.partial(attention_backward_kernel, count),
        name="attend_back",
        grid_spec=pltpu.PrefetchScalarGridSpec(
            num_scalar_prefetch=1,
            grid=(2, 2),
            in_specs=[query, keys, doc_spec, key_doc_spec, query, query, total],
            out_specs=[query, keys],
            scratch_shapes=[
                pltpu.VMEM((REPS * rows, HEAD_DIM), jnp.float32),
                pltpu.VMEM((2 * count, rows, 2 * HEAD_DIM), jnp.float32),
            ],
        ),
        out_shape=[shape((GROUPS, rows, width), jnp.bfloat16), shape(kv.shape, jnp.bfloat16)],
        compiler_params=pltpu.CompilerParams(vmem_limit_bytes=VMEM_LIMIT),
        cost_estimate=pl.CostEstimate(flops=2 * 10**9, bytes_accessed=80 * 2**20, transcendentals=0),
    )(here, q, kv, doc, key_doc, grad, full, totals)


def rms_scale(values, gain_row):
    return (
        values * lax.rsqrt(jnp.mean(values * values, axis=-1, keepdims=True) + NORM_EPS) * gain_row
    )


def gelu_tanh(values):
    return jax.nn.gelu(values, approximate=True)


def rope_tables(positions):
    half_width = HEAD_DIM // 2
    frequency = jnp.exp(
        jnp.arange(half_width, dtype=jnp.float32) * (-2.0 * math.log(ROPE_BASE) / HEAD_DIM)
    )
    angles = positions.astype(jnp.float32)[:, None] * frequency[None, :]
    cosine = jnp.concatenate([jnp.cos(angles), jnp.cos(angles)], axis=-1)
    sine = jnp.concatenate([jnp.sin(angles), jnp.sin(angles)], axis=-1)
    return cosine[:, None, :], sine[:, None, :]


def rotate(values, cosine, sine):
    half_width = HEAD_DIM // 2
    turned = jnp.concatenate([-values[..., half_width:], values[..., :half_width]], axis=-1)
    return values * cosine + turned * sine


def feed_forward_apart(
    branch_slabs, inputs, cotangent, gains, gate_up_all, down_all, count, piece
):
    rows, width = inputs.shape
    bf16 = jnp.bfloat16
    branch = branch_slabs.reshape(rows, width)
    middle = inputs + rms_scale(branch, gains[1])
    norm_three = rms_scale(middle, gains[2]).astype(bf16)
    gate_all = gate_up_all[:, :width]
    up_all = gate_up_all[:, width:]
    norm_all = all_gather_blk(norm_three, count, 4).reshape(count * rows, width)
    gate = dot(norm_all, gate_all, LAST)
    up = dot(norm_all, up_all, LAST)
    hidden = (gelu_tanh(gate) * up).astype(bf16)
    ffn_part = dot(hidden, down_all, PLAIN).astype(bf16)
    ffn_out = reduce_scatter_blk(ffn_part.reshape((count,) + piece), count, 5).reshape(rows, width)
    output = (middle + rms_scale(ffn_out, gains[3])).astype(bf16)[None]

    out_cotangent = cotangent[0].astype(jnp.float32)
    _, post_ffn_back = jax.vjp(rms_scale, ffn_out, gains[3])
    ffn_grad, gain_grad_four = post_ffn_back(out_cotangent)
    grad_all = all_gather_blk(ffn_grad.astype(bf16), count, 6).reshape(count * rows, width)
    activated, gelu_back = jax.vjp(gelu_tanh, gate)
    hidden_grad = dot(grad_all, down_all, LAST)
    gate_grad = gelu_back(hidden_grad * up)[0].astype(bf16)
    up_grad = (hidden_grad * activated).astype(bf16)
    norm_part = dot(gate_grad, gate_all, PLAIN) + dot(up_grad, up_all, PLAIN)
    norm_three_grad = reduce_scatter_blk(
        norm_part.astype(bf16).reshape((count,) + piece), count, 7
    ).reshape(rows, width)
    down_part = dot(hidden, grad_all, FIRST).astype(bf16)
    gate_up_part = jnp.concatenate(
        [dot(gate_grad, norm_all, FIRST), dot(up_grad, norm_all, FIRST)], axis=1
    ).astype(bf16)
    _, pre_ffn_back = jax.vjp(rms_scale, middle, gains[2])
    middle_part, gain_grad_three = pre_ffn_back(norm_three_grad)
    middle_grad = out_cotangent + middle_part
    _, post_attn_back = jax.vjp(rms_scale, branch, gains[1])
    branch_grad, gain_grad_two = post_attn_back(middle_grad)
    return (
        output,
        middle_grad,
        branch_grad.astype(bf16),
        gain_grad_two,
        gain_grad_three,
        gain_grad_four,
        gate_up_part,
        down_part,
    )


def shards(
    tokens, cotangent, segments, norm_gains, qkv_weight, out_weight, gate_up_weight, down_weight
):
    _, rows, width = tokens.shape
    count = lax.axis_size("blk")
    here = lax.axis_index("blk")
    mine = 2 * lax.axis_index("dp") + lax.axis_index("head")
    group_rows = GROUPS * rows
    head_width = REPS * HEAD_DIM
    bf16 = jnp.bfloat16
    slab = slabs(rows)
    piece = (rows // slab, slab, width)

    gate_up_all = lax.all_gather(gate_up_weight, ("dp", "head"), axis=0, tiled=True)
    down_all = lax.all_gather(down_weight, ("dp", "head"), axis=0, tiled=True)

    gain_rows = norm_gains.shape[0]
    gain_lanes = -(-gain_rows // 128) * 128
    gains_sent = jnp.pad(
        jnp.transpose(norm_gains).astype(jnp.float32), ((0, 4), (0, gain_lanes - gain_rows))
    )
    out_rows = out_weight.shape[0]
    out_sent = jnp.transpose(out_weight.reshape(out_rows, GROUPS, head_width), (1, 0, 2))
    qkv_rows = qkv_weight.shape[0]
    qkv_slab = slabs(qkv_rows)
    qkv_piece = (qkv_rows // qkv_slab, qkv_slab, width)
    qkv_all, out_mine, tokens_all, gains_all, docs_all = gather_first(
        qkv_weight, out_sent, tokens[0], gains_sent, segments.reshape(-1, 128), count, 1
    )
    gains = jnp.transpose(gains_all[:, :, :4, :gain_rows], (2, 0, 1, 3)).reshape(4, width)
    qkv_head = qkv_all.reshape(count * qkv_rows, width)
    docs = docs_all.reshape(2, 2, count, rows)
    key_doc = docs.reshape(2, 2 * count, 1, rows)
    own_doc = lax.dynamic_index_in_dim(docs, here, 2, keepdims=False).reshape(GROUPS, rows, 1)
    here_one = here.reshape(1)

    group_tokens = tokens_all.reshape(group_rows, width).astype(jnp.float32)
    norm_one = rms_scale(group_tokens, gains[0]).astype(bf16)
    proj = dot(norm_one, qkv_head, LAST)
    inside = jnp.arange(rows, dtype=jnp.int32)
    position = jnp.concatenate([here * rows + inside, (count + here) * rows + inside])
    cosine, sine = rope_tables(jnp.concatenate([position, position]))
    proj = proj.reshape(group_rows, REPS + 2, HEAD_DIM)
    turned = rotate(proj[:, : REPS + 1], cosine, sine)
    sent = jnp.concatenate([turned, proj[:, REPS + 1 :]], axis=1).astype(bf16)
    queries = sent[:, :REPS].reshape(GROUPS, rows, head_width)
    own_kv = sent[:, REPS:].reshape(group_rows, 2 * HEAD_DIM)
    kv_slab = slabs(group_rows)
    kv_piece = (group_rows // kv_slab, kv_slab, 2 * HEAD_DIM)
    kv, out_all = gather_second(own_kv, out_mine, count, 2)
    kv = kv.reshape(count, GROUPS, rows, 2 * HEAD_DIM)
    out_head = out_all.reshape(width, head_width)
    attn, attended, totals = attention_forward(here_one, queries, kv, own_doc, key_doc)
    attn = attn.reshape(group_rows, head_width)
    branch_part = dot(attn, out_head, LAST).astype(bf16)
    branch_slabs = reduce_scatter_group(branch_part.reshape((GROUPS,) + piece), 3)
    inputs = tokens[0].astype(jnp.float32)
    if feed_forward_fits(count, rows, width, down_all.shape[0]):
        output, middle_grad, branch_grad, gain_rest, gate_up_part, down_part = feed_forward(
            branch_slabs,
            tokens.reshape(piece),
            cotangent.reshape(piece),
            gains,
            gate_up_all,
            down_all,
            count,
            4,
        )
        output = output.reshape(tokens.shape)
        middle_grad = middle_grad.reshape(rows, width)
        branch_grad = branch_grad.reshape(rows, width)
        gain_grad_two, gain_grad_three, gain_grad_four = gain_rest[1], gain_rest[2], gain_rest[3]
    else:
        (
            output,
            middle_grad,
            branch_grad,
            gain_grad_two,
            gain_grad_three,
            gain_grad_four,
            gate_up_part,
            down_part,
        ) = feed_forward_apart(
            branch_slabs, inputs, cotangent, gains, gate_up_all, down_all, count, piece
        )
    gate_up_grad = lax.psum_scatter(
        gate_up_part, ("dp", "head"), scatter_dimension=0, tiled=True
    ).astype(jnp.float32)
    down_grad = lax.psum_scatter(
        down_part, ("dp", "head"), scatter_dimension=0, tiled=True
    ).astype(jnp.float32)
    branch_all = all_gather_group(branch_grad, 8).reshape(group_rows, width)
    attn_grad = dot(branch_all, out_head, PLAIN).astype(bf16).reshape(GROUPS, rows, head_width)
    out_part = dot(branch_all, attn, FIRST).astype(bf16)
    out_part = out_part.reshape(GROUPS, count, out_rows, head_width)
    dq, dkv_part = attention_backward(
        here_one, queries, kv, own_doc, key_doc, attn_grad, attended, totals
    )
    dkv, out_sum = reduce_middle(dkv_part.reshape((count,) + kv_piece), out_part, count, 9)
    sent_grad = jnp.concatenate(
        [
            dq.reshape(group_rows, REPS, HEAD_DIM),
            dkv.reshape(group_rows, 2, HEAD_DIM),
        ],
        axis=1,
    ).astype(jnp.float32)
    unturned = rotate(sent_grad[:, : REPS + 1], cosine, -sine)
    proj_grad = (
        jnp.concatenate([unturned, sent_grad[:, REPS + 1 :]], axis=1)
        .astype(bf16)
        .reshape(group_rows, (REPS + 2) * HEAD_DIM)
    )
    qkv_part = dot(proj_grad, norm_one, FIRST).astype(bf16)
    norm_one_part = dot(proj_grad, qkv_head, PLAIN)
    _, gain_back = jax.vjp(lambda gain: rms_scale(group_tokens, gain), gains[0])
    (gain_grad_one,) = gain_back(norm_one_part)
    gain_part = jnp.stack([gain_grad_one, gain_grad_two, gain_grad_three, gain_grad_four])
    gain_part = jnp.transpose(gain_part.reshape(4, GROUPS, count, gain_rows), (2, 1, 0, 3))
    gain_part = jnp.pad(gain_part, ((0, 0), (0, 0), (0, 4), (0, gain_lanes - gain_rows)))
    qkv_grad, norm_one_grad, gain_grad, out_grad = reduce_last(
        qkv_part.reshape((count,) + qkv_piece),
        norm_one_part.astype(bf16).reshape((GROUPS,) + piece),
        gain_part[:, :, None],
        out_sum,
        count,
        10,
    )
    qkv_grad = qkv_grad.reshape(qkv_rows, width)
    out_grad = (
        jnp.transpose(out_grad, (1, 0, 2)).reshape(out_rows, GROUPS * head_width).astype(jnp.float32)
    )
    gain_grad = jnp.transpose(gain_grad.reshape(8, gain_lanes)[:4, :gain_rows])
    _, pre_attn_back = jax.vjp(lambda values: rms_scale(values, gains[0]), inputs)
    (input_part,) = pre_attn_back(norm_one_grad.reshape(rows, width))
    tokens_grad = (middle_grad + input_part).astype(bf16)[None]
    return (output, tokens_grad, gain_grad, qkv_grad, out_grad, gate_up_grad, down_grad)


def solution(mesh):
    whole = ("dp", "head", "blk")
    return jax.shard_map(
        shards,
        mesh=mesh,
        in_specs=(
            P("dp", ("head", "blk"), None),
            P("dp", ("head", "blk"), None),
            P("dp", None),
            P(whole, None),
            P(whole, None),
            P(whole, None),
            P(whole, None),
            P(whole, None),
        ),
        out_specs=(
            P("dp", ("head", "blk"), None),
            P("dp", ("head", "blk"), None),
            P(whole, None),
            P(whole, None),
            P(whole, None),
            P(whole, None),
            P(whole, None),
        ),
        check_vma=False,
    )
```

```python
import functools
import math

import jax
import jax.numpy as jnp
from jax import lax
from jax.experimental import pallas as pl
from jax.experimental.pallas import tpu as pltpu
from jax.sharding import PartitionSpec as P

HEADS = 8
KV_HEADS = 4
HEAD_DIM = 256
REPS = HEADS // KV_HEADS
GROUPS = 4
SOFT_CAP = 50.0
NORM_EPS = 1e-06
ROPE_BASE = 10000.0
SCORE_SCALE = HEAD_DIM ** (-0.5)

MESH = pl.DeviceIdType.MESH
VMEM_LIMIT = 60 * 1024 * 1024


class Place:
    def __init__(self, count):
        self.count = count
        self.inner = 4 if count >= 32 else 2
        self.outer = count // self.inner
        self.here = lax.axis_index("blk")
        self.line = self.here // self.inner
        self.side = lax.rem(self.here, self.inner)
        self.core = lax.axis_index("dp")
        self.half = lax.axis_index("head")
        self.group = 2 * self.core + self.half

    def near(self, k):
        orders = [near_order(self.outer, line)[k] for line in range(self.outer)]
        found = jnp.int32(orders[0])
        for line in range(1, self.outer):
            found = jnp.where(self.line == line, jnp.int32(orders[line]), found)
        return found

    def at(self, line, side):
        return {"blk": line * self.inner + side}

    def beside(self, step):
        return lax.rem(self.side + step, self.inner)

    def partner(self):
        return {"dp": 1 - self.core}

    def across(self):
        return {"head": 1 - self.half}

    def corner(self):
        return {"dp": 1 - self.core, "head": 1 - self.half}


def remote(src, dst, sent, came, device):
    return pltpu.make_async_remote_copy(
        src_ref=src, dst_ref=dst, send_sem=sent, recv_sem=came, device_id=device, device_id_type=MESH
    )


def greet(place, blk=False, core=False, half=False, corner=False):
    sem = pltpu.get_barrier_semaphore()
    amount = jnp.int32(0)

    def hello(device):
        pl.semaphore_signal(sem, inc=1, device_id=device, device_id_type=MESH)

    if blk:
        up, down = place.line < place.outer - 1, place.line > 0
        pl.when(up)(lambda: hello(place.at(place.line + 1, place.side)))
        pl.when(down)(lambda: hello(place.at(place.line - 1, place.side)))
        amount = amount + up.astype(jnp.int32) + down.astype(jnp.int32) + (place.inner - 1)
        for step in range(1, place.inner):
            hello(place.at(place.line, place.beside(step)))
    for wanted, device in (
        (core, place.partner()),
        (half, place.across()),
        (corner, place.corner()),
    ):
        if wanted:
            hello(device)
            amount = amount + 1
    pl.semaphore_wait(sem, amount)


def together(*tasks):
    tasks = list(tasks)
    while tasks:
        for task in list(tasks):
            try:
                next(task)
            except StopIteration:
                tasks.remove(task)


def waiting(task, *rounds):
    for step, _ in enumerate(task):
        yield
        if step < len(rounds):
            for _ in range(rounds[step]):
                yield


def near_order(outer, line):
    ends = outer == 4
    return sorted(
        range(outer),
        key=lambda other: (abs(other - line), ends and other not in (0, outer - 1), other),
    )


def evened(place, parts):
    return parts == 2 and place.inner == 2 and place.outer == 4


def part_of(ref, h, parts):
    if parts == 1:
        return ref
    size = ref.shape[0] // parts
    return ref.at[pl.ds(h * size, size)]


def gather_blk_sems(place_count, parts=2):
    inner = 4 if place_count >= 32 else 2
    return [
        pltpu.SemaphoreType.DMA((2 + inner, place_count, parts)),
        pltpu.SemaphoreType.DMA((place_count, parts)),
        pltpu.SemaphoreType.DMA,
    ]


class GatherBlk:
    def __init__(self, place, src, view, sent, came, own):
        self.place, self.src, self.view, self.sent, self.came = place, src, view, sent, came
        self.parts = came.shape[1]
        self.evened = evened(place, self.parts)
        self.middle = (place.line > 0) & (place.line < place.outer - 1)
        self.copy = pltpu.make_async_copy(src, view(place.here), own)

    def sends(self, k, h):
        place = self.place
        there = place.near(k)
        piece = there * place.inner + place.side
        there_view = part_of(self.view(piece), h, self.parts)
        src = part_of(self.src, h, self.parts) if k == 0 else there_view

        def send(kind, device):
            return remote(
                src, there_view, self.sent.at[kind, piece, h], self.came.at[piece, h], device
            )

        line, side = place.line, place.side
        up = (there <= line) & (line < place.outer - 1)
        down = (there >= line) & (line > 0)
        aside = range(1, place.inner)
        if self.evened and h == 1 and k == place.outer - 1:
            aside = ()
        return (
            [
                (up, lambda: send(0, place.at(line + 1, side))),
                (down, lambda: send(1, place.at(line - 1, side))),
            ],
            [send(1 + step, place.at(line, place.beside(step))) for step in aside],
        )

    def forward(self, k, h):
        along, aside = self.sends(k, h)
        for needed, make in along:
            pl.when(needed)(lambda make=make: make().start())
        for one in aside:
            one.start()

    def start(self):
        self.copy.start()
        for h in range(self.parts):
            self.forward(0, h)

    def arrived(self, piece, h):
        place = self.place
        remote(
            part_of(self.src, h, self.parts),
            part_of(self.view(piece), h, self.parts),
            self.sent.at[0, piece, h],
            self.came.at[piece, h],
            place.at(place.line, place.beside(1)),
        ).wait_recv()

    def pass_on(self, k):
        for h in range(self.parts):
            self.arrived(self.place.near(k) * self.place.inner + self.place.side, h)
            self.forward(k, h)

    def extra(self, k):
        place = self.place
        piece = place.near(k) * place.inner + place.beside(1)
        to = place.near(2 if k == 1 else 1)
        half = part_of(self.view(piece), 1, 2)
        return remote(
            half,
            half,
            self.sent.at[place.inner + 1, piece, 1],
            self.came.at[piece, 1],
            place.at(to, place.side),
        )

    def pass_extra(self, k):
        if self.evened:

            @pl.when(self.middle)
            def _():
                self.arrived(self.place.near(k) * self.place.inner + self.place.beside(1), 1)
                self.extra(k).start()

    def beside_arrived(self, k):
        for step in range(1, self.place.inner):
            piece = self.place.near(k) * self.place.inner + self.place.beside(step)
            for h in range(self.parts):
                if self.evened and h == 1 and k in (1, self.place.outer - 1):
                    pl.when(jnp.logical_not(self.middle))(lambda: self.arrived(piece, 1))
                else:
                    self.arrived(piece, h)

    def finish(self):
        for k in range(self.place.outer):
            for h in range(self.parts):
                along, aside = self.sends(k, h)
                for needed, make in along:
                    pl.when(needed)(lambda make=make: make().wait_send())
                for one in aside:
                    one.wait_send()
        if self.evened:

            @pl.when(self.middle)
            def _():
                self.extra(1).wait_send()
                self.extra(self.place.outer - 1).wait_send()


def gather_blk(place, src, view, sent, came, own):
    if not callable(view):
        out = view
        view = lambda piece: out.at[piece]
    work = GatherBlk(place, src, view, sent, came, own)
    work.start()
    yield
    for k in range(1, place.outer):
        work.pass_on(k)
        if k == place.outer - 2:
            work.pass_extra(1)
        yield
    work.pass_extra(place.outer - 1)
    yield
    for k in range(place.outer):
        work.beside_arrived(k)
    work.finish()
    work.copy.wait()


def add_into(out, *terms):
    def one(i, carry):
        total = terms[0][i].astype(jnp.float32)
        for term in terms[1:]:
            total = total + term[i].astype(jnp.float32)
        out[i] = total.astype(out.dtype)
        return carry

    lax.fori_loop(0, out.shape[0], one, 0)


def reduce_blk_scratch(place_count, piece, dtype, parts=2):
    inner = 4 if place_count >= 32 else 2
    outer = place_count // inner
    half = (piece[0] // 2,) + tuple(piece[1:]) if parts == 2 and inner == 2 and outer == 4 else (1, 8, 128)
    return [
        pltpu.VMEM((outer, inner - 1) + piece, dtype),
        pltpu.VMEM((outer + 1,) + piece, dtype),
        pltpu.VMEM((outer,) + piece, dtype),
        pltpu.VMEM((4,) + half, dtype),
        pltpu.SemaphoreType.DMA((outer, inner - 1, parts)),
        pltpu.SemaphoreType.DMA((outer, inner - 1, parts)),
        pltpu.SemaphoreType.DMA((outer, parts)),
        pltpu.SemaphoreType.DMA((outer + 1, parts)),
        pltpu.SemaphoreType.DMA((2,)),
        pltpu.SemaphoreType.DMA((2,)),
    ]


REDUCE_REFS = 10


class ReduceBlk:
    def __init__(
        self,
        place,
        view,
        out,
        beside,
        along,
        held,
        spare,
        side_sent,
        side_came,
        line_sent,
        line_came,
        spare_sent,
        spare_came,
    ):
        self.place, self.view, self.out = place, view, out
        self.beside, self.along, self.held, self.spare = beside, along, held, spare
        self.side_sems, self.line_sems = (side_sent, side_came), (line_sent, line_came)
        self.spare_sems = (spare_sent, spare_came)
        self.parts = line_sent.shape[1]
        self.evened = evened(place, self.parts)
        self.middle = (place.line > 0) & (place.line < place.outer - 1)

    def part(self, ref, h):
        return part_of(ref, h, self.parts)

    def far(self, k):
        return self.place.near(self.place.outer - 1 - k)

    def alone(self, k, h):
        return self.evened and k == 0 and h == 1

    def side_copy(self, there, step, h, src=None):
        place = self.place
        to = place.beside(step)
        if src is None:
            src = self.part(self.view(there * place.inner + to), h)
        return remote(
            src,
            self.part(self.beside.at[there, place.inner - step - 1], h),
            self.side_sems[0].at[there, step - 1, h],
            self.side_sems[1].at[there, place.inner - step - 1, h],
            place.at(place.line, to),
        )

    def line_copy(self, there, slot, to, h, src=None):
        return remote(
            self.part(self.held.at[there], h) if src is None else src,
            self.part(self.along.at[slot], h),
            self.line_sems[0].at[there, h],
            self.line_sems[1].at[slot, h],
            self.place.at(to, self.place.side),
        )

    def send(self, k, h):
        for step in range(1, self.place.inner):
            self.side_copy(self.far(k), step, h).start()

    def terms(self, k, h):
        place = self.place
        there = self.far(k)
        own = [self.part(self.view(there * place.inner + place.side), h)]
        if self.alone(k, h):
            return own
        for step in range(1, place.inner):
            self.side_copy(there, step, h).wait_recv()
        return own + [self.part(self.beside.at[there, j], h) for j in range(place.inner - 1)]

    def onward(self, there, h, src=None):
        line, outer = self.place.line, self.place.outer
        to = jnp.where(there < line, line - 1, line + 1)
        slot = jnp.where(there == line + 1, outer, there)
        return self.line_copy(there, slot, to, h, src)

    def starts(self, there):
        line, outer = self.place.line, self.place.outer
        return ((there < line) & (line == outer - 1)) | ((there > line) & (line == 0))

    def pass_on(self, k, h):
        place = self.place
        line = place.line
        there = self.far(k)
        terms = self.terms(k, h)
        held = self.part(self.held.at[there], h)
        starts = self.starts(there)

        @pl.when(starts)
        def _():
            add_into(held, *terms)

        @pl.when(jnp.logical_not(starts))
        def _():
            back = jnp.where(there < line, line + 1, line - 1)
            self.line_copy(there, there, back, h).wait_recv()
            add_into(held, self.part(self.along.at[there], h), *terms)

        self.onward(there, h).start()

    def last(self, h):
        place = self.place
        line, outer = place.line, place.outer
        terms = self.terms(outer - 1, h)
        below, above = line > 0, line < outer - 1
        from_above = self.part(self.along.at[line], h)
        from_below = self.part(self.along.at[outer], h)
        out = self.part(self.out, h)

        @pl.when(above)
        def _():
            self.line_copy(line, line, line + 1, h).wait_recv()

        @pl.when(below)
        def _():
            self.line_copy(line, outer, line - 1, h).wait_recv()

        @pl.when(above & below)
        def _():
            add_into(out, from_above, from_below, *terms)

        @pl.when(above & jnp.logical_not(below))
        def _():
            add_into(out, from_above, *terms)

        @pl.when(jnp.logical_not(above) & below)
        def _():
            add_into(out, from_below, *terms)


    def spare_view(self, k):
        place = self.place
        return self.part(self.view(place.near(k) * place.inner + place.beside(1)), 1)

    def spare_first(self):
        return remote(
            self.spare_view(3),
            self.spare.at[0],
            self.spare_sems[0].at[0],
            self.spare_sems[1].at[0],
            self.place.at(self.place.near(1), self.place.side),
        )

    def spare_second(self):
        return remote(
            self.spare.at[2],
            self.spare.at[1],
            self.spare_sems[0].at[1],
            self.spare_sems[1].at[1],
            self.place.at(self.place.near(2), self.place.side),
        )

    def spare_side(self):
        return self.side_copy(self.far(2), 1, 1, self.spare.at[3])

    def opening(self):
        outer = self.place.outer
        if not self.evened:

            def every():
                for k in range(outer):
                    for h in range(self.parts):
                        self.send(k, h)

            return [every]
        ends = jnp.logical_not(self.middle)

        def along():
            self.spare_first().start()
            there = self.far(0)
            self.onward(
                there, 1, self.part(self.view(there * self.place.inner + self.place.side), 1)
            ).start()

        todo = [lambda: self.send(0, 0), lambda: pl.when(ends)(along)]
        todo += [lambda k=k, h=h: self.send(k, h) for k, h in ((1, 0), (1, 1), (2, 0))]
        todo += [
            lambda k=k, h=h: pl.when(ends)(lambda: self.send(k, h))
            for k, h in ((2, 1), (3, 0), (3, 1))
        ]
        return todo

    def start(self):
        for step in self.opening():
            step()

    def turning(self):
        def first():
            self.spare_first().wait_recv()
            add_into(self.spare.at[2], self.spare.at[0], self.spare_view(3))
            self.spare_second().start()

        def second():
            self.spare_second().wait_recv()
            add_into(self.spare.at[3], self.spare.at[1], self.spare_view(1))
            self.spare_side().start()
            for h in (0, 1):
                self.send(3, h)

        steps = (first, lambda: self.pass_on(0, 1), second)
        return [lambda step=step: pl.when(self.middle)(step) for step in steps]

    def events(self):
        outer, parts = self.place.outer, self.parts
        if self.evened:
            todo = self.turning() + [lambda: self.pass_on(0, 0)]
        else:
            todo = [lambda h=h: self.pass_on(0, h) for h in range(parts)]
        for k in range(1, outer - 1):
            for h in range(parts):
                todo.append(lambda k=k, h=h: self.pass_on(k, h))
        for h in range(parts):
            todo.append(lambda h=h: self.last(h))
        return todo

    def finish(self):
        for k in range(self.place.outer):
            for h in range(self.parts):
                if k < self.place.outer - 1:
                    self.onward(self.far(k), h).wait_send()
                if not self.alone(k, h):
                    for step in range(1, self.place.inner):
                        self.side_copy(self.far(k), step, h).wait_send()
        if self.evened:

            @pl.when(self.middle)
            def _():
                self.spare_second().wait_send()

            @pl.when(jnp.logical_not(self.middle))
            def _():
                self.spare_first().wait_send()


def reduce_blk(place, view, out, *scratch):
    if not callable(view):
        part = view
        view = lambda piece: part.at[piece]
    work = ReduceBlk(place, view, out, *scratch)
    for step in work.opening() + work.events():
        step()
        yield
    work.finish()


def gather_group_sems():
    return [pltpu.SemaphoreType.DMA((3,)), pltpu.SemaphoreType.DMA((4,)), pltpu.SemaphoreType.DMA]


def gather_group(place, src, view, sent, came, own, through=None):
    if not callable(view):
        out = view
        view = lambda g: out.at[g]
    copy = pltpu.make_async_copy(src if through is None else through, view(place.group), own)
    load = None if through is None else pltpu.make_async_copy(src, through, own)
    mine, other = place.group, 2 * place.core + (1 - place.half)
    to_half = remote(src, view(mine), sent.at[0], came.at[mine], place.across())
    to_core = remote(src, view(mine), sent.at[1], came.at[mine], place.partner())
    to_half.start()
    to_core.start()
    (load or copy).start()
    yield
    if load:
        load.wait()
        copy.start()
    remote(src, view(other), sent.at[0], came.at[other], place.across()).wait_recv()
    relay = remote(view(other), view(other), sent.at[2], came.at[other], place.partner())
    relay.start()
    yield
    for half in (0, 1):
        slot = 2 * (1 - place.core) + half
        remote(src, view(slot), sent.at[0], came.at[slot], place.partner()).wait_recv()
    to_half.wait_send()
    to_core.wait_send()
    relay.wait_send()
    copy.wait()


def share_rows(ref, parts, p):
    rows = ref.shape[0] // parts
    return ref.at[pl.ds(p * rows, rows)]


def gather_group_rows(place, src, out, parts, take):
    def task(p, refs):
        rows = src.shape[0] // parts
        view = lambda g: out.at[g, pl.ds(p * rows, rows)]
        return gather_group(place, share_rows(src, parts, p), view, *refs)

    return [task(p, take(4)) for p in range(parts)]


def gather_rows_scratch(value, parts):
    through = pltpu.VMEM((value.shape[0] // parts, value.shape[1]), value.dtype)
    return (gather_group_sems() + [through]) * parts


def fold_rows_scratch(piece, parts):
    rows, width = piece[0] // parts, piece[1]
    bf16 = jnp.bfloat16
    one = [
        pltpu.VMEM((2, rows, width), bf16),
        pltpu.VMEM((rows, width), bf16),
        pltpu.VMEM((rows, width), bf16),
        pltpu.VMEM((rows, width), bf16),
        pltpu.VMEM((rows, width), jnp.float32),
        pltpu.SemaphoreType.DMA((3,)),
        pltpu.SemaphoreType.DMA((3,)),
        pltpu.SemaphoreType.DMA((3,)),
    ]
    return one * parts


def add_rows(out, *terms):
    rows = slabs(out.shape[0])

    def one(i, carry):
        at = pl.ds(pl.multiple_of(i * rows, rows), rows)
        total = terms[0][at].astype(jnp.float32)
        for term in terms[1:]:
            total = total + term[at].astype(jnp.float32)
        out[at] = total.astype(out.dtype)
        return carry

    lax.fori_loop(0, out.shape[0] // rows, one, 0)


def fold_rows(place, part, out, parts, take):
    rows = out.shape[0] // parts
    core, half = place.core, place.half
    far, near = 2 * (1 - core) + (1 - half), 2 * (1 - core) + half
    beside = 2 * core + (1 - half)

    def task(p, from_core, from_half, held, mine, total, sent, came, local):
        at = pl.ds(p * rows, rows)
        first = remote(part.at[far, at], from_core.at[1], sent.at[0], came.at[0], place.partner())
        second = remote(part.at[near, at], from_core.at[0], sent.at[1], came.at[1], place.partner())
        third = remote(held, from_half, sent.at[2], came.at[2], place.across())
        load_held = pltpu.make_async_copy(part.at[beside, at], held, local.at[0])
        load_mine = pltpu.make_async_copy(part.at[place.group, at], mine, local.at[1])
        store = pltpu.make_async_copy(total, out.at[at], local.at[2])
        for copy in (first, load_held, second, load_mine):
            copy.start()
        yield
        first.wait_recv()
        load_held.wait()
        add_rows(held, held, from_core.at[1])
        third.start()
        yield
        second.wait_recv()
        load_mine.wait()
        third.wait_recv()
        add_rows(total, mine, from_core.at[0], from_half)
        store.start()
        yield
        for copy in (first, second, third):
            copy.wait_send()
        store.wait()

    return [task(p, *take(8)) for p in range(parts)]


ROW_PARTS = 3


def reduce_group_scratch(piece, dtype):
    return [
        pltpu.VMEM((2,) + piece, dtype),
        pltpu.VMEM(piece, dtype),
        pltpu.VMEM(piece, dtype),
        pltpu.SemaphoreType.DMA((3,)),
        pltpu.SemaphoreType.DMA((3,)),
    ]


def reduce_group(place, part, out, from_core, from_half, held, sent, came):
    far = 2 * (1 - place.core) + (1 - place.half)
    near = 2 * (1 - place.core) + place.half
    first = remote(part.at[far], from_core.at[1], sent.at[0], came.at[0], place.partner())
    second = remote(part.at[near], from_core.at[0], sent.at[1], came.at[1], place.partner())
    first.start()
    second.start()
    yield
    first.wait_recv()
    add_into(held, part.at[2 * place.core + (1 - place.half)], from_core.at[1])
    third = remote(held, from_half, sent.at[2], came.at[2], place.across())
    third.start()
    yield
    second.wait_recv()
    third.wait_recv()
    add_into(out, part.at[place.group], from_core.at[0], from_half)
    first.wait_send()
    second.wait_send()
    third.wait_send()


def exchange_group_sems():
    return [pltpu.SemaphoreType.DMA((3,)), pltpu.SemaphoreType.DMA((4,)), pltpu.SemaphoreType.DMA]


def exchange_group(place, src, out, sent, came, own):
    mine = place.group
    copy = pltpu.make_async_copy(src.at[mine], out.at[mine], own)
    copy.start()
    core, half = place.core, place.half
    links = (
        (2 * (1 - core) + (1 - half), place.corner()),
        (2 * core + (1 - half), place.across()),
        (2 * (1 - core) + half, place.partner()),
    )
    copies = [
        remote(src.at[to], out.at[mine], sent.at[k], came.at[mine], device)
        for k, (to, device) in enumerate(links)
    ]
    for one in copies:
        one.start()
    yield
    for k, (peer, device) in enumerate(links):
        remote(src.at[peer], out.at[peer], sent.at[k], came.at[peer], device).wait_recv()
    for one in copies:
        one.wait_send()
    copy.wait()


def transfer(name, number, body, ins, outs, scratch, moved, out_spaces=None, in_spaces=None):
    spaces = out_spaces or [pl.ANY] * len(outs)
    in_spaces = in_spaces or [pltpu.VMEM] * len(ins)
    return pl.pallas_call(
        body,
        name=name,
        out_shape=outs,
        in_specs=[pl.BlockSpec(memory_space=space) for space in in_spaces],
        out_specs=[pl.BlockSpec(memory_space=space) for space in spaces],
        scratch_shapes=scratch,
        compiler_params=pltpu.CompilerParams(
            collective_id=number, has_side_effects=True, vmem_limit_bytes=VMEM_LIMIT
        ),
        cost_estimate=pl.CostEstimate(flops=0, bytes_accessed=moved * 40, transcendentals=0),
    )(*ins)


def shape(dims, dtype):
    return jax.ShapeDtypeStruct(tuple(dims), dtype)


def slabs(rows):
    return math.gcd(rows, 16)


def all_gather_blk(value, count, number):
    def body(src, out, *sems):
        place = Place(count)
        greet(place, blk=True)
        together(gather_blk(place, src, out, *sems))

    return transfer(
        f"gather{number}",
        number,
        body,
        [value],
        [shape((count,) + value.shape, value.dtype)],
        gather_blk_sems(count),
        value.size * 2 * count,
    )[0]


def reduce_scatter_blk(value, count, number):
    piece = value.shape[1:]

    def body(part, out, *scratch):
        place = Place(count)
        greet(place, blk=True)
        together(reduce_blk(place, part, out, *scratch))

    return transfer(
        f"reduce{number}",
        number,
        body,
        [value],
        [shape(piece, jnp.float32)],
        reduce_blk_scratch(count, piece, value.dtype),
        value.size * 2,
        [pltpu.VMEM],
    )[0]


class Taker:
    def __init__(self, refs):
        self.refs = list(refs)

    def __call__(self, amount):
        taken = self.refs[:amount]
        del self.refs[:amount]
        return taken


def gather_first(qkv, out_parts, tokens, gains, docs, down, count, number):
    names = 6

    def body(*refs):
        qkv_ref, out_ref, tok_ref, gain_ref, doc_ref, down_ref = refs[:names]
        qkv_all, out_mine, tok_all, gain_all, doc_all, down_all = refs[names : 2 * names]
        gain_mine = refs[2 * names]
        take = Taker(refs[2 * names + 1 :])
        place = Place(count)
        greet(place, blk=True, core=True, half=True, corner=True)

        def gain_task(near, far):
            yield from gather_blk(place, gain_ref, gain_mine, *near)
            yield from gather_group(place, gain_mine, gain_all, *far)

        def doc_task(sent, came, own):
            copy = pltpu.make_async_copy(doc_ref, doc_all.at[place.core], own)
            copy.start()
            send = remote(doc_ref, doc_all.at[place.core], sent, came, place.partner())
            send.start()
            yield
            remote(doc_ref, doc_all.at[1 - place.core], sent, came, place.partner()).wait_recv()
            send.wait_send()
            copy.wait()

        together(
            gain_task(take(3), take(3)),
            gather_blk(place, qkv_ref, qkv_all, *take(3)),
            doc_task(*take(3)),
            waiting(gather_group(place, tok_ref, tok_all, *take(3)), 2),
            waiting(exchange_group(place, out_ref, out_mine, *take(3)), 3),
            *(
                waiting(task, 2 + p, 4)
                for p, task in enumerate(
                    gather_group_rows(place, down_ref, down_all, ROW_PARTS, take)
                )
            ),
        )

    ins = [qkv, out_parts, tokens, gains, docs, down]
    return transfer(
        f"first{number}",
        number,
        body,
        ins,
        [
            shape((count,) + qkv.shape, qkv.dtype),
            shape(out_parts.shape, out_parts.dtype),
            shape((GROUPS,) + tokens.shape, tokens.dtype),
            shape((GROUPS, count) + gains.shape, gains.dtype),
            shape((2,) + docs.shape, docs.dtype),
            shape((GROUPS,) + down.shape, down.dtype),
        ],
        [pltpu.VMEM((count,) + gains.shape, gains.dtype)]
        + gather_blk_sems(count, 1)
        + gather_group_sems()
        + gather_blk_sems(count)
        + [pltpu.SemaphoreType.DMA] * 3
        + gather_group_sems()
        + exchange_group_sems()
        + gather_rows_scratch(down, ROW_PARTS),
        (qkv.size + out_parts.size) * 2 * count,
        None,
        [pltpu.VMEM] * 5 + [pl.ANY],
    )


def gather_second(kv, out_mine, gate_up, count, number):
    def body(kv_ref, out_ref, gate_up_ref, kv_all, out_all, gate_up_all, *sems):
        take = Taker(sems)
        place = Place(count)
        greet(place, blk=True, core=True, half=True)
        together(
            gather_blk(place, kv_ref, kv_all, *take(3)),
            gather_blk(place, out_ref, lambda i: out_all.at[:, i], *take(3)),
            *(
                waiting(task, 2 + p, 4)
                for p, task in enumerate(
                    gather_group_rows(place, gate_up_ref, gate_up_all, ROW_PARTS, take)
                )
            ),
        )

    groups, rows, width = out_mine.shape
    return transfer(
        f"gather{number}",
        number,
        body,
        [kv, out_mine, gate_up],
        [
            shape((count,) + kv.shape, kv.dtype),
            shape((groups, count, rows, width), out_mine.dtype),
            shape((GROUPS,) + gate_up.shape, gate_up.dtype),
        ],
        gather_blk_sems(count) + gather_blk_sems(count) + gather_rows_scratch(gate_up, ROW_PARTS),
        (kv.size + out_mine.size) * 2 * count,
        None,
        [pltpu.VMEM, pltpu.VMEM, pl.ANY],
    )


def reduce_middle(dkv_part, out_part, gate_up_part, count, number):
    dkv_piece = dkv_part.shape[1:]
    out_piece = out_part.shape[:1] + out_part.shape[2:]

    gate_up_piece = gate_up_part.shape[1:]

    def body(dkv_ref, out_ref, gate_up_ref, dkv_sum, out_sum, gate_up_sum, *scratch):
        take = Taker(scratch)
        place = Place(count)
        greet(place, blk=True, core=True, half=True)
        together(
            reduce_blk(place, dkv_ref, dkv_sum, *take(REDUCE_REFS)),
            reduce_blk(place, lambda i: out_ref.at[:, i], out_sum, *take(REDUCE_REFS)),
            *(
                waiting(task, *rounds)
                for rounds, task in zip(
                    ((6, 5, 5), (8, 5, 3), (10, 6, 0)),
                    fold_rows(place, gate_up_ref, gate_up_sum, ROW_PARTS, take),
                )
            ),
        )

    return transfer(
        f"reduce{number}",
        number,
        body,
        [dkv_part, out_part, gate_up_part],
        [
            shape(dkv_piece, jnp.bfloat16),
            shape(out_piece, jnp.bfloat16),
            shape(gate_up_piece, jnp.float32),
        ],
        reduce_blk_scratch(count, dkv_piece, jnp.bfloat16)
        + reduce_blk_scratch(count, out_piece, jnp.bfloat16)
        + fold_rows_scratch(gate_up_piece, ROW_PARTS),
        (dkv_part.size + out_part.size) * 2,
        [pltpu.VMEM, pltpu.VMEM, pl.ANY],
        [pltpu.VMEM, pltpu.VMEM, pl.ANY],
    )


def reduce_last(qkv_part, norm_part, gain_part, out_sum, down_part, count, number):
    gain_piece = gain_part.shape[1:]
    qkv_piece, norm_piece = qkv_part.shape[1:], norm_part.shape[1:]

    def body(*refs):
        qkv_ref, norm_ref, gain_ref, out_ref, down_ref = refs[:5]
        qkv_sum, norm_sum, gain_sum, out_all, down_sum = refs[5:10]
        gain_mine = refs[10]
        take = Taker(refs[11:])
        place = Place(count)
        greet(place, blk=True, core=True, half=True, corner=True)

        def gain_task(near, far):
            yield from reduce_blk(place, gain_ref, gain_mine, *near)
            yield from reduce_group(place, gain_mine, gain_sum, *far)

        main = reduce_blk(place, qkv_ref, qkv_sum, *take(REDUCE_REFS))
        gain = gain_task(take(REDUCE_REFS), take(5))
        together(
            waiting(gain, 11),
            main,
            waiting(exchange_group(place, out_ref, out_all, *take(3)), 16),
            waiting(reduce_group(place, norm_ref, norm_sum, *take(5)), 7, 9),
            *(
                waiting(task, *rounds)
                for rounds, task in zip(
                    ((7, 7, 2), (8, 8, 0), (9, 9, 0)),
                    fold_rows(place, down_ref, down_sum, ROW_PARTS, take),
                )
            ),
        )

    return transfer(
        f"last{number}",
        number,
        body,
        [qkv_part, norm_part, gain_part, out_sum, down_part],
        [
            shape(qkv_piece, jnp.float32),
            shape(norm_piece, jnp.float32),
            shape(gain_piece[1:], jnp.float32),
            shape(out_sum.shape, jnp.bfloat16),
            shape(down_part.shape[1:], jnp.float32),
        ],
        [pltpu.VMEM(gain_piece, jnp.float32)]
        + reduce_blk_scratch(count, qkv_piece, jnp.bfloat16)
        + reduce_blk_scratch(count, gain_piece, jnp.float32, 1)
        + reduce_group_scratch(gain_piece[1:], jnp.float32)
        + exchange_group_sems()
        + reduce_group_scratch(norm_piece, jnp.bfloat16)
        + fold_rows_scratch(down_part.shape[1:], ROW_PARTS),
        qkv_part.size * 2,
        [pltpu.VMEM] * 4 + [pl.ANY],
        [pltpu.VMEM] * 4 + [pl.ANY],
    )


def all_gather_group(value, number):
    def body(src, out, *sems):
        place = Place(lax.axis_size("blk"))
        greet(place, core=True, half=True)
        together(gather_group(place, src, out, *sems))

    return transfer(
        f"group{number}",
        number,
        body,
        [value],
        [shape((GROUPS,) + value.shape, value.dtype)],
        gather_group_sems(),
        value.size * 8,
    )[0]


def reduce_scatter_group(value, number):
    piece = value.shape[1:]

    def body(part, out, *scratch):
        place = Place(lax.axis_size("blk"))
        greet(place, core=True, half=True)
        together(reduce_group(place, part, out, *scratch))

    return transfer(
        f"fold{number}",
        number,
        body,
        [value],
        [shape(piece, jnp.float32)],
        reduce_group_scratch(piece, value.dtype),
        value.size * 2,
        [pltpu.VMEM],
    )[0]


def dot(left, right, contract):
    return lax.dot_general(left, right, (contract, ((), ())), preferred_element_type=jnp.float32)


LAST = ((1,), (1,))
PLAIN = ((1,), (0,))
FIRST = ((0,), (0,))


LANES = 128
GELU_A = math.sqrt(2.0 / math.pi)
GELU_B = 0.044715


def feed_forward_fits(count, rows, width, hidden):
    inner = 4 if count >= 32 else 2
    outer = count // inner
    tile = rows * width * 2
    weights = 3 * hidden * width * 2
    kept = count * rows * 3 * hidden * 2
    total = weights + kept + tile * (3 * count + outer * (inner - 1) + 2 * outer + 3) + 9 * tile
    total += 3 * LANES * (count * rows + 2 * width) * 2
    return total < 58 * 2**20 and hidden % (3 * LANES) == 0 and width % 256 == 0


def feed_forward_kernel(
    count,
    branch_ref,
    token_ref,
    cot_ref,
    gain_ref,
    gate_up_hbm,
    down_hbm,
    out_ref,
    middle_grad_ref,
    branch_grad_ref,
    gain_grad_ref,
    gate_up_grad_hbm,
    down_grad_hbm,
    w_gate_up,
    w_down,
    norm_all,
    grad_all,
    act,
    hidden,
    part,
    middle,
    norm_own,
    grad_own,
    total,
    turned,
    staged,
    beside,
    along,
    held,
    spare,
    w_sems,
    out_sems,
    *sems,
):
    place = Place(count)
    rows, width = norm_all.shape[1:]
    units = hidden.shape[1]
    chunks = units // LANES
    inner, outer = place.inner, place.outer
    slab = branch_ref.shape[1]
    steps = rows // slab
    columns = width // 256
    pair = inner * rows
    take = Taker(sems)

    def weight_copies(i):
        units_at = pl.ds(pl.multiple_of(i * LANES, LANES), LANES)
        return [
            pltpu.make_async_copy(
                gate_up_hbm.at[units_at, pl.ds(0, width)],
                w_gate_up.at[i, pl.ds(0, LANES)],
                w_sems.at[3 * i],
            ),
            pltpu.make_async_copy(
                gate_up_hbm.at[units_at, pl.ds(width, width)],
                w_gate_up.at[i, pl.ds(LANES, LANES)],
                w_sems.at[3 * i + 1],
            ),
            pltpu.make_async_copy(down_hbm.at[units_at], w_down.at[units_at], w_sems.at[3 * i + 2]),
        ]

    def start_weights(i, carry):
        for copy in weight_copies(i):
            copy.start()
        return carry

    def wait_weights(i, carry):
        for copy in weight_copies(i):
            copy.wait()
        return carry

    lax.fori_loop(0, chunks, start_weights, 0)

    def scale_of(values):
        return lax.rsqrt(jnp.mean(values * values, axis=-1, keepdims=True) + NORM_EPS)

    def slab_rows(i):
        return pl.ds(pl.multiple_of(i * slab, slab), slab)

    def before(i, carry):
        value = branch_ref[i]
        mid = token_ref[i].astype(jnp.float32) + value * scale_of(value) * gain_ref[1:2]
        middle[i] = mid
        norm_own[slab_rows(i)] = (mid * scale_of(mid) * gain_ref[2:3]).astype(jnp.bfloat16)
        return carry

    lax.fori_loop(0, steps, before, 0)
    greet(place, blk=True)

    def pair_rows(k):
        return pl.ds(pl.multiple_of(place.near(k) * pair, pair), pair)

    def pair_pieces(k):
        return pl.ds(place.near(k) * inner, inner)

    def column(n):
        return pl.ds(pl.multiple_of(n * 256, 256), 256)

    def put_part(k, n, value):
        split = value.astype(jnp.bfloat16).reshape((inner, steps, slab, 256))
        part[pair_pieces(k), :, :, column(n)] = split

    def receive(gather, k):
        if k == 0:
            gather.copy.wait()
        if not gather.evened:
            if k + 1 < outer:
                gather.pass_on(k + 1)
            gather.beside_arrived(k)
            return
        ends = jnp.logical_not(gather.middle)
        if k == 0:
            gather.pass_on(1)
            pl.when(gather.middle)(lambda: gather.pass_on(2))
        elif k == 1:
            pl.when(ends)(lambda: gather.pass_on(2))
            gather.pass_extra(1)
            pl.when(gather.middle)(lambda: gather.pass_on(3))
        elif k == 2:
            pl.when(ends)(lambda: gather.pass_on(3))
            gather.pass_extra(3)
        gather.beside_arrived(k)

    gather = GatherBlk(place, norm_own, lambda i: norm_all.at[i], *take(3))
    gather.start()
    lax.fori_loop(0, chunks, wait_weights, 0)
    for k in range(outer):
        receive(gather, k)
        at = pair_rows(k)

        def up_chunk(j, carry, k=k, at=at):
            x = norm_all[pair_pieces(k)].reshape(pair, width)
            both = dot(x, w_gate_up[j], LAST)
            act[at, column(j)] = both.astype(jnp.bfloat16)
            gate, up = both[:, :LANES], both[:, LANES:]
            bent = 0.5 * gate * (1.0 + jnp.tanh(GELU_A * (gate + GELU_B * (gate * gate * gate))))
            hidden[at, pl.ds(pl.multiple_of(j * LANES, LANES), LANES)] = (bent * up).astype(
                jnp.bfloat16
            )
            return carry

        lax.fori_loop(0, chunks, up_chunk, 0)

        def down_chunk(n, carry, k=k, at=at):
            put_part(k, n, dot(hidden[at, :], w_down[:, column(n)], PLAIN))
            return carry

        lax.fori_loop(0, columns, down_chunk, 0)
    gather.finish()
    reduce = ReduceBlk(place, lambda i: part.at[i], total, beside, along, held, spare, *take(6))
    reduce.start()
    for event in reduce.events():
        event()

    gain_grad_ref[...] = jnp.zeros_like(gain_grad_ref)

    def norm_back(value, gain, incoming):
        scale = scale_of(value)
        lifted = incoming * gain
        pull = jnp.mean(lifted * value, axis=-1, keepdims=True)
        gain_grad = jnp.sum(incoming * value * scale, axis=0, keepdims=True)
        return scale * lifted - value * (scale * scale * scale) * pull, gain_grad

    def between(i, carry):
        value, cot = total[i], cot_ref[i].astype(jnp.float32)
        gain = gain_ref[3:4]
        out_ref[i] = (middle[i] + value * scale_of(value) * gain).astype(jnp.bfloat16)
        grad, gain_grad = norm_back(value, gain, cot)
        gain_grad_ref[3:4] += gain_grad
        grad_own[slab_rows(i)] = grad.astype(jnp.bfloat16)
        return carry

    lax.fori_loop(0, steps, between, 0)
    reduce.finish()

    gather = GatherBlk(place, grad_own, lambda i: grad_all.at[i], *take(3))
    gather.start()
    for k in range(outer):
        receive(gather, k)
        at = pair_rows(k)

        def back_chunk(j, carry, k=k, at=at):
            g = grad_all[pair_pieces(k)].reshape(pair, width)
            units_at = pl.ds(pl.multiple_of(j * LANES, LANES), LANES)
            grad = dot(g, w_down[units_at], LAST)
            both = act[at, column(j)].astype(jnp.float32)
            gate, up = both[:, :LANES], both[:, LANES:]
            bend = jnp.tanh(GELU_A * (gate + GELU_B * (gate * gate * gate)))
            bent = 0.5 * gate * (1.0 + bend)
            slope = 0.5 * (1.0 + bend) + (0.5 * GELU_A) * gate * (1.0 - bend * bend) * (
                1.0 + (3.0 * GELU_B) * gate * gate
            )
            pulled = jnp.concatenate([grad * up * slope, grad * bent], axis=1)
            act[at, column(j)] = pulled.astype(jnp.bfloat16)
            return carry

        lax.fori_loop(0, chunks, back_chunk, 0)

        def input_chunk(n, carry, k=k, at=at):
            w = w_gate_up[:, :, column(n)].reshape(2 * units, 256)
            put_part(k, n, dot(act[at, :], w, PLAIN))
            return carry

        lax.fori_loop(0, columns, input_chunk, 0)
    gather.finish()
    reduce = ReduceBlk(place, lambda i: part.at[i], total, beside, along, held, spare, *take(6))
    reduce.start()

    tokens = count * rows
    slots = staged.shape[0]

    def up_store(i):
        slot = lax.rem(i, slots)
        units_at = pl.ds(pl.multiple_of(i * LANES, LANES), LANES)
        return [
            pltpu.make_async_copy(
                staged.at[slot, pl.ds(h * LANES, LANES)],
                gate_up_grad_hbm.at[units_at, pl.ds(h * width, width)],
                out_sems.at[slot, h],
            )
            for h in (0, 1)
        ]

    def up_grad(i, carry):
        @pl.when(i >= slots)
        def _():
            for copy in up_store(i - slots):
                copy.wait()

        turned[pl.ds(0, 256)] = jnp.transpose(act[:, column(i)])

        def one(n, c):
            x = norm_all[:, :, column(n)].reshape(tokens, 256)
            staged[lax.rem(i, slots), pl.ds(0, 256), column(n)] = dot(
                turned[pl.ds(0, 256)], x, PLAIN
            ).astype(jnp.bfloat16)
            return c

        lax.fori_loop(0, columns, one, 0)
        for copy in up_store(i):
            copy.start()
        return carry

    three = 3 * LANES

    def down_store(i):
        slot = lax.rem(i, slots)
        return pltpu.make_async_copy(
            staged.at[slot],
            down_grad_hbm.at[pl.ds(pl.multiple_of(i * three, three), three)],
            out_sems.at[slot, 2],
        )

    def down_grad(i, carry):
        @pl.when(i >= slots)
        def _():
            down_store(i - slots).wait()

        turned[...] = jnp.transpose(hidden[:, pl.ds(pl.multiple_of(i * three, three), three)])

        def one(n, c):
            x = grad_all[:, :, column(n)].reshape(tokens, 256)
            staged[lax.rem(i, slots), :, column(n)] = dot(turned[...], x, PLAIN).astype(jnp.bfloat16)
            return c

        lax.fori_loop(0, columns, one, 0)
        down_store(i).start()
        return carry

    events = reduce.events()
    early = len(events) - 3
    bounds = [chunks * k // early for k in range(early + 1)]
    for k in range(early):
        lax.fori_loop(bounds[k], bounds[k + 1], up_grad, 0)
        events[k]()
    for i in range(max(0, chunks - slots), chunks):
        for copy in up_store(i):
            copy.wait()
    thirds = units // three
    bounds = [thirds * k // 3 for k in range(4)]
    for k in range(3):
        lax.fori_loop(bounds[k], bounds[k + 1], down_grad, 0)
        events[early + k]()

    def after(i, carry):
        value, mid, cot = branch_ref[i], middle[i], cot_ref[i].astype(jnp.float32)
        grad, gain_grad = norm_back(mid, gain_ref[2:3], total[i])
        gain_grad_ref[2:3] += gain_grad
        middle_grad = cot + grad
        middle_grad_ref[i] = middle_grad
        grad, gain_grad = norm_back(value, gain_ref[1:2], middle_grad)
        gain_grad_ref[1:2] += gain_grad
        branch_grad_ref[i] = grad.astype(jnp.bfloat16)
        return carry

    lax.fori_loop(0, steps, after, 0)
    reduce.finish()
    for i in range(max(0, thirds - slots), thirds):
        down_store(i).wait()


def feed_forward(branch, tokens, cotangent, gains, gate_up_all, down_all, count, number):
    steps, slab, width = branch.shape
    rows = steps * slab
    units = down_all.shape[0]
    inner = 4 if count >= 32 else 2
    outer = count // inner
    piece = branch.shape
    bf16, f32 = jnp.bfloat16, jnp.float32
    vmem = pl.BlockSpec(memory_space=pltpu.VMEM)
    anywhere = pl.BlockSpec(memory_space=pl.ANY)
    slots = 2
    line_scratch = reduce_blk_scratch(count, piece, bf16)
    return pl.pallas_call(
        functools.partial(feed_forward_kernel, count),
        name="feed_forward",
        out_shape=[
            shape(piece, bf16),
            shape(piece, f32),
            shape(piece, bf16),
            shape((4, width), f32),
            shape(gate_up_all.shape, bf16),
            shape(down_all.shape, bf16),
        ],
        in_specs=[vmem] * 4 + [anywhere] * 2,
        out_specs=[vmem] * 4 + [anywhere] * 2,
        scratch_shapes=[
            pltpu.VMEM((units // LANES, 2 * LANES, width), bf16),
            pltpu.VMEM((units, width), bf16),
            pltpu.VMEM((count, rows, width), bf16),
            pltpu.VMEM((count, rows, width), bf16),
            pltpu.VMEM((count * rows, 2 * units), bf16),
            pltpu.VMEM((count * rows, units), bf16),
            pltpu.VMEM((count,) + piece, bf16),
            pltpu.VMEM(piece, f32),
            pltpu.VMEM((rows, width), bf16),
            pltpu.VMEM((rows, width), bf16),
            pltpu.VMEM(piece, f32),
            pltpu.VMEM((3 * LANES, count * rows), bf16),
            pltpu.VMEM((slots, 3 * LANES, width), bf16),
        ]
        + line_scratch[:4]
        + [
            pltpu.SemaphoreType.DMA((3 * units // LANES,)),
            pltpu.SemaphoreType.DMA((slots, 3)),
        ]
        + gather_blk_sems(count)
        + line_scratch[4:]
        + gather_blk_sems(count)
        + line_scratch[4:],
        compiler_params=pltpu.CompilerParams(
            collective_id=number, has_side_effects=True, vmem_limit_bytes=67043328
        ),
        cost_estimate=pl.CostEstimate(
            flops=18 * count * rows * units * width,
            bytes_accessed=500 * 2**20,
            transcendentals=0,
        ),
    )(branch, tokens, cotangent, gains, gate_up_all, down_all)


def attention_scores(q2, k, query_pos, query_doc, key_block, key_doc, rows):
    raw = lax.dot_general(q2, k, (((1,), (1,)), ((), ())), preferred_element_type=jnp.float32)
    capped = jnp.tanh(raw * (SCORE_SCALE / SOFT_CAP))
    key_pos = key_block * rows + lax.broadcasted_iota(jnp.int32, (1, rows), 1)
    visible = (key_pos <= query_pos) & (key_doc == query_doc)
    return capped, jnp.where(visible, jnp.exp(SOFT_CAP * capped), 0.0)


def attention_query(q_ref, doc_ref, here, count, rows):
    half = pl.program_id(1)
    block = half * count + here
    q2 = jnp.concatenate([q_ref[0, :, :HEAD_DIM], q_ref[0, :, HEAD_DIM:]], axis=0)
    inside = lax.broadcasted_iota(jnp.int32, (rows, 1), 0)
    position = block * rows + jnp.concatenate([inside, inside], axis=0)
    doc = jnp.concatenate([doc_ref[0], doc_ref[0]], axis=0)
    return block, q2, position, doc


def attention_forward_kernel(
    count, here_ref, q_ref, kv_ref, doc_ref, key_doc_ref, attn_ref, full_ref, total_ref, acc, tot
):
    rows = q_ref.shape[1]
    block, q2, position, doc = attention_query(q_ref, doc_ref, here_ref[0], count, rows)
    acc[...] = jnp.zeros_like(acc)
    tot[...] = jnp.zeros_like(tot)

    def one(key_block, carry):
        key_half = (key_block >= count).astype(jnp.int32)
        kv = kv_ref.at[key_block - key_half * count, key_half]
        _, weights = attention_scores(
            q2, kv[:, :HEAD_DIM], position, doc, key_block, key_doc_ref[0, key_block], rows
        )
        tot[...] += jnp.sum(weights, axis=-1, keepdims=True)
        acc[...] += jnp.dot(
            weights.astype(jnp.bfloat16), kv[:, HEAD_DIM:], preferred_element_type=jnp.float32
        )
        return carry

    lax.fori_loop(jnp.maximum(block - count, 0), block + 1, one, 0)
    attended = acc[...] / tot[...]
    attended = jnp.concatenate([attended[:rows], attended[rows:]], axis=1)
    full_ref[0] = attended
    attn_ref[0] = attended.astype(jnp.bfloat16)
    total_ref[0] = tot[...]


def attention_backward_kernel(
    count,
    here_ref,
    q_ref,
    kv_ref,
    doc_ref,
    key_doc_ref,
    grad_ref,
    full_ref,
    total_ref,
    dq_ref,
    dkv_ref,
    acc,
    key_acc,
):
    rows = q_ref.shape[1]
    half = pl.program_id(1)
    block, q2, position, doc = attention_query(q_ref, doc_ref, here_ref[0], count, rows)
    total = total_ref[0]
    grad = grad_ref[0].astype(jnp.float32)
    grad2 = jnp.concatenate([grad[:, :HEAD_DIM], grad[:, HEAD_DIM:]], axis=0)
    full2 = jnp.concatenate([full_ref[0, :, :HEAD_DIM], full_ref[0, :, HEAD_DIM:]], axis=0)
    total_grad = -jnp.sum(grad2 * full2, axis=-1, keepdims=True) / total
    sums_grad = (grad2 / total).astype(jnp.bfloat16)
    acc[...] = jnp.zeros_like(acc)

    @pl.when(half == 0)
    def _():
        def clear(i, carry):
            key_acc[i] = jnp.zeros(key_acc.shape[1:], jnp.float32)
            return carry

        lax.fori_loop(0, key_acc.shape[0], clear, 0)

    def one(key_block, carry):
        key_half = (key_block >= count).astype(jnp.int32)
        inner = key_block - key_half * count
        kv = kv_ref.at[inner, key_half]
        keys = kv[:, :HEAD_DIM]
        capped, weights = attention_scores(
            q2, keys, position, doc, key_block, key_doc_ref[0, key_block], rows
        )
        exp_grad = lax.dot_general(
            sums_grad, kv[:, HEAD_DIM:], (((1,), (1,)), ((), ())), preferred_element_type=jnp.float32
        )
        raw_grad = (
            weights * (exp_grad + total_grad) * (1.0 - capped * capped) * SCORE_SCALE
        ).astype(jnp.bfloat16)
        acc[...] += jnp.dot(raw_grad, keys, preferred_element_type=jnp.float32)
        over_rows = (((0,), (0,)), ((), ()))
        slot = inner * 2 + key_half
        key_acc[slot, :, :HEAD_DIM] += lax.dot_general(
            raw_grad, q2, over_rows, preferred_element_type=jnp.float32
        )
        key_acc[slot, :, HEAD_DIM:] += lax.dot_general(
            weights.astype(jnp.bfloat16), sums_grad, over_rows, preferred_element_type=jnp.float32
        )
        return carry

    lax.fori_loop(jnp.maximum(block - count, 0), block + 1, one, 0)
    dq = acc[...]
    dq_ref[0] = jnp.concatenate([dq[:rows], dq[rows:]], axis=1).astype(jnp.bfloat16)

    @pl.when(half == 1)
    def _():
        def put(i, carry):
            for k in (0, 1):
                dkv_ref[i, k] = key_acc[i * 2 + k].astype(jnp.bfloat16)
            return carry

        lax.fori_loop(0, count, put, 0)


def attention_specs(count, rows, width):
    query = pl.BlockSpec((1, rows, width), lambda s, h, here: (2 * s + h, 0, 0))
    keys = pl.BlockSpec((count, 2, rows, 2 * HEAD_DIM), lambda s, h, here: (0, s, 0, 0))
    doc = pl.BlockSpec((1, rows, 1), lambda s, h, here: (2 * s + h, 0, 0))
    key_doc = pl.BlockSpec((1, 2 * count, 1, rows), lambda s, h, here: (s, 0, 0, 0))
    total = pl.BlockSpec((1, REPS * rows, 1), lambda s, h, here: (2 * s + h, 0, 0))
    return query, keys, doc, key_doc, total


def attention_forward(here, q, kv, doc, key_doc):
    count, _, rows, _ = kv.shape
    width = REPS * HEAD_DIM
    query, keys, doc_spec, key_doc_spec, total = attention_specs(count, rows, width)
    return pl.pallas_call(
        functools.partial(attention_forward_kernel, count),
        name="attend",
        grid_spec=pltpu.PrefetchScalarGridSpec(
            num_scalar_prefetch=1,
            grid=(2, 2),
            in_specs=[query, keys, doc_spec, key_doc_spec],
            out_specs=[query, query, total],
            scratch_shapes=[
                pltpu.VMEM((REPS * rows, HEAD_DIM), jnp.float32),
                pltpu.VMEM((REPS * rows, 1), jnp.float32),
            ],
        ),
        out_shape=[
            shape((GROUPS, rows, width), jnp.bfloat16),
            shape((GROUPS, rows, width), jnp.float32),
            shape((GROUPS, REPS * rows, 1), jnp.float32),
        ],
        compiler_params=pltpu.CompilerParams(vmem_limit_bytes=VMEM_LIMIT),
        cost_estimate=pl.CostEstimate(flops=10**9, bytes_accessed=40 * 2**20, transcendentals=0),
    )(here, q, kv, doc, key_doc)


def attention_backward(here, q, kv, doc, key_doc, grad, full, totals):
    count, _, rows, _ = kv.shape
    width = REPS * HEAD_DIM
    query, keys, doc_spec, key_doc_spec, total = attention_specs(count, rows, width)
    return pl.pallas_call(
        functools.partial(attention_backward_kernel, count),
        name="attend_back",
        grid_spec=pltpu.PrefetchScalarGridSpec(
            num_scalar_prefetch=1,
            grid=(2, 2),
            in_specs=[query, keys, doc_spec, key_doc_spec, query, query, total],
            out_specs=[query, keys],
            scratch_shapes=[
                pltpu.VMEM((REPS * rows, HEAD_DIM), jnp.float32),
                pltpu.VMEM((2 * count, rows, 2 * HEAD_DIM), jnp.float32),
            ],
        ),
        out_shape=[shape((GROUPS, rows, width), jnp.bfloat16), shape(kv.shape, jnp.bfloat16)],
        compiler_params=pltpu.CompilerParams(vmem_limit_bytes=VMEM_LIMIT),
        cost_estimate=pl.CostEstimate(flops=2 * 10**9, bytes_accessed=80 * 2**20, transcendentals=0),
    )(here, q, kv, doc, key_doc, grad, full, totals)


def rms_scale(values, gain_row):
    return (
        values * lax.rsqrt(jnp.mean(values * values, axis=-1, keepdims=True) + NORM_EPS) * gain_row
    )


def gelu_tanh(values):
    return jax.nn.gelu(values, approximate=True)


def rope_tables(positions):
    half_width = HEAD_DIM // 2
    frequency = jnp.exp(
        jnp.arange(half_width, dtype=jnp.float32) * (-2.0 * math.log(ROPE_BASE) / HEAD_DIM)
    )
    angles = positions.astype(jnp.float32)[:, None] * frequency[None, :]
    cosine = jnp.concatenate([jnp.cos(angles), jnp.cos(angles)], axis=-1)
    sine = jnp.concatenate([jnp.sin(angles), jnp.sin(angles)], axis=-1)
    return cosine[:, None, :], sine[:, None, :]


def rotate(values, cosine, sine):
    half_width = HEAD_DIM // 2
    turned = jnp.concatenate([-values[..., half_width:], values[..., :half_width]], axis=-1)
    return values * cosine + turned * sine


def feed_forward_apart(
    branch_slabs, inputs, cotangent, gains, gate_up_all, down_all, count, piece
):
    rows, width = inputs.shape
    bf16 = jnp.bfloat16
    branch = branch_slabs.reshape(rows, width)
    middle = inputs + rms_scale(branch, gains[1])
    norm_three = rms_scale(middle, gains[2]).astype(bf16)
    gate_all = gate_up_all[:, :width]
    up_all = gate_up_all[:, width:]
    norm_all = all_gather_blk(norm_three, count, 4).reshape(count * rows, width)
    gate = dot(norm_all, gate_all, LAST)
    up = dot(norm_all, up_all, LAST)
    hidden = (gelu_tanh(gate) * up).astype(bf16)
    ffn_part = dot(hidden, down_all, PLAIN).astype(bf16)
    ffn_out = reduce_scatter_blk(ffn_part.reshape((count,) + piece), count, 5).reshape(rows, width)
    output = (middle + rms_scale(ffn_out, gains[3])).astype(bf16)[None]

    out_cotangent = cotangent[0].astype(jnp.float32)
    _, post_ffn_back = jax.vjp(rms_scale, ffn_out, gains[3])
    ffn_grad, gain_grad_four = post_ffn_back(out_cotangent)
    grad_all = all_gather_blk(ffn_grad.astype(bf16), count, 6).reshape(count * rows, width)
    activated, gelu_back = jax.vjp(gelu_tanh, gate)
    hidden_grad = dot(grad_all, down_all, LAST)
    gate_grad = gelu_back(hidden_grad * up)[0].astype(bf16)
    up_grad = (hidden_grad * activated).astype(bf16)
    norm_part = dot(gate_grad, gate_all, PLAIN) + dot(up_grad, up_all, PLAIN)
    norm_three_grad = reduce_scatter_blk(
        norm_part.astype(bf16).reshape((count,) + piece), count, 7
    ).reshape(rows, width)
    down_part = dot(hidden, grad_all, FIRST).astype(bf16)
    gate_up_part = jnp.concatenate(
        [dot(gate_grad, norm_all, FIRST), dot(up_grad, norm_all, FIRST)], axis=1
    ).astype(bf16)
    _, pre_ffn_back = jax.vjp(rms_scale, middle, gains[2])
    middle_part, gain_grad_three = pre_ffn_back(norm_three_grad)
    middle_grad = out_cotangent + middle_part
    _, post_attn_back = jax.vjp(rms_scale, branch, gains[1])
    branch_grad, gain_grad_two = post_attn_back(middle_grad)
    return (
        output,
        middle_grad,
        branch_grad.astype(bf16),
        gain_grad_two,
        gain_grad_three,
        gain_grad_four,
        gate_up_part,
        down_part,
    )


def shards(
    tokens, cotangent, segments, norm_gains, qkv_weight, out_weight, gate_up_weight, down_weight
):
    _, rows, width = tokens.shape
    count = lax.axis_size("blk")
    here = lax.axis_index("blk")
    mine = 2 * lax.axis_index("dp") + lax.axis_index("head")
    group_rows = GROUPS * rows
    head_width = REPS * HEAD_DIM
    bf16 = jnp.bfloat16
    slab = slabs(rows)
    piece = (rows // slab, slab, width)

    gain_rows = norm_gains.shape[0]
    gain_lanes = -(-gain_rows // 128) * 128
    gains_sent = jnp.pad(
        jnp.transpose(norm_gains).astype(jnp.float32), ((0, 4), (0, gain_lanes - gain_rows))
    )
    out_rows = out_weight.shape[0]
    out_sent = jnp.transpose(out_weight.reshape(out_rows, GROUPS, head_width), (1, 0, 2))
    qkv_rows = qkv_weight.shape[0]
    qkv_slab = slabs(qkv_rows)
    qkv_piece = (qkv_rows // qkv_slab, qkv_slab, width)
    qkv_all, out_mine, tokens_all, gains_all, docs_all, down_all = gather_first(
        qkv_weight,
        out_sent,
        tokens[0],
        gains_sent,
        segments.reshape(-1, 128),
        down_weight,
        count,
        1,
    )
    down_all = down_all.reshape(-1, width)
    gains = jnp.transpose(gains_all[:, :, :4, :gain_rows], (2, 0, 1, 3)).reshape(4, width)
    qkv_head = qkv_all.reshape(count * qkv_rows, width)
    docs = docs_all.reshape(2, 2, count, rows)
    key_doc = docs.reshape(2, 2 * count, 1, rows)
    own_doc = lax.dynamic_index_in_dim(docs, here, 2, keepdims=False).reshape(GROUPS, rows, 1)
    here_one = here.reshape(1)

    group_tokens = tokens_all.reshape(group_rows, width).astype(jnp.float32)
    norm_one = rms_scale(group_tokens, gains[0]).astype(bf16)
    proj = dot(norm_one, qkv_head, LAST)
    inside = jnp.arange(rows, dtype=jnp.int32)
    position = jnp.concatenate([here * rows + inside, (count + here) * rows + inside])
    cosine, sine = rope_tables(jnp.concatenate([position, position]))
    proj = proj.reshape(group_rows, REPS + 2, HEAD_DIM)
    turned = rotate(proj[:, : REPS + 1], cosine, sine)
    sent = jnp.concatenate([turned, proj[:, REPS + 1 :]], axis=1).astype(bf16)
    queries = sent[:, :REPS].reshape(GROUPS, rows, head_width)
    own_kv = sent[:, REPS:].reshape(group_rows, 2 * HEAD_DIM)
    kv_slab = slabs(group_rows)
    kv_piece = (group_rows // kv_slab, kv_slab, 2 * HEAD_DIM)
    kv, out_all, gate_up_all = gather_second(own_kv, out_mine, gate_up_weight, count, 2)
    gate_up_all = gate_up_all.reshape(-1, 2 * width)
    kv = kv.reshape(count, GROUPS, rows, 2 * HEAD_DIM)
    out_head = out_all.reshape(width, head_width)
    attn, attended, totals = attention_forward(here_one, queries, kv, own_doc, key_doc)
    attn = attn.reshape(group_rows, head_width)
    branch_part = dot(attn, out_head, LAST).astype(bf16)
    branch_slabs = reduce_scatter_group(branch_part.reshape((GROUPS,) + piece), 3)
    inputs = tokens[0].astype(jnp.float32)
    if feed_forward_fits(count, rows, width, down_all.shape[0]):
        output, middle_grad, branch_grad, gain_rest, gate_up_part, down_part = feed_forward(
            branch_slabs,
            tokens.reshape(piece),
            cotangent.reshape(piece),
            gains,
            gate_up_all,
            down_all,
            count,
            4,
        )
        output = output.reshape(tokens.shape)
        middle_grad = middle_grad.reshape(rows, width)
        branch_grad = branch_grad.reshape(rows, width)
        gain_grad_two, gain_grad_three, gain_grad_four = gain_rest[1], gain_rest[2], gain_rest[3]
    else:
        (
            output,
            middle_grad,
            branch_grad,
            gain_grad_two,
            gain_grad_three,
            gain_grad_four,
            gate_up_part,
            down_part,
        ) = feed_forward_apart(
            branch_slabs, inputs, cotangent, gains, gate_up_all, down_all, count, piece
        )
    branch_all = all_gather_group(branch_grad, 8).reshape(group_rows, width)
    attn_grad = dot(branch_all, out_head, PLAIN).astype(bf16).reshape(GROUPS, rows, head_width)
    out_part = dot(branch_all, attn, FIRST).astype(bf16)
    out_part = out_part.reshape(GROUPS, count, out_rows, head_width)
    dq, dkv_part = attention_backward(
        here_one, queries, kv, own_doc, key_doc, attn_grad, attended, totals
    )
    dkv, out_sum, gate_up_grad = reduce_middle(
        dkv_part.reshape((count,) + kv_piece),
        out_part,
        gate_up_part.reshape((GROUPS,) + gate_up_weight.shape),
        count,
        9,
    )
    sent_grad = jnp.concatenate(
        [
            dq.reshape(group_rows, REPS, HEAD_DIM),
            dkv.reshape(group_rows, 2, HEAD_DIM),
        ],
        axis=1,
    ).astype(jnp.float32)
    unturned = rotate(sent_grad[:, : REPS + 1], cosine, -sine)
    proj_grad = (
        jnp.concatenate([unturned, sent_grad[:, REPS + 1 :]], axis=1)
        .astype(bf16)
        .reshape(group_rows, (REPS + 2) * HEAD_DIM)
    )
    qkv_part = dot(proj_grad, norm_one, FIRST).astype(bf16)
    norm_one_part = dot(proj_grad, qkv_head, PLAIN)
    _, gain_back = jax.vjp(lambda gain: rms_scale(group_tokens, gain), gains[0])
    (gain_grad_one,) = gain_back(norm_one_part)
    gain_part = jnp.stack([gain_grad_one, gain_grad_two, gain_grad_three, gain_grad_four])
    gain_part = jnp.transpose(gain_part.reshape(4, GROUPS, count, gain_rows), (2, 1, 0, 3))
    gain_part = jnp.pad(gain_part, ((0, 0), (0, 0), (0, 4), (0, gain_lanes - gain_rows)))
    qkv_grad, norm_one_grad, gain_grad, out_grad, down_grad = reduce_last(
        qkv_part.reshape((count,) + qkv_piece),
        norm_one_part.astype(bf16).reshape((GROUPS,) + piece),
        gain_part[:, :, None],
        out_sum,
        down_part.reshape((GROUPS,) + down_weight.shape),
        count,
        10,
    )
    qkv_grad = qkv_grad.reshape(qkv_rows, width)
    out_grad = (
        jnp.transpose(out_grad, (1, 0, 2)).reshape(out_rows, GROUPS * head_width).astype(jnp.float32)
    )
    gain_grad = jnp.transpose(gain_grad.reshape(8, gain_lanes)[:4, :gain_rows])
    _, pre_attn_back = jax.vjp(lambda values: rms_scale(values, gains[0]), inputs)
    (input_part,) = pre_attn_back(norm_one_grad.reshape(rows, width))
    tokens_grad = (middle_grad + input_part).astype(bf16)[None]
    return (output, tokens_grad, gain_grad, qkv_grad, out_grad, gate_up_grad, down_grad)


def solution(mesh):
    whole = ("dp", "head", "blk")
    return jax.shard_map(
        shards,
        mesh=mesh,
        in_specs=(
            P("dp", ("head", "blk"), None),
            P("dp", ("head", "blk"), None),
            P("dp", None),
            P(whole, None),
            P(whole, None),
            P(whole, None),
            P(whole, None),
            P(whole, None),
        ),
        out_specs=(
            P("dp", ("head", "blk"), None),
            P("dp", ("head", "blk"), None),
            P(whole, None),
            P(whole, None),
            P(whole, None),
            P(whole, None),
            P(whole, None),
        ),
        check_vma=False,
    )
```

```python
import functools
import math

import jax
import jax.numpy as jnp
from jax import lax
from jax.experimental import pallas as pl
from jax.experimental.pallas import tpu as pltpu
from jax.sharding import PartitionSpec as P

HEADS = 8
KV_HEADS = 4
HEAD_DIM = 256
REPS = HEADS // KV_HEADS
GROUPS = 4
SOFT_CAP = 50.0
NORM_EPS = 1e-06
ROPE_BASE = 10000.0
SCORE_SCALE = HEAD_DIM ** (-0.5)

MESH = pl.DeviceIdType.MESH
VMEM_LIMIT = 60 * 1024 * 1024


class Place:
    def __init__(self, count):
        self.count = count
        self.inner = 4 if count >= 32 else 2
        self.outer = count // self.inner
        self.here = lax.axis_index("blk")
        self.line = self.here // self.inner
        self.side = lax.rem(self.here, self.inner)
        self.core = lax.axis_index("dp")
        self.half = lax.axis_index("head")
        self.group = 2 * self.core + self.half

    def near(self, k):
        orders = [near_order(self.outer, line)[k] for line in range(self.outer)]
        found = jnp.int32(orders[0])
        for line in range(1, self.outer):
            found = jnp.where(self.line == line, jnp.int32(orders[line]), found)
        return found

    def at(self, line, side):
        return {"blk": line * self.inner + side}

    def beside(self, step):
        return lax.rem(self.side + step, self.inner)

    def partner(self):
        return {"dp": 1 - self.core}

    def across(self):
        return {"head": 1 - self.half}

    def corner(self):
        return {"dp": 1 - self.core, "head": 1 - self.half}


def remote(src, dst, sent, came, device):
    return pltpu.make_async_remote_copy(
        src_ref=src, dst_ref=dst, send_sem=sent, recv_sem=came, device_id=device, device_id_type=MESH
    )


def greet(place, blk=False, core=False, half=False, corner=False):
    sem = pltpu.get_barrier_semaphore()
    amount = jnp.int32(0)

    def hello(device):
        pl.semaphore_signal(sem, inc=1, device_id=device, device_id_type=MESH)

    if blk:
        up, down = place.line < place.outer - 1, place.line > 0
        pl.when(up)(lambda: hello(place.at(place.line + 1, place.side)))
        pl.when(down)(lambda: hello(place.at(place.line - 1, place.side)))
        amount = amount + up.astype(jnp.int32) + down.astype(jnp.int32) + (place.inner - 1)
        for step in range(1, place.inner):
            hello(place.at(place.line, place.beside(step)))
    for wanted, device in (
        (core, place.partner()),
        (half, place.across()),
        (corner, place.corner()),
    ):
        if wanted:
            hello(device)
            amount = amount + 1
    pl.semaphore_wait(sem, amount)


def together(*tasks):
    tasks = list(tasks)
    while tasks:
        for task in list(tasks):
            try:
                next(task)
            except StopIteration:
                tasks.remove(task)


def waiting(task, *rounds):
    for step, _ in enumerate(task):
        yield
        if step < len(rounds):
            for _ in range(rounds[step]):
                yield


def near_order(outer, line):
    ends = outer == 4
    return sorted(
        range(outer),
        key=lambda other: (abs(other - line), ends and other not in (0, outer - 1), other),
    )


def evened(place, parts):
    return parts == 2 and place.inner == 2 and place.outer == 4


def part_of(ref, h, parts):
    if parts == 1:
        return ref
    size = ref.shape[0] // parts
    return ref.at[pl.ds(h * size, size)]


def gather_blk_sems(place_count, parts=2):
    inner = 4 if place_count >= 32 else 2
    return [
        pltpu.SemaphoreType.DMA((2 + inner, place_count, parts)),
        pltpu.SemaphoreType.DMA((place_count, parts)),
        pltpu.SemaphoreType.DMA,
    ]


class GatherBlk:
    def __init__(self, place, src, view, sent, came, own):
        self.place, self.src, self.view, self.sent, self.came = place, src, view, sent, came
        self.parts = came.shape[1]
        self.evened = evened(place, self.parts)
        self.middle = (place.line > 0) & (place.line < place.outer - 1)
        self.copy = pltpu.make_async_copy(src, view(place.here), own)

    def sends(self, k, h):
        place = self.place
        there = place.near(k)
        piece = there * place.inner + place.side
        there_view = part_of(self.view(piece), h, self.parts)
        src = part_of(self.src, h, self.parts) if k == 0 else there_view

        def send(kind, device):
            return remote(
                src, there_view, self.sent.at[kind, piece, h], self.came.at[piece, h], device
            )

        line, side = place.line, place.side
        up = (there <= line) & (line < place.outer - 1)
        down = (there >= line) & (line > 0)
        aside = range(1, place.inner)
        if self.evened and h == 1 and k == place.outer - 1:
            aside = ()
        return (
            [
                (up, lambda: send(0, place.at(line + 1, side))),
                (down, lambda: send(1, place.at(line - 1, side))),
            ],
            [send(1 + step, place.at(line, place.beside(step))) for step in aside],
        )

    def forward(self, k, h):
        along, aside = self.sends(k, h)
        for needed, make in along:
            pl.when(needed)(lambda make=make: make().start())
        for one in aside:
            one.start()

    def start(self):
        self.copy.start()
        for h in range(self.parts):
            self.forward(0, h)

    def arrived(self, piece, h):
        place = self.place
        remote(
            part_of(self.src, h, self.parts),
            part_of(self.view(piece), h, self.parts),
            self.sent.at[0, piece, h],
            self.came.at[piece, h],
            place.at(place.line, place.beside(1)),
        ).wait_recv()

    def pass_on(self, k):
        for h in range(self.parts):
            self.arrived(self.place.near(k) * self.place.inner + self.place.side, h)
            self.forward(k, h)

    def extra(self, k):
        place = self.place
        piece = place.near(k) * place.inner + place.beside(1)
        to = place.near(2 if k == 1 else 1)
        half = part_of(self.view(piece), 1, 2)
        return remote(
            half,
            half,
            self.sent.at[place.inner + 1, piece, 1],
            self.came.at[piece, 1],
            place.at(to, place.side),
        )

    def pass_extra(self, k):
        if self.evened:

            @pl.when(self.middle)
            def _():
                self.arrived(self.place.near(k) * self.place.inner + self.place.beside(1), 1)
                self.extra(k).start()

    def beside_arrived(self, k):
        for step in range(1, self.place.inner):
            piece = self.place.near(k) * self.place.inner + self.place.beside(step)
            for h in range(self.parts):
                if self.evened and h == 1 and k in (1, self.place.outer - 1):
                    pl.when(jnp.logical_not(self.middle))(lambda: self.arrived(piece, 1))
                else:
                    self.arrived(piece, h)

    def finish(self):
        for k in range(self.place.outer):
            for h in range(self.parts):
                along, aside = self.sends(k, h)
                for needed, make in along:
                    pl.when(needed)(lambda make=make: make().wait_send())
                for one in aside:
                    one.wait_send()
        if self.evened:

            @pl.when(self.middle)
            def _():
                self.extra(1).wait_send()
                self.extra(self.place.outer - 1).wait_send()


def gather_blk(place, src, view, sent, came, own):
    if not callable(view):
        out = view
        view = lambda piece: out.at[piece]
    work = GatherBlk(place, src, view, sent, came, own)
    work.start()
    yield
    for k in range(1, place.outer):
        work.pass_on(k)
        if k == place.outer - 2:
            work.pass_extra(1)
        yield
    work.pass_extra(place.outer - 1)
    yield
    for k in range(place.outer):
        work.beside_arrived(k)
    work.finish()
    work.copy.wait()


def add_into(out, *terms):
    def one(i, carry):
        total = terms[0][i].astype(jnp.float32)
        for term in terms[1:]:
            total = total + term[i].astype(jnp.float32)
        out[i] = total.astype(out.dtype)
        return carry

    lax.fori_loop(0, out.shape[0], one, 0)


def reduce_blk_scratch(place_count, piece, dtype, parts=2):
    inner = 4 if place_count >= 32 else 2
    outer = place_count // inner
    half = (piece[0] // 2,) + tuple(piece[1:]) if parts == 2 and inner == 2 and outer == 4 else (1, 8, 128)
    return [
        pltpu.VMEM((outer, inner - 1) + piece, dtype),
        pltpu.VMEM((outer + 1,) + piece, dtype),
        pltpu.VMEM((outer,) + piece, dtype),
        pltpu.VMEM((4,) + half, dtype),
        pltpu.SemaphoreType.DMA((outer, inner - 1, parts)),
        pltpu.SemaphoreType.DMA((outer, inner - 1, parts)),
        pltpu.SemaphoreType.DMA((outer, parts)),
        pltpu.SemaphoreType.DMA((outer + 1, parts)),
        pltpu.SemaphoreType.DMA((2,)),
        pltpu.SemaphoreType.DMA((2,)),
    ]


REDUCE_REFS = 10


class ReduceBlk:
    def __init__(
        self,
        place,
        view,
        out,
        beside,
        along,
        held,
        spare,
        side_sent,
        side_came,
        line_sent,
        line_came,
        spare_sent,
        spare_came,
    ):
        self.place, self.view, self.out = place, view, out
        self.beside, self.along, self.held, self.spare = beside, along, held, spare
        self.side_sems, self.line_sems = (side_sent, side_came), (line_sent, line_came)
        self.spare_sems = (spare_sent, spare_came)
        self.parts = line_sent.shape[1]
        self.evened = evened(place, self.parts)
        self.middle = (place.line > 0) & (place.line < place.outer - 1)

    def part(self, ref, h):
        return part_of(ref, h, self.parts)

    def far(self, k):
        return self.place.near(self.place.outer - 1 - k)

    def alone(self, k, h):
        return self.evened and k == 0 and h == 1

    def side_copy(self, there, step, h, src=None):
        place = self.place
        to = place.beside(step)
        if src is None:
            src = self.part(self.view(there * place.inner + to), h)
        return remote(
            src,
            self.part(self.beside.at[there, place.inner - step - 1], h),
            self.side_sems[0].at[there, step - 1, h],
            self.side_sems[1].at[there, place.inner - step - 1, h],
            place.at(place.line, to),
        )

    def line_copy(self, there, slot, to, h, src=None):
        return remote(
            self.part(self.held.at[there], h) if src is None else src,
            self.part(self.along.at[slot], h),
            self.line_sems[0].at[there, h],
            self.line_sems[1].at[slot, h],
            self.place.at(to, self.place.side),
        )

    def send(self, k, h):
        for step in range(1, self.place.inner):
            self.side_copy(self.far(k), step, h).start()

    def terms(self, k, h):
        place = self.place
        there = self.far(k)
        own = [self.part(self.view(there * place.inner + place.side), h)]
        if self.alone(k, h):
            return own
        for step in range(1, place.inner):
            self.side_copy(there, step, h).wait_recv()
        return own + [self.part(self.beside.at[there, j], h) for j in range(place.inner - 1)]

    def onward(self, there, h, src=None):
        line, outer = self.place.line, self.place.outer
        to = jnp.where(there < line, line - 1, line + 1)
        slot = jnp.where(there == line + 1, outer, there)
        return self.line_copy(there, slot, to, h, src)

    def starts(self, there):
        line, outer = self.place.line, self.place.outer
        return ((there < line) & (line == outer - 1)) | ((there > line) & (line == 0))

    def pass_on(self, k, h):
        place = self.place
        line = place.line
        there = self.far(k)
        terms = self.terms(k, h)
        held = self.part(self.held.at[there], h)
        starts = self.starts(there)

        @pl.when(starts)
        def _():
            add_into(held, *terms)

        @pl.when(jnp.logical_not(starts))
        def _():
            back = jnp.where(there < line, line + 1, line - 1)
            self.line_copy(there, there, back, h).wait_recv()
            add_into(held, self.part(self.along.at[there], h), *terms)

        self.onward(there, h).start()

    def last(self, h):
        place = self.place
        line, outer = place.line, place.outer
        terms = self.terms(outer - 1, h)
        below, above = line > 0, line < outer - 1
        from_above = self.part(self.along.at[line], h)
        from_below = self.part(self.along.at[outer], h)
        out = self.part(self.out, h)

        @pl.when(above)
        def _():
            self.line_copy(line, line, line + 1, h).wait_recv()

        @pl.when(below)
        def _():
            self.line_copy(line, outer, line - 1, h).wait_recv()

        @pl.when(above & below)
        def _():
            add_into(out, from_above, from_below, *terms)

        @pl.when(above & jnp.logical_not(below))
        def _():
            add_into(out, from_above, *terms)

        @pl.when(jnp.logical_not(above) & below)
        def _():
            add_into(out, from_below, *terms)


    def spare_view(self, k):
        place = self.place
        return self.part(self.view(place.near(k) * place.inner + place.beside(1)), 1)

    def spare_first(self):
        return remote(
            self.spare_view(3),
            self.spare.at[0],
            self.spare_sems[0].at[0],
            self.spare_sems[1].at[0],
            self.place.at(self.place.near(1), self.place.side),
        )

    def spare_second(self):
        return remote(
            self.spare.at[2],
            self.spare.at[1],
            self.spare_sems[0].at[1],
            self.spare_sems[1].at[1],
            self.place.at(self.place.near(2), self.place.side),
        )

    def spare_side(self):
        return self.side_copy(self.far(2), 1, 1, self.spare.at[3])

    def opening(self):
        outer = self.place.outer
        if not self.evened:

            def every():
                for k in range(outer):
                    for h in range(self.parts):
                        self.send(k, h)

            return [every]
        ends = jnp.logical_not(self.middle)

        def along():
            self.spare_first().start()
            there = self.far(0)
            self.onward(
                there, 1, self.part(self.view(there * self.place.inner + self.place.side), 1)
            ).start()

        todo = [lambda: self.send(0, 0), lambda: pl.when(ends)(along)]
        todo += [lambda k=k, h=h: self.send(k, h) for k, h in ((1, 0), (1, 1), (2, 0))]
        todo += [
            lambda k=k, h=h: pl.when(ends)(lambda: self.send(k, h))
            for k, h in ((2, 1), (3, 0), (3, 1))
        ]
        return todo

    def start(self):
        for step in self.opening():
            step()

    def turning(self):
        def first():
            self.spare_first().wait_recv()
            add_into(self.spare.at[2], self.spare.at[0], self.spare_view(3))
            self.spare_second().start()

        def second():
            self.spare_second().wait_recv()
            add_into(self.spare.at[3], self.spare.at[1], self.spare_view(1))
            self.spare_side().start()
            for h in (0, 1):
                self.send(3, h)

        steps = (first, lambda: self.pass_on(0, 1), second)
        return [lambda step=step: pl.when(self.middle)(step) for step in steps]

    def events(self):
        outer, parts = self.place.outer, self.parts
        if self.evened:
            todo = self.turning() + [lambda: self.pass_on(0, 0)]
        else:
            todo = [lambda h=h: self.pass_on(0, h) for h in range(parts)]
        for k in range(1, outer - 1):
            for h in range(parts):
                todo.append(lambda k=k, h=h: self.pass_on(k, h))
        for h in range(parts):
            todo.append(lambda h=h: self.last(h))
        return todo

    def finish(self):
        for k in range(self.place.outer):
            for h in range(self.parts):
                if k < self.place.outer - 1:
                    self.onward(self.far(k), h).wait_send()
                if not self.alone(k, h):
                    for step in range(1, self.place.inner):
                        self.side_copy(self.far(k), step, h).wait_send()
        if self.evened:

            @pl.when(self.middle)
            def _():
                self.spare_second().wait_send()

            @pl.when(jnp.logical_not(self.middle))
            def _():
                self.spare_first().wait_send()


def reduce_blk(place, view, out, *scratch):
    if not callable(view):
        part = view
        view = lambda piece: part.at[piece]
    work = ReduceBlk(place, view, out, *scratch)
    for step in work.opening() + work.events():
        step()
        yield
    work.finish()


def gather_group_sems():
    return [pltpu.SemaphoreType.DMA((3,)), pltpu.SemaphoreType.DMA((4,)), pltpu.SemaphoreType.DMA]


def gather_group(place, src, view, sent, came, own, through=None):
    if not callable(view):
        out = view
        view = lambda g: out.at[g]
    copy = pltpu.make_async_copy(src if through is None else through, view(place.group), own)
    load = None if through is None else pltpu.make_async_copy(src, through, own)
    mine, other = place.group, 2 * place.core + (1 - place.half)
    to_half = remote(src, view(mine), sent.at[0], came.at[mine], place.across())
    to_core = remote(src, view(mine), sent.at[1], came.at[mine], place.partner())
    to_half.start()
    to_core.start()
    (load or copy).start()
    yield
    if load:
        load.wait()
        copy.start()
    remote(src, view(other), sent.at[0], came.at[other], place.across()).wait_recv()
    relay = remote(view(other), view(other), sent.at[2], came.at[other], place.partner())
    relay.start()
    yield
    for half in (0, 1):
        slot = 2 * (1 - place.core) + half
        remote(src, view(slot), sent.at[0], came.at[slot], place.partner()).wait_recv()
    to_half.wait_send()
    to_core.wait_send()
    relay.wait_send()
    copy.wait()


def share_rows(ref, parts, p):
    rows = ref.shape[0] // parts
    return ref.at[pl.ds(p * rows, rows)]


def gather_group_rows(place, src, out, parts, take):
    def task(p, refs):
        rows = src.shape[0] // parts
        view = lambda g: out.at[g, pl.ds(p * rows, rows)]
        return gather_group(place, share_rows(src, parts, p), view, *refs)

    return [task(p, take(4)) for p in range(parts)]


def gather_rows_scratch(value, parts):
    through = pltpu.VMEM((value.shape[0] // parts, value.shape[1]), value.dtype)
    return (gather_group_sems() + [through]) * parts


def fold_rows_scratch(piece, parts):
    rows, width = piece[0] // parts, piece[1]
    bf16 = jnp.bfloat16
    one = [
        pltpu.VMEM((2, rows, width), bf16),
        pltpu.VMEM((rows, width), bf16),
        pltpu.VMEM((rows, width), bf16),
        pltpu.VMEM((rows, width), bf16),
        pltpu.VMEM((rows, width), jnp.float32),
        pltpu.SemaphoreType.DMA((3,)),
        pltpu.SemaphoreType.DMA((3,)),
        pltpu.SemaphoreType.DMA((3,)),
    ]
    return one * parts


def add_rows(out, *terms):
    rows = slabs(out.shape[0])

    def one(i, carry):
        at = pl.ds(pl.multiple_of(i * rows, rows), rows)
        total = terms[0][at].astype(jnp.float32)
        for term in terms[1:]:
            total = total + term[at].astype(jnp.float32)
        out[at] = total.astype(out.dtype)
        return carry

    lax.fori_loop(0, out.shape[0] // rows, one, 0)


def fold_rows(place, part, out, parts, take):
    rows = out.shape[0] // parts
    core, half = place.core, place.half
    far, near = 2 * (1 - core) + (1 - half), 2 * (1 - core) + half
    beside = 2 * core + (1 - half)

    def task(p, from_core, from_half, held, mine, total, sent, came, local):
        at = pl.ds(p * rows, rows)
        first = remote(part.at[far, at], from_core.at[1], sent.at[0], came.at[0], place.partner())
        second = remote(part.at[near, at], from_core.at[0], sent.at[1], came.at[1], place.partner())
        third = remote(held, from_half, sent.at[2], came.at[2], place.across())
        load_held = pltpu.make_async_copy(part.at[beside, at], held, local.at[0])
        load_mine = pltpu.make_async_copy(part.at[place.group, at], mine, local.at[1])
        store = pltpu.make_async_copy(total, out.at[at], local.at[2])
        for copy in (first, load_held, second, load_mine):
            copy.start()
        yield
        first.wait_recv()
        load_held.wait()
        add_rows(held, held, from_core.at[1])
        third.start()
        yield
        second.wait_recv()
        load_mine.wait()
        third.wait_recv()
        add_rows(total, mine, from_core.at[0], from_half)
        store.start()
        yield
        for copy in (first, second, third):
            copy.wait_send()
        store.wait()

    return [task(p, *take(8)) for p in range(parts)]


ROW_PARTS = 3


def reduce_group_scratch(piece, dtype):
    return [
        pltpu.VMEM((2,) + piece, dtype),
        pltpu.VMEM(piece, dtype),
        pltpu.VMEM(piece, dtype),
        pltpu.SemaphoreType.DMA((3,)),
        pltpu.SemaphoreType.DMA((3,)),
    ]


def reduce_group(place, part, out, from_core, from_half, held, sent, came):
    far = 2 * (1 - place.core) + (1 - place.half)
    near = 2 * (1 - place.core) + place.half
    first = remote(part.at[far], from_core.at[1], sent.at[0], came.at[0], place.partner())
    second = remote(part.at[near], from_core.at[0], sent.at[1], came.at[1], place.partner())
    first.start()
    second.start()
    yield
    first.wait_recv()
    add_into(held, part.at[2 * place.core + (1 - place.half)], from_core.at[1])
    third = remote(held, from_half, sent.at[2], came.at[2], place.across())
    third.start()
    yield
    second.wait_recv()
    third.wait_recv()
    add_into(out, part.at[place.group], from_core.at[0], from_half)
    first.wait_send()
    second.wait_send()
    third.wait_send()


def exchange_group_sems():
    return [pltpu.SemaphoreType.DMA((3,)), pltpu.SemaphoreType.DMA((4,)), pltpu.SemaphoreType.DMA]


def exchange_group(place, src, out, sent, came, own):
    mine = place.group
    copy = pltpu.make_async_copy(src.at[mine], out.at[mine], own)
    copy.start()
    core, half = place.core, place.half
    links = (
        (2 * (1 - core) + (1 - half), place.corner()),
        (2 * core + (1 - half), place.across()),
        (2 * (1 - core) + half, place.partner()),
    )
    copies = [
        remote(src.at[to], out.at[mine], sent.at[k], came.at[mine], device)
        for k, (to, device) in enumerate(links)
    ]
    for one in copies:
        one.start()
    yield
    for k, (peer, device) in enumerate(links):
        remote(src.at[peer], out.at[peer], sent.at[k], came.at[peer], device).wait_recv()
    for one in copies:
        one.wait_send()
    copy.wait()


def transfer(name, number, body, ins, outs, scratch, moved, out_spaces=None, in_spaces=None):
    spaces = out_spaces or [pl.ANY] * len(outs)
    in_spaces = in_spaces or [pltpu.VMEM] * len(ins)
    return pl.pallas_call(
        body,
        name=name,
        out_shape=outs,
        in_specs=[pl.BlockSpec(memory_space=space) for space in in_spaces],
        out_specs=[pl.BlockSpec(memory_space=space) for space in spaces],
        scratch_shapes=scratch,
        compiler_params=pltpu.CompilerParams(
            collective_id=number, has_side_effects=True, vmem_limit_bytes=VMEM_LIMIT
        ),
        cost_estimate=pl.CostEstimate(flops=0, bytes_accessed=moved * 40, transcendentals=0),
    )(*ins)


def shape(dims, dtype):
    return jax.ShapeDtypeStruct(tuple(dims), dtype)


def slabs(rows):
    return math.gcd(rows, 16)


def all_gather_blk(value, count, number):
    def body(src, out, *sems):
        place = Place(count)
        greet(place, blk=True)
        together(gather_blk(place, src, out, *sems))

    return transfer(
        f"gather{number}",
        number,
        body,
        [value],
        [shape((count,) + value.shape, value.dtype)],
        gather_blk_sems(count),
        value.size * 2 * count,
    )[0]


def reduce_scatter_blk(value, count, number):
    piece = value.shape[1:]

    def body(part, out, *scratch):
        place = Place(count)
        greet(place, blk=True)
        together(reduce_blk(place, part, out, *scratch))

    return transfer(
        f"reduce{number}",
        number,
        body,
        [value],
        [shape(piece, jnp.float32)],
        reduce_blk_scratch(count, piece, value.dtype),
        value.size * 2,
        [pltpu.VMEM],
    )[0]


class Taker:
    def __init__(self, refs):
        self.refs = list(refs)

    def __call__(self, amount):
        taken = self.refs[:amount]
        del self.refs[:amount]
        return taken


def gather_first(qkv, out_parts, tokens, gains, docs, down, count, number):
    names = 6

    def body(*refs):
        qkv_ref, out_ref, tok_ref, gain_ref, doc_ref, down_ref = refs[:names]
        qkv_all, out_mine, tok_all, gain_all, doc_all, down_all = refs[names : 2 * names]
        gain_mine = refs[2 * names]
        take = Taker(refs[2 * names + 1 :])
        place = Place(count)
        greet(place, blk=True, core=True, half=True, corner=True)

        def gain_task(near, far):
            yield from gather_blk(place, gain_ref, gain_mine, *near)
            yield from gather_group(place, gain_mine, gain_all, *far)

        def doc_task(sent, came, own):
            copy = pltpu.make_async_copy(doc_ref, doc_all.at[place.core], own)
            copy.start()
            send = remote(doc_ref, doc_all.at[place.core], sent, came, place.partner())
            send.start()
            yield
            remote(doc_ref, doc_all.at[1 - place.core], sent, came, place.partner()).wait_recv()
            send.wait_send()
            copy.wait()

        together(
            gain_task(take(3), take(3)),
            gather_blk(place, qkv_ref, qkv_all, *take(3)),
            doc_task(*take(3)),
            waiting(gather_group(place, tok_ref, tok_all, *take(3)), 2),
            waiting(exchange_group(place, out_ref, out_mine, *take(3)), 3),
            *(
                waiting(task, 2 + p, 4)
                for p, task in enumerate(
                    gather_group_rows(place, down_ref, down_all, ROW_PARTS, take)
                )
            ),
        )

    ins = [qkv, out_parts, tokens, gains, docs, down]
    return transfer(
        f"first{number}",
        number,
        body,
        ins,
        [
            shape((count,) + qkv.shape, qkv.dtype),
            shape(out_parts.shape, out_parts.dtype),
            shape((GROUPS,) + tokens.shape, tokens.dtype),
            shape((GROUPS, count) + gains.shape, gains.dtype),
            shape((2,) + docs.shape, docs.dtype),
            shape((GROUPS,) + down.shape, down.dtype),
        ],
        [pltpu.VMEM((count,) + gains.shape, gains.dtype)]
        + gather_blk_sems(count, 1)
        + gather_group_sems()
        + gather_blk_sems(count)
        + [pltpu.SemaphoreType.DMA] * 3
        + gather_group_sems()
        + exchange_group_sems()
        + gather_rows_scratch(down, ROW_PARTS),
        (qkv.size + out_parts.size) * 2 * count,
        None,
        [pltpu.VMEM] * 5 + [pl.ANY],
    )


def attend_block(count, g, here, q_ref, kv_ref, doc_ref, key_doc_ref, attn_ref, full_ref, total_ref):
    rows = q_ref.shape[1]
    sequence, half = g // 2, g % 2
    block = half * count + here
    q2, position, doc = stacked_queries(g, block, q_ref, doc_ref)

    def one(key_block, carry):
        total, acc = carry
        key_half = (key_block >= count).astype(jnp.int32)
        at = pl.ds(pl.multiple_of((2 * sequence + key_half) * rows, rows), rows)
        kv = kv_ref.at[key_block - key_half * count, at]
        _, weights = attention_scores(
            q2, kv[:, :HEAD_DIM], position, doc, key_block, key_doc_ref[sequence, key_block], rows
        )
        total = total + jnp.sum(weights, axis=-1, keepdims=True)
        acc = acc + jnp.dot(
            weights.astype(jnp.bfloat16), kv[:, HEAD_DIM:], preferred_element_type=jnp.float32
        )
        return total, acc

    start = (
        jnp.zeros((REPS * rows, 1), jnp.float32),
        jnp.zeros((REPS * rows, HEAD_DIM), jnp.float32),
    )
    total, acc = lax.fori_loop(jnp.maximum(block - count, 0), block + 1, one, start)
    attended = acc / total
    attended = jnp.concatenate([attended[:rows], attended[rows:]], axis=1)
    full_ref[g] = attended
    attn_ref[g] = attended.astype(jnp.bfloat16)
    total_ref[g] = total


def stacked_queries(g, block, q_ref, doc_ref):
    rows = q_ref.shape[1]
    q2 = jnp.concatenate([q_ref[g, :, :HEAD_DIM], q_ref[g, :, HEAD_DIM:]], axis=0)
    inside = lax.broadcasted_iota(jnp.int32, (rows, 1), 0)
    position = block * rows + jnp.concatenate([inside, inside], axis=0)
    doc = jnp.concatenate([doc_ref[g], doc_ref[g]], axis=0)
    return q2, position, doc


def gather_attend(kv, out_mine, gate_up, queries, doc, key_doc, count, number):
    def body(*refs):
        kv_ref, out_ref, gate_up_ref, q_ref, doc_ref, key_doc_ref = refs[:6]
        kv_all, out_all, gate_up_all, attn_ref, full_ref, total_ref = refs[6:12]
        take = Taker(refs[12:])
        place = Place(count)
        greet(place, blk=True, core=True, half=True)
        gathers = (
            GatherBlk(place, kv_ref, lambda i: kv_all.at[i], *take(3)),
            GatherBlk(place, out_ref, lambda i: out_all.at[:, i], *take(3)),
        )
        groups = gather_group_rows(place, gate_up_ref, gate_up_all, ROW_PARTS, take)
        for gather in gathers:
            gather.start()
        for task in groups:
            next(task)
        for k in range(1, place.outer):
            for gather in gathers:
                gather.pass_on(k)
            if k == place.outer - 2:
                for gather in gathers:
                    gather.pass_extra(1)
                next(groups[0])
        for gather in gathers:
            gather.pass_extra(place.outer - 1)
        next(groups[1])
        gathers[0].copy.wait()
        for k in range(place.outer):
            gathers[0].beside_arrived(k)

        def attend(g, carry):
            attend_block(
                count,
                g,
                place.here,
                q_ref,
                kv_all,
                doc_ref,
                key_doc_ref,
                attn_ref,
                full_ref,
                total_ref,
            )
            return carry

        lax.fori_loop(0, GROUPS, attend, 0)
        next(groups[2])
        gathers[1].copy.wait()
        for k in range(place.outer):
            gathers[1].beside_arrived(k)
        for gather in gathers:
            gather.finish()
        together(*groups)

    groups, out_rows, width = out_mine.shape
    rows = queries.shape[1]
    return transfer(
        f"attend{number}",
        number,
        body,
        [kv, out_mine, gate_up, queries, doc, key_doc],
        [
            shape((count,) + kv.shape, kv.dtype),
            shape((groups, count, out_rows, width), out_mine.dtype),
            shape((GROUPS,) + gate_up.shape, gate_up.dtype),
            shape((GROUPS, rows, width), jnp.bfloat16),
            shape((GROUPS, rows, width), jnp.float32),
            shape((GROUPS, REPS * rows, 1), jnp.float32),
        ],
        gather_blk_sems(count) + gather_blk_sems(count) + gather_rows_scratch(gate_up, ROW_PARTS),
        (kv.size + out_mine.size) * 2 * count,
        [pltpu.VMEM, pl.ANY, pl.ANY, pltpu.VMEM, pltpu.VMEM, pltpu.VMEM],
        [pltpu.VMEM, pltpu.VMEM, pl.ANY, pltpu.VMEM, pltpu.VMEM, pltpu.VMEM],
    )


def attend_back_block(
    count, g, here, q_ref, kv_ref, doc_ref, key_doc_ref, grad_ref, full_ref, total_ref, dq_ref, key_acc
):
    rows = q_ref.shape[1]
    sequence, half = g // 2, g % 2
    block = half * count + here
    q2, position, doc = stacked_queries(g, block, q_ref, doc_ref)
    total = total_ref[g]
    grad = grad_ref[g].astype(jnp.float32)
    grad2 = jnp.concatenate([grad[:, :HEAD_DIM], grad[:, HEAD_DIM:]], axis=0)
    full2 = jnp.concatenate([full_ref[g, :, :HEAD_DIM], full_ref[g, :, HEAD_DIM:]], axis=0)
    total_grad = -jnp.sum(grad2 * full2, axis=-1, keepdims=True) / total
    sums_grad = (grad2 / total).astype(jnp.bfloat16)

    def one(key_block, acc):
        key_half = (key_block >= count).astype(jnp.int32)
        inner = key_block - key_half * count
        at = pl.ds(pl.multiple_of((2 * sequence + key_half) * rows, rows), rows)
        kv = kv_ref.at[inner, at]
        keys = kv[:, :HEAD_DIM]
        capped, weights = attention_scores(
            q2, keys, position, doc, key_block, key_doc_ref[sequence, key_block], rows
        )
        exp_grad = dot(sums_grad, kv[:, HEAD_DIM:], LAST)
        raw_grad = (
            weights * (exp_grad + total_grad) * (1.0 - capped * capped) * SCORE_SCALE
        ).astype(jnp.bfloat16)
        slot = inner * 2 + key_half
        key_acc[slot, :, :HEAD_DIM] += dot(raw_grad, q2, FIRST)
        key_acc[slot, :, HEAD_DIM:] += dot(weights.astype(jnp.bfloat16), sums_grad, FIRST)
        return acc + dot(raw_grad, keys, PLAIN)

    dq = lax.fori_loop(
        jnp.maximum(block - count, 0),
        block + 1,
        one,
        jnp.zeros((REPS * rows, HEAD_DIM), jnp.float32),
    )
    dq_ref[g] = jnp.concatenate([dq[:rows], dq[rows:]], axis=1).astype(jnp.bfloat16)


def attend_back_fits(count):
    return count == 8


def attend_back_reduce(
    queries, kv, doc, key_doc, grad, full, totals, out_part, gate_up_part, kv_piece, count, number
):
    out_piece = out_part.shape[:1] + out_part.shape[2:]
    gate_up_piece = gate_up_part.shape[1:]
    rows = queries.shape[1]
    steps = rows // kv_piece[1]
    bf16 = jnp.bfloat16

    def body(*refs):
        q_ref, kv_ref, doc_ref, key_doc_ref, grad_ref, full_ref, total_ref = refs[:7]
        out_ref, gate_up_ref = refs[7:9]
        dq_ref, dkv_sum, out_sum, gate_up_sum, dkv_part, key_acc = refs[9:15]
        take = Taker(refs[15:])
        place = Place(count)
        greet(place, blk=True, core=True, half=True)
        dkv = ReduceBlk(place, lambda i: dkv_part.at[i], dkv_sum, *take(REDUCE_REFS))
        out = ReduceBlk(place, lambda i: out_ref.at[:, i], out_sum, *take(REDUCE_REFS))
        folds = fold_rows(place, gate_up_ref, gate_up_sum, ROW_PARTS, take)
        out_events = out.events()

        def back(g):
            attend_back_block(
                count,
                g,
                place.here,
                q_ref,
                kv_ref,
                doc_ref,
                key_doc_ref,
                grad_ref,
                full_ref,
                total_ref,
                dq_ref,
                key_acc,
            )

        def clear(i, carry):
            key_acc[i] = jnp.zeros(key_acc.shape[1:], jnp.float32)
            return carry

        def put(sequence):
            def one(i, carry):
                for k in (0, 1):
                    value = key_acc[i * 2 + k].astype(bf16).reshape((steps,) + kv_piece[1:])
                    dkv_part[i, pl.ds((2 * sequence + k) * steps, steps)] = value
                return carry

            lax.fori_loop(0, count, one, 0)

        out.start()
        for fold in folds:
            next(fold)
        lax.fori_loop(0, 2 * count, clear, 0)
        back(0)
        next(folds[0])
        out_events[0]()
        back(1)
        put(0)
        out_events[1]()
        out_events[2]()
        next(folds[1])
        lax.fori_loop(0, 2 * count, clear, 0)
        back(2)
        out_events[3]()
        back(3)
        put(1)
        dkv.start()
        dkv_events = dkv.events()
        order = [(out_events, i) for i in range(4, 8)]
        order += [(folds, 2), (dkv_events, 0), (dkv_events, 1), (dkv_events, 2)]
        order += [(out_events, 8), (out_events, 9), (dkv_events, 3), (dkv_events, 4)]
        order += [(folds, 0), (dkv_events, 5), (dkv_events, 6), (folds, 1)]
        order += [(dkv_events, 7), (dkv_events, 8), (dkv_events, 9), (folds, 2)]
        for events, i in order:
            if events is folds:
                next(folds[i])
            else:
                events[i]()
        out.finish()
        dkv.finish()
        together(*folds)

    vmem = pltpu.VMEM
    return transfer(
        f"attend_back{number}",
        number,
        body,
        [queries, kv, doc, key_doc, grad, full, totals, out_part, gate_up_part],
        [
            shape(queries.shape, bf16),
            shape(kv_piece, bf16),
            shape(out_piece, bf16),
            shape(gate_up_piece, jnp.float32),
        ],
        [
            vmem((count,) + kv_piece, bf16),
            vmem((2 * count, rows, 2 * HEAD_DIM), jnp.float32),
        ]
        + reduce_blk_scratch(count, kv_piece, bf16)
        + reduce_blk_scratch(count, out_piece, bf16)
        + fold_rows_scratch(gate_up_piece, ROW_PARTS),
        (kv.size + out_part.size) * 2,
        [vmem, vmem, vmem, pl.ANY],
        [vmem] * 8 + [pl.ANY],
    )


def reduce_middle(dkv_part, out_part, gate_up_part, count, number):
    dkv_piece = dkv_part.shape[1:]
    out_piece = out_part.shape[:1] + out_part.shape[2:]

    gate_up_piece = gate_up_part.shape[1:]

    def body(dkv_ref, out_ref, gate_up_ref, dkv_sum, out_sum, gate_up_sum, *scratch):
        take = Taker(scratch)
        place = Place(count)
        greet(place, blk=True, core=True, half=True)
        together(
            reduce_blk(place, dkv_ref, dkv_sum, *take(REDUCE_REFS)),
            reduce_blk(place, lambda i: out_ref.at[:, i], out_sum, *take(REDUCE_REFS)),
            *(
                waiting(task, *rounds)
                for rounds, task in zip(
                    ((6, 5, 5), (8, 5, 3), (10, 6, 0)),
                    fold_rows(place, gate_up_ref, gate_up_sum, ROW_PARTS, take),
                )
            ),
        )

    return transfer(
        f"reduce{number}",
        number,
        body,
        [dkv_part, out_part, gate_up_part],
        [
            shape(dkv_piece, jnp.bfloat16),
            shape(out_piece, jnp.bfloat16),
            shape(gate_up_piece, jnp.float32),
        ],
        reduce_blk_scratch(count, dkv_piece, jnp.bfloat16)
        + reduce_blk_scratch(count, out_piece, jnp.bfloat16)
        + fold_rows_scratch(gate_up_piece, ROW_PARTS),
        (dkv_part.size + out_part.size) * 2,
        [pltpu.VMEM, pltpu.VMEM, pl.ANY],
        [pltpu.VMEM, pltpu.VMEM, pl.ANY],
    )


def reduce_last(qkv_part, norm_part, gain_part, out_sum, down_part, count, number):
    gain_piece = gain_part.shape[1:]
    qkv_piece, norm_piece = qkv_part.shape[1:], norm_part.shape[1:]

    def body(*refs):
        qkv_ref, norm_ref, gain_ref, out_ref, down_ref = refs[:5]
        qkv_sum, norm_sum, gain_sum, out_all, down_sum = refs[5:10]
        gain_mine = refs[10]
        take = Taker(refs[11:])
        place = Place(count)
        greet(place, blk=True, core=True, half=True, corner=True)

        def gain_task(near, far):
            yield from reduce_blk(place, gain_ref, gain_mine, *near)
            yield from reduce_group(place, gain_mine, gain_sum, *far)

        main = reduce_blk(place, qkv_ref, qkv_sum, *take(REDUCE_REFS))
        gain = gain_task(take(REDUCE_REFS), take(5))
        together(
            waiting(gain, 11),
            main,
            waiting(exchange_group(place, out_ref, out_all, *take(3)), 16),
            waiting(reduce_group(place, norm_ref, norm_sum, *take(5)), 7, 9),
            *(
                waiting(task, *rounds)
                for rounds, task in zip(
                    ((7, 7, 2), (8, 8, 0), (9, 9, 0)),
                    fold_rows(place, down_ref, down_sum, ROW_PARTS, take),
                )
            ),
        )

    return transfer(
        f"last{number}",
        number,
        body,
        [qkv_part, norm_part, gain_part, out_sum, down_part],
        [
            shape(qkv_piece, jnp.float32),
            shape(norm_piece, jnp.float32),
            shape(gain_piece[1:], jnp.float32),
            shape(out_sum.shape, jnp.bfloat16),
            shape(down_part.shape[1:], jnp.float32),
        ],
        [pltpu.VMEM(gain_piece, jnp.float32)]
        + reduce_blk_scratch(count, qkv_piece, jnp.bfloat16)
        + reduce_blk_scratch(count, gain_piece, jnp.float32, 1)
        + reduce_group_scratch(gain_piece[1:], jnp.float32)
        + exchange_group_sems()
        + reduce_group_scratch(norm_piece, jnp.bfloat16)
        + fold_rows_scratch(down_part.shape[1:], ROW_PARTS),
        qkv_part.size * 2,
        [pltpu.VMEM] * 4 + [pl.ANY],
        [pltpu.VMEM] * 4 + [pl.ANY],
    )


def all_gather_group(value, number):
    def body(src, out, *sems):
        place = Place(lax.axis_size("blk"))
        greet(place, core=True, half=True)
        together(gather_group(place, src, out, *sems))

    return transfer(
        f"group{number}",
        number,
        body,
        [value],
        [shape((GROUPS,) + value.shape, value.dtype)],
        gather_group_sems(),
        value.size * 8,
    )[0]


def reduce_scatter_group(value, number):
    piece = value.shape[1:]

    def body(part, out, *scratch):
        place = Place(lax.axis_size("blk"))
        greet(place, core=True, half=True)
        together(reduce_group(place, part, out, *scratch))

    return transfer(
        f"fold{number}",
        number,
        body,
        [value],
        [shape(piece, jnp.float32)],
        reduce_group_scratch(piece, value.dtype),
        value.size * 2,
        [pltpu.VMEM],
    )[0]


def dot(left, right, contract):
    return lax.dot_general(left, right, (contract, ((), ())), preferred_element_type=jnp.float32)


LAST = ((1,), (1,))
PLAIN = ((1,), (0,))
FIRST = ((0,), (0,))


LANES = 128
GELU_A = math.sqrt(2.0 / math.pi)
GELU_B = 0.044715


def feed_forward_fits(count, rows, width, hidden):
    inner = 4 if count >= 32 else 2
    outer = count // inner
    tile = rows * width * 2
    weights = 3 * hidden * width * 2
    kept = count * rows * 3 * hidden * 2
    total = weights + kept + tile * (3 * count + outer * (inner - 1) + 2 * outer + 3) + 9 * tile
    total += 3 * LANES * (count * rows + 2 * width) * 2
    return total < 58 * 2**20 and hidden % (3 * LANES) == 0 and width % 256 == 0


def feed_forward_kernel(
    count,
    branch_ref,
    token_ref,
    cot_ref,
    gain_ref,
    gate_up_hbm,
    down_hbm,
    out_ref,
    middle_grad_ref,
    branch_grad_ref,
    gain_grad_ref,
    gate_up_grad_hbm,
    down_grad_hbm,
    w_gate_up,
    w_down,
    norm_all,
    grad_all,
    act,
    hidden,
    part,
    middle,
    norm_own,
    grad_own,
    total,
    turned,
    staged,
    beside,
    along,
    held,
    spare,
    w_sems,
    out_sems,
    *sems,
):
    place = Place(count)
    rows, width = norm_all.shape[1:]
    units = hidden.shape[1]
    chunks = units // LANES
    inner, outer = place.inner, place.outer
    slab = branch_ref.shape[1]
    steps = rows // slab
    columns = width // 256
    pair = inner * rows
    take = Taker(sems)

    def weight_copies(i):
        units_at = pl.ds(pl.multiple_of(i * LANES, LANES), LANES)
        return [
            pltpu.make_async_copy(
                gate_up_hbm.at[units_at, pl.ds(0, width)],
                w_gate_up.at[i, pl.ds(0, LANES)],
                w_sems.at[3 * i],
            ),
            pltpu.make_async_copy(
                gate_up_hbm.at[units_at, pl.ds(width, width)],
                w_gate_up.at[i, pl.ds(LANES, LANES)],
                w_sems.at[3 * i + 1],
            ),
            pltpu.make_async_copy(down_hbm.at[units_at], w_down.at[units_at], w_sems.at[3 * i + 2]),
        ]

    def start_weights(i, carry):
        for copy in weight_copies(i):
            copy.start()
        return carry

    def wait_weights(i, carry):
        for copy in weight_copies(i):
            copy.wait()
        return carry

    lax.fori_loop(0, chunks, start_weights, 0)

    def scale_of(values):
        return lax.rsqrt(jnp.mean(values * values, axis=-1, keepdims=True) + NORM_EPS)

    def slab_rows(i):
        return pl.ds(pl.multiple_of(i * slab, slab), slab)

    def before(i, carry):
        value = branch_ref[i]
        mid = token_ref[i].astype(jnp.float32) + value * scale_of(value) * gain_ref[1:2]
        middle[i] = mid
        norm_own[slab_rows(i)] = (mid * scale_of(mid) * gain_ref[2:3]).astype(jnp.bfloat16)
        return carry

    lax.fori_loop(0, steps, before, 0)
    greet(place, blk=True)

    def pair_rows(k):
        return pl.ds(pl.multiple_of(place.near(k) * pair, pair), pair)

    def pair_pieces(k):
        return pl.ds(place.near(k) * inner, inner)

    def column(n):
        return pl.ds(pl.multiple_of(n * 256, 256), 256)

    def put_part(k, n, value):
        split = value.astype(jnp.bfloat16).reshape((inner, steps, slab, 256))
        part[pair_pieces(k), :, :, column(n)] = split

    def receive(gather, k):
        if k == 0:
            gather.copy.wait()
        if not gather.evened:
            if k + 1 < outer:
                gather.pass_on(k + 1)
            gather.beside_arrived(k)
            return
        ends = jnp.logical_not(gather.middle)
        if k == 0:
            gather.pass_on(1)
            pl.when(gather.middle)(lambda: gather.pass_on(2))
        elif k == 1:
            pl.when(ends)(lambda: gather.pass_on(2))
            gather.pass_extra(1)
            pl.when(gather.middle)(lambda: gather.pass_on(3))
        elif k == 2:
            pl.when(ends)(lambda: gather.pass_on(3))
            gather.pass_extra(3)
        gather.beside_arrived(k)

    gather = GatherBlk(place, norm_own, lambda i: norm_all.at[i], *take(3))
    gather.start()
    lax.fori_loop(0, chunks, wait_weights, 0)
    for k in range(outer):
        receive(gather, k)
        at = pair_rows(k)

        def up_chunk(j, carry, k=k, at=at):
            x = norm_all[pair_pieces(k)].reshape(pair, width)
            both = dot(x, w_gate_up[j], LAST)
            act[at, column(j)] = both.astype(jnp.bfloat16)
            gate, up = both[:, :LANES], both[:, LANES:]
            bent = 0.5 * gate * (1.0 + jnp.tanh(GELU_A * (gate + GELU_B * (gate * gate * gate))))
            hidden[at, pl.ds(pl.multiple_of(j * LANES, LANES), LANES)] = (bent * up).astype(
                jnp.bfloat16
            )
            return carry

        lax.fori_loop(0, chunks, up_chunk, 0)

        def down_chunk(n, carry, k=k, at=at):
            put_part(k, n, dot(hidden[at, :], w_down[:, column(n)], PLAIN))
            return carry

        lax.fori_loop(0, columns, down_chunk, 0)
    gather.finish()
    reduce = ReduceBlk(place, lambda i: part.at[i], total, beside, along, held, spare, *take(6))
    reduce.start()
    for event in reduce.events():
        event()

    gain_grad_ref[...] = jnp.zeros_like(gain_grad_ref)

    def norm_back(value, gain, incoming):
        scale = scale_of(value)
        lifted = incoming * gain
        pull = jnp.mean(lifted * value, axis=-1, keepdims=True)
        gain_grad = jnp.sum(incoming * value * scale, axis=0, keepdims=True)
        return scale * lifted - value * (scale * scale * scale) * pull, gain_grad

    def between(i, carry):
        value, cot = total[i], cot_ref[i].astype(jnp.float32)
        gain = gain_ref[3:4]
        out_ref[i] = (middle[i] + value * scale_of(value) * gain).astype(jnp.bfloat16)
        grad, gain_grad = norm_back(value, gain, cot)
        gain_grad_ref[3:4] += gain_grad
        grad_own[slab_rows(i)] = grad.astype(jnp.bfloat16)
        return carry

    lax.fori_loop(0, steps, between, 0)
    reduce.finish()

    gather = GatherBlk(place, grad_own, lambda i: grad_all.at[i], *take(3))
    gather.start()
    for k in range(outer):
        receive(gather, k)
        at = pair_rows(k)

        def back_chunk(j, carry, k=k, at=at):
            g = grad_all[pair_pieces(k)].reshape(pair, width)
            units_at = pl.ds(pl.multiple_of(j * LANES, LANES), LANES)
            grad = dot(g, w_down[units_at], LAST)
            both = act[at, column(j)].astype(jnp.float32)
            gate, up = both[:, :LANES], both[:, LANES:]
            bend = jnp.tanh(GELU_A * (gate + GELU_B * (gate * gate * gate)))
            bent = 0.5 * gate * (1.0 + bend)
            slope = 0.5 * (1.0 + bend) + (0.5 * GELU_A) * gate * (1.0 - bend * bend) * (
                1.0 + (3.0 * GELU_B) * gate * gate
            )
            pulled = jnp.concatenate([grad * up * slope, grad * bent], axis=1)
            act[at, column(j)] = pulled.astype(jnp.bfloat16)
            return carry

        lax.fori_loop(0, chunks, back_chunk, 0)

        def input_chunk(n, carry, k=k, at=at):
            w = w_gate_up[:, :, column(n)].reshape(2 * units, 256)
            put_part(k, n, dot(act[at, :], w, PLAIN))
            return carry

        lax.fori_loop(0, columns, input_chunk, 0)
    gather.finish()
    reduce = ReduceBlk(place, lambda i: part.at[i], total, beside, along, held, spare, *take(6))
    reduce.start()

    tokens = count * rows
    slots = staged.shape[0]

    def up_store(i):
        slot = lax.rem(i, slots)
        units_at = pl.ds(pl.multiple_of(i * LANES, LANES), LANES)
        return [
            pltpu.make_async_copy(
                staged.at[slot, pl.ds(h * LANES, LANES)],
                gate_up_grad_hbm.at[units_at, pl.ds(h * width, width)],
                out_sems.at[slot, h],
            )
            for h in (0, 1)
        ]

    def up_grad(i, carry):
        @pl.when(i >= slots)
        def _():
            for copy in up_store(i - slots):
                copy.wait()

        turned[pl.ds(0, 256)] = jnp.transpose(act[:, column(i)])

        def one(n, c):
            x = norm_all[:, :, column(n)].reshape(tokens, 256)
            staged[lax.rem(i, slots), pl.ds(0, 256), column(n)] = dot(
                turned[pl.ds(0, 256)], x, PLAIN
            ).astype(jnp.bfloat16)
            return c

        lax.fori_loop(0, columns, one, 0)
        for copy in up_store(i):
            copy.start()
        return carry

    three = 3 * LANES

    def down_store(i):
        slot = lax.rem(i, slots)
        return pltpu.make_async_copy(
            staged.at[slot],
            down_grad_hbm.at[pl.ds(pl.multiple_of(i * three, three), three)],
            out_sems.at[slot, 2],
        )

    def down_grad(i, carry):
        @pl.when(i >= slots)
        def _():
            down_store(i - slots).wait()

        turned[...] = jnp.transpose(hidden[:, pl.ds(pl.multiple_of(i * three, three), three)])

        def one(n, c):
            x = grad_all[:, :, column(n)].reshape(tokens, 256)
            staged[lax.rem(i, slots), :, column(n)] = dot(turned[...], x, PLAIN).astype(jnp.bfloat16)
            return c

        lax.fori_loop(0, columns, one, 0)
        down_store(i).start()
        return carry

    events = reduce.events()
    early = len(events) - 3
    bounds = [chunks * k // early for k in range(early + 1)]
    for k in range(early):
        lax.fori_loop(bounds[k], bounds[k + 1], up_grad, 0)
        events[k]()
    for i in range(max(0, chunks - slots), chunks):
        for copy in up_store(i):
            copy.wait()
    thirds = units // three
    bounds = [thirds * k // 3 for k in range(4)]
    for k in range(3):
        lax.fori_loop(bounds[k], bounds[k + 1], down_grad, 0)
        events[early + k]()

    def after(i, carry):
        value, mid, cot = branch_ref[i], middle[i], cot_ref[i].astype(jnp.float32)
        grad, gain_grad = norm_back(mid, gain_ref[2:3], total[i])
        gain_grad_ref[2:3] += gain_grad
        middle_grad = cot + grad
        middle_grad_ref[i] = middle_grad
        grad, gain_grad = norm_back(value, gain_ref[1:2], middle_grad)
        gain_grad_ref[1:2] += gain_grad
        branch_grad_ref[i] = grad.astype(jnp.bfloat16)
        return carry

    lax.fori_loop(0, steps, after, 0)
    reduce.finish()
    for i in range(max(0, thirds - slots), thirds):
        down_store(i).wait()


def feed_forward(branch, tokens, cotangent, gains, gate_up_all, down_all, count, number):
    steps, slab, width = branch.shape
    rows = steps * slab
    units = down_all.shape[0]
    inner = 4 if count >= 32 else 2
    outer = count // inner
    piece = branch.shape
    bf16, f32 = jnp.bfloat16, jnp.float32
    vmem = pl.BlockSpec(memory_space=pltpu.VMEM)
    anywhere = pl.BlockSpec(memory_space=pl.ANY)
    slots = 2
    line_scratch = reduce_blk_scratch(count, piece, bf16)
    return pl.pallas_call(
        functools.partial(feed_forward_kernel, count),
        name="feed_forward",
        out_shape=[
            shape(piece, bf16),
            shape(piece, f32),
            shape(piece, bf16),
            shape((4, width), f32),
            shape(gate_up_all.shape, bf16),
            shape(down_all.shape, bf16),
        ],
        in_specs=[vmem] * 4 + [anywhere] * 2,
        out_specs=[vmem] * 4 + [anywhere] * 2,
        scratch_shapes=[
            pltpu.VMEM((units // LANES, 2 * LANES, width), bf16),
            pltpu.VMEM((units, width), bf16),
            pltpu.VMEM((count, rows, width), bf16),
            pltpu.VMEM((count, rows, width), bf16),
            pltpu.VMEM((count * rows, 2 * units), bf16),
            pltpu.VMEM((count * rows, units), bf16),
            pltpu.VMEM((count,) + piece, bf16),
            pltpu.VMEM(piece, f32),
            pltpu.VMEM((rows, width), bf16),
            pltpu.VMEM((rows, width), bf16),
            pltpu.VMEM(piece, f32),
            pltpu.VMEM((3 * LANES, count * rows), bf16),
            pltpu.VMEM((slots, 3 * LANES, width), bf16),
        ]
        + line_scratch[:4]
        + [
            pltpu.SemaphoreType.DMA((3 * units // LANES,)),
            pltpu.SemaphoreType.DMA((slots, 3)),
        ]
        + gather_blk_sems(count)
        + line_scratch[4:]
        + gather_blk_sems(count)
        + line_scratch[4:],
        compiler_params=pltpu.CompilerParams(
            collective_id=number, has_side_effects=True, vmem_limit_bytes=67043328
        ),
        cost_estimate=pl.CostEstimate(
            flops=18 * count * rows * units * width,
            bytes_accessed=500 * 2**20,
            transcendentals=0,
        ),
    )(branch, tokens, cotangent, gains, gate_up_all, down_all)


def attention_scores(q2, k, query_pos, query_doc, key_block, key_doc, rows):
    raw = lax.dot_general(q2, k, (((1,), (1,)), ((), ())), preferred_element_type=jnp.float32)
    capped = jnp.tanh(raw * (SCORE_SCALE / SOFT_CAP))
    key_pos = key_block * rows + lax.broadcasted_iota(jnp.int32, (1, rows), 1)
    visible = (key_pos <= query_pos) & (key_doc == query_doc)
    return capped, jnp.where(visible, jnp.exp(SOFT_CAP * capped), 0.0)


def attention_query(q_ref, doc_ref, here, count, rows):
    half = pl.program_id(1)
    block = half * count + here
    q2 = jnp.concatenate([q_ref[0, :, :HEAD_DIM], q_ref[0, :, HEAD_DIM:]], axis=0)
    inside = lax.broadcasted_iota(jnp.int32, (rows, 1), 0)
    position = block * rows + jnp.concatenate([inside, inside], axis=0)
    doc = jnp.concatenate([doc_ref[0], doc_ref[0]], axis=0)
    return block, q2, position, doc


def attention_backward_kernel(
    count,
    here_ref,
    q_ref,
    kv_ref,
    doc_ref,
    key_doc_ref,
    grad_ref,
    full_ref,
    total_ref,
    dq_ref,
    dkv_ref,
    acc,
    key_acc,
):
    rows = q_ref.shape[1]
    half = pl.program_id(1)
    block, q2, position, doc = attention_query(q_ref, doc_ref, here_ref[0], count, rows)
    total = total_ref[0]
    grad = grad_ref[0].astype(jnp.float32)
    grad2 = jnp.concatenate([grad[:, :HEAD_DIM], grad[:, HEAD_DIM:]], axis=0)
    full2 = jnp.concatenate([full_ref[0, :, :HEAD_DIM], full_ref[0, :, HEAD_DIM:]], axis=0)
    total_grad = -jnp.sum(grad2 * full2, axis=-1, keepdims=True) / total
    sums_grad = (grad2 / total).astype(jnp.bfloat16)
    acc[...] = jnp.zeros_like(acc)

    @pl.when(half == 0)
    def _():
        def clear(i, carry):
            key_acc[i] = jnp.zeros(key_acc.shape[1:], jnp.float32)
            return carry

        lax.fori_loop(0, key_acc.shape[0], clear, 0)

    def one(key_block, carry):
        key_half = (key_block >= count).astype(jnp.int32)
        inner = key_block - key_half * count
        kv = kv_ref.at[inner, key_half]
        keys = kv[:, :HEAD_DIM]
        capped, weights = attention_scores(
            q2, keys, position, doc, key_block, key_doc_ref[0, key_block], rows
        )
        exp_grad = lax.dot_general(
            sums_grad, kv[:, HEAD_DIM:], (((1,), (1,)), ((), ())), preferred_element_type=jnp.float32
        )
        raw_grad = (
            weights * (exp_grad + total_grad) * (1.0 - capped * capped) * SCORE_SCALE
        ).astype(jnp.bfloat16)
        acc[...] += jnp.dot(raw_grad, keys, preferred_element_type=jnp.float32)
        over_rows = (((0,), (0,)), ((), ()))
        slot = inner * 2 + key_half
        key_acc[slot, :, :HEAD_DIM] += lax.dot_general(
            raw_grad, q2, over_rows, preferred_element_type=jnp.float32
        )
        key_acc[slot, :, HEAD_DIM:] += lax.dot_general(
            weights.astype(jnp.bfloat16), sums_grad, over_rows, preferred_element_type=jnp.float32
        )
        return carry

    lax.fori_loop(jnp.maximum(block - count, 0), block + 1, one, 0)
    dq = acc[...]
    dq_ref[0] = jnp.concatenate([dq[:rows], dq[rows:]], axis=1).astype(jnp.bfloat16)

    @pl.when(half == 1)
    def _():
        def put(i, carry):
            for k in (0, 1):
                dkv_ref[i, k] = key_acc[i * 2 + k].astype(jnp.bfloat16)
            return carry

        lax.fori_loop(0, count, put, 0)


def attention_specs(count, rows, width):
    query = pl.BlockSpec((1, rows, width), lambda s, h, here: (2 * s + h, 0, 0))
    keys = pl.BlockSpec((count, 2, rows, 2 * HEAD_DIM), lambda s, h, here: (0, s, 0, 0))
    doc = pl.BlockSpec((1, rows, 1), lambda s, h, here: (2 * s + h, 0, 0))
    key_doc = pl.BlockSpec((1, 2 * count, 1, rows), lambda s, h, here: (s, 0, 0, 0))
    total = pl.BlockSpec((1, REPS * rows, 1), lambda s, h, here: (2 * s + h, 0, 0))
    return query, keys, doc, key_doc, total


def attention_backward(here, q, kv, doc, key_doc, grad, full, totals):
    count, _, rows, _ = kv.shape
    width = REPS * HEAD_DIM
    query, keys, doc_spec, key_doc_spec, total = attention_specs(count, rows, width)
    return pl.pallas_call(
        functools.partial(attention_backward_kernel, count),
        name="attend_back",
        grid_spec=pltpu.PrefetchScalarGridSpec(
            num_scalar_prefetch=1,
            grid=(2, 2),
            in_specs=[query, keys, doc_spec, key_doc_spec, query, query, total],
            out_specs=[query, keys],
            scratch_shapes=[
                pltpu.VMEM((REPS * rows, HEAD_DIM), jnp.float32),
                pltpu.VMEM((2 * count, rows, 2 * HEAD_DIM), jnp.float32),
            ],
        ),
        out_shape=[shape((GROUPS, rows, width), jnp.bfloat16), shape(kv.shape, jnp.bfloat16)],
        compiler_params=pltpu.CompilerParams(vmem_limit_bytes=VMEM_LIMIT),
        cost_estimate=pl.CostEstimate(flops=2 * 10**9, bytes_accessed=80 * 2**20, transcendentals=0),
    )(here, q, kv, doc, key_doc, grad, full, totals)


def rms_scale(values, gain_row):
    return (
        values * lax.rsqrt(jnp.mean(values * values, axis=-1, keepdims=True) + NORM_EPS) * gain_row
    )


def gelu_tanh(values):
    return jax.nn.gelu(values, approximate=True)


def rope_tables(positions):
    half_width = HEAD_DIM // 2
    frequency = jnp.exp(
        jnp.arange(half_width, dtype=jnp.float32) * (-2.0 * math.log(ROPE_BASE) / HEAD_DIM)
    )
    angles = positions.astype(jnp.float32)[:, None] * frequency[None, :]
    cosine = jnp.concatenate([jnp.cos(angles), jnp.cos(angles)], axis=-1)
    sine = jnp.concatenate([jnp.sin(angles), jnp.sin(angles)], axis=-1)
    return cosine[:, None, :], sine[:, None, :]


def rotate(values, cosine, sine):
    half_width = HEAD_DIM // 2
    turned = jnp.concatenate([-values[..., half_width:], values[..., :half_width]], axis=-1)
    return values * cosine + turned * sine


def feed_forward_apart(
    branch_slabs, inputs, cotangent, gains, gate_up_all, down_all, count, piece
):
    rows, width = inputs.shape
    bf16 = jnp.bfloat16
    branch = branch_slabs.reshape(rows, width)
    middle = inputs + rms_scale(branch, gains[1])
    norm_three = rms_scale(middle, gains[2]).astype(bf16)
    gate_all = gate_up_all[:, :width]
    up_all = gate_up_all[:, width:]
    norm_all = all_gather_blk(norm_three, count, 4).reshape(count * rows, width)
    gate = dot(norm_all, gate_all, LAST)
    up = dot(norm_all, up_all, LAST)
    hidden = (gelu_tanh(gate) * up).astype(bf16)
    ffn_part = dot(hidden, down_all, PLAIN).astype(bf16)
    ffn_out = reduce_scatter_blk(ffn_part.reshape((count,) + piece), count, 5).reshape(rows, width)
    output = (middle + rms_scale(ffn_out, gains[3])).astype(bf16)[None]

    out_cotangent = cotangent[0].astype(jnp.float32)
    _, post_ffn_back = jax.vjp(rms_scale, ffn_out, gains[3])
    ffn_grad, gain_grad_four = post_ffn_back(out_cotangent)
    grad_all = all_gather_blk(ffn_grad.astype(bf16), count, 6).reshape(count * rows, width)
    activated, gelu_back = jax.vjp(gelu_tanh, gate)
    hidden_grad = dot(grad_all, down_all, LAST)
    gate_grad = gelu_back(hidden_grad * up)[0].astype(bf16)
    up_grad = (hidden_grad * activated).astype(bf16)
    norm_part = dot(gate_grad, gate_all, PLAIN) + dot(up_grad, up_all, PLAIN)
    norm_three_grad = reduce_scatter_blk(
        norm_part.astype(bf16).reshape((count,) + piece), count, 7
    ).reshape(rows, width)
    down_part = dot(hidden, grad_all, FIRST).astype(bf16)
    gate_up_part = jnp.concatenate(
        [dot(gate_grad, norm_all, FIRST), dot(up_grad, norm_all, FIRST)], axis=1
    ).astype(bf16)
    _, pre_ffn_back = jax.vjp(rms_scale, middle, gains[2])
    middle_part, gain_grad_three = pre_ffn_back(norm_three_grad)
    middle_grad = out_cotangent + middle_part
    _, post_attn_back = jax.vjp(rms_scale, branch, gains[1])
    branch_grad, gain_grad_two = post_attn_back(middle_grad)
    return (
        output,
        middle_grad,
        branch_grad.astype(bf16),
        gain_grad_two,
        gain_grad_three,
        gain_grad_four,
        gate_up_part,
        down_part,
    )


def shards(
    tokens, cotangent, segments, norm_gains, qkv_weight, out_weight, gate_up_weight, down_weight
):
    _, rows, width = tokens.shape
    count = lax.axis_size("blk")
    here = lax.axis_index("blk")
    mine = 2 * lax.axis_index("dp") + lax.axis_index("head")
    group_rows = GROUPS * rows
    head_width = REPS * HEAD_DIM
    bf16 = jnp.bfloat16
    slab = slabs(rows)
    piece = (rows // slab, slab, width)

    gain_rows = norm_gains.shape[0]
    gain_lanes = -(-gain_rows // 128) * 128
    gains_sent = jnp.pad(
        jnp.transpose(norm_gains).astype(jnp.float32), ((0, 4), (0, gain_lanes - gain_rows))
    )
    out_rows = out_weight.shape[0]
    out_sent = jnp.transpose(out_weight.reshape(out_rows, GROUPS, head_width), (1, 0, 2))
    qkv_rows = qkv_weight.shape[0]
    qkv_slab = slabs(qkv_rows)
    qkv_piece = (qkv_rows // qkv_slab, qkv_slab, width)
    qkv_all, out_mine, tokens_all, gains_all, docs_all, down_all = gather_first(
        qkv_weight,
        out_sent,
        tokens[0],
        gains_sent,
        segments.reshape(-1, 128),
        down_weight,
        count,
        1,
    )
    down_all = down_all.reshape(-1, width)
    gains = jnp.transpose(gains_all[:, :, :4, :gain_rows], (2, 0, 1, 3)).reshape(4, width)
    qkv_head = qkv_all.reshape(count * qkv_rows, width)
    docs = docs_all.reshape(2, 2, count, rows)
    key_doc = docs.reshape(2, 2 * count, 1, rows)
    own_doc = lax.dynamic_index_in_dim(docs, here, 2, keepdims=False).reshape(GROUPS, rows, 1)
    here_one = here.reshape(1)

    group_tokens = tokens_all.reshape(group_rows, width).astype(jnp.float32)
    norm_one = rms_scale(group_tokens, gains[0]).astype(bf16)
    proj = dot(norm_one, qkv_head, LAST)
    inside = jnp.arange(rows, dtype=jnp.int32)
    position = jnp.concatenate([here * rows + inside, (count + here) * rows + inside])
    cosine, sine = rope_tables(jnp.concatenate([position, position]))
    proj = proj.reshape(group_rows, REPS + 2, HEAD_DIM)
    turned = rotate(proj[:, : REPS + 1], cosine, sine)
    sent = jnp.concatenate([turned, proj[:, REPS + 1 :]], axis=1).astype(bf16)
    queries = sent[:, :REPS].reshape(GROUPS, rows, head_width)
    own_kv = sent[:, REPS:].reshape(group_rows, 2 * HEAD_DIM)
    kv_slab = slabs(group_rows)
    kv_piece = (group_rows // kv_slab, kv_slab, 2 * HEAD_DIM)
    kv, out_all, gate_up_all, attn, attended, totals = gather_attend(
        own_kv, out_mine, gate_up_weight, queries, own_doc, key_doc, count, 2
    )
    gate_up_all = gate_up_all.reshape(-1, 2 * width)
    out_head = out_all.reshape(width, head_width)
    attn = attn.reshape(group_rows, head_width)
    branch_part = dot(attn, out_head, LAST).astype(bf16)
    branch_slabs = reduce_scatter_group(branch_part.reshape((GROUPS,) + piece), 3)
    inputs = tokens[0].astype(jnp.float32)
    if feed_forward_fits(count, rows, width, down_all.shape[0]):
        output, middle_grad, branch_grad, gain_rest, gate_up_part, down_part = feed_forward(
            branch_slabs,
            tokens.reshape(piece),
            cotangent.reshape(piece),
            gains,
            gate_up_all,
            down_all,
            count,
            4,
        )
        output = output.reshape(tokens.shape)
        middle_grad = middle_grad.reshape(rows, width)
        branch_grad = branch_grad.reshape(rows, width)
        gain_grad_two, gain_grad_three, gain_grad_four = gain_rest[1], gain_rest[2], gain_rest[3]
    else:
        (
            output,
            middle_grad,
            branch_grad,
            gain_grad_two,
            gain_grad_three,
            gain_grad_four,
            gate_up_part,
            down_part,
        ) = feed_forward_apart(
            branch_slabs, inputs, cotangent, gains, gate_up_all, down_all, count, piece
        )
    branch_all = all_gather_group(branch_grad, 8).reshape(group_rows, width)
    attn_grad = dot(branch_all, out_head, PLAIN).astype(bf16).reshape(GROUPS, rows, head_width)
    out_part = dot(branch_all, attn, FIRST).astype(bf16)
    out_part = out_part.reshape(GROUPS, count, out_rows, head_width)
    gate_up_part = gate_up_part.reshape((GROUPS,) + gate_up_weight.shape)
    if attend_back_fits(count):
        dq, dkv, out_sum, gate_up_grad = attend_back_reduce(
            queries,
            kv,
            own_doc,
            key_doc,
            attn_grad,
            attended,
            totals,
            out_part,
            gate_up_part,
            kv_piece,
            count,
            9,
        )
    else:
        kv = kv.reshape(count, GROUPS, rows, 2 * HEAD_DIM)
        dq, dkv_part = attention_backward(
            here_one, queries, kv, own_doc, key_doc, attn_grad, attended, totals
        )
        dkv, out_sum, gate_up_grad = reduce_middle(
            dkv_part.reshape((count,) + kv_piece), out_part, gate_up_part, count, 9
        )
    sent_grad = jnp.concatenate(
        [
            dq.reshape(group_rows, REPS, HEAD_DIM),
            dkv.reshape(group_rows, 2, HEAD_DIM),
        ],
        axis=1,
    ).astype(jnp.float32)
    unturned = rotate(sent_grad[:, : REPS + 1], cosine, -sine)
    proj_grad = (
        jnp.concatenate([unturned, sent_grad[:, REPS + 1 :]], axis=1)
        .astype(bf16)
        .reshape(group_rows, (REPS + 2) * HEAD_DIM)
    )
    qkv_part = dot(proj_grad, norm_one, FIRST).astype(bf16)
    norm_one_part = dot(proj_grad, qkv_head, PLAIN)
    _, gain_back = jax.vjp(lambda gain: rms_scale(group_tokens, gain), gains[0])
    (gain_grad_one,) = gain_back(norm_one_part)
    gain_part = jnp.stack([gain_grad_one, gain_grad_two, gain_grad_three, gain_grad_four])
    gain_part = jnp.transpose(gain_part.reshape(4, GROUPS, count, gain_rows), (2, 1, 0, 3))
    gain_part = jnp.pad(gain_part, ((0, 0), (0, 0), (0, 4), (0, gain_lanes - gain_rows)))
    qkv_grad, norm_one_grad, gain_grad, out_grad, down_grad = reduce_last(
        qkv_part.reshape((count,) + qkv_piece),
        norm_one_part.astype(bf16).reshape((GROUPS,) + piece),
        gain_part[:, :, None],
        out_sum,
        down_part.reshape((GROUPS,) + down_weight.shape),
        count,
        10,
    )
    qkv_grad = qkv_grad.reshape(qkv_rows, width)
    out_grad = (
        jnp.transpose(out_grad, (1, 0, 2)).reshape(out_rows, GROUPS * head_width).astype(jnp.float32)
    )
    gain_grad = jnp.transpose(gain_grad.reshape(8, gain_lanes)[:4, :gain_rows])
    _, pre_attn_back = jax.vjp(lambda values: rms_scale(values, gains[0]), inputs)
    (input_part,) = pre_attn_back(norm_one_grad.reshape(rows, width))
    tokens_grad = (middle_grad + input_part).astype(bf16)[None]
    return (output, tokens_grad, gain_grad, qkv_grad, out_grad, gate_up_grad, down_grad)


def solution(mesh):
    whole = ("dp", "head", "blk")
    return jax.shard_map(
        shards,
        mesh=mesh,
        in_specs=(
            P("dp", ("head", "blk"), None),
            P("dp", ("head", "blk"), None),
            P("dp", None),
            P(whole, None),
            P(whole, None),
            P(whole, None),
            P(whole, None),
            P(whole, None),
        ),
        out_specs=(
            P("dp", ("head", "blk"), None),
            P("dp", ("head", "blk"), None),
            P(whole, None),
            P(whole, None),
            P(whole, None),
            P(whole, None),
            P(whole, None),
        ),
        check_vma=False,
    )
```

```python
import functools
import math

import jax
import jax.numpy as jnp
from jax import lax
from jax.experimental import pallas as pl
from jax.experimental.pallas import tpu as pltpu
from jax.sharding import PartitionSpec as P

HEADS = 8
KV_HEADS = 4
HEAD_DIM = 256
REPS = HEADS // KV_HEADS
GROUPS = 4
SOFT_CAP = 50.0
NORM_EPS = 1e-06
ROPE_BASE = 10000.0
SCORE_SCALE = HEAD_DIM ** (-0.5)

MESH = pl.DeviceIdType.MESH
VMEM_LIMIT = 60 * 1024 * 1024


class Place:
    def __init__(self, count):
        self.count = count
        self.inner = 4 if count >= 32 else 2
        self.outer = count // self.inner
        self.here = lax.axis_index("blk")
        self.line = self.here // self.inner
        self.side = lax.rem(self.here, self.inner)
        self.core = lax.axis_index("dp")
        self.half = lax.axis_index("head")
        self.group = 2 * self.core + self.half

    def near(self, k):
        orders = [near_order(self.outer, line)[k] for line in range(self.outer)]
        found = jnp.int32(orders[0])
        for line in range(1, self.outer):
            found = jnp.where(self.line == line, jnp.int32(orders[line]), found)
        return found

    def at(self, line, side):
        return {"blk": line * self.inner + side}

    def beside(self, step):
        return lax.rem(self.side + step, self.inner)

    def partner(self):
        return {"dp": 1 - self.core}

    def across(self):
        return {"head": 1 - self.half}

    def corner(self):
        return {"dp": 1 - self.core, "head": 1 - self.half}


def remote(src, dst, sent, came, device):
    return pltpu.make_async_remote_copy(
        src_ref=src, dst_ref=dst, send_sem=sent, recv_sem=came, device_id=device, device_id_type=MESH
    )


def greet(place, blk=False, core=False, half=False, corner=False):
    sem = pltpu.get_barrier_semaphore()
    amount = jnp.int32(0)

    def hello(device):
        pl.semaphore_signal(sem, inc=1, device_id=device, device_id_type=MESH)

    if blk:
        up, down = place.line < place.outer - 1, place.line > 0
        pl.when(up)(lambda: hello(place.at(place.line + 1, place.side)))
        pl.when(down)(lambda: hello(place.at(place.line - 1, place.side)))
        amount = amount + up.astype(jnp.int32) + down.astype(jnp.int32) + (place.inner - 1)
        for step in range(1, place.inner):
            hello(place.at(place.line, place.beside(step)))
    for wanted, device in (
        (core, place.partner()),
        (half, place.across()),
        (corner, place.corner()),
    ):
        if wanted:
            hello(device)
            amount = amount + 1
    pl.semaphore_wait(sem, amount)


def together(*tasks):
    tasks = list(tasks)
    while tasks:
        for task in list(tasks):
            try:
                next(task)
            except StopIteration:
                tasks.remove(task)


def waiting(task, *rounds):
    for step, _ in enumerate(task):
        yield
        if step < len(rounds):
            for _ in range(rounds[step]):
                yield


def near_order(outer, line):
    ends = outer == 4
    return sorted(
        range(outer),
        key=lambda other: (abs(other - line), ends and other not in (0, outer - 1), other),
    )


def evened(place, parts):
    return parts == 2 and place.inner == 2 and place.outer == 4


def part_of(ref, h, parts):
    if parts == 1:
        return ref
    size = ref.shape[0] // parts
    return ref.at[pl.ds(h * size, size)]


def gather_blk_sems(place_count, parts=2):
    inner = 4 if place_count >= 32 else 2
    return [
        pltpu.SemaphoreType.DMA((2 + inner, place_count, parts)),
        pltpu.SemaphoreType.DMA((place_count, parts)),
        pltpu.SemaphoreType.DMA,
    ]


class GatherBlk:
    def __init__(self, place, src, view, sent, came, own):
        self.place, self.src, self.view, self.sent, self.came = place, src, view, sent, came
        self.parts = came.shape[1]
        self.evened = evened(place, self.parts)
        self.middle = (place.line > 0) & (place.line < place.outer - 1)
        self.copy = pltpu.make_async_copy(src, view(place.here), own)

    def sends(self, k, h):
        place = self.place
        there = place.near(k)
        piece = there * place.inner + place.side
        there_view = part_of(self.view(piece), h, self.parts)
        src = part_of(self.src, h, self.parts) if k == 0 else there_view

        def send(kind, device):
            return remote(
                src, there_view, self.sent.at[kind, piece, h], self.came.at[piece, h], device
            )

        line, side = place.line, place.side
        up = (there <= line) & (line < place.outer - 1)
        down = (there >= line) & (line > 0)
        aside = range(1, place.inner)
        if self.evened and h == 1 and k == place.outer - 1:
            aside = ()
        return (
            [
                (up, lambda: send(0, place.at(line + 1, side))),
                (down, lambda: send(1, place.at(line - 1, side))),
            ],
            [send(1 + step, place.at(line, place.beside(step))) for step in aside],
        )

    def forward(self, k, h):
        along, aside = self.sends(k, h)
        for needed, make in along:
            pl.when(needed)(lambda make=make: make().start())
        for one in aside:
            one.start()

    def start(self):
        self.copy.start()
        for h in range(self.parts):
            self.forward(0, h)

    def arrived(self, piece, h):
        place = self.place
        remote(
            part_of(self.src, h, self.parts),
            part_of(self.view(piece), h, self.parts),
            self.sent.at[0, piece, h],
            self.came.at[piece, h],
            place.at(place.line, place.beside(1)),
        ).wait_recv()

    def pass_on(self, k):
        for h in range(self.parts):
            self.arrived(self.place.near(k) * self.place.inner + self.place.side, h)
            self.forward(k, h)

    def extra(self, k):
        place = self.place
        piece = place.near(k) * place.inner + place.beside(1)
        to = place.near(2 if k == 1 else 1)
        half = part_of(self.view(piece), 1, 2)
        return remote(
            half,
            half,
            self.sent.at[place.inner + 1, piece, 1],
            self.came.at[piece, 1],
            place.at(to, place.side),
        )

    def pass_extra(self, k):
        if self.evened:

            @pl.when(self.middle)
            def _():
                self.arrived(self.place.near(k) * self.place.inner + self.place.beside(1), 1)
                self.extra(k).start()

    def beside_arrived(self, k):
        for step in range(1, self.place.inner):
            piece = self.place.near(k) * self.place.inner + self.place.beside(step)
            for h in range(self.parts):
                if self.evened and h == 1 and k in (1, self.place.outer - 1):
                    pl.when(jnp.logical_not(self.middle))(lambda: self.arrived(piece, 1))
                else:
                    self.arrived(piece, h)

    def finish(self):
        for k in range(self.place.outer):
            for h in range(self.parts):
                along, aside = self.sends(k, h)
                for needed, make in along:
                    pl.when(needed)(lambda make=make: make().wait_send())
                for one in aside:
                    one.wait_send()
        if self.evened:

            @pl.when(self.middle)
            def _():
                self.extra(1).wait_send()
                self.extra(self.place.outer - 1).wait_send()


def advance(gathers, k):
    place = gathers[0].place

    def each(name, *args):
        for gather in gathers:
            getattr(gather, name)(*args)

    if not gathers[0].evened:
        if k + 1 < place.outer:
            each("pass_on", k + 1)
        return
    middle = gathers[0].middle
    ends = jnp.logical_not(middle)
    if k == 0:
        each("pass_on", 1)
        pl.when(middle)(lambda: each("pass_on", 2))
    elif k == 1:
        pl.when(ends)(lambda: each("pass_on", 2))
        each("pass_extra", 1)
        pl.when(middle)(lambda: each("pass_on", 3))
    elif k == 2:
        pl.when(ends)(lambda: each("pass_on", 3))
        each("pass_extra", 3)


def gather_blk(place, src, view, sent, came, own):
    if not callable(view):
        out = view
        view = lambda piece: out.at[piece]
    work = GatherBlk(place, src, view, sent, came, own)
    work.start()
    yield
    for k in range(1, place.outer):
        work.pass_on(k)
        if k == place.outer - 2:
            work.pass_extra(1)
        yield
    work.pass_extra(place.outer - 1)
    yield
    for k in range(place.outer):
        work.beside_arrived(k)
    work.finish()
    work.copy.wait()


def add_into(out, *terms):
    def one(i, carry):
        total = terms[0][i].astype(jnp.float32)
        for term in terms[1:]:
            total = total + term[i].astype(jnp.float32)
        out[i] = total.astype(out.dtype)
        return carry

    lax.fori_loop(0, out.shape[0], one, 0)


def reduce_blk_scratch(place_count, piece, dtype, parts=2):
    inner = 4 if place_count >= 32 else 2
    outer = place_count // inner
    half = (piece[0] // 2,) + tuple(piece[1:]) if parts == 2 and inner == 2 and outer == 4 else (1, 8, 128)
    return [
        pltpu.VMEM((outer, inner - 1) + piece, dtype),
        pltpu.VMEM((outer + 1,) + piece, dtype),
        pltpu.VMEM((outer,) + piece, dtype),
        pltpu.VMEM((4,) + half, dtype),
        pltpu.SemaphoreType.DMA((outer, inner - 1, parts)),
        pltpu.SemaphoreType.DMA((outer, inner - 1, parts)),
        pltpu.SemaphoreType.DMA((outer, parts)),
        pltpu.SemaphoreType.DMA((outer + 1, parts)),
        pltpu.SemaphoreType.DMA((2,)),
        pltpu.SemaphoreType.DMA((2,)),
    ]


REDUCE_REFS = 10


class ReduceBlk:
    def __init__(
        self,
        place,
        view,
        out,
        beside,
        along,
        held,
        spare,
        side_sent,
        side_came,
        line_sent,
        line_came,
        spare_sent,
        spare_came,
    ):
        self.place, self.view, self.out = place, view, out
        self.beside, self.along, self.held, self.spare = beside, along, held, spare
        self.side_sems, self.line_sems = (side_sent, side_came), (line_sent, line_came)
        self.spare_sems = (spare_sent, spare_came)
        self.parts = line_sent.shape[1]
        self.evened = evened(place, self.parts)
        self.middle = (place.line > 0) & (place.line < place.outer - 1)

    def part(self, ref, h):
        return part_of(ref, h, self.parts)

    def far(self, k):
        return self.place.near(self.place.outer - 1 - k)

    def alone(self, k, h):
        return self.evened and k == 0 and h == 1

    def side_copy(self, there, step, h, src=None):
        place = self.place
        to = place.beside(step)
        if src is None:
            src = self.part(self.view(there * place.inner + to), h)
        return remote(
            src,
            self.part(self.beside.at[there, place.inner - step - 1], h),
            self.side_sems[0].at[there, step - 1, h],
            self.side_sems[1].at[there, place.inner - step - 1, h],
            place.at(place.line, to),
        )

    def line_copy(self, there, slot, to, h, src=None):
        return remote(
            self.part(self.held.at[there], h) if src is None else src,
            self.part(self.along.at[slot], h),
            self.line_sems[0].at[there, h],
            self.line_sems[1].at[slot, h],
            self.place.at(to, self.place.side),
        )

    def send(self, k, h):
        for step in range(1, self.place.inner):
            self.side_copy(self.far(k), step, h).start()

    def terms(self, k, h):
        place = self.place
        there = self.far(k)
        own = [self.part(self.view(there * place.inner + place.side), h)]
        if self.alone(k, h):
            return own
        for step in range(1, place.inner):
            self.side_copy(there, step, h).wait_recv()
        return own + [self.part(self.beside.at[there, j], h) for j in range(place.inner - 1)]

    def onward(self, there, h, src=None):
        line, outer = self.place.line, self.place.outer
        to = jnp.where(there < line, line - 1, line + 1)
        slot = jnp.where(there == line + 1, outer, there)
        return self.line_copy(there, slot, to, h, src)

    def starts(self, there):
        line, outer = self.place.line, self.place.outer
        return ((there < line) & (line == outer - 1)) | ((there > line) & (line == 0))

    def pass_on(self, k, h, middle=None):
        place = self.place
        line = place.line
        there = self.far(k)
        terms = self.terms(k, h)
        held = self.part(self.held.at[there], h)

        def first():
            add_into(held, *terms)

        def later():
            back = jnp.where(there < line, line + 1, line - 1)
            self.line_copy(there, there, back, h).wait_recv()
            add_into(held, self.part(self.along.at[there], h), *terms)

        if middle is None:
            starts = self.starts(there)
            pl.when(starts)(first)
            pl.when(jnp.logical_not(starts))(later)
        elif middle:
            later()
        else:
            first()
        self.onward(there, h).start()

    def last(self, h):
        place = self.place
        line, outer = place.line, place.outer
        terms = self.terms(outer - 1, h)
        below, above = line > 0, line < outer - 1
        from_above = self.part(self.along.at[line], h)
        from_below = self.part(self.along.at[outer], h)
        out = self.part(self.out, h)

        @pl.when(above)
        def _():
            self.line_copy(line, line, line + 1, h).wait_recv()

        @pl.when(below)
        def _():
            self.line_copy(line, outer, line - 1, h).wait_recv()

        @pl.when(above & below)
        def _():
            add_into(out, from_above, from_below, *terms)

        @pl.when(above & jnp.logical_not(below))
        def _():
            add_into(out, from_above, *terms)

        @pl.when(jnp.logical_not(above) & below)
        def _():
            add_into(out, from_below, *terms)


    def spare_view(self, k):
        place = self.place
        return self.part(self.view(place.near(k) * place.inner + place.beside(1)), 1)

    def spare_first(self):
        return remote(
            self.spare_view(3),
            self.spare.at[0],
            self.spare_sems[0].at[0],
            self.spare_sems[1].at[0],
            self.place.at(self.place.near(1), self.place.side),
        )

    def spare_second(self):
        return remote(
            self.spare.at[2],
            self.spare.at[1],
            self.spare_sems[0].at[1],
            self.spare_sems[1].at[1],
            self.place.at(self.place.near(2), self.place.side),
        )

    def spare_side(self):
        return self.side_copy(self.far(2), 1, 1, self.spare.at[3])

    def opening(self):
        outer = self.place.outer
        if not self.evened:

            def every():
                for k in range(outer):
                    for h in range(self.parts):
                        self.send(k, h)

            return [every]
        ends = jnp.logical_not(self.middle)

        def along():
            self.spare_first().start()
            there = self.far(0)
            self.onward(
                there, 1, self.part(self.view(there * self.place.inner + self.place.side), 1)
            ).start()

        todo = [lambda: self.send(0, 0), lambda: pl.when(ends)(along)]
        todo += [lambda k=k, h=h: self.send(k, h) for k, h in ((1, 0), (1, 1), (2, 0))]
        todo += [
            lambda k=k, h=h: pl.when(ends)(lambda: self.send(k, h))
            for k, h in ((2, 1), (3, 0), (3, 1))
        ]
        return todo

    def start(self):
        for step in self.opening():
            step()

    def turning(self):
        def first():
            self.spare_first().wait_recv()
            add_into(self.spare.at[2], self.spare.at[0], self.spare_view(3))
            self.spare_second().start()

        def second():
            self.spare_second().wait_recv()
            add_into(self.spare.at[3], self.spare.at[1], self.spare_view(1))
            self.spare_side().start()
            for h in (0, 1):
                self.send(3, h)

        steps = (first, lambda: self.pass_on(0, 1, True), second)
        return steps

    def events(self):
        outer, parts = self.place.outer, self.parts
        if self.evened:
            todo = [lambda step=step: pl.when(self.middle)(step) for step in self.turning()]
            todo.append(lambda: self.pass_on(0, 0))
        else:
            todo = [lambda h=h: self.pass_on(0, h) for h in range(parts)]
        for k in range(1, outer - 1):
            for h in range(parts):
                todo.append(lambda k=k, h=h: self.pass_on(k, h))
        for h in range(parts):
            todo.append(lambda h=h: self.last(h))
        return todo

    def finish(self):
        for k in range(self.place.outer):
            for h in range(self.parts):
                if k < self.place.outer - 1:
                    self.onward(self.far(k), h).wait_send()
                if not self.alone(k, h):
                    for step in range(1, self.place.inner):
                        self.side_copy(self.far(k), step, h).wait_send()
        if self.evened:

            @pl.when(self.middle)
            def _():
                self.spare_second().wait_send()

            @pl.when(jnp.logical_not(self.middle))
            def _():
                self.spare_first().wait_send()


def reduce_blk(place, view, out, *scratch):
    if not callable(view):
        part = view
        view = lambda piece: part.at[piece]
    work = ReduceBlk(place, view, out, *scratch)
    for step in work.opening() + work.events():
        step()
        yield
    work.finish()


def gather_group_sems():
    return [pltpu.SemaphoreType.DMA((3,)), pltpu.SemaphoreType.DMA((4,)), pltpu.SemaphoreType.DMA]


def gather_group(place, src, view, sent, came, own, through=None):
    if not callable(view):
        out = view
        view = lambda g: out.at[g]
    copy = pltpu.make_async_copy(src if through is None else through, view(place.group), own)
    load = None if through is None else pltpu.make_async_copy(src, through, own)
    mine, other = place.group, 2 * place.core + (1 - place.half)
    to_half = remote(src, view(mine), sent.at[0], came.at[mine], place.across())
    to_core = remote(src, view(mine), sent.at[1], came.at[mine], place.partner())
    to_half.start()
    to_core.start()
    (load or copy).start()
    yield
    if load:
        load.wait()
        copy.start()
    remote(src, view(other), sent.at[0], came.at[other], place.across()).wait_recv()
    relay = remote(view(other), view(other), sent.at[2], came.at[other], place.partner())
    relay.start()
    yield
    for half in (0, 1):
        slot = 2 * (1 - place.core) + half
        remote(src, view(slot), sent.at[0], came.at[slot], place.partner()).wait_recv()
    to_half.wait_send()
    to_core.wait_send()
    relay.wait_send()
    copy.wait()


def share_rows(ref, parts, p):
    rows = ref.shape[0] // parts
    return ref.at[pl.ds(p * rows, rows)]


def gather_group_rows(place, src, out, parts, take, through=True):
    def task(p, refs):
        rows = src.shape[0] // parts
        view = lambda g: out.at[g, pl.ds(p * rows, rows)]
        return gather_group(place, share_rows(src, parts, p), view, *refs)

    return [task(p, take(4 if through else 3)) for p in range(parts)]


def gather_rows_scratch(value, parts):
    through = pltpu.VMEM((value.shape[0] // parts, value.shape[1]), value.dtype)
    return (gather_group_sems() + [through]) * parts


def fold_rows_scratch(piece, parts):
    rows, width = piece[0] // parts, piece[1]
    bf16 = jnp.bfloat16
    one = [
        pltpu.VMEM((2, rows, width), bf16),
        pltpu.VMEM((rows, width), bf16),
        pltpu.VMEM((rows, width), bf16),
        pltpu.VMEM((rows, width), bf16),
        pltpu.VMEM((rows, width), jnp.float32),
        pltpu.SemaphoreType.DMA((3,)),
        pltpu.SemaphoreType.DMA((3,)),
        pltpu.SemaphoreType.DMA((3,)),
    ]
    return one * parts


def add_rows(out, *terms):
    rows = slabs(out.shape[0])

    def one(i, carry):
        at = pl.ds(pl.multiple_of(i * rows, rows), rows)
        total = terms[0][at].astype(jnp.float32)
        for term in terms[1:]:
            total = total + term[at].astype(jnp.float32)
        out[at] = total.astype(out.dtype)
        return carry

    lax.fori_loop(0, out.shape[0] // rows, one, 0)


def fold_rows(place, part, out, parts, take):
    rows = out.shape[0] // parts
    core, half = place.core, place.half
    far, near = 2 * (1 - core) + (1 - half), 2 * (1 - core) + half
    beside = 2 * core + (1 - half)

    def task(p, from_core, from_half, held, mine, total, sent, came, local):
        at = pl.ds(p * rows, rows)
        first = remote(part.at[far, at], from_core.at[1], sent.at[0], came.at[0], place.partner())
        second = remote(part.at[near, at], from_core.at[0], sent.at[1], came.at[1], place.partner())
        third = remote(held, from_half, sent.at[2], came.at[2], place.across())
        load_held = pltpu.make_async_copy(part.at[beside, at], held, local.at[0])
        load_mine = pltpu.make_async_copy(part.at[place.group, at], mine, local.at[1])
        store = pltpu.make_async_copy(total, out.at[at], local.at[2])
        for copy in (first, load_held, second, load_mine):
            copy.start()
        yield
        first.wait_recv()
        load_held.wait()
        add_rows(held, held, from_core.at[1])
        third.start()
        yield
        second.wait_recv()
        load_mine.wait()
        third.wait_recv()
        add_rows(total, mine, from_core.at[0], from_half)
        store.start()
        yield
        for copy in (first, second, third):
            copy.wait_send()
        store.wait()

    return [task(p, *take(8)) for p in range(parts)]


ROW_PARTS = 3


def reduce_group_scratch(piece, dtype):
    return [
        pltpu.VMEM((2,) + piece, dtype),
        pltpu.VMEM(piece, dtype),
        pltpu.VMEM(piece, dtype),
        pltpu.SemaphoreType.DMA((3,)),
        pltpu.SemaphoreType.DMA((3,)),
    ]


def reduce_group(place, view, out, from_core, from_half, held, sent, came):
    if not callable(view):
        part = view
        view = lambda g: part.at[g]
    far = 2 * (1 - place.core) + (1 - place.half)
    near = 2 * (1 - place.core) + place.half
    first = remote(view(far), from_core.at[1], sent.at[0], came.at[0], place.partner())
    second = remote(view(near), from_core.at[0], sent.at[1], came.at[1], place.partner())
    first.start()
    second.start()
    yield
    first.wait_recv()
    add_into(held, view(2 * place.core + (1 - place.half)), from_core.at[1])
    third = remote(held, from_half, sent.at[2], came.at[2], place.across())
    third.start()
    yield
    second.wait_recv()
    third.wait_recv()
    add_into(out, view(place.group), from_core.at[0], from_half)
    first.wait_send()
    second.wait_send()
    third.wait_send()


def exchange_group_sems():
    return [pltpu.SemaphoreType.DMA((3,)), pltpu.SemaphoreType.DMA((4,)), pltpu.SemaphoreType.DMA]


def exchange_group(place, src, out, sent, came, own):
    mine = place.group
    copy = pltpu.make_async_copy(src.at[mine], out.at[mine], own)
    copy.start()
    core, half = place.core, place.half
    links = (
        (2 * (1 - core) + (1 - half), place.corner()),
        (2 * core + (1 - half), place.across()),
        (2 * (1 - core) + half, place.partner()),
    )
    copies = [
        remote(src.at[to], out.at[mine], sent.at[k], came.at[mine], device)
        for k, (to, device) in enumerate(links)
    ]
    for one in copies:
        one.start()
    yield
    for k, (peer, device) in enumerate(links):
        remote(src.at[peer], out.at[peer], sent.at[k], came.at[peer], device).wait_recv()
    for one in copies:
        one.wait_send()
    copy.wait()


def transfer(name, number, body, ins, outs, scratch, moved, out_spaces=None, in_spaces=None):
    spaces = out_spaces or [pl.ANY] * len(outs)
    in_spaces = in_spaces or [pltpu.VMEM] * len(ins)
    return pl.pallas_call(
        body,
        name=name,
        out_shape=outs,
        in_specs=[pl.BlockSpec(memory_space=space) for space in in_spaces],
        out_specs=[pl.BlockSpec(memory_space=space) for space in spaces],
        scratch_shapes=scratch,
        compiler_params=pltpu.CompilerParams(
            collective_id=number, has_side_effects=True, vmem_limit_bytes=VMEM_LIMIT
        ),
        cost_estimate=pl.CostEstimate(flops=0, bytes_accessed=moved * 40, transcendentals=0),
    )(*ins)


def shape(dims, dtype):
    return jax.ShapeDtypeStruct(tuple(dims), dtype)


def slabs(rows):
    return math.gcd(rows, 16)


def all_gather_blk(value, count, number):
    def body(src, out, *sems):
        place = Place(count)
        greet(place, blk=True)
        together(gather_blk(place, src, out, *sems))

    return transfer(
        f"gather{number}",
        number,
        body,
        [value],
        [shape((count,) + value.shape, value.dtype)],
        gather_blk_sems(count),
        value.size * 2 * count,
    )[0]


def reduce_scatter_blk(value, count, number):
    piece = value.shape[1:]

    def body(part, out, *scratch):
        place = Place(count)
        greet(place, blk=True)
        together(reduce_blk(place, part, out, *scratch))

    return transfer(
        f"reduce{number}",
        number,
        body,
        [value],
        [shape(piece, jnp.float32)],
        reduce_blk_scratch(count, piece, value.dtype),
        value.size * 2,
        [pltpu.VMEM],
    )[0]


class Taker:
    def __init__(self, refs):
        self.refs = list(refs)

    def __call__(self, amount):
        taken = self.refs[:amount]
        del self.refs[:amount]
        return taken


def gather_first(qkv, out_parts, tokens, gains, docs, down, count, number):
    names = 6

    def body(*refs):
        qkv_ref, out_ref, tok_ref, gain_ref, doc_ref, down_ref = refs[:names]
        qkv_all, out_mine, tok_all, gain_all, doc_all, down_all = refs[names : 2 * names]
        gain_mine = refs[2 * names]
        take = Taker(refs[2 * names + 1 :])
        place = Place(count)
        greet(place, blk=True, core=True, half=True, corner=True)

        def gain_task(near, far):
            yield from gather_blk(place, gain_ref, gain_mine, *near)
            yield from gather_group(place, gain_mine, gain_all, *far)

        def doc_task(sent, came, own):
            copy = pltpu.make_async_copy(doc_ref, doc_all.at[place.core], own)
            copy.start()
            send = remote(doc_ref, doc_all.at[place.core], sent, came, place.partner())
            send.start()
            yield
            remote(doc_ref, doc_all.at[1 - place.core], sent, came, place.partner()).wait_recv()
            send.wait_send()
            copy.wait()

        together(
            gain_task(take(3), take(3)),
            gather_blk(place, qkv_ref, qkv_all, *take(3)),
            doc_task(*take(3)),
            waiting(gather_group(place, tok_ref, tok_all, *take(3)), 2),
            waiting(exchange_group(place, out_ref, out_mine, *take(3)), 3),
            *(
                waiting(task, 2 + p, 4)
                for p, task in enumerate(
                    gather_group_rows(place, down_ref, down_all, ROW_PARTS, take)
                )
            ),
        )

    ins = [qkv, out_parts, tokens, gains, docs, down]
    return transfer(
        f"first{number}",
        number,
        body,
        ins,
        [
            shape((count,) + qkv.shape, qkv.dtype),
            shape(out_parts.shape, out_parts.dtype),
            shape((GROUPS,) + tokens.shape, tokens.dtype),
            shape((GROUPS, count) + gains.shape, gains.dtype),
            shape((2,) + docs.shape, docs.dtype),
            shape((GROUPS,) + down.shape, down.dtype),
        ],
        [pltpu.VMEM((count,) + gains.shape, gains.dtype)]
        + gather_blk_sems(count, 1)
        + gather_group_sems()
        + gather_blk_sems(count)
        + [pltpu.SemaphoreType.DMA] * 3
        + gather_group_sems()
        + exchange_group_sems()
        + gather_rows_scratch(down, ROW_PARTS),
        (qkv.size + out_parts.size) * 2 * count,
        None,
        [pltpu.VMEM] * 5 + [pl.ANY],
    )


def attend_step(count, g, here, key_half, key_at, q_ref, kv_ref, doc_ref, key_doc_ref, acc, tot):
    rows = q_ref.shape[1]
    sequence, half = g // 2, g % 2
    q2, position, doc = stacked_queries(g, half * count + here, q_ref, doc_ref)
    key_block = key_half * count + key_at
    at = pl.ds(pl.multiple_of((2 * sequence + key_half) * rows, rows), rows)
    kv = kv_ref.at[key_at, at]
    _, weights = attention_scores(
        q2, kv[:, :HEAD_DIM], position, doc, key_block, key_doc_ref[sequence, key_block], rows
    )
    tot[g] += jnp.sum(weights, axis=-1, keepdims=True)
    acc[g] += jnp.dot(
        weights.astype(jnp.bfloat16), kv[:, HEAD_DIM:], preferred_element_type=jnp.float32
    )


def stacked_queries(g, block, q_ref, doc_ref):
    rows = q_ref.shape[1]
    q2 = jnp.concatenate([q_ref[g, :, :HEAD_DIM], q_ref[g, :, HEAD_DIM:]], axis=0)
    inside = lax.broadcasted_iota(jnp.int32, (rows, 1), 0)
    position = block * rows + jnp.concatenate([inside, inside], axis=0)
    doc = jnp.concatenate([doc_ref[g], doc_ref[g]], axis=0)
    return q2, position, doc


def gather_attend(kv, out_mine, gate_up, queries, doc, key_doc, count, number):
    groups, out_rows, width = out_mine.shape
    rows = queries.shape[1]

    def body(*refs):
        kv_ref, out_ref, gate_up_ref, q_ref, doc_ref, key_doc_ref = refs[:6]
        kv_all, out_all, gate_up_all, attn_ref, full_ref, total_ref = refs[6:12]
        acc, tot = refs[12:14]
        take = Taker(refs[14:])
        place = Place(count)
        greet(place, blk=True, core=True, half=True)
        gathers = (
            GatherBlk(place, kv_ref, lambda i: kv_all.at[i], *take(3)),
            GatherBlk(place, out_ref, lambda i: out_all.at[:, i], *take(3)),
        )
        groups = gather_group_rows(place, gate_up_ref, gate_up_all, ROW_PARTS, take)
        for gather in gathers:
            gather.start()
        for task in groups:
            next(task)
        acc[...] = jnp.zeros_like(acc)
        tot[...] = jnp.zeros_like(tot)
        here, inner = place.here, place.inner

        def attend(k):
            def one(c, carry):
                key_at = place.near(k) * inner + c // 6
                sequence, kind = (c % 6) // 3, c % 3
                half = jnp.minimum(kind, 1)
                needed = jnp.where(kind == 1, key_at >= here, key_at <= here)

                @pl.when(needed)
                def _():
                    attend_step(
                        count,
                        2 * sequence + half,
                        here,
                        kind // 2,
                        key_at,
                        q_ref,
                        kv_all,
                        doc_ref,
                        key_doc_ref,
                        acc,
                        tot,
                    )

                return carry

            lax.fori_loop(0, inner * 6, one, 0)

        gathers[0].copy.wait()
        for k in range(place.outer):
            advance(gathers, k)
            gathers[0].beside_arrived(k)
            if 0 < k < place.outer - 1 and k <= 2:
                next(groups[k - 1])
            attend(k)

        def put(g, carry):
            total = tot[g]
            attended = acc[g] / total
            attended = jnp.concatenate([attended[:rows], attended[rows:]], axis=1)
            full_ref[g] = attended
            attn_ref[g] = attended.astype(jnp.bfloat16)
            total_ref[g] = total
            return carry

        lax.fori_loop(0, GROUPS, put, 0)
        next(groups[2])
        gathers[1].copy.wait()
        for k in range(place.outer):
            gathers[1].beside_arrived(k)
        for gather in gathers:
            gather.finish()
        together(*groups)

    return transfer(
        f"attend{number}",
        number,
        body,
        [kv, out_mine, gate_up, queries, doc, key_doc],
        [
            shape((count,) + kv.shape, kv.dtype),
            shape((groups, count, out_rows, width), out_mine.dtype),
            shape((GROUPS,) + gate_up.shape, gate_up.dtype),
            shape((GROUPS, rows, width), jnp.bfloat16),
            shape((GROUPS, rows, width), jnp.float32),
            shape((GROUPS, REPS * rows, 1), jnp.float32),
        ],
        [
            pltpu.VMEM((GROUPS, REPS * rows, HEAD_DIM), jnp.float32),
            pltpu.VMEM((GROUPS, REPS * rows, 1), jnp.float32),
        ]
        + gather_blk_sems(count)
        + gather_blk_sems(count)
        + gather_rows_scratch(gate_up, ROW_PARTS),
        (kv.size + out_mine.size) * 2 * count,
        [pltpu.VMEM, pl.ANY, pl.ANY, pltpu.VMEM, pltpu.VMEM, pltpu.VMEM],
        [pltpu.VMEM, pltpu.VMEM, pl.ANY, pltpu.VMEM, pltpu.VMEM, pltpu.VMEM],
    )


def attend_back_block(
    count, g, here, q_ref, kv_ref, doc_ref, key_doc_ref, grad_ref, full_ref, total_ref, dq_ref, key_acc
):
    rows = q_ref.shape[1]
    sequence, half = g // 2, g % 2
    block = half * count + here
    q2, position, doc = stacked_queries(g, block, q_ref, doc_ref)
    total = total_ref[g]
    grad = grad_ref[g].astype(jnp.float32)
    grad2 = jnp.concatenate([grad[:, :HEAD_DIM], grad[:, HEAD_DIM:]], axis=0)
    full2 = jnp.concatenate([full_ref[g, :, :HEAD_DIM], full_ref[g, :, HEAD_DIM:]], axis=0)
    total_grad = -jnp.sum(grad2 * full2, axis=-1, keepdims=True) / total
    sums_grad = (grad2 / total).astype(jnp.bfloat16)

    def one(key_block, acc):
        key_half = (key_block >= count).astype(jnp.int32)
        inner = key_block - key_half * count
        at = pl.ds(pl.multiple_of((2 * sequence + key_half) * rows, rows), rows)
        kv = kv_ref.at[inner, at]
        keys = kv[:, :HEAD_DIM]
        capped, weights = attention_scores(
            q2, keys, position, doc, key_block, key_doc_ref[sequence, key_block], rows
        )
        exp_grad = dot(sums_grad, kv[:, HEAD_DIM:], LAST)
        raw_grad = (
            weights * (exp_grad + total_grad) * (1.0 - capped * capped) * SCORE_SCALE
        ).astype(jnp.bfloat16)
        slot = inner * 2 + key_half
        key_acc[slot, :, :HEAD_DIM] += dot(raw_grad, q2, FIRST)
        key_acc[slot, :, HEAD_DIM:] += dot(weights.astype(jnp.bfloat16), sums_grad, FIRST)
        return acc + dot(raw_grad, keys, PLAIN)

    dq = lax.fori_loop(
        jnp.maximum(block - count, 0),
        block + 1,
        one,
        jnp.zeros((REPS * rows, HEAD_DIM), jnp.float32),
    )
    dq_ref[g] = jnp.concatenate([dq[:rows], dq[rows:]], axis=1).astype(jnp.bfloat16)


def attend_back_fits(count):
    return count == 8


def attend_back_reduce(
    queries, kv, doc, key_doc, grad, full, totals, out_part, gate_up_part, kv_piece, count, number
):
    out_piece = out_part.shape[:1] + out_part.shape[2:]
    gate_up_piece = gate_up_part.shape[1:]
    rows = queries.shape[1]
    steps = rows // kv_piece[1]
    bf16 = jnp.bfloat16

    def body(*refs):
        q_ref, kv_ref, doc_ref, key_doc_ref, grad_ref, full_ref, total_ref = refs[:7]
        out_ref, gate_up_ref = refs[7:9]
        dq_ref, dkv_sum, out_sum, gate_up_sum, dkv_part, key_acc = refs[9:15]
        take = Taker(refs[15:])
        place = Place(count)
        greet(place, blk=True, core=True, half=True)
        dkv = ReduceBlk(place, lambda i: dkv_part.at[i], dkv_sum, *take(REDUCE_REFS))
        out = ReduceBlk(place, lambda i: out_ref.at[:, i], out_sum, *take(REDUCE_REFS))
        folds = fold_rows(place, gate_up_ref, gate_up_sum, ROW_PARTS, take)
        out_events = out.events()

        def back(g):
            attend_back_block(
                count,
                g,
                place.here,
                q_ref,
                kv_ref,
                doc_ref,
                key_doc_ref,
                grad_ref,
                full_ref,
                total_ref,
                dq_ref,
                key_acc,
            )

        def clear(i, carry):
            key_acc[i] = jnp.zeros(key_acc.shape[1:], jnp.float32)
            return carry

        def put(sequence):
            def one(i, carry):
                for k in (0, 1):
                    value = key_acc[i * 2 + k].astype(bf16).reshape((steps,) + kv_piece[1:])
                    dkv_part[i, pl.ds((2 * sequence + k) * steps, steps)] = value
                return carry

            lax.fori_loop(0, count, one, 0)

        ends = jnp.logical_not(out.middle)

        turning = out.turning()

        def middle(*steps):
            @pl.when(out.middle)
            def _():
                for step in steps:
                    if isinstance(step, int):
                        turning[step]()
                    else:
                        out.pass_on(*step, True)

        def outside(*steps):
            @pl.when(ends)
            def _():
                for step in steps:
                    out.pass_on(*step, False)

        out.start()
        for fold in folds:
            next(fold)
        lax.fori_loop(0, 2 * count, clear, 0)
        back(0)
        next(folds[0])
        middle(0)
        back(1)
        put(0)
        middle(1, 2)
        outside((0, 0), (1, 0), (1, 1))
        next(folds[1])
        lax.fori_loop(0, 2 * count, clear, 0)
        back(2)
        outside((2, 0), (2, 1))
        middle((0, 0))
        back(3)
        put(1)
        middle((1, 0), (1, 1), (2, 0), (2, 1))
        dkv.start()
        dkv_events = dkv.events()
        order = [(folds, 2), (dkv_events, 0), (dkv_events, 1), (dkv_events, 2)]
        order += [(out_events, 8), (out_events, 9), (dkv_events, 3), (dkv_events, 4)]
        order += [(folds, 0), (dkv_events, 5), (dkv_events, 6), (folds, 1)]
        order += [(dkv_events, 7), (dkv_events, 8), (dkv_events, 9), (folds, 2)]
        for events, i in order:
            if events is folds:
                next(folds[i])
            else:
                events[i]()
        out.finish()
        dkv.finish()
        together(*folds)

    vmem = pltpu.VMEM
    return transfer(
        f"attend_back{number}",
        number,
        body,
        [queries, kv, doc, key_doc, grad, full, totals, out_part, gate_up_part],
        [
            shape(queries.shape, bf16),
            shape(kv_piece, bf16),
            shape(out_piece, bf16),
            shape(gate_up_piece, jnp.float32),
        ],
        [
            vmem((count,) + kv_piece, bf16),
            vmem((2 * count, rows, 2 * HEAD_DIM), jnp.float32),
        ]
        + reduce_blk_scratch(count, kv_piece, bf16)
        + reduce_blk_scratch(count, out_piece, bf16)
        + fold_rows_scratch(gate_up_piece, ROW_PARTS),
        (kv.size + out_part.size) * 2,
        [vmem, vmem, vmem, pl.ANY],
        [vmem] * 8 + [pl.ANY],
    )


def reduce_middle(dkv_part, out_part, gate_up_part, count, number):
    dkv_piece = dkv_part.shape[1:]
    out_piece = out_part.shape[:1] + out_part.shape[2:]

    gate_up_piece = gate_up_part.shape[1:]

    def body(dkv_ref, out_ref, gate_up_ref, dkv_sum, out_sum, gate_up_sum, *scratch):
        take = Taker(scratch)
        place = Place(count)
        greet(place, blk=True, core=True, half=True)
        together(
            reduce_blk(place, dkv_ref, dkv_sum, *take(REDUCE_REFS)),
            reduce_blk(place, lambda i: out_ref.at[:, i], out_sum, *take(REDUCE_REFS)),
            *(
                waiting(task, *rounds)
                for rounds, task in zip(
                    ((6, 5, 5), (8, 5, 3), (10, 6, 0)),
                    fold_rows(place, gate_up_ref, gate_up_sum, ROW_PARTS, take),
                )
            ),
        )

    return transfer(
        f"reduce{number}",
        number,
        body,
        [dkv_part, out_part, gate_up_part],
        [
            shape(dkv_piece, jnp.bfloat16),
            shape(out_piece, jnp.bfloat16),
            shape(gate_up_piece, jnp.float32),
        ],
        reduce_blk_scratch(count, dkv_piece, jnp.bfloat16)
        + reduce_blk_scratch(count, out_piece, jnp.bfloat16)
        + fold_rows_scratch(gate_up_piece, ROW_PARTS),
        (dkv_part.size + out_part.size) * 2,
        [pltpu.VMEM, pltpu.VMEM, pl.ANY],
        [pltpu.VMEM, pltpu.VMEM, pl.ANY],
    )


def reduce_last(qkv_part, norm_part, gain_part, out_sum, down_part, count, number):
    gain_piece = gain_part.shape[1:]
    qkv_piece, norm_piece = qkv_part.shape[1:], norm_part.shape[1:]

    def body(*refs):
        qkv_ref, norm_ref, gain_ref, out_ref, down_ref = refs[:5]
        qkv_sum, norm_sum, gain_sum, out_all, down_sum = refs[5:10]
        gain_mine = refs[10]
        take = Taker(refs[11:])
        place = Place(count)
        greet(place, blk=True, core=True, half=True, corner=True)

        def gain_task(near, far):
            yield from reduce_blk(place, gain_ref, gain_mine, *near)
            yield from reduce_group(place, gain_mine, gain_sum, *far)

        main = reduce_blk(place, qkv_ref, qkv_sum, *take(REDUCE_REFS))
        gain = gain_task(take(REDUCE_REFS), take(5))
        together(
            waiting(gain, 11),
            main,
            waiting(exchange_group(place, out_ref, out_all, *take(3)), 16),
            waiting(reduce_group(place, norm_ref, norm_sum, *take(5)), 7, 9),
            *(
                waiting(task, *rounds)
                for rounds, task in zip(
                    ((7, 7, 2), (8, 8, 0), (9, 9, 0)),
                    fold_rows(place, down_ref, down_sum, ROW_PARTS, take),
                )
            ),
        )

    return transfer(
        f"last{number}",
        number,
        body,
        [qkv_part, norm_part, gain_part, out_sum, down_part],
        [
            shape(qkv_piece, jnp.float32),
            shape(norm_piece, jnp.float32),
            shape(gain_piece[1:], jnp.float32),
            shape(out_sum.shape, jnp.bfloat16),
            shape(down_part.shape[1:], jnp.float32),
        ],
        [pltpu.VMEM(gain_piece, jnp.float32)]
        + reduce_blk_scratch(count, qkv_piece, jnp.bfloat16)
        + reduce_blk_scratch(count, gain_piece, jnp.float32, 1)
        + reduce_group_scratch(gain_piece[1:], jnp.float32)
        + exchange_group_sems()
        + reduce_group_scratch(norm_piece, jnp.bfloat16)
        + fold_rows_scratch(down_part.shape[1:], ROW_PARTS),
        qkv_part.size * 2,
        [pltpu.VMEM] * 4 + [pl.ANY],
        [pltpu.VMEM] * 4 + [pl.ANY],
    )


GROUP_PARTS = 4


def all_gather_group(value, number):
    parts = GROUP_PARTS

    def body(src, out, *sems):
        place = Place(lax.axis_size("blk"))
        greet(place, core=True, half=True)
        together(*gather_group_rows(place, src, out, parts, Taker(sems), False))

    return transfer(
        f"group{number}",
        number,
        body,
        [value],
        [shape((GROUPS,) + value.shape, value.dtype)],
        gather_group_sems() * parts,
        value.size * 8,
    )[0]


def reduce_scatter_group(value, number):
    piece = value.shape[1:]
    parts = GROUP_PARTS
    steps = piece[0] // parts

    def body(part, out, *scratch):
        take = Taker(scratch)
        place = Place(lax.axis_size("blk"))
        greet(place, core=True, half=True)

        def task(p):
            at = pl.ds(p * steps, steps)
            return reduce_group(place, lambda g: part.at[g, at], out.at[at], *take(5))

        together(*[task(p) for p in range(parts)])

    return transfer(
        f"fold{number}",
        number,
        body,
        [value],
        [shape(piece, jnp.float32)],
        reduce_group_scratch((steps,) + piece[1:], value.dtype) * parts,
        value.size * 2,
        [pltpu.VMEM],
    )[0]


def dot(left, right, contract):
    return lax.dot_general(left, right, (contract, ((), ())), preferred_element_type=jnp.float32)


LAST = ((1,), (1,))
PLAIN = ((1,), (0,))
FIRST = ((0,), (0,))


LANES = 128
GELU_A = math.sqrt(2.0 / math.pi)
GELU_B = 0.044715


def feed_forward_fits(count, rows, width, hidden):
    inner = 4 if count >= 32 else 2
    outer = count // inner
    tile = rows * width * 2
    weights = 3 * hidden * width * 2
    kept = count * rows * 3 * hidden * 2
    total = weights + kept + tile * (3 * count + outer * (inner - 1) + 2 * outer + 3) + 9 * tile
    total += 3 * LANES * (count * rows + 2 * width) * 2
    return total < 58 * 2**20 and hidden % (3 * LANES) == 0 and width % 256 == 0


def feed_forward_kernel(
    count,
    branch_ref,
    token_ref,
    cot_ref,
    gain_ref,
    gate_up_hbm,
    down_hbm,
    out_ref,
    middle_grad_ref,
    branch_grad_ref,
    gain_grad_ref,
    gate_up_grad_hbm,
    down_grad_hbm,
    w_gate_up,
    w_down,
    norm_all,
    grad_all,
    act,
    hidden,
    part,
    middle,
    norm_own,
    grad_own,
    total,
    turned,
    staged,
    beside,
    along,
    held,
    spare,
    w_sems,
    out_sems,
    *sems,
):
    place = Place(count)
    rows, width = norm_all.shape[1:]
    units = hidden.shape[1]
    chunks = units // LANES
    inner, outer = place.inner, place.outer
    slab = branch_ref.shape[1]
    steps = rows // slab
    columns = width // 256
    pair = inner * rows
    take = Taker(sems)

    def weight_copies(i):
        units_at = pl.ds(pl.multiple_of(i * LANES, LANES), LANES)
        return [
            pltpu.make_async_copy(
                gate_up_hbm.at[units_at, pl.ds(0, width)],
                w_gate_up.at[i, pl.ds(0, LANES)],
                w_sems.at[3 * i],
            ),
            pltpu.make_async_copy(
                gate_up_hbm.at[units_at, pl.ds(width, width)],
                w_gate_up.at[i, pl.ds(LANES, LANES)],
                w_sems.at[3 * i + 1],
            ),
            pltpu.make_async_copy(down_hbm.at[units_at], w_down.at[units_at], w_sems.at[3 * i + 2]),
        ]

    def start_weights(i, carry):
        for copy in weight_copies(i):
            copy.start()
        return carry

    def wait_weights(i, carry):
        for copy in weight_copies(i):
            copy.wait()
        return carry

    lax.fori_loop(0, chunks, start_weights, 0)

    def scale_of(values):
        return lax.rsqrt(jnp.mean(values * values, axis=-1, keepdims=True) + NORM_EPS)

    def slab_rows(i):
        return pl.ds(pl.multiple_of(i * slab, slab), slab)

    def before(i, carry):
        value = branch_ref[i]
        mid = token_ref[i].astype(jnp.float32) + value * scale_of(value) * gain_ref[1:2]
        middle[i] = mid
        norm_own[slab_rows(i)] = (mid * scale_of(mid) * gain_ref[2:3]).astype(jnp.bfloat16)
        return carry

    lax.fori_loop(0, steps, before, 0)
    greet(place, blk=True)

    def pair_rows(k):
        return pl.ds(pl.multiple_of(place.near(k) * pair, pair), pair)

    def pair_pieces(k):
        return pl.ds(place.near(k) * inner, inner)

    def column(n):
        return pl.ds(pl.multiple_of(n * 256, 256), 256)

    def put_part(k, n, value):
        split = value.astype(jnp.bfloat16).reshape((inner, steps, slab, 256))
        part[pair_pieces(k), :, :, column(n)] = split

    def receive(gather, k):
        if k == 0:
            gather.copy.wait()
        advance([gather], k)
        gather.beside_arrived(k)

    gather = GatherBlk(place, norm_own, lambda i: norm_all.at[i], *take(3))
    gather.start()
    lax.fori_loop(0, chunks, wait_weights, 0)
    for k in range(outer):
        receive(gather, k)
        at = pair_rows(k)

        def up_chunk(j, carry, k=k, at=at):
            x = norm_all[pair_pieces(k)].reshape(pair, width)
            both = dot(x, w_gate_up[j], LAST)
            act[at, column(j)] = both.astype(jnp.bfloat16)
            gate, up = both[:, :LANES], both[:, LANES:]
            bent = 0.5 * gate * (1.0 + jnp.tanh(GELU_A * (gate + GELU_B * (gate * gate * gate))))
            hidden[at, pl.ds(pl.multiple_of(j * LANES, LANES), LANES)] = (bent * up).astype(
                jnp.bfloat16
            )
            return carry

        lax.fori_loop(0, chunks, up_chunk, 0)

        def down_chunk(n, carry, k=k, at=at):
            put_part(k, n, dot(hidden[at, :], w_down[:, column(n)], PLAIN))
            return carry

        lax.fori_loop(0, columns, down_chunk, 0)
    gather.finish()
    reduce = ReduceBlk(place, lambda i: part.at[i], total, beside, along, held, spare, *take(6))
    reduce.start()
    for event in reduce.events():
        event()

    gain_grad_ref[...] = jnp.zeros_like(gain_grad_ref)

    def norm_back(value, gain, incoming):
        scale = scale_of(value)
        lifted = incoming * gain
        pull = jnp.mean(lifted * value, axis=-1, keepdims=True)
        gain_grad = jnp.sum(incoming * value * scale, axis=0, keepdims=True)
        return scale * lifted - value * (scale * scale * scale) * pull, gain_grad

    def between(i, carry):
        value, cot = total[i], cot_ref[i].astype(jnp.float32)
        gain = gain_ref[3:4]
        out_ref[i] = (middle[i] + value * scale_of(value) * gain).astype(jnp.bfloat16)
        grad, gain_grad = norm_back(value, gain, cot)
        gain_grad_ref[3:4] += gain_grad
        grad_own[slab_rows(i)] = grad.astype(jnp.bfloat16)
        return carry

    lax.fori_loop(0, steps, between, 0)
    reduce.finish()

    gather = GatherBlk(place, grad_own, lambda i: grad_all.at[i], *take(3))
    gather.start()
    for k in range(outer):
        receive(gather, k)
        at = pair_rows(k)

        def back_chunk(j, carry, k=k, at=at):
            g = grad_all[pair_pieces(k)].reshape(pair, width)
            units_at = pl.ds(pl.multiple_of(j * LANES, LANES), LANES)
            grad = dot(g, w_down[units_at], LAST)
            both = act[at, column(j)].astype(jnp.float32)
            gate, up = both[:, :LANES], both[:, LANES:]
            bend = jnp.tanh(GELU_A * (gate + GELU_B * (gate * gate * gate)))
            bent = 0.5 * gate * (1.0 + bend)
            slope = 0.5 * (1.0 + bend) + (0.5 * GELU_A) * gate * (1.0 - bend * bend) * (
                1.0 + (3.0 * GELU_B) * gate * gate
            )
            pulled = jnp.concatenate([grad * up * slope, grad * bent], axis=1)
            act[at, column(j)] = pulled.astype(jnp.bfloat16)
            return carry

        lax.fori_loop(0, chunks, back_chunk, 0)

        def input_chunk(n, carry, k=k, at=at):
            w = w_gate_up[:, :, column(n)].reshape(2 * units, 256)
            put_part(k, n, dot(act[at, :], w, PLAIN))
            return carry

        lax.fori_loop(0, columns, input_chunk, 0)
    gather.finish()
    reduce = ReduceBlk(place, lambda i: part.at[i], total, beside, along, held, spare, *take(6))
    reduce.start()

    tokens = count * rows
    slots = staged.shape[0]

    def up_store(i):
        slot = lax.rem(i, slots)
        units_at = pl.ds(pl.multiple_of(i * LANES, LANES), LANES)
        return [
            pltpu.make_async_copy(
                staged.at[slot, pl.ds(h * LANES, LANES)],
                gate_up_grad_hbm.at[units_at, pl.ds(h * width, width)],
                out_sems.at[slot, h],
            )
            for h in (0, 1)
        ]

    def up_grad(i, carry):
        @pl.when(i >= slots)
        def _():
            for copy in up_store(i - slots):
                copy.wait()

        turned[pl.ds(0, 256)] = jnp.transpose(act[:, column(i)])

        def one(n, c):
            x = norm_all[:, :, column(n)].reshape(tokens, 256)
            staged[lax.rem(i, slots), pl.ds(0, 256), column(n)] = dot(
                turned[pl.ds(0, 256)], x, PLAIN
            ).astype(jnp.bfloat16)
            return c

        lax.fori_loop(0, columns, one, 0)
        for copy in up_store(i):
            copy.start()
        return carry

    three = 3 * LANES

    def down_store(i):
        slot = lax.rem(i, slots)
        return pltpu.make_async_copy(
            staged.at[slot],
            down_grad_hbm.at[pl.ds(pl.multiple_of(i * three, three), three)],
            out_sems.at[slot, 2],
        )

    def down_grad(i, carry):
        @pl.when(i >= slots)
        def _():
            down_store(i - slots).wait()

        turned[...] = jnp.transpose(hidden[:, pl.ds(pl.multiple_of(i * three, three), three)])

        def one(n, c):
            x = grad_all[:, :, column(n)].reshape(tokens, 256)
            staged[lax.rem(i, slots), :, column(n)] = dot(turned[...], x, PLAIN).astype(jnp.bfloat16)
            return c

        lax.fori_loop(0, columns, one, 0)
        down_store(i).start()
        return carry

    events = reduce.events()
    early = len(events) - 3
    bounds = [chunks * k // early for k in range(early + 1)]
    for k in range(early):
        lax.fori_loop(bounds[k], bounds[k + 1], up_grad, 0)
        events[k]()
    for i in range(max(0, chunks - slots), chunks):
        for copy in up_store(i):
            copy.wait()
    thirds = units // three
    bounds = [thirds * k // 3 for k in range(4)]
    for k in range(3):
        lax.fori_loop(bounds[k], bounds[k + 1], down_grad, 0)
        events[early + k]()

    def after(i, carry):
        value, mid, cot = branch_ref[i], middle[i], cot_ref[i].astype(jnp.float32)
        grad, gain_grad = norm_back(mid, gain_ref[2:3], total[i])
        gain_grad_ref[2:3] += gain_grad
        middle_grad = cot + grad
        middle_grad_ref[i] = middle_grad
        grad, gain_grad = norm_back(value, gain_ref[1:2], middle_grad)
        gain_grad_ref[1:2] += gain_grad
        branch_grad_ref[i] = grad.astype(jnp.bfloat16)
        return carry

    lax.fori_loop(0, steps, after, 0)
    reduce.finish()
    for i in range(max(0, thirds - slots), thirds):
        down_store(i).wait()


def feed_forward(branch, tokens, cotangent, gains, gate_up_all, down_all, count, number):
    steps, slab, width = branch.shape
    rows = steps * slab
    units = down_all.shape[0]
    inner = 4 if count >= 32 else 2
    outer = count // inner
    piece = branch.shape
    bf16, f32 = jnp.bfloat16, jnp.float32
    vmem = pl.BlockSpec(memory_space=pltpu.VMEM)
    anywhere = pl.BlockSpec(memory_space=pl.ANY)
    slots = 2
    line_scratch = reduce_blk_scratch(count, piece, bf16)
    return pl.pallas_call(
        functools.partial(feed_forward_kernel, count),
        name="feed_forward",
        out_shape=[
            shape(piece, bf16),
            shape(piece, f32),
            shape(piece, bf16),
            shape((4, width), f32),
            shape(gate_up_all.shape, bf16),
            shape(down_all.shape, bf16),
        ],
        in_specs=[vmem] * 4 + [anywhere] * 2,
        out_specs=[vmem] * 4 + [anywhere] * 2,
        scratch_shapes=[
            pltpu.VMEM((units // LANES, 2 * LANES, width), bf16),
            pltpu.VMEM((units, width), bf16),
            pltpu.VMEM((count, rows, width), bf16),
            pltpu.VMEM((count, rows, width), bf16),
            pltpu.VMEM((count * rows, 2 * units), bf16),
            pltpu.VMEM((count * rows, units), bf16),
            pltpu.VMEM((count,) + piece, bf16),
            pltpu.VMEM(piece, f32),
            pltpu.VMEM((rows, width), bf16),
            pltpu.VMEM((rows, width), bf16),
            pltpu.VMEM(piece, f32),
            pltpu.VMEM((3 * LANES, count * rows), bf16),
            pltpu.VMEM((slots, 3 * LANES, width), bf16),
        ]
        + line_scratch[:4]
        + [
            pltpu.SemaphoreType.DMA((3 * units // LANES,)),
            pltpu.SemaphoreType.DMA((slots, 3)),
        ]
        + gather_blk_sems(count)
        + line_scratch[4:]
        + gather_blk_sems(count)
        + line_scratch[4:],
        compiler_params=pltpu.CompilerParams(
            collective_id=number, has_side_effects=True, vmem_limit_bytes=67043328
        ),
        cost_estimate=pl.CostEstimate(
            flops=18 * count * rows * units * width,
            bytes_accessed=500 * 2**20,
            transcendentals=0,
        ),
    )(branch, tokens, cotangent, gains, gate_up_all, down_all)


def attention_scores(q2, k, query_pos, query_doc, key_block, key_doc, rows):
    raw = lax.dot_general(q2, k, (((1,), (1,)), ((), ())), preferred_element_type=jnp.float32)
    capped = jnp.tanh(raw * (SCORE_SCALE / SOFT_CAP))
    key_pos = key_block * rows + lax.broadcasted_iota(jnp.int32, (1, rows), 1)
    visible = (key_pos <= query_pos) & (key_doc == query_doc)
    return capped, jnp.where(visible, jnp.exp(SOFT_CAP * capped), 0.0)


def attention_query(q_ref, doc_ref, here, count, rows):
    half = pl.program_id(1)
    block = half * count + here
    q2 = jnp.concatenate([q_ref[0, :, :HEAD_DIM], q_ref[0, :, HEAD_DIM:]], axis=0)
    inside = lax.broadcasted_iota(jnp.int32, (rows, 1), 0)
    position = block * rows + jnp.concatenate([inside, inside], axis=0)
    doc = jnp.concatenate([doc_ref[0], doc_ref[0]], axis=0)
    return block, q2, position, doc


def attention_backward_kernel(
    count,
    here_ref,
    q_ref,
    kv_ref,
    doc_ref,
    key_doc_ref,
    grad_ref,
    full_ref,
    total_ref,
    dq_ref,
    dkv_ref,
    acc,
    key_acc,
):
    rows = q_ref.shape[1]
    half = pl.program_id(1)
    block, q2, position, doc = attention_query(q_ref, doc_ref, here_ref[0], count, rows)
    total = total_ref[0]
    grad = grad_ref[0].astype(jnp.float32)
    grad2 = jnp.concatenate([grad[:, :HEAD_DIM], grad[:, HEAD_DIM:]], axis=0)
    full2 = jnp.concatenate([full_ref[0, :, :HEAD_DIM], full_ref[0, :, HEAD_DIM:]], axis=0)
    total_grad = -jnp.sum(grad2 * full2, axis=-1, keepdims=True) / total
    sums_grad = (grad2 / total).astype(jnp.bfloat16)
    acc[...] = jnp.zeros_like(acc)

    @pl.when(half == 0)
    def _():
        def clear(i, carry):
            key_acc[i] = jnp.zeros(key_acc.shape[1:], jnp.float32)
            return carry

        lax.fori_loop(0, key_acc.shape[0], clear, 0)

    def one(key_block, carry):
        key_half = (key_block >= count).astype(jnp.int32)
        inner = key_block - key_half * count
        kv = kv_ref.at[inner, key_half]
        keys = kv[:, :HEAD_DIM]
        capped, weights = attention_scores(
            q2, keys, position, doc, key_block, key_doc_ref[0, key_block], rows
        )
        exp_grad = lax.dot_general(
            sums_grad, kv[:, HEAD_DIM:], (((1,), (1,)), ((), ())), preferred_element_type=jnp.float32
        )
        raw_grad = (
            weights * (exp_grad + total_grad) * (1.0 - capped * capped) * SCORE_SCALE
        ).astype(jnp.bfloat16)
        acc[...] += jnp.dot(raw_grad, keys, preferred_element_type=jnp.float32)
        over_rows = (((0,), (0,)), ((), ()))
        slot = inner * 2 + key_half
        key_acc[slot, :, :HEAD_DIM] += lax.dot_general(
            raw_grad, q2, over_rows, preferred_element_type=jnp.float32
        )
        key_acc[slot, :, HEAD_DIM:] += lax.dot_general(
            weights.astype(jnp.bfloat16), sums_grad, over_rows, preferred_element_type=jnp.float32
        )
        return carry

    lax.fori_loop(jnp.maximum(block - count, 0), block + 1, one, 0)
    dq = acc[...]
    dq_ref[0] = jnp.concatenate([dq[:rows], dq[rows:]], axis=1).astype(jnp.bfloat16)

    @pl.when(half == 1)
    def _():
        def put(i, carry):
            for k in (0, 1):
                dkv_ref[i, k] = key_acc[i * 2 + k].astype(jnp.bfloat16)
            return carry

        lax.fori_loop(0, count, put, 0)


def attention_specs(count, rows, width):
    query = pl.BlockSpec((1, rows, width), lambda s, h, here: (2 * s + h, 0, 0))
    keys = pl.BlockSpec((count, 2, rows, 2 * HEAD_DIM), lambda s, h, here: (0, s, 0, 0))
    doc = pl.BlockSpec((1, rows, 1), lambda s, h, here: (2 * s + h, 0, 0))
    key_doc = pl.BlockSpec((1, 2 * count, 1, rows), lambda s, h, here: (s, 0, 0, 0))
    total = pl.BlockSpec((1, REPS * rows, 1), lambda s, h, here: (2 * s + h, 0, 0))
    return query, keys, doc, key_doc, total


def attention_backward(here, q, kv, doc, key_doc, grad, full, totals):
    count, _, rows, _ = kv.shape
    width = REPS * HEAD_DIM
    query, keys, doc_spec, key_doc_spec, total = attention_specs(count, rows, width)
    return pl.pallas_call(
        functools.partial(attention_backward_kernel, count),
        name="attend_back",
        grid_spec=pltpu.PrefetchScalarGridSpec(
            num_scalar_prefetch=1,
            grid=(2, 2),
            in_specs=[query, keys, doc_spec, key_doc_spec, query, query, total],
            out_specs=[query, keys],
            scratch_shapes=[
                pltpu.VMEM((REPS * rows, HEAD_DIM), jnp.float32),
                pltpu.VMEM((2 * count, rows, 2 * HEAD_DIM), jnp.float32),
            ],
        ),
        out_shape=[shape((GROUPS, rows, width), jnp.bfloat16), shape(kv.shape, jnp.bfloat16)],
        compiler_params=pltpu.CompilerParams(vmem_limit_bytes=VMEM_LIMIT),
        cost_estimate=pl.CostEstimate(flops=2 * 10**9, bytes_accessed=80 * 2**20, transcendentals=0),
    )(here, q, kv, doc, key_doc, grad, full, totals)


def rms_scale(values, gain_row):
    return (
        values * lax.rsqrt(jnp.mean(values * values, axis=-1, keepdims=True) + NORM_EPS) * gain_row
    )


def gelu_tanh(values):
    return jax.nn.gelu(values, approximate=True)


def rope_tables(positions):
    half_width = HEAD_DIM // 2
    frequency = jnp.exp(
        jnp.arange(half_width, dtype=jnp.float32) * (-2.0 * math.log(ROPE_BASE) / HEAD_DIM)
    )
    angles = positions.astype(jnp.float32)[:, None] * frequency[None, :]
    cosine = jnp.concatenate([jnp.cos(angles), jnp.cos(angles)], axis=-1)
    sine = jnp.concatenate([jnp.sin(angles), jnp.sin(angles)], axis=-1)
    return cosine[:, None, :], sine[:, None, :]


def rotate(values, cosine, sine):
    half_width = HEAD_DIM // 2
    turned = jnp.concatenate([-values[..., half_width:], values[..., :half_width]], axis=-1)
    return values * cosine + turned * sine


def feed_forward_apart(
    branch_slabs, inputs, cotangent, gains, gate_up_all, down_all, count, piece
):
    rows, width = inputs.shape
    bf16 = jnp.bfloat16
    branch = branch_slabs.reshape(rows, width)
    middle = inputs + rms_scale(branch, gains[1])
    norm_three = rms_scale(middle, gains[2]).astype(bf16)
    gate_all = gate_up_all[:, :width]
    up_all = gate_up_all[:, width:]
    norm_all = all_gather_blk(norm_three, count, 4).reshape(count * rows, width)
    gate = dot(norm_all, gate_all, LAST)
    up = dot(norm_all, up_all, LAST)
    hidden = (gelu_tanh(gate) * up).astype(bf16)
    ffn_part = dot(hidden, down_all, PLAIN).astype(bf16)
    ffn_out = reduce_scatter_blk(ffn_part.reshape((count,) + piece), count, 5).reshape(rows, width)
    output = (middle + rms_scale(ffn_out, gains[3])).astype(bf16)[None]

    out_cotangent = cotangent[0].astype(jnp.float32)
    _, post_ffn_back = jax.vjp(rms_scale, ffn_out, gains[3])
    ffn_grad, gain_grad_four = post_ffn_back(out_cotangent)
    grad_all = all_gather_blk(ffn_grad.astype(bf16), count, 6).reshape(count * rows, width)
    activated, gelu_back = jax.vjp(gelu_tanh, gate)
    hidden_grad = dot(grad_all, down_all, LAST)
    gate_grad = gelu_back(hidden_grad * up)[0].astype(bf16)
    up_grad = (hidden_grad * activated).astype(bf16)
    norm_part = dot(gate_grad, gate_all, PLAIN) + dot(up_grad, up_all, PLAIN)
    norm_three_grad = reduce_scatter_blk(
        norm_part.astype(bf16).reshape((count,) + piece), count, 7
    ).reshape(rows, width)
    down_part = dot(hidden, grad_all, FIRST).astype(bf16)
    gate_up_part = jnp.concatenate(
        [dot(gate_grad, norm_all, FIRST), dot(up_grad, norm_all, FIRST)], axis=1
    ).astype(bf16)
    _, pre_ffn_back = jax.vjp(rms_scale, middle, gains[2])
    middle_part, gain_grad_three = pre_ffn_back(norm_three_grad)
    middle_grad = out_cotangent + middle_part
    _, post_attn_back = jax.vjp(rms_scale, branch, gains[1])
    branch_grad, gain_grad_two = post_attn_back(middle_grad)
    return (
        output,
        middle_grad,
        branch_grad.astype(bf16),
        gain_grad_two,
        gain_grad_three,
        gain_grad_four,
        gate_up_part,
        down_part,
    )


def shards(
    tokens, cotangent, segments, norm_gains, qkv_weight, out_weight, gate_up_weight, down_weight
):
    _, rows, width = tokens.shape
    count = lax.axis_size("blk")
    here = lax.axis_index("blk")
    mine = 2 * lax.axis_index("dp") + lax.axis_index("head")
    group_rows = GROUPS * rows
    head_width = REPS * HEAD_DIM
    bf16 = jnp.bfloat16
    slab = slabs(rows)
    piece = (rows // slab, slab, width)

    gain_rows = norm_gains.shape[0]
    gain_lanes = -(-gain_rows // 128) * 128
    gains_sent = jnp.pad(
        jnp.transpose(norm_gains).astype(jnp.float32), ((0, 4), (0, gain_lanes - gain_rows))
    )
    out_rows = out_weight.shape[0]
    out_sent = jnp.transpose(out_weight.reshape(out_rows, GROUPS, head_width), (1, 0, 2))
    qkv_rows = qkv_weight.shape[0]
    qkv_slab = slabs(qkv_rows)
    qkv_piece = (qkv_rows // qkv_slab, qkv_slab, width)
    qkv_all, out_mine, tokens_all, gains_all, docs_all, down_all = gather_first(
        qkv_weight,
        out_sent,
        tokens[0],
        gains_sent,
        segments.reshape(-1, 128),
        down_weight,
        count,
        1,
    )
    down_all = down_all.reshape(-1, width)
    gains = jnp.transpose(gains_all[:, :, :4, :gain_rows], (2, 0, 1, 3)).reshape(4, width)
    qkv_head = qkv_all.reshape(count * qkv_rows, width)
    docs = docs_all.reshape(2, 2, count, rows)
    key_doc = docs.reshape(2, 2 * count, 1, rows)
    own_doc = lax.dynamic_index_in_dim(docs, here, 2, keepdims=False).reshape(GROUPS, rows, 1)
    here_one = here.reshape(1)

    group_tokens = tokens_all.reshape(group_rows, width).astype(jnp.float32)
    norm_one = rms_scale(group_tokens, gains[0]).astype(bf16)
    proj = dot(norm_one, qkv_head, LAST)
    inside = jnp.arange(rows, dtype=jnp.int32)
    position = jnp.concatenate([here * rows + inside, (count + here) * rows + inside])
    cosine, sine = rope_tables(jnp.concatenate([position, position]))
    proj = proj.reshape(group_rows, REPS + 2, HEAD_DIM)
    turned = rotate(proj[:, : REPS + 1], cosine, sine)
    sent = jnp.concatenate([turned, proj[:, REPS + 1 :]], axis=1).astype(bf16)
    queries = sent[:, :REPS].reshape(GROUPS, rows, head_width)
    own_kv = sent[:, REPS:].reshape(group_rows, 2 * HEAD_DIM)
    kv_slab = slabs(group_rows)
    kv_piece = (group_rows // kv_slab, kv_slab, 2 * HEAD_DIM)
    kv, out_all, gate_up_all, attn, attended, totals = gather_attend(
        own_kv, out_mine, gate_up_weight, queries, own_doc, key_doc, count, 2
    )
    gate_up_all = gate_up_all.reshape(-1, 2 * width)
    out_head = out_all.reshape(width, head_width)
    attn = attn.reshape(group_rows, head_width)
    branch_part = dot(attn, out_head, LAST).astype(bf16)
    branch_slabs = reduce_scatter_group(branch_part.reshape((GROUPS,) + piece), 3)
    inputs = tokens[0].astype(jnp.float32)
    if feed_forward_fits(count, rows, width, down_all.shape[0]):
        output, middle_grad, branch_grad, gain_rest, gate_up_part, down_part = feed_forward(
            branch_slabs,
            tokens.reshape(piece),
            cotangent.reshape(piece),
            gains,
            gate_up_all,
            down_all,
            count,
            4,
        )
        output = output.reshape(tokens.shape)
        middle_grad = middle_grad.reshape(rows, width)
        branch_grad = branch_grad.reshape(rows, width)
        gain_grad_two, gain_grad_three, gain_grad_four = gain_rest[1], gain_rest[2], gain_rest[3]
    else:
        (
            output,
            middle_grad,
            branch_grad,
            gain_grad_two,
            gain_grad_three,
            gain_grad_four,
            gate_up_part,
            down_part,
        ) = feed_forward_apart(
            branch_slabs, inputs, cotangent, gains, gate_up_all, down_all, count, piece
        )
    branch_all = all_gather_group(branch_grad, 8).reshape(group_rows, width)
    attn_grad = dot(branch_all, out_head, PLAIN).astype(bf16).reshape(GROUPS, rows, head_width)
    out_part = dot(branch_all, attn, FIRST).astype(bf16)
    out_part = out_part.reshape(GROUPS, count, out_rows, head_width)
    gate_up_part = gate_up_part.reshape((GROUPS,) + gate_up_weight.shape)
    if attend_back_fits(count):
        dq, dkv, out_sum, gate_up_grad = attend_back_reduce(
            queries,
            kv,
            own_doc,
            key_doc,
            attn_grad,
            attended,
            totals,
            out_part,
            gate_up_part,
            kv_piece,
            count,
            9,
        )
    else:
        kv = kv.reshape(count, GROUPS, rows, 2 * HEAD_DIM)
        dq, dkv_part = attention_backward(
            here_one, queries, kv, own_doc, key_doc, attn_grad, attended, totals
        )
        dkv, out_sum, gate_up_grad = reduce_middle(
            dkv_part.reshape((count,) + kv_piece), out_part, gate_up_part, count, 9
        )
    sent_grad = jnp.concatenate(
        [
            dq.reshape(group_rows, REPS, HEAD_DIM),
            dkv.reshape(group_rows, 2, HEAD_DIM),
        ],
        axis=1,
    ).astype(jnp.float32)
    unturned = rotate(sent_grad[:, : REPS + 1], cosine, -sine)
    proj_grad = (
        jnp.concatenate([unturned, sent_grad[:, REPS + 1 :]], axis=1)
        .astype(bf16)
        .reshape(group_rows, (REPS + 2) * HEAD_DIM)
    )
    qkv_part = dot(proj_grad, norm_one, FIRST).astype(bf16)
    norm_one_part = dot(proj_grad, qkv_head, PLAIN)
    _, gain_back = jax.vjp(lambda gain: rms_scale(group_tokens, gain), gains[0])
    (gain_grad_one,) = gain_back(norm_one_part)
    gain_part = jnp.stack([gain_grad_one, gain_grad_two, gain_grad_three, gain_grad_four])
    gain_part = jnp.transpose(gain_part.reshape(4, GROUPS, count, gain_rows), (2, 1, 0, 3))
    gain_part = jnp.pad(gain_part, ((0, 0), (0, 0), (0, 4), (0, gain_lanes - gain_rows)))
    qkv_grad, norm_one_grad, gain_grad, out_grad, down_grad = reduce_last(
        qkv_part.reshape((count,) + qkv_piece),
        norm_one_part.astype(bf16).reshape((GROUPS,) + piece),
        gain_part[:, :, None],
        out_sum,
        down_part.reshape((GROUPS,) + down_weight.shape),
        count,
        10,
    )
    qkv_grad = qkv_grad.reshape(qkv_rows, width)
    out_grad = (
        jnp.transpose(out_grad, (1, 0, 2)).reshape(out_rows, GROUPS * head_width).astype(jnp.float32)
    )
    gain_grad = jnp.transpose(gain_grad.reshape(8, gain_lanes)[:4, :gain_rows])
    _, pre_attn_back = jax.vjp(lambda values: rms_scale(values, gains[0]), inputs)
    (input_part,) = pre_attn_back(norm_one_grad.reshape(rows, width))
    tokens_grad = (middle_grad + input_part).astype(bf16)[None]
    return (output, tokens_grad, gain_grad, qkv_grad, out_grad, gate_up_grad, down_grad)


def solution(mesh):
    whole = ("dp", "head", "blk")
    return jax.shard_map(
        shards,
        mesh=mesh,
        in_specs=(
            P("dp", ("head", "blk"), None),
            P("dp", ("head", "blk"), None),
            P("dp", None),
            P(whole, None),
            P(whole, None),
            P(whole, None),
            P(whole, None),
            P(whole, None),
        ),
        out_specs=(
            P("dp", ("head", "blk"), None),
            P("dp", ("head", "blk"), None),
            P(whole, None),
            P(whole, None),
            P(whole, None),
            P(whole, None),
            P(whole, None),
        ),
        check_vma=False,
    )
```

```python
import functools
import math

import jax
import jax.numpy as jnp
from jax import lax
from jax.experimental import pallas as pl
from jax.experimental.pallas import tpu as pltpu
from jax.sharding import PartitionSpec as P

HEADS = 8
KV_HEADS = 4
HEAD_DIM = 256
REPS = HEADS // KV_HEADS
GROUPS = 4
SOFT_CAP = 50.0
NORM_EPS = 1e-06
ROPE_BASE = 10000.0
SCORE_SCALE = HEAD_DIM ** (-0.5)

MESH = pl.DeviceIdType.MESH
VMEM_LIMIT = 60 * 1024 * 1024


class Place:
    def __init__(self, count):
        self.count = count
        self.inner = 4 if count >= 32 else 2
        self.outer = count // self.inner
        self.here = lax.axis_index("blk")
        self.line = self.here // self.inner
        self.side = lax.rem(self.here, self.inner)
        self.core = lax.axis_index("dp")
        self.half = lax.axis_index("head")
        self.group = 2 * self.core + self.half

    def near(self, k):
        orders = [near_order(self.outer, line)[k] for line in range(self.outer)]
        found = jnp.int32(orders[0])
        for line in range(1, self.outer):
            found = jnp.where(self.line == line, jnp.int32(orders[line]), found)
        return found

    def near_at(self, k):
        found = self.near(0)
        for static in range(1, self.outer):
            found = jnp.where(k == static, self.near(static), found)
        return found

    def at(self, line, side):
        return {"blk": line * self.inner + side}

    def beside(self, step):
        return lax.rem(self.side + step, self.inner)

    def partner(self):
        return {"dp": 1 - self.core}

    def across(self):
        return {"head": 1 - self.half}

    def corner(self):
        return {"dp": 1 - self.core, "head": 1 - self.half}


def remote(src, dst, sent, came, device):
    return pltpu.make_async_remote_copy(
        src_ref=src, dst_ref=dst, send_sem=sent, recv_sem=came, device_id=device, device_id_type=MESH
    )


def greet(place, blk=False, core=False, half=False, corner=False):
    sem = pltpu.get_barrier_semaphore()
    amount = jnp.int32(0)

    def hello(device):
        pl.semaphore_signal(sem, inc=1, device_id=device, device_id_type=MESH)

    if blk:
        up, down = place.line < place.outer - 1, place.line > 0
        pl.when(up)(lambda: hello(place.at(place.line + 1, place.side)))
        pl.when(down)(lambda: hello(place.at(place.line - 1, place.side)))
        amount = amount + up.astype(jnp.int32) + down.astype(jnp.int32) + (place.inner - 1)
        for step in range(1, place.inner):
            hello(place.at(place.line, place.beside(step)))
    for wanted, device in (
        (core, place.partner()),
        (half, place.across()),
        (corner, place.corner()),
    ):
        if wanted:
            hello(device)
            amount = amount + 1
    pl.semaphore_wait(sem, amount)


def together(*tasks):
    tasks = list(tasks)
    while tasks:
        for task in list(tasks):
            try:
                next(task)
            except StopIteration:
                tasks.remove(task)


def waiting(task, *rounds):
    for step, _ in enumerate(task):
        yield
        if step < len(rounds):
            for _ in range(rounds[step]):
                yield


def near_order(outer, line):
    ends = outer == 4
    return sorted(
        range(outer),
        key=lambda other: (abs(other - line), ends and other not in (0, outer - 1), other),
    )


def evened(place, parts):
    return parts == 2 and place.inner == 2 and place.outer == 4


def part_of(ref, h, parts):
    if parts == 1:
        return ref
    size = ref.shape[0] // parts
    return ref.at[pl.ds(h * size, size)]


def gather_blk_sems(place_count, parts=2):
    inner = 4 if place_count >= 32 else 2
    return [
        pltpu.SemaphoreType.DMA((2 + inner, place_count, parts)),
        pltpu.SemaphoreType.DMA((place_count, parts)),
        pltpu.SemaphoreType.DMA,
    ]


class GatherBlk:
    def __init__(self, place, src, view, sent, came, own):
        self.place, self.src, self.view, self.sent, self.came = place, src, view, sent, came
        self.parts = came.shape[1]
        self.evened = evened(place, self.parts)
        self.middle = (place.line > 0) & (place.line < place.outer - 1)
        self.copy = pltpu.make_async_copy(src, view(place.here), own)

    def sends(self, k, h):
        place = self.place
        there = place.near(k)
        piece = there * place.inner + place.side
        there_view = part_of(self.view(piece), h, self.parts)
        src = part_of(self.src, h, self.parts) if k == 0 else there_view

        def send(kind, device):
            return remote(
                src, there_view, self.sent.at[kind, piece, h], self.came.at[piece, h], device
            )

        line, side = place.line, place.side
        up = (there <= line) & (line < place.outer - 1)
        down = (there >= line) & (line > 0)
        aside = range(1, place.inner)
        if self.evened and h == 1 and k == place.outer - 1:
            aside = ()
        return (
            [
                (up, lambda: send(0, place.at(line + 1, side))),
                (down, lambda: send(1, place.at(line - 1, side))),
            ],
            [send(1 + step, place.at(line, place.beside(step))) for step in aside],
        )

    def forward(self, k, h):
        along, aside = self.sends(k, h)
        for needed, make in along:
            pl.when(needed)(lambda make=make: make().start())
        for one in aside:
            one.start()

    def start(self):
        self.copy.start()
        for h in range(self.parts):
            self.forward(0, h)

    def arrived(self, piece, h):
        place = self.place
        remote(
            part_of(self.src, h, self.parts),
            part_of(self.view(piece), h, self.parts),
            self.sent.at[0, piece, h],
            self.came.at[piece, h],
            place.at(place.line, place.beside(1)),
        ).wait_recv()

    def pass_on(self, k):
        for h in range(self.parts):
            self.arrived(self.place.near(k) * self.place.inner + self.place.side, h)
            self.forward(k, h)

    def extra(self, k):
        place = self.place
        piece = place.near(k) * place.inner + place.beside(1)
        to = place.near(2 if k == 1 else 1)
        half = part_of(self.view(piece), 1, 2)
        return remote(
            half,
            half,
            self.sent.at[place.inner + 1, piece, 1],
            self.came.at[piece, 1],
            place.at(to, place.side),
        )

    def pass_extra(self, k):
        if self.evened:

            @pl.when(self.middle)
            def _():
                self.arrived(self.place.near(k) * self.place.inner + self.place.beside(1), 1)
                self.extra(k).start()

    def beside_arrived(self, k):
        for step in range(1, self.place.inner):
            piece = self.place.near(k) * self.place.inner + self.place.beside(step)
            for h in range(self.parts):
                if self.evened and h == 1 and k in (1, self.place.outer - 1):
                    pl.when(jnp.logical_not(self.middle))(lambda: self.arrived(piece, 1))
                else:
                    self.arrived(piece, h)

    def finish(self):
        for k in range(self.place.outer):
            for h in range(self.parts):
                along, aside = self.sends(k, h)
                for needed, make in along:
                    pl.when(needed)(lambda make=make: make().wait_send())
                for one in aside:
                    one.wait_send()
        if self.evened:

            @pl.when(self.middle)
            def _():
                self.extra(1).wait_send()
                self.extra(self.place.outer - 1).wait_send()


def advance(gathers, k):
    place = gathers[0].place

    def each(name, *args):
        for gather in gathers:
            getattr(gather, name)(*args)

    if not gathers[0].evened:
        if k + 1 < place.outer:
            each("pass_on", k + 1)
        return
    middle = gathers[0].middle
    ends = jnp.logical_not(middle)
    if k == 0:
        each("pass_on", 1)
        pl.when(middle)(lambda: each("pass_on", 2))
    elif k == 1:
        pl.when(ends)(lambda: each("pass_on", 2))
        each("pass_extra", 1)
        pl.when(middle)(lambda: each("pass_on", 3))
    elif k == 2:
        pl.when(ends)(lambda: each("pass_on", 3))
        each("pass_extra", 3)


def gather_blk(place, src, view, sent, came, own):
    if not callable(view):
        out = view
        view = lambda piece: out.at[piece]
    work = GatherBlk(place, src, view, sent, came, own)
    work.start()
    yield
    for k in range(1, place.outer):
        work.pass_on(k)
        if k == place.outer - 2:
            work.pass_extra(1)
        yield
    work.pass_extra(place.outer - 1)
    yield
    for k in range(place.outer):
        work.beside_arrived(k)
    work.finish()
    work.copy.wait()


def add_into(out, *terms):
    lanes = out.shape[-1]
    parts = 3 if lanes % 384 == 0 and lanes > 1024 else 1
    step = lanes // parts

    def one(i, carry):
        at = i if parts == 1 else i // parts
        columns = pl.ds(pl.multiple_of((i % parts) * step, step), step) if parts > 1 else slice(None)
        index = (at,) + (slice(None),) * (len(out.shape) - 2) + (columns,)
        total = terms[0][index].astype(jnp.float32)
        for term in terms[1:]:
            total = total + term[index].astype(jnp.float32)
        out[index] = total.astype(out.dtype)
        return carry

    lax.fori_loop(0, out.shape[0] * parts, one, 0)


def reduce_blk_scratch(place_count, piece, dtype, parts=2):
    inner = 4 if place_count >= 32 else 2
    outer = place_count // inner
    half = (piece[0] // 2,) + tuple(piece[1:]) if parts == 2 and inner == 2 and outer == 4 else (1, 8, 128)
    return [
        pltpu.VMEM((outer, inner - 1) + piece, dtype),
        pltpu.VMEM((outer + 1,) + piece, dtype),
        pltpu.VMEM((outer,) + piece, dtype),
        pltpu.VMEM((4,) + half, dtype),
        pltpu.SemaphoreType.DMA((outer, inner - 1, parts)),
        pltpu.SemaphoreType.DMA((outer, inner - 1, parts)),
        pltpu.SemaphoreType.DMA((outer, parts)),
        pltpu.SemaphoreType.DMA((outer + 1, parts)),
        pltpu.SemaphoreType.DMA((2,)),
        pltpu.SemaphoreType.DMA((2,)),
    ]


REDUCE_REFS = 10


class ReduceBlk:
    def __init__(
        self,
        place,
        view,
        out,
        beside,
        along,
        held,
        spare,
        side_sent,
        side_came,
        line_sent,
        line_came,
        spare_sent,
        spare_came,
    ):
        self.place, self.view, self.out = place, view, out
        self.beside, self.along, self.held, self.spare = beside, along, held, spare
        self.side_sems, self.line_sems = (side_sent, side_came), (line_sent, line_came)
        self.spare_sems = (spare_sent, spare_came)
        self.parts = line_sent.shape[1]
        self.evened = evened(place, self.parts)
        self.middle = (place.line > 0) & (place.line < place.outer - 1)

    def part(self, ref, h):
        return part_of(ref, h, self.parts)

    def far(self, k):
        return self.place.near(self.place.outer - 1 - k)

    def alone(self, k, h):
        return self.evened and k == 0 and h == 1

    def side_copy(self, there, step, h, src=None):
        place = self.place
        to = place.beside(step)
        if src is None:
            src = self.part(self.view(there * place.inner + to), h)
        return remote(
            src,
            self.part(self.beside.at[there, place.inner - step - 1], h),
            self.side_sems[0].at[there, step - 1, h],
            self.side_sems[1].at[there, place.inner - step - 1, h],
            place.at(place.line, to),
        )

    def line_copy(self, there, slot, to, h, src=None):
        return remote(
            self.part(self.held.at[there], h) if src is None else src,
            self.part(self.along.at[slot], h),
            self.line_sems[0].at[there, h],
            self.line_sems[1].at[slot, h],
            self.place.at(to, self.place.side),
        )

    def send(self, k, h):
        for step in range(1, self.place.inner):
            self.side_copy(self.far(k), step, h).start()

    def terms(self, k, h):
        place = self.place
        there = self.far(k)
        own = [self.part(self.view(there * place.inner + place.side), h)]
        if self.alone(k, h):
            return own
        for step in range(1, place.inner):
            self.side_copy(there, step, h).wait_recv()
        return own + [self.part(self.beside.at[there, j], h) for j in range(place.inner - 1)]

    def onward(self, there, h, src=None):
        line, outer = self.place.line, self.place.outer
        to = jnp.where(there < line, line - 1, line + 1)
        slot = jnp.where(there == line + 1, outer, there)
        return self.line_copy(there, slot, to, h, src)

    def starts(self, there):
        line, outer = self.place.line, self.place.outer
        return ((there < line) & (line == outer - 1)) | ((there > line) & (line == 0))

    def pass_on(self, k, h, middle=None):
        place = self.place
        line = place.line
        there = self.far(k)
        terms = self.terms(k, h)
        held = self.part(self.held.at[there], h)

        def first():
            add_into(held, *terms)

        def later():
            back = jnp.where(there < line, line + 1, line - 1)
            self.line_copy(there, there, back, h).wait_recv()
            add_into(held, self.part(self.along.at[there], h), *terms)

        if middle is None:
            starts = self.starts(there)
            pl.when(starts)(first)
            pl.when(jnp.logical_not(starts))(later)
        elif middle:
            later()
        else:
            first()
        self.onward(there, h).start()

    def last(self, h):
        place = self.place
        line, outer = place.line, place.outer
        terms = self.terms(outer - 1, h)
        out = self.part(self.out, h)

        @pl.when(self.middle)
        def _():
            self.line_copy(line, line, line + 1, h).wait_recv()
            self.line_copy(line, outer, line - 1, h).wait_recv()
            from_above = self.part(self.along.at[line], h)
            add_into(out, from_above, self.part(self.along.at[outer], h), *terms)

        @pl.when(jnp.logical_not(self.middle))
        def _():
            slot = jnp.where(line == 0, line, outer)
            back = jnp.where(line == 0, line + 1, line - 1)
            self.line_copy(line, slot, back, h).wait_recv()
            add_into(out, self.part(self.along.at[slot], h), *terms)


    def spare_view(self, k):
        place = self.place
        return self.part(self.view(place.near(k) * place.inner + place.beside(1)), 1)

    def spare_first(self):
        return remote(
            self.spare_view(3),
            self.spare.at[0],
            self.spare_sems[0].at[0],
            self.spare_sems[1].at[0],
            self.place.at(self.place.near(1), self.place.side),
        )

    def spare_second(self):
        return remote(
            self.spare.at[2],
            self.spare.at[1],
            self.spare_sems[0].at[1],
            self.spare_sems[1].at[1],
            self.place.at(self.place.near(2), self.place.side),
        )

    def spare_side(self):
        return self.side_copy(self.far(2), 1, 1, self.spare.at[3])

    def opening(self):
        outer = self.place.outer
        if not self.evened:

            def every():
                for k in range(outer):
                    for h in range(self.parts):
                        self.send(k, h)

            return [every]
        ends = jnp.logical_not(self.middle)

        def along():
            self.spare_first().start()
            there = self.far(0)
            self.onward(
                there, 1, self.part(self.view(there * self.place.inner + self.place.side), 1)
            ).start()

        todo = [lambda: self.send(0, 0), lambda: pl.when(ends)(along)]
        todo += [lambda k=k, h=h: self.send(k, h) for k, h in ((1, 0), (1, 1), (2, 0))]
        todo += [
            lambda k=k, h=h: pl.when(ends)(lambda: self.send(k, h))
            for k, h in ((2, 1), (3, 0), (3, 1))
        ]
        return todo

    def start(self):
        for step in self.opening():
            step()

    def turning(self):
        def first():
            self.spare_first().wait_recv()
            add_into(self.spare.at[2], self.spare.at[0], self.spare_view(3))
            self.spare_second().start()

        def second():
            self.spare_second().wait_recv()
            add_into(self.spare.at[3], self.spare.at[1], self.spare_view(1))
            self.spare_side().start()
            for h in (0, 1):
                self.send(3, h)

        steps = (first, lambda: self.pass_on(0, 1, True), second)
        return steps

    def events(self):
        outer, parts = self.place.outer, self.parts
        if self.evened:
            todo = [lambda step=step: pl.when(self.middle)(step) for step in self.turning()]
            todo.append(lambda: self.pass_on(0, 0))
        else:
            todo = [lambda h=h: self.pass_on(0, h) for h in range(parts)]
        for k in range(1, outer - 1):
            for h in range(parts):
                todo.append(lambda k=k, h=h: self.pass_on(k, h))
        for h in range(parts):
            todo.append(lambda h=h: self.last(h))
        return todo

    def finish(self):
        for k in range(self.place.outer):
            for h in range(self.parts):
                if k < self.place.outer - 1:
                    self.onward(self.far(k), h).wait_send()
                if not self.alone(k, h):
                    for step in range(1, self.place.inner):
                        self.side_copy(self.far(k), step, h).wait_send()
        if self.evened:

            @pl.when(self.middle)
            def _():
                self.spare_second().wait_send()

            @pl.when(jnp.logical_not(self.middle))
            def _():
                self.spare_first().wait_send()


def reduce_blk(place, view, out, *scratch):
    if not callable(view):
        part = view
        view = lambda piece: part.at[piece]
    work = ReduceBlk(place, view, out, *scratch)
    for step in work.opening() + work.events():
        step()
        yield
    work.finish()


def gather_group_sems():
    return [pltpu.SemaphoreType.DMA((3,)), pltpu.SemaphoreType.DMA((4,)), pltpu.SemaphoreType.DMA]


def gather_group(place, src, view, sent, came, own, through=None):
    if not callable(view):
        out = view
        view = lambda g: out.at[g]
    copy = pltpu.make_async_copy(src if through is None else through, view(place.group), own)
    load = None if through is None else pltpu.make_async_copy(src, through, own)
    mine, other = place.group, 2 * place.core + (1 - place.half)
    to_half = remote(src, view(mine), sent.at[0], came.at[mine], place.across())
    to_core = remote(src, view(mine), sent.at[1], came.at[mine], place.partner())
    to_half.start()
    to_core.start()
    (load or copy).start()
    yield
    if load:
        load.wait()
        copy.start()
    remote(src, view(other), sent.at[0], came.at[other], place.across()).wait_recv()
    relay = remote(view(other), view(other), sent.at[2], came.at[other], place.partner())
    relay.start()
    yield
    for half in (0, 1):
        slot = 2 * (1 - place.core) + half
        remote(src, view(slot), sent.at[0], came.at[slot], place.partner()).wait_recv()
    to_half.wait_send()
    to_core.wait_send()
    relay.wait_send()
    copy.wait()


def share_rows(ref, parts, p):
    rows = ref.shape[0] // parts
    return ref.at[pl.ds(p * rows, rows)]


def gather_group_rows(place, src, out, parts, take, through=True):
    def task(p, refs):
        rows = src.shape[0] // parts
        view = lambda g: out.at[g, pl.ds(p * rows, rows)]
        return gather_group(place, share_rows(src, parts, p), view, *refs)

    return [task(p, take(4 if through else 3)) for p in range(parts)]


def gather_rows_scratch(value, parts):
    through = pltpu.VMEM((value.shape[0] // parts, value.shape[1]), value.dtype)
    return (gather_group_sems() + [through]) * parts


def fold_rows_scratch(piece, parts):
    rows, width = piece[0] // parts, piece[1]
    bf16 = jnp.bfloat16
    one = [
        pltpu.VMEM((2, rows, width), bf16),
        pltpu.VMEM((rows, width), bf16),
        pltpu.VMEM((rows, width), bf16),
        pltpu.VMEM((rows, width), bf16),
        pltpu.VMEM((rows, width), jnp.float32),
        pltpu.SemaphoreType.DMA((3,)),
        pltpu.SemaphoreType.DMA((3,)),
        pltpu.SemaphoreType.DMA((3,)),
    ]
    return one * parts


def add_rows(out, *terms):
    rows = slabs(out.shape[0])

    def one(i, carry):
        at = pl.ds(pl.multiple_of(i * rows, rows), rows)
        total = terms[0][at].astype(jnp.float32)
        for term in terms[1:]:
            total = total + term[at].astype(jnp.float32)
        out[at] = total.astype(out.dtype)
        return carry

    lax.fori_loop(0, out.shape[0] // rows, one, 0)


def fold_rows(place, part, out, parts, take):
    rows = out.shape[0] // parts
    core, half = place.core, place.half
    far, near = 2 * (1 - core) + (1 - half), 2 * (1 - core) + half
    beside = 2 * core + (1 - half)

    def task(p, from_core, from_half, held, mine, total, sent, came, local):
        at = pl.ds(p * rows, rows)
        first = remote(part.at[far, at], from_core.at[1], sent.at[0], came.at[0], place.partner())
        second = remote(part.at[near, at], from_core.at[0], sent.at[1], came.at[1], place.partner())
        third = remote(held, from_half, sent.at[2], came.at[2], place.across())
        load_held = pltpu.make_async_copy(part.at[beside, at], held, local.at[0])
        load_mine = pltpu.make_async_copy(part.at[place.group, at], mine, local.at[1])
        store = pltpu.make_async_copy(total, out.at[at], local.at[2])
        for copy in (first, load_held, second, load_mine):
            copy.start()
        yield
        first.wait_recv()
        load_held.wait()
        add_rows(held, held, from_core.at[1])
        third.start()
        yield
        second.wait_recv()
        load_mine.wait()
        third.wait_recv()
        add_rows(total, mine, from_core.at[0], from_half)
        store.start()
        yield
        for copy in (first, second, third):
            copy.wait_send()
        store.wait()

    return [task(p, *take(8)) for p in range(parts)]


ROW_PARTS = 3


def reduce_group_scratch(piece, dtype):
    return [
        pltpu.VMEM((2,) + piece, dtype),
        pltpu.VMEM(piece, dtype),
        pltpu.VMEM(piece, dtype),
        pltpu.SemaphoreType.DMA((3,)),
        pltpu.SemaphoreType.DMA((3,)),
    ]


def reduce_group(place, view, out, from_core, from_half, held, sent, came):
    if not callable(view):
        part = view
        view = lambda g: part.at[g]
    far = 2 * (1 - place.core) + (1 - place.half)
    near = 2 * (1 - place.core) + place.half
    first = remote(view(far), from_core.at[1], sent.at[0], came.at[0], place.partner())
    second = remote(view(near), from_core.at[0], sent.at[1], came.at[1], place.partner())
    first.start()
    second.start()
    yield
    first.wait_recv()
    add_into(held, view(2 * place.core + (1 - place.half)), from_core.at[1])
    third = remote(held, from_half, sent.at[2], came.at[2], place.across())
    third.start()
    yield
    second.wait_recv()
    third.wait_recv()
    add_into(out, view(place.group), from_core.at[0], from_half)
    first.wait_send()
    second.wait_send()
    third.wait_send()


def exchange_group_sems():
    return [pltpu.SemaphoreType.DMA((3,)), pltpu.SemaphoreType.DMA((4,)), pltpu.SemaphoreType.DMA]


def exchange_group(place, src, out, sent, came, own):
    mine = place.group
    copy = pltpu.make_async_copy(src.at[mine], out.at[mine], own)
    copy.start()
    core, half = place.core, place.half
    links = (
        (2 * (1 - core) + (1 - half), place.corner()),
        (2 * core + (1 - half), place.across()),
        (2 * (1 - core) + half, place.partner()),
    )
    copies = [
        remote(src.at[to], out.at[mine], sent.at[k], came.at[mine], device)
        for k, (to, device) in enumerate(links)
    ]
    for one in copies:
        one.start()
    yield
    for k, (peer, device) in enumerate(links):
        remote(src.at[peer], out.at[peer], sent.at[k], came.at[peer], device).wait_recv()
    for one in copies:
        one.wait_send()
    copy.wait()


def transfer(name, number, body, ins, outs, scratch, moved, out_spaces=None, in_spaces=None):
    spaces = out_spaces or [pl.ANY] * len(outs)
    in_spaces = in_spaces or [pltpu.VMEM] * len(ins)
    return pl.pallas_call(
        body,
        name=name,
        out_shape=outs,
        in_specs=[pl.BlockSpec(memory_space=space) for space in in_spaces],
        out_specs=[pl.BlockSpec(memory_space=space) for space in spaces],
        scratch_shapes=scratch,
        compiler_params=pltpu.CompilerParams(
            collective_id=number, has_side_effects=True, vmem_limit_bytes=VMEM_LIMIT
        ),
        cost_estimate=pl.CostEstimate(flops=0, bytes_accessed=moved * 40, transcendentals=0),
    )(*ins)


def shape(dims, dtype):
    return jax.ShapeDtypeStruct(tuple(dims), dtype)


def slabs(rows):
    return math.gcd(rows, 16)


def all_gather_blk(value, count, number):
    def body(src, out, *sems):
        place = Place(count)
        greet(place, blk=True)
        together(gather_blk(place, src, out, *sems))

    return transfer(
        f"gather{number}",
        number,
        body,
        [value],
        [shape((count,) + value.shape, value.dtype)],
        gather_blk_sems(count),
        value.size * 2 * count,
    )[0]


def reduce_scatter_blk(value, count, number):
    piece = value.shape[1:]

    def body(part, out, *scratch):
        place = Place(count)
        greet(place, blk=True)
        together(reduce_blk(place, part, out, *scratch))

    return transfer(
        f"reduce{number}",
        number,
        body,
        [value],
        [shape(piece, jnp.float32)],
        reduce_blk_scratch(count, piece, value.dtype),
        value.size * 2,
        [pltpu.VMEM],
    )[0]


class Taker:
    def __init__(self, refs):
        self.refs = list(refs)

    def __call__(self, amount):
        taken = self.refs[:amount]
        del self.refs[:amount]
        return taken


def gather_first(qkv, out_parts, tokens, gains, docs, down, count, number):
    names = 6

    def body(*refs):
        qkv_ref, out_ref, tok_ref, gain_ref, doc_ref, down_ref = refs[:names]
        qkv_all, out_mine, tok_all, gain_all, doc_all, down_all = refs[names : 2 * names]
        gain_mine = refs[2 * names]
        take = Taker(refs[2 * names + 1 :])
        place = Place(count)
        greet(place, blk=True, core=True, half=True, corner=True)

        def gain_task(near, far):
            yield from gather_blk(place, gain_ref, gain_mine, *near)
            yield from gather_group(place, gain_mine, gain_all, *far)

        def doc_task(sent, came, own):
            copy = pltpu.make_async_copy(doc_ref, doc_all.at[place.core], own)
            copy.start()
            send = remote(doc_ref, doc_all.at[place.core], sent, came, place.partner())
            send.start()
            yield
            remote(doc_ref, doc_all.at[1 - place.core], sent, came, place.partner()).wait_recv()
            send.wait_send()
            copy.wait()

        together(
            gain_task(take(3), take(3)),
            gather_blk(place, qkv_ref, qkv_all, *take(3)),
            doc_task(*take(3)),
            waiting(gather_group(place, tok_ref, tok_all, *take(3)), 2),
            waiting(exchange_group(place, out_ref, out_mine, *take(3)), 3),
            *(
                waiting(task, 2 + p, 4)
                for p, task in enumerate(
                    gather_group_rows(place, down_ref, down_all, ROW_PARTS, take)
                )
            ),
        )

    ins = [qkv, out_parts, tokens, gains, docs, down]
    return transfer(
        f"first{number}",
        number,
        body,
        ins,
        [
            shape((count,) + qkv.shape, qkv.dtype),
            shape(out_parts.shape, out_parts.dtype),
            shape((GROUPS,) + tokens.shape, tokens.dtype),
            shape((GROUPS, count) + gains.shape, gains.dtype),
            shape((2,) + docs.shape, docs.dtype),
            shape((GROUPS,) + down.shape, down.dtype),
        ],
        [pltpu.VMEM((count,) + gains.shape, gains.dtype)]
        + gather_blk_sems(count, 1)
        + gather_group_sems()
        + gather_blk_sems(count)
        + [pltpu.SemaphoreType.DMA] * 3
        + gather_group_sems()
        + exchange_group_sems()
        + gather_rows_scratch(down, ROW_PARTS),
        (qkv.size + out_parts.size) * 2 * count,
        None,
        [pltpu.VMEM] * 5 + [pl.ANY],
    )


def attend_step(count, g, here, key_half, key_at, q_ref, kv_ref, doc_ref, key_doc_ref, acc, tot):
    rows = q_ref.shape[1]
    sequence, half = g // 2, g % 2
    q2, position, doc = stacked_queries(g, half * count + here, q_ref, doc_ref)
    key_block = key_half * count + key_at
    at = pl.ds(pl.multiple_of((2 * sequence + key_half) * rows, rows), rows)
    kv = kv_ref.at[key_at, at]
    _, weights = attention_scores(
        q2, kv[:, :HEAD_DIM], position, doc, key_block, key_doc_ref[sequence, key_block], rows
    )
    tot[g] += jnp.sum(weights, axis=-1, keepdims=True)
    acc[g] += jnp.dot(
        weights.astype(jnp.bfloat16), kv[:, HEAD_DIM:], preferred_element_type=jnp.float32
    )


def stacked_queries(g, block, q_ref, doc_ref):
    rows = q_ref.shape[1]
    q2 = jnp.concatenate([q_ref[g, :, :HEAD_DIM], q_ref[g, :, HEAD_DIM:]], axis=0)
    inside = lax.broadcasted_iota(jnp.int32, (rows, 1), 0)
    position = block * rows + jnp.concatenate([inside, inside], axis=0)
    doc = jnp.concatenate([doc_ref[g], doc_ref[g]], axis=0)
    return q2, position, doc


def gather_attend(kv, out_mine, gate_up, queries, doc, key_doc, count, number):
    groups, out_rows, width = out_mine.shape
    rows = queries.shape[1]

    def body(*refs):
        kv_ref, out_ref, gate_up_ref, q_ref, doc_ref, key_doc_ref = refs[:6]
        kv_all, out_all, gate_up_all, attn_ref, full_ref, total_ref = refs[6:12]
        acc, tot = refs[12:14]
        take = Taker(refs[14:])
        place = Place(count)
        greet(place, blk=True, core=True, half=True)
        gathers = (
            GatherBlk(place, kv_ref, lambda i: kv_all.at[i], *take(3)),
            GatherBlk(place, out_ref, lambda i: out_all.at[:, i], *take(3)),
        )
        groups = gather_group_rows(place, gate_up_ref, gate_up_all, ROW_PARTS, take)
        for gather in gathers:
            gather.start()
        for task in groups:
            next(task)
        acc[...] = jnp.zeros_like(acc)
        tot[...] = jnp.zeros_like(tot)
        here, inner = place.here, place.inner

        def attend(k):
            def one(c, carry):
                key_at = place.near(k) * inner + c // 6
                sequence, kind = (c % 6) // 3, c % 3
                half = jnp.minimum(kind, 1)
                needed = jnp.where(kind == 1, key_at >= here, key_at <= here)

                @pl.when(needed)
                def _():
                    attend_step(
                        count,
                        2 * sequence + half,
                        here,
                        kind // 2,
                        key_at,
                        q_ref,
                        kv_all,
                        doc_ref,
                        key_doc_ref,
                        acc,
                        tot,
                    )

                return carry

            lax.fori_loop(0, inner * 6, one, 0)

        gathers[0].copy.wait()
        for k in range(place.outer):
            advance(gathers, k)
            gathers[0].beside_arrived(k)
            if 0 < k < place.outer - 1 and k <= 2:
                next(groups[k - 1])
            attend(k)

        def put(g, carry):
            total = tot[g]
            attended = acc[g] / total
            attended = jnp.concatenate([attended[:rows], attended[rows:]], axis=1)
            full_ref[g] = attended
            attn_ref[g] = attended.astype(jnp.bfloat16)
            total_ref[g] = total
            return carry

        lax.fori_loop(0, GROUPS, put, 0)
        next(groups[2])
        gathers[1].copy.wait()
        for k in range(place.outer):
            gathers[1].beside_arrived(k)
        for gather in gathers:
            gather.finish()
        together(*groups)

    return transfer(
        f"attend{number}",
        number,
        body,
        [kv, out_mine, gate_up, queries, doc, key_doc],
        [
            shape((count,) + kv.shape, kv.dtype),
            shape((groups, count, out_rows, width), out_mine.dtype),
            shape((GROUPS,) + gate_up.shape, gate_up.dtype),
            shape((GROUPS, rows, width), jnp.bfloat16),
            shape((GROUPS, rows, width), jnp.float32),
            shape((GROUPS, REPS * rows, 1), jnp.float32),
        ],
        [
            pltpu.VMEM((GROUPS, REPS * rows, HEAD_DIM), jnp.float32),
            pltpu.VMEM((GROUPS, REPS * rows, 1), jnp.float32),
        ]
        + gather_blk_sems(count)
        + gather_blk_sems(count)
        + gather_rows_scratch(gate_up, ROW_PARTS),
        (kv.size + out_mine.size) * 2 * count,
        [pltpu.VMEM, pl.ANY, pl.ANY, pltpu.VMEM, pltpu.VMEM, pltpu.VMEM],
        [pltpu.VMEM, pltpu.VMEM, pl.ANY, pltpu.VMEM, pltpu.VMEM, pltpu.VMEM],
    )


def attend_back_block(
    count, g, here, q_ref, kv_ref, doc_ref, key_doc_ref, grad_ref, full_ref, total_ref, dq_ref, key_acc
):
    rows = q_ref.shape[1]
    sequence, half = g // 2, g % 2
    block = half * count + here
    q2, position, doc = stacked_queries(g, block, q_ref, doc_ref)
    total = total_ref[g]
    grad = grad_ref[g].astype(jnp.float32)
    grad2 = jnp.concatenate([grad[:, :HEAD_DIM], grad[:, HEAD_DIM:]], axis=0)
    full2 = jnp.concatenate([full_ref[g, :, :HEAD_DIM], full_ref[g, :, HEAD_DIM:]], axis=0)
    total_grad = -jnp.sum(grad2 * full2, axis=-1, keepdims=True) / total
    sums_grad = (grad2 / total).astype(jnp.bfloat16)

    def one(key_block, acc):
        key_half = (key_block >= count).astype(jnp.int32)
        inner = key_block - key_half * count
        at = pl.ds(pl.multiple_of((2 * sequence + key_half) * rows, rows), rows)
        kv = kv_ref.at[inner, at]
        keys = kv[:, :HEAD_DIM]
        capped, weights = attention_scores(
            q2, keys, position, doc, key_block, key_doc_ref[sequence, key_block], rows
        )
        exp_grad = dot(sums_grad, kv[:, HEAD_DIM:], LAST)
        raw_grad = (
            weights * (exp_grad + total_grad) * (1.0 - capped * capped) * SCORE_SCALE
        ).astype(jnp.bfloat16)
        slot = inner * 2 + key_half
        key_acc[slot, :, :HEAD_DIM] += dot(raw_grad, q2, FIRST)
        key_acc[slot, :, HEAD_DIM:] += dot(weights.astype(jnp.bfloat16), sums_grad, FIRST)
        return acc + dot(raw_grad, keys, PLAIN)

    dq = lax.fori_loop(
        jnp.maximum(block - count, 0),
        block + 1,
        one,
        jnp.zeros((REPS * rows, HEAD_DIM), jnp.float32),
    )
    dq_ref[g] = jnp.concatenate([dq[:rows], dq[rows:]], axis=1).astype(jnp.bfloat16)


def attend_back_fits(count):
    return count == 8


def attend_back_reduce(
    queries, kv, doc, key_doc, grad, full, totals, out_part, gate_up_part, kv_piece, count, number
):
    out_piece = out_part.shape[:1] + out_part.shape[2:]
    gate_up_piece = gate_up_part.shape[1:]
    rows = queries.shape[1]
    steps = rows // kv_piece[1]
    bf16 = jnp.bfloat16

    def body(*refs):
        q_ref, kv_ref, doc_ref, key_doc_ref, grad_ref, full_ref, total_ref = refs[:7]
        out_ref, gate_up_ref = refs[7:9]
        dq_ref, dkv_sum, out_sum, gate_up_sum, dkv_part, key_acc = refs[9:15]
        take = Taker(refs[15:])
        place = Place(count)
        greet(place, blk=True, core=True, half=True)
        dkv = ReduceBlk(place, lambda i: dkv_part.at[i], dkv_sum, *take(REDUCE_REFS))
        out = ReduceBlk(place, lambda i: out_ref.at[:, i], out_sum, *take(REDUCE_REFS))
        folds = fold_rows(place, gate_up_ref, gate_up_sum, ROW_PARTS, take)
        out_events = out.events()

        def back(g):
            attend_back_block(
                count,
                g,
                place.here,
                q_ref,
                kv_ref,
                doc_ref,
                key_doc_ref,
                grad_ref,
                full_ref,
                total_ref,
                dq_ref,
                key_acc,
            )

        def clear(i, carry):
            key_acc[i] = jnp.zeros(key_acc.shape[1:], jnp.float32)
            return carry

        def put(sequence):
            def one(i, carry):
                for k in (0, 1):
                    value = key_acc[i * 2 + k].astype(bf16).reshape((steps,) + kv_piece[1:])
                    dkv_part[i, pl.ds((2 * sequence + k) * steps, steps)] = value
                return carry

            lax.fori_loop(0, count, one, 0)

        ends = jnp.logical_not(out.middle)

        turning = out.turning()

        def middle(*steps):
            @pl.when(out.middle)
            def _():
                for step in steps:
                    if isinstance(step, int):
                        turning[step]()
                    else:
                        out.pass_on(*step, True)

        def outside(*steps):
            @pl.when(ends)
            def _():
                for step in steps:
                    out.pass_on(*step, False)

        out.start()
        for fold in folds:
            next(fold)
        lax.fori_loop(0, 2 * count, clear, 0)
        back(0)
        next(folds[0])
        middle(0)
        back(1)
        put(0)
        middle(1, 2)
        outside((0, 0), (1, 0), (1, 1))
        next(folds[1])
        lax.fori_loop(0, 2 * count, clear, 0)
        back(2)
        outside((2, 0), (2, 1))
        middle((0, 0))
        back(3)
        put(1)
        middle((1, 0), (1, 1), (2, 0), (2, 1))
        dkv.start()
        dkv_events = dkv.events()
        order = [(folds, 2), (dkv_events, 0), (dkv_events, 1), (dkv_events, 2)]
        order += [(out_events, 8), (out_events, 9), (dkv_events, 3), (dkv_events, 4)]
        order += [(folds, 0), (dkv_events, 5), (dkv_events, 6), (folds, 1)]
        order += [(dkv_events, 7), (dkv_events, 8), (dkv_events, 9), (folds, 2)]
        for events, i in order:
            if events is folds:
                next(folds[i])
            else:
                events[i]()
        out.finish()
        dkv.finish()
        together(*folds)

    vmem = pltpu.VMEM
    return transfer(
        f"attend_back{number}",
        number,
        body,
        [queries, kv, doc, key_doc, grad, full, totals, out_part, gate_up_part],
        [
            shape(queries.shape, bf16),
            shape(kv_piece, bf16),
            shape(out_piece, bf16),
            shape(gate_up_piece, jnp.float32),
        ],
        [
            vmem((count,) + kv_piece, bf16),
            vmem((2 * count, rows, 2 * HEAD_DIM), jnp.float32),
        ]
        + reduce_blk_scratch(count, kv_piece, bf16)
        + reduce_blk_scratch(count, out_piece, bf16)
        + fold_rows_scratch(gate_up_piece, ROW_PARTS),
        (kv.size + out_part.size) * 2,
        [vmem, vmem, vmem, pl.ANY],
        [vmem] * 8 + [pl.ANY],
    )


def reduce_middle(dkv_part, out_part, gate_up_part, count, number):
    dkv_piece = dkv_part.shape[1:]
    out_piece = out_part.shape[:1] + out_part.shape[2:]

    gate_up_piece = gate_up_part.shape[1:]

    def body(dkv_ref, out_ref, gate_up_ref, dkv_sum, out_sum, gate_up_sum, *scratch):
        take = Taker(scratch)
        place = Place(count)
        greet(place, blk=True, core=True, half=True)
        together(
            reduce_blk(place, dkv_ref, dkv_sum, *take(REDUCE_REFS)),
            reduce_blk(place, lambda i: out_ref.at[:, i], out_sum, *take(REDUCE_REFS)),
            *(
                waiting(task, *rounds)
                for rounds, task in zip(
                    ((6, 5, 5), (8, 5, 3), (10, 6, 0)),
                    fold_rows(place, gate_up_ref, gate_up_sum, ROW_PARTS, take),
                )
            ),
        )

    return transfer(
        f"reduce{number}",
        number,
        body,
        [dkv_part, out_part, gate_up_part],
        [
            shape(dkv_piece, jnp.bfloat16),
            shape(out_piece, jnp.bfloat16),
            shape(gate_up_piece, jnp.float32),
        ],
        reduce_blk_scratch(count, dkv_piece, jnp.bfloat16)
        + reduce_blk_scratch(count, out_piece, jnp.bfloat16)
        + fold_rows_scratch(gate_up_piece, ROW_PARTS),
        (dkv_part.size + out_part.size) * 2,
        [pltpu.VMEM, pltpu.VMEM, pl.ANY],
        [pltpu.VMEM, pltpu.VMEM, pl.ANY],
    )


def reduce_last(qkv_part, norm_part, gain_part, out_sum, down_part, count, number):
    gain_piece = gain_part.shape[1:]
    qkv_piece, norm_piece = qkv_part.shape[1:], norm_part.shape[1:]

    def body(*refs):
        qkv_ref, norm_ref, gain_ref, out_ref, down_ref = refs[:5]
        qkv_sum, norm_sum, gain_sum, out_all, down_sum = refs[5:10]
        gain_mine = refs[10]
        take = Taker(refs[11:])
        place = Place(count)
        greet(place, blk=True, core=True, half=True, corner=True)

        def gain_task(near, far):
            yield from reduce_blk(place, gain_ref, gain_mine, *near)
            yield from reduce_group(place, gain_mine, gain_sum, *far)

        main = reduce_blk(place, qkv_ref, qkv_sum, *take(REDUCE_REFS))
        gain = gain_task(take(REDUCE_REFS), take(5))
        together(
            waiting(gain, 11),
            main,
            waiting(exchange_group(place, out_ref, out_all, *take(3)), 16),
            waiting(reduce_group(place, norm_ref, norm_sum, *take(5)), 7, 9),
            *(
                waiting(task, *rounds)
                for rounds, task in zip(
                    ((7, 7, 2), (8, 8, 0), (9, 9, 0)),
                    fold_rows(place, down_ref, down_sum, ROW_PARTS, take),
                )
            ),
        )

    return transfer(
        f"last{number}",
        number,
        body,
        [qkv_part, norm_part, gain_part, out_sum, down_part],
        [
            shape(qkv_piece, jnp.float32),
            shape(norm_piece, jnp.float32),
            shape(gain_piece[1:], jnp.float32),
            shape(out_sum.shape, jnp.bfloat16),
            shape(down_part.shape[1:], jnp.float32),
        ],
        [pltpu.VMEM(gain_piece, jnp.float32)]
        + reduce_blk_scratch(count, qkv_piece, jnp.bfloat16)
        + reduce_blk_scratch(count, gain_piece, jnp.float32, 1)
        + reduce_group_scratch(gain_piece[1:], jnp.float32)
        + exchange_group_sems()
        + reduce_group_scratch(norm_piece, jnp.bfloat16)
        + fold_rows_scratch(down_part.shape[1:], ROW_PARTS),
        qkv_part.size * 2,
        [pltpu.VMEM] * 4 + [pl.ANY],
        [pltpu.VMEM] * 4 + [pl.ANY],
    )


GROUP_PARTS = 4


def all_gather_group(value, number):
    parts = GROUP_PARTS

    def body(src, out, *sems):
        place = Place(lax.axis_size("blk"))
        greet(place, core=True, half=True)
        together(*gather_group_rows(place, src, out, parts, Taker(sems), False))

    return transfer(
        f"group{number}",
        number,
        body,
        [value],
        [shape((GROUPS,) + value.shape, value.dtype)],
        gather_group_sems() * parts,
        value.size * 8,
    )[0]


def reduce_scatter_group(value, number):
    piece = value.shape[1:]
    parts = GROUP_PARTS
    steps = piece[0] // parts

    def body(part, out, *scratch):
        take = Taker(scratch)
        place = Place(lax.axis_size("blk"))
        greet(place, core=True, half=True)

        def task(p):
            at = pl.ds(p * steps, steps)
            return reduce_group(place, lambda g: part.at[g, at], out.at[at], *take(5))

        together(*[task(p) for p in range(parts)])

    return transfer(
        f"fold{number}",
        number,
        body,
        [value],
        [shape(piece, jnp.float32)],
        reduce_group_scratch((steps,) + piece[1:], value.dtype) * parts,
        value.size * 2,
        [pltpu.VMEM],
    )[0]


def dot(left, right, contract):
    return lax.dot_general(left, right, (contract, ((), ())), preferred_element_type=jnp.float32)


LAST = ((1,), (1,))
PLAIN = ((1,), (0,))
FIRST = ((0,), (0,))


LANES = 128
GELU_A = math.sqrt(2.0 / math.pi)
GELU_B = 0.044715


def feed_forward_fits(count, rows, width, hidden):
    inner = 4 if count >= 32 else 2
    outer = count // inner
    tile = rows * width * 2
    weights = 3 * hidden * width * 2
    kept = count * rows * 3 * hidden * 2
    total = weights + kept + tile * (3 * count + outer * (inner - 1) + 2 * outer + 3) + 9 * tile
    total += 6 * LANES * (count * rows + 3 * 256) * 2
    return total < 58 * 2**20 and hidden % (3 * LANES) == 0 and width % 256 == 0


def feed_forward_kernel(
    count,
    branch_ref,
    token_ref,
    cot_ref,
    gain_ref,
    gate_up_hbm,
    down_hbm,
    out_ref,
    middle_grad_ref,
    branch_grad_ref,
    gain_grad_ref,
    gate_up_grad_hbm,
    down_grad_hbm,
    w_gate_up,
    w_down,
    norm_all,
    grad_all,
    act,
    hidden,
    part,
    middle,
    norm_own,
    grad_own,
    total,
    turned,
    staged,
    beside,
    along,
    held,
    spare,
    w_sems,
    out_sems,
    *sems,
):
    place = Place(count)
    rows, width = norm_all.shape[1:]
    units = hidden.shape[1]
    chunks = units // LANES
    inner, outer = place.inner, place.outer
    slab = branch_ref.shape[1]
    steps = rows // slab
    columns = width // 256
    pair = inner * rows
    take = Taker(sems)

    def weight_copies(i):
        units_at = pl.ds(pl.multiple_of(i * LANES, LANES), LANES)
        return [
            pltpu.make_async_copy(
                gate_up_hbm.at[units_at, pl.ds(0, width)],
                w_gate_up.at[i, pl.ds(0, LANES)],
                w_sems.at[3 * i],
            ),
            pltpu.make_async_copy(
                gate_up_hbm.at[units_at, pl.ds(width, width)],
                w_gate_up.at[i, pl.ds(LANES, LANES)],
                w_sems.at[3 * i + 1],
            ),
            pltpu.make_async_copy(down_hbm.at[units_at], w_down.at[units_at], w_sems.at[3 * i + 2]),
        ]

    def start_weights(i, carry):
        for copy in weight_copies(i):
            copy.start()
        return carry

    def wait_weights(i, carry):
        for copy in weight_copies(i):
            copy.wait()
        return carry

    lax.fori_loop(0, chunks, start_weights, 0)

    def scale_of(values):
        return lax.rsqrt(jnp.mean(values * values, axis=-1, keepdims=True) + NORM_EPS)

    def slab_rows(i):
        return pl.ds(pl.multiple_of(i * slab, slab), slab)

    def before(i, carry):
        value = branch_ref[i]
        mid = token_ref[i].astype(jnp.float32) + value * scale_of(value) * gain_ref[1:2]
        middle[i] = mid
        norm_own[slab_rows(i)] = (mid * scale_of(mid) * gain_ref[2:3]).astype(jnp.bfloat16)
        return carry

    lax.fori_loop(0, steps, before, 0)
    greet(place, blk=True)

    def pair_rows(k):
        return pl.ds(pl.multiple_of(place.near_at(k) * pair, pair), pair)

    def pair_pieces(k):
        return pl.ds(place.near_at(k) * inner, inner)

    def column(n):
        return pl.ds(pl.multiple_of(n * 256, 256), 256)

    def put_part(k, n, value):
        split = value.astype(jnp.bfloat16).reshape((inner, steps, slab, 256))
        part[pair_pieces(k), :, :, column(n)] = split

    def receive(gather, k):
        def one(static):
            if static == 0:
                gather.copy.wait()
            advance([gather], static)
            gather.beside_arrived(static)

        for static in range(outer):
            pl.when(k == static)(lambda static=static: one(static))

    gather = GatherBlk(place, norm_own, lambda i: norm_all.at[i], *take(3))
    gather.start()
    lax.fori_loop(0, chunks, wait_weights, 0)
    def forward(k, carry):
        receive(gather, k)
        at = pair_rows(k)

        def up_chunk(j, carry):
            x = norm_all[pair_pieces(k)].reshape(pair, width)
            both = dot(x, w_gate_up[j], LAST)
            act[at, column(j)] = both.astype(jnp.bfloat16)
            gate, up = both[:, :LANES], both[:, LANES:]
            bent = 0.5 * gate * (1.0 + jnp.tanh(GELU_A * (gate + GELU_B * (gate * gate * gate))))
            hidden[at, pl.ds(pl.multiple_of(j * LANES, LANES), LANES)] = (bent * up).astype(
                jnp.bfloat16
            )
            return carry

        lax.fori_loop(0, chunks, up_chunk, 0)

        def down_chunk(n, carry):
            put_part(k, n, dot(hidden[at, :], w_down[:, column(n)], PLAIN))
            return carry

        lax.fori_loop(0, columns, down_chunk, 0)
        return carry

    lax.fori_loop(0, outer, forward, 0)
    gather.finish()
    reduce = ReduceBlk(place, lambda i: part.at[i], total, beside, along, held, spare, *take(6))
    reduce.start()
    for event in reduce.events():
        event()

    gain_grad_ref[...] = jnp.zeros_like(gain_grad_ref)

    def norm_back(value, gain, incoming):
        scale = scale_of(value)
        lifted = incoming * gain
        pull = jnp.mean(lifted * value, axis=-1, keepdims=True)
        gain_grad = jnp.sum(incoming * value * scale, axis=0, keepdims=True)
        return scale * lifted - value * (scale * scale * scale) * pull, gain_grad

    def between(i, carry):
        value, cot = total[i], cot_ref[i].astype(jnp.float32)
        gain = gain_ref[3:4]
        out_ref[i] = (middle[i] + value * scale_of(value) * gain).astype(jnp.bfloat16)
        grad, gain_grad = norm_back(value, gain, cot)
        gain_grad_ref[3:4] += gain_grad
        grad_own[slab_rows(i)] = grad.astype(jnp.bfloat16)
        return carry

    lax.fori_loop(0, steps, between, 0)
    reduce.finish()

    gather = GatherBlk(place, grad_own, lambda i: grad_all.at[i], *take(3))
    gather.start()
    def backward(k, carry):
        receive(gather, k)
        at = pair_rows(k)

        def back_chunk(j, carry):
            g = grad_all[pair_pieces(k)].reshape(pair, width)
            units_at = pl.ds(pl.multiple_of(j * LANES, LANES), LANES)
            grad = dot(g, w_down[units_at], LAST)
            both = act[at, column(j)].astype(jnp.float32)
            gate, up = both[:, :LANES], both[:, LANES:]
            bend = jnp.tanh(GELU_A * (gate + GELU_B * (gate * gate * gate)))
            bent = 0.5 * gate * (1.0 + bend)
            slope = 0.5 * (1.0 + bend) + (0.5 * GELU_A) * gate * (1.0 - bend * bend) * (
                1.0 + (3.0 * GELU_B) * gate * gate
            )
            pulled = jnp.concatenate([grad * up * slope, grad * bent], axis=1)
            act[at, column(j)] = pulled.astype(jnp.bfloat16)
            return carry

        lax.fori_loop(0, chunks, back_chunk, 0)

        def input_chunk(n, carry):
            w = w_gate_up[:, :, column(n)].reshape(2 * units, 256)
            put_part(k, n, dot(act[at, :], w, PLAIN))
            return carry

        lax.fori_loop(0, columns, input_chunk, 0)
        return carry

    lax.fori_loop(0, outer, backward, 0)
    gather.finish()
    reduce = ReduceBlk(place, lambda i: part.at[i], total, beside, along, held, spare, *take(6))
    reduce.start()

    tokens = count * rows
    slots = staged.shape[0]
    three = 3 * LANES

    def up_store(step):
        slot = lax.rem(step, slots)
        i, n = step // columns, lax.rem(step, columns)
        return [
            pltpu.make_async_copy(
                staged.at[slot, pl.ds((2 * q + h) * LANES, LANES)],
                gate_up_grad_hbm.at[
                    pl.ds(pl.multiple_of((3 * i + q) * LANES, LANES), LANES),
                    pl.ds(pl.multiple_of(h * width + n * 256, 256), 256),
                ],
                out_sems.at[slot, 2 * q + h],
            )
            for q in range(3)
            for h in (0, 1)
        ]

    def up_grad(step, carry):
        slot = lax.rem(step, slots)
        i, n = step // columns, lax.rem(step, columns)

        @pl.when(step >= slots)
        def _():
            for copy in up_store(step - slots):
                copy.wait()

        @pl.when(n == 0)
        def _():
            turned[...] = jnp.transpose(act[:, pl.ds(pl.multiple_of(2 * i * three, three), 2 * three)])

        x = norm_all[:, :, column(n)].reshape(tokens, 256)
        staged[slot] = dot(turned[...], x, PLAIN).astype(jnp.bfloat16)
        for copy in up_store(step):
            copy.start()
        return carry

    def down_store(step):
        slot = lax.rem(step, slots)
        i, n = step // columns, lax.rem(step, columns)
        return pltpu.make_async_copy(
            staged.at[slot, pl.ds(0, three)],
            down_grad_hbm.at[pl.ds(pl.multiple_of(i * three, three), three), column(n)],
            out_sems.at[slot, 6],
        )

    def down_grad(step, carry):
        slot = lax.rem(step, slots)
        i, n = step // columns, lax.rem(step, columns)

        @pl.when(step >= slots)
        def _():
            down_store(step - slots).wait()

        @pl.when(n == 0)
        def _():
            turned[pl.ds(0, three)] = jnp.transpose(
                hidden[:, pl.ds(pl.multiple_of(i * three, three), three)]
            )

        x = grad_all[:, :, column(n)].reshape(tokens, 256)
        staged[slot, pl.ds(0, three)] = dot(turned[pl.ds(0, three)], x, PLAIN).astype(jnp.bfloat16)
        down_store(step).start()
        return carry

    ups, downs = chunks // 3 * columns, units // three * columns
    events = reduce.events()
    early = len(events) - 3
    for k in range(early):
        lax.fori_loop(ups * k // early, ups * (k + 1) // early, up_grad, 0)
        events[k]()
    for step in range(max(0, ups - slots), ups):
        for copy in up_store(step):
            copy.wait()
    for k in range(3):
        lax.fori_loop(downs * k // 3, downs * (k + 1) // 3, down_grad, 0)
        events[early + k]()

    def after(i, carry):
        value, mid, cot = branch_ref[i], middle[i], cot_ref[i].astype(jnp.float32)
        grad, gain_grad = norm_back(mid, gain_ref[2:3], total[i])
        gain_grad_ref[2:3] += gain_grad
        middle_grad = cot + grad
        middle_grad_ref[i] = middle_grad
        grad, gain_grad = norm_back(value, gain_ref[1:2], middle_grad)
        gain_grad_ref[1:2] += gain_grad
        branch_grad_ref[i] = grad.astype(jnp.bfloat16)
        return carry

    lax.fori_loop(0, steps, after, 0)
    reduce.finish()
    for step in range(max(0, downs - slots), downs):
        down_store(step).wait()


def feed_forward(branch, tokens, cotangent, gains, gate_up_all, down_all, count, number):
    steps, slab, width = branch.shape
    rows = steps * slab
    units = down_all.shape[0]
    inner = 4 if count >= 32 else 2
    outer = count // inner
    piece = branch.shape
    bf16, f32 = jnp.bfloat16, jnp.float32
    vmem = pl.BlockSpec(memory_space=pltpu.VMEM)
    anywhere = pl.BlockSpec(memory_space=pl.ANY)
    slots = 3
    line_scratch = reduce_blk_scratch(count, piece, bf16)
    return pl.pallas_call(
        functools.partial(feed_forward_kernel, count),
        name="feed_forward",
        out_shape=[
            shape(piece, bf16),
            shape(piece, f32),
            shape(piece, bf16),
            shape((4, width), f32),
            shape(gate_up_all.shape, bf16),
            shape(down_all.shape, bf16),
        ],
        in_specs=[vmem] * 4 + [anywhere] * 2,
        out_specs=[vmem] * 4 + [anywhere] * 2,
        scratch_shapes=[
            pltpu.VMEM((units // LANES, 2 * LANES, width), bf16),
            pltpu.VMEM((units, width), bf16),
            pltpu.VMEM((count, rows, width), bf16),
            pltpu.VMEM((count, rows, width), bf16),
            pltpu.VMEM((count * rows, 2 * units), bf16),
            pltpu.VMEM((count * rows, units), bf16),
            pltpu.VMEM((count,) + piece, bf16),
            pltpu.VMEM(piece, f32),
            pltpu.VMEM((rows, width), bf16),
            pltpu.VMEM((rows, width), bf16),
            pltpu.VMEM(piece, f32),
            pltpu.VMEM((6 * LANES, count * rows), bf16),
            pltpu.VMEM((slots, 6 * LANES, 256), bf16),
        ]
        + line_scratch[:4]
        + [
            pltpu.SemaphoreType.DMA((3 * units // LANES,)),
            pltpu.SemaphoreType.DMA((slots, 7)),
        ]
        + gather_blk_sems(count)
        + line_scratch[4:]
        + gather_blk_sems(count)
        + line_scratch[4:],
        compiler_params=pltpu.CompilerParams(
            collective_id=number, has_side_effects=True, vmem_limit_bytes=67043328
        ),
        cost_estimate=pl.CostEstimate(
            flops=18 * count * rows * units * width,
            bytes_accessed=500 * 2**20,
            transcendentals=0,
        ),
    )(branch, tokens, cotangent, gains, gate_up_all, down_all)


def attention_scores(q2, k, query_pos, query_doc, key_block, key_doc, rows):
    raw = lax.dot_general(q2, k, (((1,), (1,)), ((), ())), preferred_element_type=jnp.float32)
    capped = jnp.tanh(raw * (SCORE_SCALE / SOFT_CAP))
    key_pos = key_block * rows + lax.broadcasted_iota(jnp.int32, (1, rows), 1)
    visible = (key_pos <= query_pos) & (key_doc == query_doc)
    return capped, jnp.where(visible, jnp.exp(SOFT_CAP * capped), 0.0)


def attention_query(q_ref, doc_ref, here, count, rows):
    half = pl.program_id(1)
    block = half * count + here
    q2 = jnp.concatenate([q_ref[0, :, :HEAD_DIM], q_ref[0, :, HEAD_DIM:]], axis=0)
    inside = lax.broadcasted_iota(jnp.int32, (rows, 1), 0)
    position = block * rows + jnp.concatenate([inside, inside], axis=0)
    doc = jnp.concatenate([doc_ref[0], doc_ref[0]], axis=0)
    return block, q2, position, doc


def attention_backward_kernel(
    count,
    here_ref,
    q_ref,
    kv_ref,
    doc_ref,
    key_doc_ref,
    grad_ref,
    full_ref,
    total_ref,
    dq_ref,
    dkv_ref,
    acc,
    key_acc,
):
    rows = q_ref.shape[1]
    half = pl.program_id(1)
    block, q2, position, doc = attention_query(q_ref, doc_ref, here_ref[0], count, rows)
    total = total_ref[0]
    grad = grad_ref[0].astype(jnp.float32)
    grad2 = jnp.concatenate([grad[:, :HEAD_DIM], grad[:, HEAD_DIM:]], axis=0)
    full2 = jnp.concatenate([full_ref[0, :, :HEAD_DIM], full_ref[0, :, HEAD_DIM:]], axis=0)
    total_grad = -jnp.sum(grad2 * full2, axis=-1, keepdims=True) / total
    sums_grad = (grad2 / total).astype(jnp.bfloat16)
    acc[...] = jnp.zeros_like(acc)

    @pl.when(half == 0)
    def _():
        def clear(i, carry):
            key_acc[i] = jnp.zeros(key_acc.shape[1:], jnp.float32)
            return carry

        lax.fori_loop(0, key_acc.shape[0], clear, 0)

    def one(key_block, carry):
        key_half = (key_block >= count).astype(jnp.int32)
        inner = key_block - key_half * count
        kv = kv_ref.at[inner, key_half]
        keys = kv[:, :HEAD_DIM]
        capped, weights = attention_scores(
            q2, keys, position, doc, key_block, key_doc_ref[0, key_block], rows
        )
        exp_grad = lax.dot_general(
            sums_grad, kv[:, HEAD_DIM:], (((1,), (1,)), ((), ())), preferred_element_type=jnp.float32
        )
        raw_grad = (
            weights * (exp_grad + total_grad) * (1.0 - capped * capped) * SCORE_SCALE
        ).astype(jnp.bfloat16)
        acc[...] += jnp.dot(raw_grad, keys, preferred_element_type=jnp.float32)
        over_rows = (((0,), (0,)), ((), ()))
        slot = inner * 2 + key_half
        key_acc[slot, :, :HEAD_DIM] += lax.dot_general(
            raw_grad, q2, over_rows, preferred_element_type=jnp.float32
        )
        key_acc[slot, :, HEAD_DIM:] += lax.dot_general(
            weights.astype(jnp.bfloat16), sums_grad, over_rows, preferred_element_type=jnp.float32
        )
        return carry

    lax.fori_loop(jnp.maximum(block - count, 0), block + 1, one, 0)
    dq = acc[...]
    dq_ref[0] = jnp.concatenate([dq[:rows], dq[rows:]], axis=1).astype(jnp.bfloat16)

    @pl.when(half == 1)
    def _():
        def put(i, carry):
            for k in (0, 1):
                dkv_ref[i, k] = key_acc[i * 2 + k].astype(jnp.bfloat16)
            return carry

        lax.fori_loop(0, count, put, 0)


def attention_specs(count, rows, width):
    query = pl.BlockSpec((1, rows, width), lambda s, h, here: (2 * s + h, 0, 0))
    keys = pl.BlockSpec((count, 2, rows, 2 * HEAD_DIM), lambda s, h, here: (0, s, 0, 0))
    doc = pl.BlockSpec((1, rows, 1), lambda s, h, here: (2 * s + h, 0, 0))
    key_doc = pl.BlockSpec((1, 2 * count, 1, rows), lambda s, h, here: (s, 0, 0, 0))
    total = pl.BlockSpec((1, REPS * rows, 1), lambda s, h, here: (2 * s + h, 0, 0))
    return query, keys, doc, key_doc, total


def attention_backward(here, q, kv, doc, key_doc, grad, full, totals):
    count, _, rows, _ = kv.shape
    width = REPS * HEAD_DIM
    query, keys, doc_spec, key_doc_spec, total = attention_specs(count, rows, width)
    return pl.pallas_call(
        functools.partial(attention_backward_kernel, count),
        name="attend_back",
        grid_spec=pltpu.PrefetchScalarGridSpec(
            num_scalar_prefetch=1,
            grid=(2, 2),
            in_specs=[query, keys, doc_spec, key_doc_spec, query, query, total],
            out_specs=[query, keys],
            scratch_shapes=[
                pltpu.VMEM((REPS * rows, HEAD_DIM), jnp.float32),
                pltpu.VMEM((2 * count, rows, 2 * HEAD_DIM), jnp.float32),
            ],
        ),
        out_shape=[shape((GROUPS, rows, width), jnp.bfloat16), shape(kv.shape, jnp.bfloat16)],
        compiler_params=pltpu.CompilerParams(vmem_limit_bytes=VMEM_LIMIT),
        cost_estimate=pl.CostEstimate(flops=2 * 10**9, bytes_accessed=80 * 2**20, transcendentals=0),
    )(here, q, kv, doc, key_doc, grad, full, totals)


def rms_scale(values, gain_row):
    return (
        values * lax.rsqrt(jnp.mean(values * values, axis=-1, keepdims=True) + NORM_EPS) * gain_row
    )


def gelu_tanh(values):
    return jax.nn.gelu(values, approximate=True)


def rope_tables(positions):
    half_width = HEAD_DIM // 2
    frequency = jnp.exp(
        jnp.arange(half_width, dtype=jnp.float32) * (-2.0 * math.log(ROPE_BASE) / HEAD_DIM)
    )
    angles = positions.astype(jnp.float32)[:, None] * frequency[None, :]
    cosine = jnp.concatenate([jnp.cos(angles), jnp.cos(angles)], axis=-1)
    sine = jnp.concatenate([jnp.sin(angles), jnp.sin(angles)], axis=-1)
    return cosine[:, None, :], sine[:, None, :]


def rotate(values, cosine, sine):
    half_width = HEAD_DIM // 2
    turned = jnp.concatenate([-values[..., half_width:], values[..., :half_width]], axis=-1)
    return values * cosine + turned * sine


def feed_forward_apart(
    branch_slabs, inputs, cotangent, gains, gate_up_all, down_all, count, piece
):
    rows, width = inputs.shape
    bf16 = jnp.bfloat16
    branch = branch_slabs.reshape(rows, width)
    middle = inputs + rms_scale(branch, gains[1])
    norm_three = rms_scale(middle, gains[2]).astype(bf16)
    gate_all = gate_up_all[:, :width]
    up_all = gate_up_all[:, width:]
    norm_all = all_gather_blk(norm_three, count, 4).reshape(count * rows, width)
    gate = dot(norm_all, gate_all, LAST)
    up = dot(norm_all, up_all, LAST)
    hidden = (gelu_tanh(gate) * up).astype(bf16)
    ffn_part = dot(hidden, down_all, PLAIN).astype(bf16)
    ffn_out = reduce_scatter_blk(ffn_part.reshape((count,) + piece), count, 5).reshape(rows, width)
    output = (middle + rms_scale(ffn_out, gains[3])).astype(bf16)[None]

    out_cotangent = cotangent[0].astype(jnp.float32)
    _, post_ffn_back = jax.vjp(rms_scale, ffn_out, gains[3])
    ffn_grad, gain_grad_four = post_ffn_back(out_cotangent)
    grad_all = all_gather_blk(ffn_grad.astype(bf16), count, 6).reshape(count * rows, width)
    activated, gelu_back = jax.vjp(gelu_tanh, gate)
    hidden_grad = dot(grad_all, down_all, LAST)
    gate_grad = gelu_back(hidden_grad * up)[0].astype(bf16)
    up_grad = (hidden_grad * activated).astype(bf16)
    norm_part = dot(gate_grad, gate_all, PLAIN) + dot(up_grad, up_all, PLAIN)
    norm_three_grad = reduce_scatter_blk(
        norm_part.astype(bf16).reshape((count,) + piece), count, 7
    ).reshape(rows, width)
    down_part = dot(hidden, grad_all, FIRST).astype(bf16)
    gate_up_part = jnp.concatenate(
        [dot(gate_grad, norm_all, FIRST), dot(up_grad, norm_all, FIRST)], axis=1
    ).astype(bf16)
    _, pre_ffn_back = jax.vjp(rms_scale, middle, gains[2])
    middle_part, gain_grad_three = pre_ffn_back(norm_three_grad)
    middle_grad = out_cotangent + middle_part
    _, post_attn_back = jax.vjp(rms_scale, branch, gains[1])
    branch_grad, gain_grad_two = post_attn_back(middle_grad)
    return (
        output,
        middle_grad,
        branch_grad.astype(bf16),
        gain_grad_two,
        gain_grad_three,
        gain_grad_four,
        gate_up_part,
        down_part,
    )


def shards(
    tokens, cotangent, segments, norm_gains, qkv_weight, out_weight, gate_up_weight, down_weight
):
    _, rows, width = tokens.shape
    count = lax.axis_size("blk")
    here = lax.axis_index("blk")
    mine = 2 * lax.axis_index("dp") + lax.axis_index("head")
    group_rows = GROUPS * rows
    head_width = REPS * HEAD_DIM
    bf16 = jnp.bfloat16
    slab = slabs(rows)
    piece = (rows // slab, slab, width)

    gain_rows = norm_gains.shape[0]
    gain_lanes = -(-gain_rows // 128) * 128
    gains_sent = jnp.pad(
        jnp.transpose(norm_gains).astype(jnp.float32), ((0, 4), (0, gain_lanes - gain_rows))
    )
    out_rows = out_weight.shape[0]
    out_sent = jnp.transpose(out_weight.reshape(out_rows, GROUPS, head_width), (1, 0, 2))
    qkv_rows = qkv_weight.shape[0]
    qkv_slab = slabs(qkv_rows)
    qkv_piece = (qkv_rows // qkv_slab, qkv_slab, width)
    qkv_all, out_mine, tokens_all, gains_all, docs_all, down_all = gather_first(
        qkv_weight,
        out_sent,
        tokens[0],
        gains_sent,
        segments.reshape(-1, 128),
        down_weight,
        count,
        1,
    )
    down_all = down_all.reshape(-1, width)
    gains = jnp.transpose(gains_all[:, :, :4, :gain_rows], (2, 0, 1, 3)).reshape(4, width)
    qkv_head = qkv_all.reshape(count * qkv_rows, width)
    docs = docs_all.reshape(2, 2, count, rows)
    key_doc = docs.reshape(2, 2 * count, 1, rows)
    own_doc = lax.dynamic_index_in_dim(docs, here, 2, keepdims=False).reshape(GROUPS, rows, 1)
    here_one = here.reshape(1)

    group_tokens = tokens_all.reshape(group_rows, width).astype(jnp.float32)
    norm_one = rms_scale(group_tokens, gains[0]).astype(bf16)
    proj = dot(norm_one, qkv_head, LAST)
    inside = jnp.arange(rows, dtype=jnp.int32)
    position = jnp.concatenate([here * rows + inside, (count + here) * rows + inside])
    cosine, sine = rope_tables(jnp.concatenate([position, position]))
    proj = proj.reshape(group_rows, REPS + 2, HEAD_DIM)
    turned = rotate(proj[:, : REPS + 1], cosine, sine)
    sent = jnp.concatenate([turned, proj[:, REPS + 1 :]], axis=1).astype(bf16)
    queries = sent[:, :REPS].reshape(GROUPS, rows, head_width)
    own_kv = sent[:, REPS:].reshape(group_rows, 2 * HEAD_DIM)
    kv_slab = slabs(group_rows)
    kv_piece = (group_rows // kv_slab, kv_slab, 2 * HEAD_DIM)
    kv, out_all, gate_up_all, attn, attended, totals = gather_attend(
        own_kv, out_mine, gate_up_weight, queries, own_doc, key_doc, count, 2
    )
    gate_up_all = gate_up_all.reshape(-1, 2 * width)
    out_head = out_all.reshape(width, head_width)
    attn = attn.reshape(group_rows, head_width)
    branch_part = dot(attn, out_head, LAST).astype(bf16)
    branch_slabs = reduce_scatter_group(branch_part.reshape((GROUPS,) + piece), 3)
    inputs = tokens[0].astype(jnp.float32)
    if feed_forward_fits(count, rows, width, down_all.shape[0]):
        output, middle_grad, branch_grad, gain_rest, gate_up_part, down_part = feed_forward(
            branch_slabs,
            tokens.reshape(piece),
            cotangent.reshape(piece),
            gains,
            gate_up_all,
            down_all,
            count,
            4,
        )
        output = output.reshape(tokens.shape)
        middle_grad = middle_grad.reshape(rows, width)
        branch_grad = branch_grad.reshape(rows, width)
        gain_grad_two, gain_grad_three, gain_grad_four = gain_rest[1], gain_rest[2], gain_rest[3]
    else:
        (
            output,
            middle_grad,
            branch_grad,
            gain_grad_two,
            gain_grad_three,
            gain_grad_four,
            gate_up_part,
            down_part,
        ) = feed_forward_apart(
            branch_slabs, inputs, cotangent, gains, gate_up_all, down_all, count, piece
        )
    branch_all = all_gather_group(branch_grad, 8).reshape(group_rows, width)
    attn_grad = dot(branch_all, out_head, PLAIN).astype(bf16).reshape(GROUPS, rows, head_width)
    out_part = dot(branch_all, attn, FIRST).astype(bf16)
    out_part = out_part.reshape(GROUPS, count, out_rows, head_width)
    gate_up_part = gate_up_part.reshape((GROUPS,) + gate_up_weight.shape)
    if attend_back_fits(count):
        dq, dkv, out_sum, gate_up_grad = attend_back_reduce(
            queries,
            kv,
            own_doc,
            key_doc,
            attn_grad,
            attended,
            totals,
            out_part,
            gate_up_part,
            kv_piece,
            count,
            9,
        )
    else:
        kv = kv.reshape(count, GROUPS, rows, 2 * HEAD_DIM)
        dq, dkv_part = attention_backward(
            here_one, queries, kv, own_doc, key_doc, attn_grad, attended, totals
        )
        dkv, out_sum, gate_up_grad = reduce_middle(
            dkv_part.reshape((count,) + kv_piece), out_part, gate_up_part, count, 9
        )
    sent_grad = jnp.concatenate(
        [
            dq.reshape(group_rows, REPS, HEAD_DIM),
            dkv.reshape(group_rows, 2, HEAD_DIM),
        ],
        axis=1,
    ).astype(jnp.float32)
    unturned = rotate(sent_grad[:, : REPS + 1], cosine, -sine)
    proj_grad = (
        jnp.concatenate([unturned, sent_grad[:, REPS + 1 :]], axis=1)
        .astype(bf16)
        .reshape(group_rows, (REPS + 2) * HEAD_DIM)
    )
    qkv_part = dot(proj_grad, norm_one, FIRST).astype(bf16)
    norm_one_part = dot(proj_grad, qkv_head, PLAIN)
    _, gain_back = jax.vjp(lambda gain: rms_scale(group_tokens, gain), gains[0])
    (gain_grad_one,) = gain_back(norm_one_part)
    gain_part = jnp.stack([gain_grad_one, gain_grad_two, gain_grad_three, gain_grad_four])
    gain_part = jnp.transpose(gain_part.reshape(4, GROUPS, count, gain_rows), (2, 1, 0, 3))
    gain_part = jnp.pad(gain_part, ((0, 0), (0, 0), (0, 4), (0, gain_lanes - gain_rows)))
    qkv_grad, norm_one_grad, gain_grad, out_grad, down_grad = reduce_last(
        qkv_part.reshape((count,) + qkv_piece),
        norm_one_part.astype(bf16).reshape((GROUPS,) + piece),
        gain_part[:, :, None],
        out_sum,
        down_part.reshape((GROUPS,) + down_weight.shape),
        count,
        10,
    )
    qkv_grad = qkv_grad.reshape(qkv_rows, width)
    out_grad = (
        jnp.transpose(out_grad, (1, 0, 2)).reshape(out_rows, GROUPS * head_width).astype(jnp.float32)
    )
    gain_grad = jnp.transpose(gain_grad.reshape(8, gain_lanes)[:4, :gain_rows])
    _, pre_attn_back = jax.vjp(lambda values: rms_scale(values, gains[0]), inputs)
    (input_part,) = pre_attn_back(norm_one_grad.reshape(rows, width))
    tokens_grad = (middle_grad + input_part).astype(bf16)[None]
    return (output, tokens_grad, gain_grad, qkv_grad, out_grad, gate_up_grad, down_grad)


def solution(mesh):
    whole = ("dp", "head", "blk")
    return jax.shard_map(
        shards,
        mesh=mesh,
        in_specs=(
            P("dp", ("head", "blk"), None),
            P("dp", ("head", "blk"), None),
            P("dp", None),
            P(whole, None),
            P(whole, None),
            P(whole, None),
            P(whole, None),
            P(whole, None),
        ),
        out_specs=(
            P("dp", ("head", "blk"), None),
            P("dp", ("head", "blk"), None),
            P(whole, None),
            P(whole, None),
            P(whole, None),
            P(whole, None),
            P(whole, None),
        ),
        check_vma=False,
    )
```

```python
import functools
import math

import jax
import jax.numpy as jnp
from jax import lax
from jax.experimental import pallas as pl
from jax.experimental.pallas import tpu as pltpu
from jax.sharding import PartitionSpec as P

HEADS = 8
KV_HEADS = 4
HEAD_DIM = 256
REPS = HEADS // KV_HEADS
GROUPS = 4
SOFT_CAP = 50.0
NORM_EPS = 1e-06
ROPE_BASE = 10000.0
SCORE_SCALE = HEAD_DIM ** (-0.5)

MESH = pl.DeviceIdType.MESH
VMEM_LIMIT = 60 * 1024 * 1024


class Place:
    def __init__(self, count):
        self.count = count
        self.inner = 4 if count >= 32 else 2
        self.outer = count // self.inner
        self.here = lax.axis_index("blk")
        self.line = self.here // self.inner
        self.side = lax.rem(self.here, self.inner)
        self.core = lax.axis_index("dp")
        self.half = lax.axis_index("head")
        self.group = 2 * self.core + self.half

    def near(self, k):
        orders = [near_order(self.outer, line)[k] for line in range(self.outer)]
        found = jnp.int32(orders[0])
        for line in range(1, self.outer):
            found = jnp.where(self.line == line, jnp.int32(orders[line]), found)
        return found

    def near_at(self, k):
        found = self.near(0)
        for static in range(1, self.outer):
            found = jnp.where(k == static, self.near(static), found)
        return found

    def at(self, line, side):
        return {"blk": line * self.inner + side}

    def beside(self, step):
        return lax.rem(self.side + step, self.inner)

    def partner(self):
        return {"dp": 1 - self.core}

    def across(self):
        return {"head": 1 - self.half}

    def corner(self):
        return {"dp": 1 - self.core, "head": 1 - self.half}


def remote(src, dst, sent, came, device):
    return pltpu.make_async_remote_copy(
        src_ref=src, dst_ref=dst, send_sem=sent, recv_sem=came, device_id=device, device_id_type=MESH
    )


def greet(place, blk=False, core=False, half=False, corner=False):
    sem = pltpu.get_barrier_semaphore()
    amount = jnp.int32(0)

    def hello(device):
        pl.semaphore_signal(sem, inc=1, device_id=device, device_id_type=MESH)

    if blk:
        up, down = place.line < place.outer - 1, place.line > 0
        pl.when(up)(lambda: hello(place.at(place.line + 1, place.side)))
        pl.when(down)(lambda: hello(place.at(place.line - 1, place.side)))
        amount = amount + up.astype(jnp.int32) + down.astype(jnp.int32) + (place.inner - 1)
        for step in range(1, place.inner):
            hello(place.at(place.line, place.beside(step)))
    for wanted, device in (
        (core, place.partner()),
        (half, place.across()),
        (corner, place.corner()),
    ):
        if wanted:
            hello(device)
            amount = amount + 1
    pl.semaphore_wait(sem, amount)


def together(*tasks):
    tasks = list(tasks)
    while tasks:
        for task in list(tasks):
            try:
                next(task)
            except StopIteration:
                tasks.remove(task)


def waiting(task, *rounds):
    for step, _ in enumerate(task):
        yield
        if step < len(rounds):
            for _ in range(rounds[step]):
                yield


def near_order(outer, line):
    ends = outer == 4
    return sorted(
        range(outer),
        key=lambda other: (abs(other - line), ends and other not in (0, outer - 1), other),
    )


def evened(place, parts):
    return parts == 2 and place.inner == 2 and place.outer == 4


def part_of(ref, h, parts):
    if parts == 1:
        return ref
    size = ref.shape[0] // parts
    return ref.at[pl.ds(h * size, size)]


def gather_blk_sems(place_count, parts=2):
    inner = 4 if place_count >= 32 else 2
    return [
        pltpu.SemaphoreType.DMA((2 + inner, place_count, parts)),
        pltpu.SemaphoreType.DMA((place_count, parts)),
        pltpu.SemaphoreType.DMA,
    ]


class GatherBlk:
    def __init__(self, place, src, view, sent, came, own):
        self.place, self.src, self.view, self.sent, self.came = place, src, view, sent, came
        self.parts = came.shape[1]
        self.evened = evened(place, self.parts)
        self.middle = (place.line > 0) & (place.line < place.outer - 1)
        self.copy = pltpu.make_async_copy(src, view(place.here), own)

    def sends(self, k, h):
        place = self.place
        there = place.near(k)
        piece = there * place.inner + place.side
        there_view = part_of(self.view(piece), h, self.parts)
        src = part_of(self.src, h, self.parts) if k == 0 else there_view

        def send(kind, device):
            return remote(
                src, there_view, self.sent.at[kind, piece, h], self.came.at[piece, h], device
            )

        line, side = place.line, place.side
        up = (there <= line) & (line < place.outer - 1)
        down = (there >= line) & (line > 0)
        aside = range(1, place.inner)
        if self.evened and h == 1 and k == place.outer - 1:
            aside = ()
        return (
            [
                (up, lambda: send(0, place.at(line + 1, side))),
                (down, lambda: send(1, place.at(line - 1, side))),
            ],
            [send(1 + step, place.at(line, place.beside(step))) for step in aside],
        )

    def forward(self, k, h):
        along, aside = self.sends(k, h)
        for needed, make in along:
            pl.when(needed)(lambda make=make: make().start())
        for one in aside:
            one.start()

    def start(self):
        self.copy.start()
        for h in range(self.parts):
            self.forward(0, h)

    def arrived(self, piece, h):
        place = self.place
        remote(
            part_of(self.src, h, self.parts),
            part_of(self.view(piece), h, self.parts),
            self.sent.at[0, piece, h],
            self.came.at[piece, h],
            place.at(place.line, place.beside(1)),
        ).wait_recv()

    def pass_on(self, k):
        for h in range(self.parts):
            self.arrived(self.place.near(k) * self.place.inner + self.place.side, h)
            self.forward(k, h)

    def extra(self, k):
        place = self.place
        piece = place.near(k) * place.inner + place.beside(1)
        to = place.near(2 if k == 1 else 1)
        half = part_of(self.view(piece), 1, 2)
        return remote(
            half,
            half,
            self.sent.at[place.inner + 1, piece, 1],
            self.came.at[piece, 1],
            place.at(to, place.side),
        )

    def pass_extra(self, k):
        if self.evened:

            @pl.when(self.middle)
            def _():
                self.arrived(self.place.near(k) * self.place.inner + self.place.beside(1), 1)
                self.extra(k).start()

    def beside_arrived(self, k):
        for step in range(1, self.place.inner):
            piece = self.place.near(k) * self.place.inner + self.place.beside(step)
            for h in range(self.parts):
                if self.evened and h == 1 and k in (1, self.place.outer - 1):
                    pl.when(jnp.logical_not(self.middle))(lambda: self.arrived(piece, 1))
                else:
                    self.arrived(piece, h)

    def finish(self):
        for k in range(self.place.outer):
            for h in range(self.parts):
                along, aside = self.sends(k, h)
                for needed, make in along:
                    pl.when(needed)(lambda make=make: make().wait_send())
                for one in aside:
                    one.wait_send()
        if self.evened:

            @pl.when(self.middle)
            def _():
                self.extra(1).wait_send()
                self.extra(self.place.outer - 1).wait_send()


def advance(gathers, k):
    place = gathers[0].place

    def each(name, *args):
        for gather in gathers:
            getattr(gather, name)(*args)

    if not gathers[0].evened:
        if k + 1 < place.outer:
            each("pass_on", k + 1)
        return
    middle = gathers[0].middle
    ends = jnp.logical_not(middle)
    if k == 0:
        each("pass_on", 1)
        pl.when(middle)(lambda: each("pass_on", 2))
    elif k == 1:
        pl.when(ends)(lambda: each("pass_on", 2))
        each("pass_extra", 1)
        pl.when(middle)(lambda: each("pass_on", 3))
    elif k == 2:
        pl.when(ends)(lambda: each("pass_on", 3))
        each("pass_extra", 3)


def gather_blk(place, src, view, sent, came, own):
    if not callable(view):
        out = view
        view = lambda piece: out.at[piece]
    work = GatherBlk(place, src, view, sent, came, own)
    work.start()
    yield
    for k in range(1, place.outer):
        work.pass_on(k)
        if k == place.outer - 2:
            work.pass_extra(1)
        yield
    work.pass_extra(place.outer - 1)
    yield
    for k in range(place.outer):
        work.beside_arrived(k)
    work.finish()
    work.copy.wait()


def add_into(out, *terms):
    lanes = out.shape[-1]
    parts = 3 if lanes % 384 == 0 and lanes > 1024 else 1
    step = lanes // parts

    def one(i, carry):
        at = i if parts == 1 else i // parts
        columns = pl.ds(pl.multiple_of((i % parts) * step, step), step) if parts > 1 else slice(None)
        index = (at,) + (slice(None),) * (len(out.shape) - 2) + (columns,)
        total = terms[0][index].astype(jnp.float32)
        for term in terms[1:]:
            total = total + term[index].astype(jnp.float32)
        out[index] = total.astype(out.dtype)
        return carry

    lax.fori_loop(0, out.shape[0] * parts, one, 0)


def reduce_blk_scratch(place_count, piece, dtype, parts=2):
    inner = 4 if place_count >= 32 else 2
    outer = place_count // inner
    half = (piece[0] // 2,) + tuple(piece[1:]) if parts == 2 and inner == 2 and outer == 4 else (1, 8, 128)
    return [
        pltpu.VMEM((outer, inner - 1) + piece, dtype),
        pltpu.VMEM((outer + 1,) + piece, dtype),
        pltpu.VMEM((outer,) + piece, dtype),
        pltpu.VMEM((4,) + half, dtype),
        pltpu.SemaphoreType.DMA((outer, inner - 1, parts)),
        pltpu.SemaphoreType.DMA((outer, inner - 1, parts)),
        pltpu.SemaphoreType.DMA((outer, parts)),
        pltpu.SemaphoreType.DMA((outer + 1, parts)),
        pltpu.SemaphoreType.DMA((2,)),
        pltpu.SemaphoreType.DMA((2,)),
    ]


REDUCE_REFS = 10


class ReduceBlk:
    def __init__(
        self,
        place,
        view,
        out,
        beside,
        along,
        held,
        spare,
        side_sent,
        side_came,
        line_sent,
        line_came,
        spare_sent,
        spare_came,
    ):
        self.place, self.view, self.out = place, view, out
        self.beside, self.along, self.held, self.spare = beside, along, held, spare
        self.side_sems, self.line_sems = (side_sent, side_came), (line_sent, line_came)
        self.spare_sems = (spare_sent, spare_came)
        self.parts = line_sent.shape[1]
        self.evened = evened(place, self.parts)
        self.middle = (place.line > 0) & (place.line < place.outer - 1)

    def part(self, ref, h):
        return part_of(ref, h, self.parts)

    def far(self, k):
        return self.place.near(self.place.outer - 1 - k)

    def alone(self, k, h):
        return self.evened and k == 0 and h == 1

    def side_copy(self, there, step, h, src=None):
        place = self.place
        to = place.beside(step)
        if src is None:
            src = self.part(self.view(there * place.inner + to), h)
        return remote(
            src,
            self.part(self.beside.at[there, place.inner - step - 1], h),
            self.side_sems[0].at[there, step - 1, h],
            self.side_sems[1].at[there, place.inner - step - 1, h],
            place.at(place.line, to),
        )

    def line_copy(self, there, slot, to, h, src=None):
        return remote(
            self.part(self.held.at[there], h) if src is None else src,
            self.part(self.along.at[slot], h),
            self.line_sems[0].at[there, h],
            self.line_sems[1].at[slot, h],
            self.place.at(to, self.place.side),
        )

    def send(self, k, h):
        for step in range(1, self.place.inner):
            self.side_copy(self.far(k), step, h).start()

    def terms(self, k, h):
        place = self.place
        there = self.far(k)
        own = [self.part(self.view(there * place.inner + place.side), h)]
        if self.alone(k, h):
            return own
        for step in range(1, place.inner):
            self.side_copy(there, step, h).wait_recv()
        return own + [self.part(self.beside.at[there, j], h) for j in range(place.inner - 1)]

    def onward(self, there, h, src=None):
        line, outer = self.place.line, self.place.outer
        to = jnp.where(there < line, line - 1, line + 1)
        slot = jnp.where(there == line + 1, outer, there)
        return self.line_copy(there, slot, to, h, src)

    def starts(self, there):
        line, outer = self.place.line, self.place.outer
        return ((there < line) & (line == outer - 1)) | ((there > line) & (line == 0))

    def pass_on(self, k, h, middle=None):
        place = self.place
        line = place.line
        there = self.far(k)
        terms = self.terms(k, h)
        held = self.part(self.held.at[there], h)

        def first():
            add_into(held, *terms)

        def later():
            back = jnp.where(there < line, line + 1, line - 1)
            self.line_copy(there, there, back, h).wait_recv()
            add_into(held, self.part(self.along.at[there], h), *terms)

        if middle is None:
            starts = self.starts(there)
            pl.when(starts)(first)
            pl.when(jnp.logical_not(starts))(later)
        elif middle:
            later()
        else:
            first()
        self.onward(there, h).start()

    def last(self, h):
        place = self.place
        line, outer = place.line, place.outer
        terms = self.terms(outer - 1, h)
        out = self.part(self.out, h)

        @pl.when(self.middle)
        def _():
            self.line_copy(line, line, line + 1, h).wait_recv()
            self.line_copy(line, outer, line - 1, h).wait_recv()
            from_above = self.part(self.along.at[line], h)
            add_into(out, from_above, self.part(self.along.at[outer], h), *terms)

        @pl.when(jnp.logical_not(self.middle))
        def _():
            slot = jnp.where(line == 0, line, outer)
            back = jnp.where(line == 0, line + 1, line - 1)
            self.line_copy(line, slot, back, h).wait_recv()
            add_into(out, self.part(self.along.at[slot], h), *terms)


    def spare_view(self, k):
        place = self.place
        return self.part(self.view(place.near(k) * place.inner + place.beside(1)), 1)

    def spare_first(self):
        return remote(
            self.spare_view(3),
            self.spare.at[0],
            self.spare_sems[0].at[0],
            self.spare_sems[1].at[0],
            self.place.at(self.place.near(1), self.place.side),
        )

    def spare_second(self):
        return remote(
            self.spare.at[2],
            self.spare.at[1],
            self.spare_sems[0].at[1],
            self.spare_sems[1].at[1],
            self.place.at(self.place.near(2), self.place.side),
        )

    def spare_side(self):
        return self.side_copy(self.far(2), 1, 1, self.spare.at[3])

    def opening(self):
        outer = self.place.outer
        if not self.evened:

            def every():
                for k in range(outer):
                    for h in range(self.parts):
                        self.send(k, h)

            return [every]
        ends = jnp.logical_not(self.middle)

        def along():
            self.spare_first().start()
            there = self.far(0)
            self.onward(
                there, 1, self.part(self.view(there * self.place.inner + self.place.side), 1)
            ).start()

        todo = [lambda: self.send(0, 0), lambda: pl.when(ends)(along)]
        todo += [lambda k=k, h=h: self.send(k, h) for k, h in ((1, 0), (1, 1), (2, 0))]
        todo += [
            lambda k=k, h=h: pl.when(ends)(lambda: self.send(k, h))
            for k, h in ((2, 1), (3, 0), (3, 1))
        ]
        return todo

    def start(self):
        for step in self.opening():
            step()

    def turning(self):
        def first():
            self.spare_first().wait_recv()
            add_into(self.spare.at[2], self.spare.at[0], self.spare_view(3))
            self.spare_second().start()

        def second():
            self.spare_second().wait_recv()
            add_into(self.spare.at[3], self.spare.at[1], self.spare_view(1))
            self.spare_side().start()
            for h in (0, 1):
                self.send(3, h)

        steps = (first, lambda: self.pass_on(0, 1, True), second)
        return steps

    def events(self):
        outer, parts = self.place.outer, self.parts
        if self.evened:
            todo = [lambda step=step: pl.when(self.middle)(step) for step in self.turning()]
            todo.append(lambda: self.pass_on(0, 0))
        else:
            todo = [lambda h=h: self.pass_on(0, h) for h in range(parts)]
        for k in range(1, outer - 1):
            for h in range(parts):
                todo.append(lambda k=k, h=h: self.pass_on(k, h))
        for h in range(parts):
            todo.append(lambda h=h: self.last(h))
        return todo

    def finish(self):
        for k in range(self.place.outer):
            for h in range(self.parts):
                if k < self.place.outer - 1:
                    self.onward(self.far(k), h).wait_send()
                if not self.alone(k, h):
                    for step in range(1, self.place.inner):
                        self.side_copy(self.far(k), step, h).wait_send()
        if self.evened:

            @pl.when(self.middle)
            def _():
                self.spare_second().wait_send()

            @pl.when(jnp.logical_not(self.middle))
            def _():
                self.spare_first().wait_send()


def reduce_blk(place, view, out, *scratch):
    if not callable(view):
        part = view
        view = lambda piece: part.at[piece]
    work = ReduceBlk(place, view, out, *scratch)
    for step in work.opening() + work.events():
        step()
        yield
    work.finish()


def gather_group_sems():
    return [pltpu.SemaphoreType.DMA((3,)), pltpu.SemaphoreType.DMA((4,)), pltpu.SemaphoreType.DMA]


def gather_group(place, src, view, sent, came, own, through=None):
    if not callable(view):
        out = view
        view = lambda g: out.at[g]
    copy = pltpu.make_async_copy(src if through is None else through, view(place.group), own)
    load = None if through is None else pltpu.make_async_copy(src, through, own)
    mine, other = place.group, 2 * place.core + (1 - place.half)
    to_half = remote(src, view(mine), sent.at[0], came.at[mine], place.across())
    to_core = remote(src, view(mine), sent.at[1], came.at[mine], place.partner())
    to_half.start()
    to_core.start()
    (load or copy).start()
    yield
    if load:
        load.wait()
        copy.start()
    remote(src, view(other), sent.at[0], came.at[other], place.across()).wait_recv()
    relay = remote(view(other), view(other), sent.at[2], came.at[other], place.partner())
    relay.start()
    yield
    for half in (0, 1):
        slot = 2 * (1 - place.core) + half
        remote(src, view(slot), sent.at[0], came.at[slot], place.partner()).wait_recv()
    to_half.wait_send()
    to_core.wait_send()
    relay.wait_send()
    copy.wait()


def share_rows(ref, parts, p):
    rows = ref.shape[0] // parts
    return ref.at[pl.ds(p * rows, rows)]


def gather_group_rows(place, src, out, parts, take, through=True):
    def task(p, refs):
        rows = src.shape[0] // parts
        view = lambda g: out.at[g, pl.ds(p * rows, rows)]
        return gather_group(place, share_rows(src, parts, p), view, *refs)

    return [task(p, take(4 if through else 3)) for p in range(parts)]


def gather_rows_scratch(value, parts):
    through = pltpu.VMEM((value.shape[0] // parts, value.shape[1]), value.dtype)
    return (gather_group_sems() + [through]) * parts


def fold_rows_scratch(piece, parts):
    rows, width = piece[0] // parts, piece[1]
    bf16 = jnp.bfloat16
    one = [
        pltpu.VMEM((2, rows, width), bf16),
        pltpu.VMEM((rows, width), bf16),
        pltpu.VMEM((rows, width), bf16),
        pltpu.VMEM((rows, width), bf16),
        pltpu.VMEM((rows, width), jnp.float32),
        pltpu.SemaphoreType.DMA((3,)),
        pltpu.SemaphoreType.DMA((3,)),
        pltpu.SemaphoreType.DMA((3,)),
    ]
    return one * parts


def add_rows(out, *terms):
    rows = slabs(out.shape[0])

    def one(i, carry):
        at = pl.ds(pl.multiple_of(i * rows, rows), rows)
        total = terms[0][at].astype(jnp.float32)
        for term in terms[1:]:
            total = total + term[at].astype(jnp.float32)
        out[at] = total.astype(out.dtype)
        return carry

    lax.fori_loop(0, out.shape[0] // rows, one, 0)


def fold_rows(place, part, out, parts, take):
    rows = out.shape[0] // parts
    core, half = place.core, place.half
    far, near = 2 * (1 - core) + (1 - half), 2 * (1 - core) + half
    beside = 2 * core + (1 - half)

    def task(p, from_core, from_half, held, mine, total, sent, came, local):
        at = pl.ds(p * rows, rows)
        first = remote(part.at[far, at], from_core.at[1], sent.at[0], came.at[0], place.partner())
        second = remote(part.at[near, at], from_core.at[0], sent.at[1], came.at[1], place.partner())
        third = remote(held, from_half, sent.at[2], came.at[2], place.across())
        load_held = pltpu.make_async_copy(part.at[beside, at], held, local.at[0])
        load_mine = pltpu.make_async_copy(part.at[place.group, at], mine, local.at[1])
        store = pltpu.make_async_copy(total, out.at[at], local.at[2])
        for copy in (first, load_held, second, load_mine):
            copy.start()
        yield
        first.wait_recv()
        load_held.wait()
        add_rows(held, held, from_core.at[1])
        third.start()
        yield
        second.wait_recv()
        load_mine.wait()
        third.wait_recv()
        add_rows(total, mine, from_core.at[0], from_half)
        store.start()
        yield
        for copy in (first, second, third):
            copy.wait_send()
        store.wait()

    return [task(p, *take(8)) for p in range(parts)]


ROW_PARTS = 3


def reduce_group_scratch(piece, dtype):
    return [
        pltpu.VMEM((2,) + piece, dtype),
        pltpu.VMEM(piece, dtype),
        pltpu.VMEM(piece, dtype),
        pltpu.SemaphoreType.DMA((3,)),
        pltpu.SemaphoreType.DMA((3,)),
    ]


def reduce_group(place, view, out, from_core, from_half, held, sent, came):
    if not callable(view):
        part = view
        view = lambda g: part.at[g]
    far = 2 * (1 - place.core) + (1 - place.half)
    near = 2 * (1 - place.core) + place.half
    first = remote(view(far), from_core.at[1], sent.at[0], came.at[0], place.partner())
    second = remote(view(near), from_core.at[0], sent.at[1], came.at[1], place.partner())
    first.start()
    yield
    second.start()
    yield
    first.wait_recv()
    add_into(held, view(2 * place.core + (1 - place.half)), from_core.at[1])
    third = remote(held, from_half, sent.at[2], came.at[2], place.across())
    third.start()
    yield
    second.wait_recv()
    third.wait_recv()
    add_into(out, view(place.group), from_core.at[0], from_half)
    first.wait_send()
    second.wait_send()
    third.wait_send()


def exchange_group_sems():
    return [pltpu.SemaphoreType.DMA((3,)), pltpu.SemaphoreType.DMA((4,)), pltpu.SemaphoreType.DMA]


def exchange_group(place, src, out, sent, came, own):
    mine = place.group
    copy = pltpu.make_async_copy(src.at[mine], out.at[mine], own)
    copy.start()
    core, half = place.core, place.half
    links = (
        (2 * (1 - core) + (1 - half), place.corner()),
        (2 * core + (1 - half), place.across()),
        (2 * (1 - core) + half, place.partner()),
    )
    copies = [
        remote(src.at[to], out.at[mine], sent.at[k], came.at[mine], device)
        for k, (to, device) in enumerate(links)
    ]
    for one in copies:
        one.start()
    yield
    for k, (peer, device) in enumerate(links):
        remote(src.at[peer], out.at[peer], sent.at[k], came.at[peer], device).wait_recv()
    for one in copies:
        one.wait_send()
    copy.wait()


def transfer(name, number, body, ins, outs, scratch, moved, out_spaces=None, in_spaces=None):
    spaces = out_spaces or [pl.ANY] * len(outs)
    in_spaces = in_spaces or [pltpu.VMEM] * len(ins)
    return pl.pallas_call(
        body,
        name=name,
        out_shape=outs,
        in_specs=[pl.BlockSpec(memory_space=space) for space in in_spaces],
        out_specs=[pl.BlockSpec(memory_space=space) for space in spaces],
        scratch_shapes=scratch,
        compiler_params=pltpu.CompilerParams(
            collective_id=number, has_side_effects=True, vmem_limit_bytes=VMEM_LIMIT
        ),
        cost_estimate=pl.CostEstimate(flops=0, bytes_accessed=moved * 40, transcendentals=0),
    )(*ins)


def shape(dims, dtype):
    return jax.ShapeDtypeStruct(tuple(dims), dtype)


def slabs(rows):
    return math.gcd(rows, 16)


def all_gather_blk(value, count, number):
    def body(src, out, *sems):
        place = Place(count)
        greet(place, blk=True)
        together(gather_blk(place, src, out, *sems))

    return transfer(
        f"gather{number}",
        number,
        body,
        [value],
        [shape((count,) + value.shape, value.dtype)],
        gather_blk_sems(count),
        value.size * 2 * count,
    )[0]


def reduce_scatter_blk(value, count, number):
    piece = value.shape[1:]

    def body(part, out, *scratch):
        place = Place(count)
        greet(place, blk=True)
        together(reduce_blk(place, part, out, *scratch))

    return transfer(
        f"reduce{number}",
        number,
        body,
        [value],
        [shape(piece, jnp.float32)],
        reduce_blk_scratch(count, piece, value.dtype),
        value.size * 2,
        [pltpu.VMEM],
    )[0]


class Taker:
    def __init__(self, refs):
        self.refs = list(refs)

    def __call__(self, amount):
        taken = self.refs[:amount]
        del self.refs[:amount]
        return taken


def gather_first(qkv, out_parts, tokens, gains, docs, down, count, number):
    names = 6

    def body(*refs):
        qkv_ref, out_ref, tok_ref, gain_ref, doc_ref, down_ref = refs[:names]
        qkv_all, out_mine, tok_all, gain_all, doc_all, down_all = refs[names : 2 * names]
        gain_mine = refs[2 * names]
        take = Taker(refs[2 * names + 1 :])
        place = Place(count)
        greet(place, blk=True, core=True, half=True, corner=True)

        def gain_task(near, far):
            yield from gather_blk(place, gain_ref, gain_mine, *near)
            yield from gather_group(place, gain_mine, gain_all, *far)

        def doc_task(sent, came, own):
            copy = pltpu.make_async_copy(doc_ref, doc_all.at[place.core], own)
            copy.start()
            send = remote(doc_ref, doc_all.at[place.core], sent, came, place.partner())
            send.start()
            yield
            remote(doc_ref, doc_all.at[1 - place.core], sent, came, place.partner()).wait_recv()
            send.wait_send()
            copy.wait()

        together(
            gain_task(take(3), take(3)),
            gather_blk(place, qkv_ref, qkv_all, *take(3)),
            doc_task(*take(3)),
            waiting(gather_group(place, tok_ref, tok_all, *take(3)), 2),
            waiting(exchange_group(place, out_ref, out_mine, *take(3)), 3),
            *(
                waiting(task, 2 + p, 4)
                for p, task in enumerate(
                    gather_group_rows(place, down_ref, down_all, ROW_PARTS, take)
                )
            ),
        )

    ins = [qkv, out_parts, tokens, gains, docs, down]
    return transfer(
        f"first{number}",
        number,
        body,
        ins,
        [
            shape((count,) + qkv.shape, qkv.dtype),
            shape(out_parts.shape, out_parts.dtype),
            shape((GROUPS,) + tokens.shape, tokens.dtype),
            shape((GROUPS, count) + gains.shape, gains.dtype),
            shape((2,) + docs.shape, docs.dtype),
            shape((GROUPS,) + down.shape, down.dtype),
        ],
        [pltpu.VMEM((count,) + gains.shape, gains.dtype)]
        + gather_blk_sems(count, 1)
        + gather_group_sems()
        + gather_blk_sems(count)
        + [pltpu.SemaphoreType.DMA] * 3
        + gather_group_sems()
        + exchange_group_sems()
        + gather_rows_scratch(down, ROW_PARTS),
        (qkv.size + out_parts.size) * 2 * count,
        None,
        [pltpu.VMEM] * 5 + [pl.ANY],
    )


def attend_step(count, g, here, key_half, key_at, q_ref, kv_ref, doc_ref, key_doc_ref, acc, tot):
    rows = q_ref.shape[1]
    sequence, half = g // 2, g % 2
    q2, position, doc = stacked_queries(g, half * count + here, q_ref, doc_ref)
    key_block = key_half * count + key_at
    at = pl.ds(pl.multiple_of((2 * sequence + key_half) * rows, rows), rows)
    kv = kv_ref.at[key_at, at]
    _, weights = attention_scores(
        q2, kv[:, :HEAD_DIM], position, doc, key_block, key_doc_ref[sequence, key_block], rows
    )
    tot[g] += jnp.sum(weights, axis=-1, keepdims=True)
    acc[g] += jnp.dot(
        weights.astype(jnp.bfloat16), kv[:, HEAD_DIM:], preferred_element_type=jnp.float32
    )


def stacked_queries(g, block, q_ref, doc_ref):
    rows = q_ref.shape[1]
    q2 = jnp.concatenate([q_ref[g, :, :HEAD_DIM], q_ref[g, :, HEAD_DIM:]], axis=0)
    inside = lax.broadcasted_iota(jnp.int32, (rows, 1), 0)
    position = block * rows + jnp.concatenate([inside, inside], axis=0)
    doc = jnp.concatenate([doc_ref[g], doc_ref[g]], axis=0)
    return q2, position, doc


def gather_attend(kv, out_mine, gate_up, queries, doc, key_doc, count, number):
    groups, out_rows, width = out_mine.shape
    rows = queries.shape[1]

    def body(*refs):
        kv_ref, out_ref, gate_up_ref, q_ref, doc_ref, key_doc_ref = refs[:6]
        kv_all, out_all, gate_up_all, attn_ref, full_ref, total_ref = refs[6:12]
        acc, tot = refs[12:14]
        take = Taker(refs[14:])
        place = Place(count)
        greet(place, blk=True, core=True, half=True)
        gathers = (
            GatherBlk(place, kv_ref, lambda i: kv_all.at[i], *take(3)),
            GatherBlk(place, out_ref, lambda i: out_all.at[:, i], *take(3)),
        )
        groups = gather_group_rows(place, gate_up_ref, gate_up_all, ROW_PARTS, take)
        for gather in gathers:
            gather.start()
        for task in groups:
            next(task)
        acc[...] = jnp.zeros_like(acc)
        tot[...] = jnp.zeros_like(tot)
        here, inner = place.here, place.inner

        def attend(k):
            def one(c, carry):
                key_at = place.near(k) * inner + c // 6
                sequence, kind = (c % 6) // 3, c % 3
                half = jnp.minimum(kind, 1)
                needed = jnp.where(kind == 1, key_at >= here, key_at <= here)

                @pl.when(needed)
                def _():
                    attend_step(
                        count,
                        2 * sequence + half,
                        here,
                        kind // 2,
                        key_at,
                        q_ref,
                        kv_all,
                        doc_ref,
                        key_doc_ref,
                        acc,
                        tot,
                    )

                return carry

            lax.fori_loop(0, inner * 6, one, 0)

        gathers[0].copy.wait()
        for k in range(place.outer):
            advance(gathers, k)
            gathers[0].beside_arrived(k)
            if 0 < k < place.outer - 1 and k <= 2:
                next(groups[k - 1])
            attend(k)

        def put(g, carry):
            total = tot[g]
            attended = acc[g] / total
            attended = jnp.concatenate([attended[:rows], attended[rows:]], axis=1)
            full_ref[g] = attended
            attn_ref[g] = attended.astype(jnp.bfloat16)
            total_ref[g] = total
            return carry

        lax.fori_loop(0, GROUPS, put, 0)
        next(groups[2])
        gathers[1].copy.wait()
        for k in range(place.outer):
            gathers[1].beside_arrived(k)
        for gather in gathers:
            gather.finish()
        together(*groups)

    return transfer(
        f"attend{number}",
        number,
        body,
        [kv, out_mine, gate_up, queries, doc, key_doc],
        [
            shape((count,) + kv.shape, kv.dtype),
            shape((groups, count, out_rows, width), out_mine.dtype),
            shape((GROUPS,) + gate_up.shape, gate_up.dtype),
            shape((GROUPS, rows, width), jnp.bfloat16),
            shape((GROUPS, rows, width), jnp.float32),
            shape((GROUPS, REPS * rows, 1), jnp.float32),
        ],
        [
            pltpu.VMEM((GROUPS, REPS * rows, HEAD_DIM), jnp.float32),
            pltpu.VMEM((GROUPS, REPS * rows, 1), jnp.float32),
        ]
        + gather_blk_sems(count)
        + gather_blk_sems(count)
        + gather_rows_scratch(gate_up, ROW_PARTS),
        (kv.size + out_mine.size) * 2 * count,
        [pltpu.VMEM, pl.ANY, pl.ANY, pltpu.VMEM, pltpu.VMEM, pltpu.VMEM],
        [pltpu.VMEM, pltpu.VMEM, pl.ANY, pltpu.VMEM, pltpu.VMEM, pltpu.VMEM],
    )


def attend_back_block(
    count, g, here, q_ref, kv_ref, doc_ref, key_doc_ref, grad_ref, full_ref, total_ref, dq_ref, key_acc
):
    rows = q_ref.shape[1]
    sequence, half = g // 2, g % 2
    block = half * count + here
    q2, position, doc = stacked_queries(g, block, q_ref, doc_ref)
    total = total_ref[g]
    grad = grad_ref[g].astype(jnp.float32)
    grad2 = jnp.concatenate([grad[:, :HEAD_DIM], grad[:, HEAD_DIM:]], axis=0)
    full2 = jnp.concatenate([full_ref[g, :, :HEAD_DIM], full_ref[g, :, HEAD_DIM:]], axis=0)
    total_grad = -jnp.sum(grad2 * full2, axis=-1, keepdims=True) / total
    sums_grad = (grad2 / total).astype(jnp.bfloat16)

    def one(key_block, acc):
        key_half = (key_block >= count).astype(jnp.int32)
        inner = key_block - key_half * count
        at = pl.ds(pl.multiple_of((2 * sequence + key_half) * rows, rows), rows)
        kv = kv_ref.at[inner, at]
        keys = kv[:, :HEAD_DIM]
        capped, weights = attention_scores(
            q2, keys, position, doc, key_block, key_doc_ref[sequence, key_block], rows
        )
        exp_grad = dot(sums_grad, kv[:, HEAD_DIM:], LAST)
        raw_grad = (
            weights * (exp_grad + total_grad) * (1.0 - capped * capped) * SCORE_SCALE
        ).astype(jnp.bfloat16)
        slot = inner * 2 + key_half
        key_acc[slot, :, :HEAD_DIM] += dot(raw_grad, q2, FIRST)
        key_acc[slot, :, HEAD_DIM:] += dot(weights.astype(jnp.bfloat16), sums_grad, FIRST)
        return acc + dot(raw_grad, keys, PLAIN)

    dq = lax.fori_loop(
        jnp.maximum(block - count, 0),
        block + 1,
        one,
        jnp.zeros((REPS * rows, HEAD_DIM), jnp.float32),
    )
    dq_ref[g] = jnp.concatenate([dq[:rows], dq[rows:]], axis=1).astype(jnp.bfloat16)


def attend_back_fits(count):
    return count == 8


def attend_back_reduce(
    queries, kv, doc, key_doc, grad, full, totals, out_part, gate_up_part, kv_piece, count, number
):
    out_piece = out_part.shape[:1] + out_part.shape[2:]
    gate_up_piece = gate_up_part.shape[1:]
    rows = queries.shape[1]
    steps = rows // kv_piece[1]
    bf16 = jnp.bfloat16

    def body(*refs):
        q_ref, kv_ref, doc_ref, key_doc_ref, grad_ref, full_ref, total_ref = refs[:7]
        out_ref, gate_up_ref = refs[7:9]
        dq_ref, dkv_sum, out_sum, gate_up_sum, dkv_part, key_acc = refs[9:15]
        take = Taker(refs[15:])
        place = Place(count)
        greet(place, blk=True, core=True, half=True)
        dkv = ReduceBlk(place, lambda i: dkv_part.at[i], dkv_sum, *take(REDUCE_REFS))
        out = ReduceBlk(place, lambda i: out_ref.at[:, i], out_sum, *take(REDUCE_REFS))
        folds = fold_rows(place, gate_up_ref, gate_up_sum, ROW_PARTS, take)
        out_events = out.events()

        def back(g):
            attend_back_block(
                count,
                g,
                place.here,
                q_ref,
                kv_ref,
                doc_ref,
                key_doc_ref,
                grad_ref,
                full_ref,
                total_ref,
                dq_ref,
                key_acc,
            )

        def clear(i, carry):
            key_acc[i] = jnp.zeros(key_acc.shape[1:], jnp.float32)
            return carry

        def put(sequence):
            def one(i, carry):
                for k in (0, 1):
                    value = key_acc[i * 2 + k].astype(bf16).reshape((steps,) + kv_piece[1:])
                    dkv_part[i, pl.ds((2 * sequence + k) * steps, steps)] = value
                return carry

            lax.fori_loop(0, count, one, 0)

        ends = jnp.logical_not(out.middle)

        turning = out.turning()

        def middle(*steps):
            @pl.when(out.middle)
            def _():
                for step in steps:
                    if isinstance(step, int):
                        turning[step]()
                    else:
                        out.pass_on(*step, True)

        def outside(*steps):
            @pl.when(ends)
            def _():
                for step in steps:
                    out.pass_on(*step, False)

        out.start()
        for fold in folds:
            next(fold)
        lax.fori_loop(0, 2 * count, clear, 0)
        back(0)
        next(folds[0])
        middle(0)
        back(1)
        put(0)
        middle(1, 2)
        outside((0, 0), (1, 0), (1, 1))
        next(folds[1])
        lax.fori_loop(0, 2 * count, clear, 0)
        back(2)
        outside((2, 0), (2, 1))
        middle((0, 0))
        back(3)
        put(1)
        middle((1, 0), (1, 1), (2, 0), (2, 1))
        dkv.start()
        dkv_events = dkv.events()
        order = [(folds, 2), (dkv_events, 0), (dkv_events, 1), (dkv_events, 2)]
        order += [(out_events, 8), (out_events, 9), (dkv_events, 3), (dkv_events, 4)]
        order += [(folds, 0), (dkv_events, 5), (dkv_events, 6), (folds, 1)]
        order += [(dkv_events, 7), (dkv_events, 8), (dkv_events, 9), (folds, 2)]
        for events, i in order:
            if events is folds:
                next(folds[i])
            else:
                events[i]()
        out.finish()
        dkv.finish()
        together(*folds)

    vmem = pltpu.VMEM
    return transfer(
        f"attend_back{number}",
        number,
        body,
        [queries, kv, doc, key_doc, grad, full, totals, out_part, gate_up_part],
        [
            shape(queries.shape, bf16),
            shape(kv_piece, bf16),
            shape(out_piece, bf16),
            shape(gate_up_piece, jnp.float32),
        ],
        [
            vmem((count,) + kv_piece, bf16),
            vmem((2 * count, rows, 2 * HEAD_DIM), jnp.float32),
        ]
        + reduce_blk_scratch(count, kv_piece, bf16)
        + reduce_blk_scratch(count, out_piece, bf16)
        + fold_rows_scratch(gate_up_piece, ROW_PARTS),
        (kv.size + out_part.size) * 2,
        [vmem, vmem, vmem, pl.ANY],
        [vmem] * 8 + [pl.ANY],
    )


def reduce_middle(dkv_part, out_part, gate_up_part, count, number):
    dkv_piece = dkv_part.shape[1:]
    out_piece = out_part.shape[:1] + out_part.shape[2:]

    gate_up_piece = gate_up_part.shape[1:]

    def body(dkv_ref, out_ref, gate_up_ref, dkv_sum, out_sum, gate_up_sum, *scratch):
        take = Taker(scratch)
        place = Place(count)
        greet(place, blk=True, core=True, half=True)
        together(
            reduce_blk(place, dkv_ref, dkv_sum, *take(REDUCE_REFS)),
            reduce_blk(place, lambda i: out_ref.at[:, i], out_sum, *take(REDUCE_REFS)),
            *(
                waiting(task, *rounds)
                for rounds, task in zip(
                    ((6, 5, 5), (8, 5, 3), (10, 6, 0)),
                    fold_rows(place, gate_up_ref, gate_up_sum, ROW_PARTS, take),
                )
            ),
        )

    return transfer(
        f"reduce{number}",
        number,
        body,
        [dkv_part, out_part, gate_up_part],
        [
            shape(dkv_piece, jnp.bfloat16),
            shape(out_piece, jnp.bfloat16),
            shape(gate_up_piece, jnp.float32),
        ],
        reduce_blk_scratch(count, dkv_piece, jnp.bfloat16)
        + reduce_blk_scratch(count, out_piece, jnp.bfloat16)
        + fold_rows_scratch(gate_up_piece, ROW_PARTS),
        (dkv_part.size + out_part.size) * 2,
        [pltpu.VMEM, pltpu.VMEM, pl.ANY],
        [pltpu.VMEM, pltpu.VMEM, pl.ANY],
    )


def reduce_last(qkv_part, norm_part, gain_part, out_sum, down_part, count, number):
    gain_piece = gain_part.shape[1:]
    qkv_piece, norm_piece = qkv_part.shape[1:], norm_part.shape[1:]

    def body(*refs):
        qkv_ref, norm_ref, gain_ref, out_ref, down_ref = refs[:5]
        qkv_sum, norm_sum, gain_sum, out_all, down_sum = refs[5:10]
        gain_mine = refs[10]
        take = Taker(refs[11:])
        place = Place(count)
        greet(place, blk=True, core=True, half=True, corner=True)

        def gain_task(near, far):
            yield from reduce_blk(place, gain_ref, gain_mine, *near)
            yield from reduce_group(place, gain_mine, gain_sum, *far)

        main = reduce_blk(place, qkv_ref, qkv_sum, *take(REDUCE_REFS))
        gain = gain_task(take(REDUCE_REFS), take(5))
        together(
            waiting(gain, 11),
            main,
            waiting(exchange_group(place, out_ref, out_all, *take(3)), 16),
            waiting(reduce_group(place, norm_ref, norm_sum, *take(5)), 0, 6, 9),
            *(
                waiting(task, *rounds)
                for rounds, task in zip(
                    ((7, 7, 2), (8, 8, 0), (9, 9, 0)),
                    fold_rows(place, down_ref, down_sum, ROW_PARTS, take),
                )
            ),
        )

    return transfer(
        f"last{number}",
        number,
        body,
        [qkv_part, norm_part, gain_part, out_sum, down_part],
        [
            shape(qkv_piece, jnp.float32),
            shape(norm_piece, jnp.float32),
            shape(gain_piece[1:], jnp.float32),
            shape(out_sum.shape, jnp.bfloat16),
            shape(down_part.shape[1:], jnp.float32),
        ],
        [pltpu.VMEM(gain_piece, jnp.float32)]
        + reduce_blk_scratch(count, qkv_piece, jnp.bfloat16)
        + reduce_blk_scratch(count, gain_piece, jnp.float32, 1)
        + reduce_group_scratch(gain_piece[1:], jnp.float32)
        + exchange_group_sems()
        + reduce_group_scratch(norm_piece, jnp.bfloat16)
        + fold_rows_scratch(down_part.shape[1:], ROW_PARTS),
        qkv_part.size * 2,
        [pltpu.VMEM] * 4 + [pl.ANY],
        [pltpu.VMEM] * 4 + [pl.ANY],
    )


GROUP_PARTS = 4


def all_gather_group(value, number):
    parts = GROUP_PARTS

    def body(src, out, *sems):
        place = Place(lax.axis_size("blk"))
        greet(place, core=True, half=True)
        together(*gather_group_rows(place, src, out, parts, Taker(sems), False))

    return transfer(
        f"group{number}",
        number,
        body,
        [value],
        [shape((GROUPS,) + value.shape, value.dtype)],
        gather_group_sems() * parts,
        value.size * 8,
    )[0]


def project_group(attn, weight, piece, number):
    width = weight.shape[0]
    parts = 3 if width % 768 == 0 else 1
    columns = width // parts
    bf16 = jnp.bfloat16

    def body(attn_ref, weight_ref, out, part, *scratch):
        take = Taker(scratch)
        place = Place(lax.axis_size("blk"))
        greet(place, core=True, half=True)

        def multiply(n, carry):
            at = pl.ds(pl.multiple_of(n * 256, 256), 256)
            left = attn_ref[...].reshape(-1, attn.shape[-1])
            value = dot(left, weight_ref[at], LAST).astype(bf16)
            part[:, :, :, at] = value.reshape((GROUPS,) + piece[:2] + (256,))
            return carry

        def task(p):
            at = pl.ds(p * columns, columns)
            return reduce_group(
                place, lambda g: part.at[g, :, :, at], out.at[:, :, at], *take(5)
            )

        tasks = [task(p) for p in range(parts)]
        for p in range(parts):
            lax.fori_loop(p * columns // 256, (p + 1) * columns // 256, multiply, 0)
            next(tasks[p])
            next(tasks[p])
        together(*tasks)

    return transfer(
        f"fold{number}",
        number,
        body,
        [attn, weight],
        [shape(piece, jnp.float32)],
        [pltpu.VMEM((GROUPS,) + piece, bf16)]
        + reduce_group_scratch(piece[:2] + (columns,), bf16) * parts,
        attn.size * 8,
        [pltpu.VMEM],
    )[0]


def dot(left, right, contract):
    return lax.dot_general(left, right, (contract, ((), ())), preferred_element_type=jnp.float32)


LAST = ((1,), (1,))
PLAIN = ((1,), (0,))
FIRST = ((0,), (0,))


LANES = 128
GELU_A = math.sqrt(2.0 / math.pi)
GELU_B = 0.044715


def feed_forward_fits(count, rows, width, hidden):
    inner = 4 if count >= 32 else 2
    outer = count // inner
    tile = rows * width * 2
    weights = 3 * hidden * width * 2
    kept = count * rows * 3 * hidden * 2
    total = weights + kept + tile * (3 * count + outer * (inner - 1) + 2 * outer + 3) + 9 * tile
    total += 6 * LANES * (count * rows + 3 * 256) * 2
    return total < 58 * 2**20 and hidden % (3 * LANES) == 0 and width % 256 == 0


def feed_forward_kernel(
    count,
    branch_ref,
    token_ref,
    cot_ref,
    gain_ref,
    gate_up_hbm,
    down_hbm,
    out_ref,
    middle_grad_ref,
    branch_grad_ref,
    gain_grad_ref,
    gate_up_grad_hbm,
    down_grad_hbm,
    w_gate_up,
    w_down,
    norm_all,
    grad_all,
    act,
    hidden,
    part,
    middle,
    norm_own,
    grad_own,
    total,
    turned,
    staged,
    beside,
    along,
    held,
    spare,
    w_sems,
    out_sems,
    *sems,
):
    place = Place(count)
    rows, width = norm_all.shape[1:]
    units = hidden.shape[1]
    chunks = units // LANES
    inner, outer = place.inner, place.outer
    slab = branch_ref.shape[1]
    steps = rows // slab
    columns = width // 256
    pair = inner * rows
    take = Taker(sems)

    def weight_copies(i):
        units_at = pl.ds(pl.multiple_of(i * LANES, LANES), LANES)
        return [
            pltpu.make_async_copy(
                gate_up_hbm.at[units_at, pl.ds(0, width)],
                w_gate_up.at[i, pl.ds(0, LANES)],
                w_sems.at[3 * i],
            ),
            pltpu.make_async_copy(
                gate_up_hbm.at[units_at, pl.ds(width, width)],
                w_gate_up.at[i, pl.ds(LANES, LANES)],
                w_sems.at[3 * i + 1],
            ),
            pltpu.make_async_copy(down_hbm.at[units_at], w_down.at[units_at], w_sems.at[3 * i + 2]),
        ]

    def start_weights(i, carry):
        for copy in weight_copies(i):
            copy.start()
        return carry

    def wait_weights(i, carry):
        for copy in weight_copies(i):
            copy.wait()
        return carry

    lax.fori_loop(0, chunks, start_weights, 0)

    def scale_of(values):
        return lax.rsqrt(jnp.mean(values * values, axis=-1, keepdims=True) + NORM_EPS)

    def slab_rows(i):
        return pl.ds(pl.multiple_of(i * slab, slab), slab)

    def before(i, carry):
        value = branch_ref[i]
        mid = token_ref[i].astype(jnp.float32) + value * scale_of(value) * gain_ref[1:2]
        middle[i] = mid
        norm_own[slab_rows(i)] = (mid * scale_of(mid) * gain_ref[2:3]).astype(jnp.bfloat16)
        return carry

    lax.fori_loop(0, steps, before, 0)
    greet(place, blk=True)

    def pair_rows(k):
        return pl.ds(pl.multiple_of(place.near_at(k) * pair, pair), pair)

    def pair_pieces(k):
        return pl.ds(place.near_at(k) * inner, inner)

    def column(n):
        return pl.ds(pl.multiple_of(n * 256, 256), 256)

    def put_part(k, n, value):
        split = value.astype(jnp.bfloat16).reshape((inner, steps, slab, 256))
        part[pair_pieces(k), :, :, column(n)] = split

    def receive(gather, k):
        def one(static):
            if static == 0:
                gather.copy.wait()
            advance([gather], static)
            gather.beside_arrived(static)

        for static in range(outer):
            pl.when(k == static)(lambda static=static: one(static))

    gather = GatherBlk(place, norm_own, lambda i: norm_all.at[i], *take(3))
    gather.start()
    lax.fori_loop(0, chunks, wait_weights, 0)
    def forward(k, carry):
        receive(gather, k)
        at = pair_rows(k)

        def up_chunk(j, carry):
            x = norm_all[pair_pieces(k)].reshape(pair, width)
            both = dot(x, w_gate_up[j], LAST)
            act[at, column(j)] = both.astype(jnp.bfloat16)
            gate, up = both[:, :LANES], both[:, LANES:]
            bent = 0.5 * gate * (1.0 + jnp.tanh(GELU_A * (gate + GELU_B * (gate * gate * gate))))
            hidden[at, pl.ds(pl.multiple_of(j * LANES, LANES), LANES)] = (bent * up).astype(
                jnp.bfloat16
            )
            return carry

        lax.fori_loop(0, chunks, up_chunk, 0)

        def down_chunk(n, carry):
            put_part(k, n, dot(hidden[at, :], w_down[:, column(n)], PLAIN))
            return carry

        lax.fori_loop(0, columns, down_chunk, 0)
        return carry

    lax.fori_loop(0, outer, forward, 0)
    gather.finish()
    reduce = ReduceBlk(place, lambda i: part.at[i], total, beside, along, held, spare, *take(6))
    reduce.start()
    for event in reduce.events():
        event()

    gain_grad_ref[...] = jnp.zeros_like(gain_grad_ref)

    def norm_back(value, gain, incoming):
        scale = scale_of(value)
        lifted = incoming * gain
        pull = jnp.mean(lifted * value, axis=-1, keepdims=True)
        gain_grad = jnp.sum(incoming * value * scale, axis=0, keepdims=True)
        return scale * lifted - value * (scale * scale * scale) * pull, gain_grad

    def between(i, carry):
        value, cot = total[i], cot_ref[i].astype(jnp.float32)
        gain = gain_ref[3:4]
        out_ref[i] = (middle[i] + value * scale_of(value) * gain).astype(jnp.bfloat16)
        grad, gain_grad = norm_back(value, gain, cot)
        gain_grad_ref[3:4] += gain_grad
        grad_own[slab_rows(i)] = grad.astype(jnp.bfloat16)
        return carry

    lax.fori_loop(0, steps, between, 0)
    reduce.finish()

    gather = GatherBlk(place, grad_own, lambda i: grad_all.at[i], *take(3))
    gather.start()
    def backward(k, carry):
        receive(gather, k)
        at = pair_rows(k)

        def back_chunk(j, carry):
            g = grad_all[pair_pieces(k)].reshape(pair, width)
            units_at = pl.ds(pl.multiple_of(j * LANES, LANES), LANES)
            grad = dot(g, w_down[units_at], LAST)
            both = act[at, column(j)].astype(jnp.float32)
            gate, up = both[:, :LANES], both[:, LANES:]
            bend = jnp.tanh(GELU_A * (gate + GELU_B * (gate * gate * gate)))
            bent = 0.5 * gate * (1.0 + bend)
            slope = 0.5 * (1.0 + bend) + (0.5 * GELU_A) * gate * (1.0 - bend * bend) * (
                1.0 + (3.0 * GELU_B) * gate * gate
            )
            pulled = jnp.concatenate([grad * up * slope, grad * bent], axis=1)
            act[at, column(j)] = pulled.astype(jnp.bfloat16)
            return carry

        lax.fori_loop(0, chunks, back_chunk, 0)

        def input_chunk(n, carry):
            w = w_gate_up[:, :, column(n)].reshape(2 * units, 256)
            put_part(k, n, dot(act[at, :], w, PLAIN))
            return carry

        lax.fori_loop(0, columns, input_chunk, 0)
        return carry

    lax.fori_loop(0, outer, backward, 0)
    gather.finish()
    reduce = ReduceBlk(place, lambda i: part.at[i], total, beside, along, held, spare, *take(6))
    reduce.start()

    tokens = count * rows
    slots = staged.shape[0]
    three = 3 * LANES

    def up_store(step):
        slot = lax.rem(step, slots)
        i, n = step // columns, lax.rem(step, columns)
        return [
            pltpu.make_async_copy(
                staged.at[slot, pl.ds((2 * q + h) * LANES, LANES)],
                gate_up_grad_hbm.at[
                    pl.ds(pl.multiple_of((3 * i + q) * LANES, LANES), LANES),
                    pl.ds(pl.multiple_of(h * width + n * 256, 256), 256),
                ],
                out_sems.at[slot, 2 * q + h],
            )
            for q in range(3)
            for h in (0, 1)
        ]

    def up_grad(step, carry):
        slot = lax.rem(step, slots)
        i, n = step // columns, lax.rem(step, columns)

        @pl.when(step >= slots)
        def _():
            for copy in up_store(step - slots):
                copy.wait()

        @pl.when(n == 0)
        def _():
            turned[...] = jnp.transpose(act[:, pl.ds(pl.multiple_of(2 * i * three, three), 2 * three)])

        x = norm_all[:, :, column(n)].reshape(tokens, 256)
        staged[slot] = dot(turned[...], x, PLAIN).astype(jnp.bfloat16)
        for copy in up_store(step):
            copy.start()
        return carry

    def down_store(step):
        slot = lax.rem(step, slots)
        i, n = step // columns, lax.rem(step, columns)
        return pltpu.make_async_copy(
            staged.at[slot, pl.ds(0, three)],
            down_grad_hbm.at[pl.ds(pl.multiple_of(i * three, three), three), column(n)],
            out_sems.at[slot, 6],
        )

    def down_grad(step, carry):
        slot = lax.rem(step, slots)
        i, n = step // columns, lax.rem(step, columns)

        @pl.when(step >= slots)
        def _():
            down_store(step - slots).wait()

        @pl.when(n == 0)
        def _():
            turned[pl.ds(0, three)] = jnp.transpose(
                hidden[:, pl.ds(pl.multiple_of(i * three, three), three)]
            )

        x = grad_all[:, :, column(n)].reshape(tokens, 256)
        staged[slot, pl.ds(0, three)] = dot(turned[pl.ds(0, three)], x, PLAIN).astype(jnp.bfloat16)
        down_store(step).start()
        return carry

    ups, downs = chunks // 3 * columns, units // three * columns
    events = reduce.events()
    early = len(events) - 3
    for k in range(early):
        lax.fori_loop(ups * k // early, ups * (k + 1) // early, up_grad, 0)
        events[k]()
    for step in range(max(0, ups - slots), ups):
        for copy in up_store(step):
            copy.wait()
    for k in range(3):
        lax.fori_loop(downs * k // 3, downs * (k + 1) // 3, down_grad, 0)
        events[early + k]()

    def after(i, carry):
        value, mid, cot = branch_ref[i], middle[i], cot_ref[i].astype(jnp.float32)
        grad, gain_grad = norm_back(mid, gain_ref[2:3], total[i])
        gain_grad_ref[2:3] += gain_grad
        middle_grad = cot + grad
        middle_grad_ref[i] = middle_grad
        grad, gain_grad = norm_back(value, gain_ref[1:2], middle_grad)
        gain_grad_ref[1:2] += gain_grad
        branch_grad_ref[i] = grad.astype(jnp.bfloat16)
        return carry

    lax.fori_loop(0, steps, after, 0)
    reduce.finish()
    for step in range(max(0, downs - slots), downs):
        down_store(step).wait()


def feed_forward(branch, tokens, cotangent, gains, gate_up_all, down_all, count, number):
    steps, slab, width = branch.shape
    rows = steps * slab
    units = down_all.shape[0]
    inner = 4 if count >= 32 else 2
    outer = count // inner
    piece = branch.shape
    bf16, f32 = jnp.bfloat16, jnp.float32
    vmem = pl.BlockSpec(memory_space=pltpu.VMEM)
    anywhere = pl.BlockSpec(memory_space=pl.ANY)
    slots = 3
    line_scratch = reduce_blk_scratch(count, piece, bf16)
    return pl.pallas_call(
        functools.partial(feed_forward_kernel, count),
        name="feed_forward",
        out_shape=[
            shape(piece, bf16),
            shape(piece, f32),
            shape(piece, bf16),
            shape((4, width), f32),
            shape(gate_up_all.shape, bf16),
            shape(down_all.shape, bf16),
        ],
        in_specs=[vmem] * 4 + [anywhere] * 2,
        out_specs=[vmem] * 4 + [anywhere] * 2,
        scratch_shapes=[
            pltpu.VMEM((units // LANES, 2 * LANES, width), bf16),
            pltpu.VMEM((units, width), bf16),
            pltpu.VMEM((count, rows, width), bf16),
            pltpu.VMEM((count, rows, width), bf16),
            pltpu.VMEM((count * rows, 2 * units), bf16),
            pltpu.VMEM((count * rows, units), bf16),
            pltpu.VMEM((count,) + piece, bf16),
            pltpu.VMEM(piece, f32),
            pltpu.VMEM((rows, width), bf16),
            pltpu.VMEM((rows, width), bf16),
            pltpu.VMEM(piece, f32),
            pltpu.VMEM((6 * LANES, count * rows), bf16),
            pltpu.VMEM((slots, 6 * LANES, 256), bf16),
        ]
        + line_scratch[:4]
        + [
            pltpu.SemaphoreType.DMA((3 * units // LANES,)),
            pltpu.SemaphoreType.DMA((slots, 7)),
        ]
        + gather_blk_sems(count)
        + line_scratch[4:]
        + gather_blk_sems(count)
        + line_scratch[4:],
        compiler_params=pltpu.CompilerParams(
            collective_id=number, has_side_effects=True, vmem_limit_bytes=67043328
        ),
        cost_estimate=pl.CostEstimate(
            flops=18 * count * rows * units * width,
            bytes_accessed=500 * 2**20,
            transcendentals=0,
        ),
    )(branch, tokens, cotangent, gains, gate_up_all, down_all)


def attention_scores(q2, k, query_pos, query_doc, key_block, key_doc, rows):
    raw = lax.dot_general(q2, k, (((1,), (1,)), ((), ())), preferred_element_type=jnp.float32)
    capped = jnp.tanh(raw * (SCORE_SCALE / SOFT_CAP))
    key_pos = key_block * rows + lax.broadcasted_iota(jnp.int32, (1, rows), 1)
    visible = (key_pos <= query_pos) & (key_doc == query_doc)
    return capped, jnp.where(visible, jnp.exp(SOFT_CAP * capped), 0.0)


def attention_query(q_ref, doc_ref, here, count, rows):
    half = pl.program_id(1)
    block = half * count + here
    q2 = jnp.concatenate([q_ref[0, :, :HEAD_DIM], q_ref[0, :, HEAD_DIM:]], axis=0)
    inside = lax.broadcasted_iota(jnp.int32, (rows, 1), 0)
    position = block * rows + jnp.concatenate([inside, inside], axis=0)
    doc = jnp.concatenate([doc_ref[0], doc_ref[0]], axis=0)
    return block, q2, position, doc


def attention_backward_kernel(
    count,
    here_ref,
    q_ref,
    kv_ref,
    doc_ref,
    key_doc_ref,
    grad_ref,
    full_ref,
    total_ref,
    dq_ref,
    dkv_ref,
    acc,
    key_acc,
):
    rows = q_ref.shape[1]
    half = pl.program_id(1)
    block, q2, position, doc = attention_query(q_ref, doc_ref, here_ref[0], count, rows)
    total = total_ref[0]
    grad = grad_ref[0].astype(jnp.float32)
    grad2 = jnp.concatenate([grad[:, :HEAD_DIM], grad[:, HEAD_DIM:]], axis=0)
    full2 = jnp.concatenate([full_ref[0, :, :HEAD_DIM], full_ref[0, :, HEAD_DIM:]], axis=0)
    total_grad = -jnp.sum(grad2 * full2, axis=-1, keepdims=True) / total
    sums_grad = (grad2 / total).astype(jnp.bfloat16)
    acc[...] = jnp.zeros_like(acc)

    @pl.when(half == 0)
    def _():
        def clear(i, carry):
            key_acc[i] = jnp.zeros(key_acc.shape[1:], jnp.float32)
            return carry

        lax.fori_loop(0, key_acc.shape[0], clear, 0)

    def one(key_block, carry):
        key_half = (key_block >= count).astype(jnp.int32)
        inner = key_block - key_half * count
        kv = kv_ref.at[inner, key_half]
        keys = kv[:, :HEAD_DIM]
        capped, weights = attention_scores(
            q2, keys, position, doc, key_block, key_doc_ref[0, key_block], rows
        )
        exp_grad = lax.dot_general(
            sums_grad, kv[:, HEAD_DIM:], (((1,), (1,)), ((), ())), preferred_element_type=jnp.float32
        )
        raw_grad = (
            weights * (exp_grad + total_grad) * (1.0 - capped * capped) * SCORE_SCALE
        ).astype(jnp.bfloat16)
        acc[...] += jnp.dot(raw_grad, keys, preferred_element_type=jnp.float32)
        over_rows = (((0,), (0,)), ((), ()))
        slot = inner * 2 + key_half
        key_acc[slot, :, :HEAD_DIM] += lax.dot_general(
            raw_grad, q2, over_rows, preferred_element_type=jnp.float32
        )
        key_acc[slot, :, HEAD_DIM:] += lax.dot_general(
            weights.astype(jnp.bfloat16), sums_grad, over_rows, preferred_element_type=jnp.float32
        )
        return carry

    lax.fori_loop(jnp.maximum(block - count, 0), block + 1, one, 0)
    dq = acc[...]
    dq_ref[0] = jnp.concatenate([dq[:rows], dq[rows:]], axis=1).astype(jnp.bfloat16)

    @pl.when(half == 1)
    def _():
        def put(i, carry):
            for k in (0, 1):
                dkv_ref[i, k] = key_acc[i * 2 + k].astype(jnp.bfloat16)
            return carry

        lax.fori_loop(0, count, put, 0)


def attention_specs(count, rows, width):
    query = pl.BlockSpec((1, rows, width), lambda s, h, here: (2 * s + h, 0, 0))
    keys = pl.BlockSpec((count, 2, rows, 2 * HEAD_DIM), lambda s, h, here: (0, s, 0, 0))
    doc = pl.BlockSpec((1, rows, 1), lambda s, h, here: (2 * s + h, 0, 0))
    key_doc = pl.BlockSpec((1, 2 * count, 1, rows), lambda s, h, here: (s, 0, 0, 0))
    total = pl.BlockSpec((1, REPS * rows, 1), lambda s, h, here: (2 * s + h, 0, 0))
    return query, keys, doc, key_doc, total


def attention_backward(here, q, kv, doc, key_doc, grad, full, totals):
    count, _, rows, _ = kv.shape
    width = REPS * HEAD_DIM
    query, keys, doc_spec, key_doc_spec, total = attention_specs(count, rows, width)
    return pl.pallas_call(
        functools.partial(attention_backward_kernel, count),
        name="attend_back",
        grid_spec=pltpu.PrefetchScalarGridSpec(
            num_scalar_prefetch=1,
            grid=(2, 2),
            in_specs=[query, keys, doc_spec, key_doc_spec, query, query, total],
            out_specs=[query, keys],
            scratch_shapes=[
                pltpu.VMEM((REPS * rows, HEAD_DIM), jnp.float32),
                pltpu.VMEM((2 * count, rows, 2 * HEAD_DIM), jnp.float32),
            ],
        ),
        out_shape=[shape((GROUPS, rows, width), jnp.bfloat16), shape(kv.shape, jnp.bfloat16)],
        compiler_params=pltpu.CompilerParams(vmem_limit_bytes=VMEM_LIMIT),
        cost_estimate=pl.CostEstimate(flops=2 * 10**9, bytes_accessed=80 * 2**20, transcendentals=0),
    )(here, q, kv, doc, key_doc, grad, full, totals)


def rms_scale(values, gain_row):
    return (
        values * lax.rsqrt(jnp.mean(values * values, axis=-1, keepdims=True) + NORM_EPS) * gain_row
    )


def gelu_tanh(values):
    return jax.nn.gelu(values, approximate=True)


def rope_tables(positions):
    half_width = HEAD_DIM // 2
    frequency = jnp.exp(
        jnp.arange(half_width, dtype=jnp.float32) * (-2.0 * math.log(ROPE_BASE) / HEAD_DIM)
    )
    angles = positions.astype(jnp.float32)[:, None] * frequency[None, :]
    cosine = jnp.concatenate([jnp.cos(angles), jnp.cos(angles)], axis=-1)
    sine = jnp.concatenate([jnp.sin(angles), jnp.sin(angles)], axis=-1)
    return cosine[:, None, :], sine[:, None, :]


def rotate(values, cosine, sine):
    half_width = HEAD_DIM // 2
    turned = jnp.concatenate([-values[..., half_width:], values[..., :half_width]], axis=-1)
    return values * cosine + turned * sine


def feed_forward_apart(
    branch_slabs, inputs, cotangent, gains, gate_up_all, down_all, count, piece
):
    rows, width = inputs.shape
    bf16 = jnp.bfloat16
    branch = branch_slabs.reshape(rows, width)
    middle = inputs + rms_scale(branch, gains[1])
    norm_three = rms_scale(middle, gains[2]).astype(bf16)
    gate_all = gate_up_all[:, :width]
    up_all = gate_up_all[:, width:]
    norm_all = all_gather_blk(norm_three, count, 4).reshape(count * rows, width)
    gate = dot(norm_all, gate_all, LAST)
    up = dot(norm_all, up_all, LAST)
    hidden = (gelu_tanh(gate) * up).astype(bf16)
    ffn_part = dot(hidden, down_all, PLAIN).astype(bf16)
    ffn_out = reduce_scatter_blk(ffn_part.reshape((count,) + piece), count, 5).reshape(rows, width)
    output = (middle + rms_scale(ffn_out, gains[3])).astype(bf16)[None]

    out_cotangent = cotangent[0].astype(jnp.float32)
    _, post_ffn_back = jax.vjp(rms_scale, ffn_out, gains[3])
    ffn_grad, gain_grad_four = post_ffn_back(out_cotangent)
    grad_all = all_gather_blk(ffn_grad.astype(bf16), count, 6).reshape(count * rows, width)
    activated, gelu_back = jax.vjp(gelu_tanh, gate)
    hidden_grad = dot(grad_all, down_all, LAST)
    gate_grad = gelu_back(hidden_grad * up)[0].astype(bf16)
    up_grad = (hidden_grad * activated).astype(bf16)
    norm_part = dot(gate_grad, gate_all, PLAIN) + dot(up_grad, up_all, PLAIN)
    norm_three_grad = reduce_scatter_blk(
        norm_part.astype(bf16).reshape((count,) + piece), count, 7
    ).reshape(rows, width)
    down_part = dot(hidden, grad_all, FIRST).astype(bf16)
    gate_up_part = jnp.concatenate(
        [dot(gate_grad, norm_all, FIRST), dot(up_grad, norm_all, FIRST)], axis=1
    ).astype(bf16)
    _, pre_ffn_back = jax.vjp(rms_scale, middle, gains[2])
    middle_part, gain_grad_three = pre_ffn_back(norm_three_grad)
    middle_grad = out_cotangent + middle_part
    _, post_attn_back = jax.vjp(rms_scale, branch, gains[1])
    branch_grad, gain_grad_two = post_attn_back(middle_grad)
    return (
        output,
        middle_grad,
        branch_grad.astype(bf16),
        gain_grad_two,
        gain_grad_three,
        gain_grad_four,
        gate_up_part,
        down_part,
    )


def shards(
    tokens, cotangent, segments, norm_gains, qkv_weight, out_weight, gate_up_weight, down_weight
):
    _, rows, width = tokens.shape
    count = lax.axis_size("blk")
    here = lax.axis_index("blk")
    mine = 2 * lax.axis_index("dp") + lax.axis_index("head")
    group_rows = GROUPS * rows
    head_width = REPS * HEAD_DIM
    bf16 = jnp.bfloat16
    slab = slabs(rows)
    piece = (rows // slab, slab, width)

    gain_rows = norm_gains.shape[0]
    gain_lanes = -(-gain_rows // 128) * 128
    gains_sent = jnp.pad(
        jnp.transpose(norm_gains).astype(jnp.float32), ((0, 4), (0, gain_lanes - gain_rows))
    )
    out_rows = out_weight.shape[0]
    out_sent = jnp.transpose(out_weight.reshape(out_rows, GROUPS, head_width), (1, 0, 2))
    qkv_rows = qkv_weight.shape[0]
    qkv_slab = slabs(qkv_rows)
    qkv_piece = (qkv_rows // qkv_slab, qkv_slab, width)
    qkv_all, out_mine, tokens_all, gains_all, docs_all, down_all = gather_first(
        qkv_weight,
        out_sent,
        tokens[0],
        gains_sent,
        segments.reshape(-1, 128),
        down_weight,
        count,
        1,
    )
    down_all = down_all.reshape(-1, width)
    gains = jnp.transpose(gains_all[:, :, :4, :gain_rows], (2, 0, 1, 3)).reshape(4, width)
    qkv_head = qkv_all.reshape(count * qkv_rows, width)
    docs = docs_all.reshape(2, 2, count, rows)
    key_doc = docs.reshape(2, 2 * count, 1, rows)
    own_doc = lax.dynamic_index_in_dim(docs, here, 2, keepdims=False).reshape(GROUPS, rows, 1)
    here_one = here.reshape(1)

    group_tokens = tokens_all.reshape(group_rows, width).astype(jnp.float32)
    norm_one = rms_scale(group_tokens, gains[0]).astype(bf16)
    proj = dot(norm_one, qkv_head, LAST)
    inside = jnp.arange(rows, dtype=jnp.int32)
    position = jnp.concatenate([here * rows + inside, (count + here) * rows + inside])
    cosine, sine = rope_tables(jnp.concatenate([position, position]))
    proj = proj.reshape(group_rows, REPS + 2, HEAD_DIM)
    turned = rotate(proj[:, : REPS + 1], cosine, sine)
    sent = jnp.concatenate([turned, proj[:, REPS + 1 :]], axis=1).astype(bf16)
    queries = sent[:, :REPS].reshape(GROUPS, rows, head_width)
    own_kv = sent[:, REPS:].reshape(group_rows, 2 * HEAD_DIM)
    kv_slab = slabs(group_rows)
    kv_piece = (group_rows // kv_slab, kv_slab, 2 * HEAD_DIM)
    kv, out_all, gate_up_all, attn, attended, totals = gather_attend(
        own_kv, out_mine, gate_up_weight, queries, own_doc, key_doc, count, 2
    )
    gate_up_all = gate_up_all.reshape(-1, 2 * width)
    out_head = out_all.reshape(width, head_width)
    attn = attn.reshape(group_rows, head_width)
    branch_slabs = project_group(attn.reshape(queries.shape), out_head, piece, 3)
    inputs = tokens[0].astype(jnp.float32)
    if feed_forward_fits(count, rows, width, down_all.shape[0]):
        output, middle_grad, branch_grad, gain_rest, gate_up_part, down_part = feed_forward(
            branch_slabs,
            tokens.reshape(piece),
            cotangent.reshape(piece),
            gains,
            gate_up_all,
            down_all,
            count,
            4,
        )
        output = output.reshape(tokens.shape)
        middle_grad = middle_grad.reshape(rows, width)
        branch_grad = branch_grad.reshape(rows, width)
        gain_grad_two, gain_grad_three, gain_grad_four = gain_rest[1], gain_rest[2], gain_rest[3]
    else:
        (
            output,
            middle_grad,
            branch_grad,
            gain_grad_two,
            gain_grad_three,
            gain_grad_four,
            gate_up_part,
            down_part,
        ) = feed_forward_apart(
            branch_slabs, inputs, cotangent, gains, gate_up_all, down_all, count, piece
        )
    branch_all = all_gather_group(branch_grad, 8).reshape(group_rows, width)
    attn_grad = dot(branch_all, out_head, PLAIN).astype(bf16).reshape(GROUPS, rows, head_width)
    out_part = dot(branch_all, attn, FIRST).astype(bf16)
    out_part = out_part.reshape(GROUPS, count, out_rows, head_width)
    gate_up_part = gate_up_part.reshape((GROUPS,) + gate_up_weight.shape)
    if attend_back_fits(count):
        dq, dkv, out_sum, gate_up_grad = attend_back_reduce(
            queries,
            kv,
            own_doc,
            key_doc,
            attn_grad,
            attended,
            totals,
            out_part,
            gate_up_part,
            kv_piece,
            count,
            9,
        )
    else:
        kv = kv.reshape(count, GROUPS, rows, 2 * HEAD_DIM)
        dq, dkv_part = attention_backward(
            here_one, queries, kv, own_doc, key_doc, attn_grad, attended, totals
        )
        dkv, out_sum, gate_up_grad = reduce_middle(
            dkv_part.reshape((count,) + kv_piece), out_part, gate_up_part, count, 9
        )
    sent_grad = jnp.concatenate(
        [
            dq.reshape(group_rows, REPS, HEAD_DIM),
            dkv.reshape(group_rows, 2, HEAD_DIM),
        ],
        axis=1,
    ).astype(jnp.float32)
    unturned = rotate(sent_grad[:, : REPS + 1], cosine, -sine)
    proj_grad = (
        jnp.concatenate([unturned, sent_grad[:, REPS + 1 :]], axis=1)
        .astype(bf16)
        .reshape(group_rows, (REPS + 2) * HEAD_DIM)
    )
    qkv_part = dot(proj_grad, norm_one, FIRST).astype(bf16)
    norm_one_part = dot(proj_grad, qkv_head, PLAIN)
    _, gain_back = jax.vjp(lambda gain: rms_scale(group_tokens, gain), gains[0])
    (gain_grad_one,) = gain_back(norm_one_part)
    gain_part = jnp.stack([gain_grad_one, gain_grad_two, gain_grad_three, gain_grad_four])
    gain_part = jnp.transpose(gain_part.reshape(4, GROUPS, count, gain_rows), (2, 1, 0, 3))
    gain_part = jnp.pad(gain_part, ((0, 0), (0, 0), (0, 4), (0, gain_lanes - gain_rows)))
    qkv_grad, norm_one_grad, gain_grad, out_grad, down_grad = reduce_last(
        qkv_part.reshape((count,) + qkv_piece),
        norm_one_part.astype(bf16).reshape((GROUPS,) + piece),
        gain_part[:, :, None],
        out_sum,
        down_part.reshape((GROUPS,) + down_weight.shape),
        count,
        10,
    )
    qkv_grad = qkv_grad.reshape(qkv_rows, width)
    out_grad = (
        jnp.transpose(out_grad, (1, 0, 2)).reshape(out_rows, GROUPS * head_width).astype(jnp.float32)
    )
    gain_grad = jnp.transpose(gain_grad.reshape(8, gain_lanes)[:4, :gain_rows])
    _, pre_attn_back = jax.vjp(lambda values: rms_scale(values, gains[0]), inputs)
    (input_part,) = pre_attn_back(norm_one_grad.reshape(rows, width))
    tokens_grad = (middle_grad + input_part).astype(bf16)[None]
    return (output, tokens_grad, gain_grad, qkv_grad, out_grad, gate_up_grad, down_grad)


def solution(mesh):
    whole = ("dp", "head", "blk")
    return jax.shard_map(
        shards,
        mesh=mesh,
        in_specs=(
            P("dp", ("head", "blk"), None),
            P("dp", ("head", "blk"), None),
            P("dp", None),
            P(whole, None),
            P(whole, None),
            P(whole, None),
            P(whole, None),
            P(whole, None),
        ),
        out_specs=(
            P("dp", ("head", "blk"), None),
            P("dp", ("head", "blk"), None),
            P(whole, None),
            P(whole, None),
            P(whole, None),
            P(whole, None),
            P(whole, None),
        ),
        check_vma=False,
    )
```

```python
import functools
import math

import jax
import jax.numpy as jnp
from jax import lax
from jax.experimental import pallas as pl
from jax.experimental.pallas import tpu as pltpu
from jax.sharding import PartitionSpec as P

HEADS = 8
KV_HEADS = 4
HEAD_DIM = 256
REPS = HEADS // KV_HEADS
GROUPS = 4
SOFT_CAP = 50.0
NORM_EPS = 1e-06
ROPE_BASE = 10000.0
SCORE_SCALE = HEAD_DIM ** (-0.5)

MESH = pl.DeviceIdType.MESH
VMEM_LIMIT = 60 * 1024 * 1024


class Place:
    def __init__(self, count):
        self.count = count
        self.inner = 4 if count >= 32 else 2
        self.outer = count // self.inner
        self.here = lax.axis_index("blk")
        self.line = self.here // self.inner
        self.side = lax.rem(self.here, self.inner)
        self.core = lax.axis_index("dp")
        self.half = lax.axis_index("head")
        self.group = 2 * self.core + self.half

    def near(self, k):
        orders = [near_order(self.outer, line)[k] for line in range(self.outer)]
        found = jnp.int32(orders[0])
        for line in range(1, self.outer):
            found = jnp.where(self.line == line, jnp.int32(orders[line]), found)
        return found

    def near_at(self, k):
        found = self.near(0)
        for static in range(1, self.outer):
            found = jnp.where(k == static, self.near(static), found)
        return found

    def at(self, line, side):
        return {"blk": line * self.inner + side}

    def beside(self, step):
        return lax.rem(self.side + step, self.inner)

    def partner(self):
        return {"dp": 1 - self.core}

    def across(self):
        return {"head": 1 - self.half}

    def corner(self):
        return {"dp": 1 - self.core, "head": 1 - self.half}


def remote(src, dst, sent, came, device):
    return pltpu.make_async_remote_copy(
        src_ref=src, dst_ref=dst, send_sem=sent, recv_sem=came, device_id=device, device_id_type=MESH
    )


def greet(place, blk=False, core=False, half=False, corner=False, meanwhile=None):
    sem = pltpu.get_barrier_semaphore()
    amount = jnp.int32(0)

    def hello(device):
        pl.semaphore_signal(sem, inc=1, device_id=device, device_id_type=MESH)

    if blk:
        up, down = place.line < place.outer - 1, place.line > 0
        pl.when(up)(lambda: hello(place.at(place.line + 1, place.side)))
        pl.when(down)(lambda: hello(place.at(place.line - 1, place.side)))
        amount = amount + up.astype(jnp.int32) + down.astype(jnp.int32) + (place.inner - 1)
        for step in range(1, place.inner):
            hello(place.at(place.line, place.beside(step)))
    for wanted, device in (
        (core, place.partner()),
        (half, place.across()),
        (corner, place.corner()),
    ):
        if wanted:
            hello(device)
            amount = amount + 1
    if meanwhile:
        meanwhile()
    pl.semaphore_wait(sem, amount)


def together(*tasks):
    tasks = list(tasks)
    while tasks:
        for task in list(tasks):
            try:
                next(task)
            except StopIteration:
                tasks.remove(task)


def waiting(task, *rounds):
    for step, _ in enumerate(task):
        yield
        if step < len(rounds):
            for _ in range(rounds[step]):
                yield


def near_order(outer, line):
    ends = outer == 4
    return sorted(
        range(outer),
        key=lambda other: (abs(other - line), ends and other not in (0, outer - 1), other),
    )


def evened(place, parts):
    return parts == 2 and place.inner == 2 and place.outer == 4


def part_of(ref, h, parts):
    if parts == 1:
        return ref
    size = ref.shape[0] // parts
    return ref.at[pl.ds(h * size, size)]


def gather_blk_sems(place_count, parts=2):
    inner = 4 if place_count >= 32 else 2
    return [
        pltpu.SemaphoreType.DMA((2 + inner, place_count, parts)),
        pltpu.SemaphoreType.DMA((place_count, parts)),
        pltpu.SemaphoreType.DMA,
    ]


class GatherBlk:
    def __init__(self, place, src, view, sent, came, own):
        self.place, self.src, self.view, self.sent, self.came = place, src, view, sent, came
        self.parts = came.shape[1]
        self.evened = evened(place, self.parts)
        self.middle = (place.line > 0) & (place.line < place.outer - 1)
        self.copy = pltpu.make_async_copy(src, view(place.here), own)

    def sends(self, k, h):
        place = self.place
        there = place.near(k)
        piece = there * place.inner + place.side
        there_view = part_of(self.view(piece), h, self.parts)
        src = part_of(self.src, h, self.parts) if k == 0 else there_view

        def send(kind, device):
            return remote(
                src, there_view, self.sent.at[kind, piece, h], self.came.at[piece, h], device
            )

        line, side = place.line, place.side
        up = (there <= line) & (line < place.outer - 1)
        down = (there >= line) & (line > 0)
        aside = range(1, place.inner)
        if self.evened and h == 1 and k == place.outer - 1:
            aside = ()
        return (
            [
                (up, lambda: send(0, place.at(line + 1, side))),
                (down, lambda: send(1, place.at(line - 1, side))),
            ],
            [send(1 + step, place.at(line, place.beside(step))) for step in aside],
        )

    def forward(self, k, h):
        along, aside = self.sends(k, h)
        for needed, make in along:
            pl.when(needed)(lambda make=make: make().start())
        for one in aside:
            one.start()

    def start(self):
        self.copy.start()
        for h in range(self.parts):
            self.forward(0, h)

    def arrived(self, piece, h):
        place = self.place
        remote(
            part_of(self.src, h, self.parts),
            part_of(self.view(piece), h, self.parts),
            self.sent.at[0, piece, h],
            self.came.at[piece, h],
            place.at(place.line, place.beside(1)),
        ).wait_recv()

    def pass_on(self, k):
        for h in range(self.parts):
            self.arrived(self.place.near(k) * self.place.inner + self.place.side, h)
            self.forward(k, h)

    def extra(self, k):
        place = self.place
        piece = place.near(k) * place.inner + place.beside(1)
        to = place.near(2 if k == 1 else 1)
        half = part_of(self.view(piece), 1, 2)
        return remote(
            half,
            half,
            self.sent.at[place.inner + 1, piece, 1],
            self.came.at[piece, 1],
            place.at(to, place.side),
        )

    def pass_extra(self, k):
        if self.evened:

            @pl.when(self.middle)
            def _():
                self.arrived(self.place.near(k) * self.place.inner + self.place.beside(1), 1)
                self.extra(k).start()

    def beside_arrived(self, k):
        for step in range(1, self.place.inner):
            piece = self.place.near(k) * self.place.inner + self.place.beside(step)
            for h in range(self.parts):
                if self.evened and h == 1 and k in (1, self.place.outer - 1):
                    pl.when(jnp.logical_not(self.middle))(lambda: self.arrived(piece, 1))
                else:
                    self.arrived(piece, h)

    def finish(self):
        for k in range(self.place.outer):
            for h in range(self.parts):
                along, aside = self.sends(k, h)
                for needed, make in along:
                    pl.when(needed)(lambda make=make: make().wait_send())
                for one in aside:
                    one.wait_send()
        if self.evened:

            @pl.when(self.middle)
            def _():
                self.extra(1).wait_send()
                self.extra(self.place.outer - 1).wait_send()


def advance(gathers, k):
    place = gathers[0].place

    def each(name, *args):
        for gather in gathers:
            getattr(gather, name)(*args)

    if not gathers[0].evened:
        if k + 1 < place.outer:
            each("pass_on", k + 1)
        return
    middle = gathers[0].middle
    ends = jnp.logical_not(middle)
    if k == 0:
        each("pass_on", 1)
        pl.when(middle)(lambda: each("pass_on", 2))
    elif k == 1:
        pl.when(ends)(lambda: each("pass_on", 2))
        each("pass_extra", 1)
        pl.when(middle)(lambda: each("pass_on", 3))
    elif k == 2:
        pl.when(ends)(lambda: each("pass_on", 3))
        each("pass_extra", 3)


def gather_blk(place, src, view, sent, came, own):
    if not callable(view):
        out = view
        view = lambda piece: out.at[piece]
    work = GatherBlk(place, src, view, sent, came, own)
    work.start()
    yield
    for k in range(1, place.outer):
        work.pass_on(k)
        if k == place.outer - 2:
            work.pass_extra(1)
        yield
    work.pass_extra(place.outer - 1)
    yield
    for k in range(place.outer):
        work.beside_arrived(k)
    work.finish()
    work.copy.wait()


def add_into(out, *terms):
    lanes = out.shape[-1]
    parts = 3 if lanes % 384 == 0 and lanes > 1024 else 1
    step = lanes // parts

    def one(i, carry):
        at = i if parts == 1 else i // parts
        columns = pl.ds(pl.multiple_of((i % parts) * step, step), step) if parts > 1 else slice(None)
        index = (at,) + (slice(None),) * (len(out.shape) - 2) + (columns,)
        total = terms[0][index].astype(jnp.float32)
        for term in terms[1:]:
            total = total + term[index].astype(jnp.float32)
        out[index] = total.astype(out.dtype)
        return carry

    lax.fori_loop(0, out.shape[0] * parts, one, 0)


def reduce_blk_scratch(place_count, piece, dtype, parts=2):
    inner = 4 if place_count >= 32 else 2
    outer = place_count // inner
    half = (piece[0] // 2,) + tuple(piece[1:]) if parts == 2 and inner == 2 and outer == 4 else (1, 8, 128)
    return [
        pltpu.VMEM((outer, inner - 1) + piece, dtype),
        pltpu.VMEM((outer + 1,) + piece, dtype),
        pltpu.VMEM((outer,) + piece, dtype),
        pltpu.VMEM((4,) + half, dtype),
        pltpu.SemaphoreType.DMA((outer, inner - 1, parts)),
        pltpu.SemaphoreType.DMA((outer, inner - 1, parts)),
        pltpu.SemaphoreType.DMA((outer, parts)),
        pltpu.SemaphoreType.DMA((outer + 1, parts)),
        pltpu.SemaphoreType.DMA((2,)),
        pltpu.SemaphoreType.DMA((2,)),
    ]


REDUCE_REFS = 10


class ReduceBlk:
    def __init__(
        self,
        place,
        view,
        out,
        beside,
        along,
        held,
        spare,
        side_sent,
        side_came,
        line_sent,
        line_came,
        spare_sent,
        spare_came,
    ):
        self.place, self.view, self.out = place, view, out
        self.beside, self.along, self.held, self.spare = beside, along, held, spare
        self.side_sems, self.line_sems = (side_sent, side_came), (line_sent, line_came)
        self.spare_sems = (spare_sent, spare_came)
        self.parts = line_sent.shape[1]
        self.evened = evened(place, self.parts)
        self.middle = (place.line > 0) & (place.line < place.outer - 1)

    def part(self, ref, h):
        return part_of(ref, h, self.parts)

    def far(self, k):
        return self.place.near(self.place.outer - 1 - k)

    def alone(self, k, h):
        return self.evened and k == 0 and h == 1

    def side_copy(self, there, step, h, src=None):
        place = self.place
        to = place.beside(step)
        if src is None:
            src = self.part(self.view(there * place.inner + to), h)
        return remote(
            src,
            self.part(self.beside.at[there, place.inner - step - 1], h),
            self.side_sems[0].at[there, step - 1, h],
            self.side_sems[1].at[there, place.inner - step - 1, h],
            place.at(place.line, to),
        )

    def line_copy(self, there, slot, to, h, src=None):
        return remote(
            self.part(self.held.at[there], h) if src is None else src,
            self.part(self.along.at[slot], h),
            self.line_sems[0].at[there, h],
            self.line_sems[1].at[slot, h],
            self.place.at(to, self.place.side),
        )

    def send(self, k, h):
        for step in range(1, self.place.inner):
            self.side_copy(self.far(k), step, h).start()

    def terms(self, k, h):
        place = self.place
        there = self.far(k)
        own = [self.part(self.view(there * place.inner + place.side), h)]
        if self.alone(k, h):
            return own
        for step in range(1, place.inner):
            self.side_copy(there, step, h).wait_recv()
        return own + [self.part(self.beside.at[there, j], h) for j in range(place.inner - 1)]

    def onward(self, there, h, src=None):
        line, outer = self.place.line, self.place.outer
        to = jnp.where(there < line, line - 1, line + 1)
        slot = jnp.where(there == line + 1, outer, there)
        return self.line_copy(there, slot, to, h, src)

    def starts(self, there):
        line, outer = self.place.line, self.place.outer
        return ((there < line) & (line == outer - 1)) | ((there > line) & (line == 0))

    def pass_on(self, k, h, middle=None):
        place = self.place
        line = place.line
        there = self.far(k)
        terms = self.terms(k, h)
        held = self.part(self.held.at[there], h)

        def first():
            add_into(held, *terms)

        def later():
            back = jnp.where(there < line, line + 1, line - 1)
            self.line_copy(there, there, back, h).wait_recv()
            add_into(held, self.part(self.along.at[there], h), *terms)

        if middle is None:
            starts = self.starts(there)
            pl.when(starts)(first)
            pl.when(jnp.logical_not(starts))(later)
        elif middle:
            later()
        else:
            first()
        self.onward(there, h).start()

    def last(self, h):
        place = self.place
        line, outer = place.line, place.outer
        terms = self.terms(outer - 1, h)
        out = self.part(self.out, h)

        @pl.when(self.middle)
        def _():
            self.line_copy(line, line, line + 1, h).wait_recv()
            self.line_copy(line, outer, line - 1, h).wait_recv()
            from_above = self.part(self.along.at[line], h)
            add_into(out, from_above, self.part(self.along.at[outer], h), *terms)

        @pl.when(jnp.logical_not(self.middle))
        def _():
            slot = jnp.where(line == 0, line, outer)
            back = jnp.where(line == 0, line + 1, line - 1)
            self.line_copy(line, slot, back, h).wait_recv()
            add_into(out, self.part(self.along.at[slot], h), *terms)


    def spare_view(self, k):
        place = self.place
        return self.part(self.view(place.near(k) * place.inner + place.beside(1)), 1)

    def spare_first(self):
        return remote(
            self.spare_view(3),
            self.spare.at[0],
            self.spare_sems[0].at[0],
            self.spare_sems[1].at[0],
            self.place.at(self.place.near(1), self.place.side),
        )

    def spare_second(self):
        return remote(
            self.spare.at[2],
            self.spare.at[1],
            self.spare_sems[0].at[1],
            self.spare_sems[1].at[1],
            self.place.at(self.place.near(2), self.place.side),
        )

    def spare_side(self):
        return self.side_copy(self.far(2), 1, 1, self.spare.at[3])

    def opening(self):
        outer = self.place.outer
        if not self.evened:

            def every():
                for k in range(outer):
                    for h in range(self.parts):
                        self.send(k, h)

            return [every]
        ends = jnp.logical_not(self.middle)

        def along():
            self.spare_first().start()
            there = self.far(0)
            self.onward(
                there, 1, self.part(self.view(there * self.place.inner + self.place.side), 1)
            ).start()

        todo = [lambda: self.send(0, 0), lambda: pl.when(ends)(along)]
        todo += [lambda k=k, h=h: self.send(k, h) for k, h in ((1, 0), (1, 1), (2, 0))]
        todo += [
            lambda k=k, h=h: pl.when(ends)(lambda: self.send(k, h))
            for k, h in ((2, 1), (3, 0), (3, 1))
        ]
        return todo

    def start(self):
        for step in self.opening():
            step()

    def turning(self):
        def first():
            self.spare_first().wait_recv()
            add_into(self.spare.at[2], self.spare.at[0], self.spare_view(3))
            self.spare_second().start()

        def second():
            self.spare_second().wait_recv()
            add_into(self.spare.at[3], self.spare.at[1], self.spare_view(1))
            self.spare_side().start()
            for h in (0, 1):
                self.send(3, h)

        steps = (first, lambda: self.pass_on(0, 1, True), second)
        return steps

    def events(self):
        outer, parts = self.place.outer, self.parts
        if self.evened:
            todo = [lambda step=step: pl.when(self.middle)(step) for step in self.turning()]
            todo.append(lambda: self.pass_on(0, 0))
        else:
            todo = [lambda h=h: self.pass_on(0, h) for h in range(parts)]
        for k in range(1, outer - 1):
            for h in range(parts):
                todo.append(lambda k=k, h=h: self.pass_on(k, h))
        for h in range(parts):
            todo.append(lambda h=h: self.last(h))
        return todo

    def finish(self):
        for k in range(self.place.outer):
            for h in range(self.parts):
                if k < self.place.outer - 1:
                    self.onward(self.far(k), h).wait_send()
                if not self.alone(k, h):
                    for step in range(1, self.place.inner):
                        self.side_copy(self.far(k), step, h).wait_send()
        if self.evened:

            @pl.when(self.middle)
            def _():
                self.spare_second().wait_send()

            @pl.when(jnp.logical_not(self.middle))
            def _():
                self.spare_first().wait_send()


def reduce_blk(place, view, out, *scratch):
    if not callable(view):
        part = view
        view = lambda piece: part.at[piece]
    work = ReduceBlk(place, view, out, *scratch)
    for step in work.opening() + work.events():
        step()
        yield
    work.finish()


def gather_group_sems():
    return [pltpu.SemaphoreType.DMA((3,)), pltpu.SemaphoreType.DMA((4,)), pltpu.SemaphoreType.DMA]


def gather_group(place, src, view, sent, came, own, through=None):
    if not callable(view):
        out = view
        view = lambda g: out.at[g]
    copy = pltpu.make_async_copy(src if through is None else through, view(place.group), own)
    load = None if through is None else pltpu.make_async_copy(src, through, own)
    mine, other = place.group, 2 * place.core + (1 - place.half)
    to_half = remote(src, view(mine), sent.at[0], came.at[mine], place.across())
    to_core = remote(src, view(mine), sent.at[1], came.at[mine], place.partner())
    to_half.start()
    to_core.start()
    (load or copy).start()
    yield
    if load:
        load.wait()
        copy.start()
    remote(src, view(other), sent.at[0], came.at[other], place.across()).wait_recv()
    relay = remote(view(other), view(other), sent.at[2], came.at[other], place.partner())
    relay.start()
    yield
    for half in (0, 1):
        slot = 2 * (1 - place.core) + half
        remote(src, view(slot), sent.at[0], came.at[slot], place.partner()).wait_recv()
    to_half.wait_send()
    to_core.wait_send()
    relay.wait_send()
    copy.wait()


def share_rows(ref, parts, p):
    rows = ref.shape[0] // parts
    return ref.at[pl.ds(p * rows, rows)]


def gather_group_rows(place, src, out, parts, take, through=True):
    def task(p, refs):
        rows = src.shape[0] // parts
        view = lambda g: out.at[g, pl.ds(p * rows, rows)]
        return gather_group(place, share_rows(src, parts, p), view, *refs)

    return [task(p, take(4 if through else 3)) for p in range(parts)]


def gather_rows_scratch(value, parts):
    through = pltpu.VMEM((value.shape[0] // parts, value.shape[1]), value.dtype)
    return (gather_group_sems() + [through]) * parts


def fold_rows_scratch(piece, parts):
    rows, width = piece[0] // parts, piece[1]
    bf16 = jnp.bfloat16
    one = [
        pltpu.VMEM((2, rows, width), bf16),
        pltpu.VMEM((rows, width), bf16),
        pltpu.VMEM((rows, width), bf16),
        pltpu.VMEM((rows, width), bf16),
        pltpu.VMEM((rows, width), jnp.float32),
        pltpu.SemaphoreType.DMA((3,)),
        pltpu.SemaphoreType.DMA((3,)),
        pltpu.SemaphoreType.DMA((3,)),
    ]
    return one * parts


def add_rows(out, *terms):
    rows = slabs(out.shape[0])

    def one(i, carry):
        at = pl.ds(pl.multiple_of(i * rows, rows), rows)
        total = terms[0][at].astype(jnp.float32)
        for term in terms[1:]:
            total = total + term[at].astype(jnp.float32)
        out[at] = total.astype(out.dtype)
        return carry

    lax.fori_loop(0, out.shape[0] // rows, one, 0)


def fold_rows(place, part, out, parts, take):
    rows = out.shape[0] // parts
    core, half = place.core, place.half
    far, near = 2 * (1 - core) + (1 - half), 2 * (1 - core) + half
    beside = 2 * core + (1 - half)

    def task(p, from_core, from_half, held, mine, total, sent, came, local):
        at = pl.ds(p * rows, rows)
        first = remote(part.at[far, at], from_core.at[1], sent.at[0], came.at[0], place.partner())
        second = remote(part.at[near, at], from_core.at[0], sent.at[1], came.at[1], place.partner())
        third = remote(held, from_half, sent.at[2], came.at[2], place.across())
        load_held = pltpu.make_async_copy(part.at[beside, at], held, local.at[0])
        load_mine = pltpu.make_async_copy(part.at[place.group, at], mine, local.at[1])
        store = pltpu.make_async_copy(total, out.at[at], local.at[2])
        for copy in (first, load_held, second, load_mine):
            copy.start()
        yield
        first.wait_recv()
        load_held.wait()
        add_rows(held, held, from_core.at[1])
        third.start()
        yield
        second.wait_recv()
        load_mine.wait()
        third.wait_recv()
        add_rows(total, mine, from_core.at[0], from_half)
        store.start()
        yield
        for copy in (first, second, third):
            copy.wait_send()
        store.wait()

    return [task(p, *take(8)) for p in range(parts)]


ROW_PARTS = 3


def reduce_group_scratch(piece, dtype):
    return [
        pltpu.VMEM((2,) + piece, dtype),
        pltpu.VMEM(piece, dtype),
        pltpu.VMEM(piece, dtype),
        pltpu.SemaphoreType.DMA((3,)),
        pltpu.SemaphoreType.DMA((3,)),
    ]


def reduce_group(place, view, out, from_core, from_half, held, sent, came):
    if not callable(view):
        part = view
        view = lambda g: part.at[g]
    far = 2 * (1 - place.core) + (1 - place.half)
    near = 2 * (1 - place.core) + place.half
    first = remote(view(far), from_core.at[1], sent.at[0], came.at[0], place.partner())
    second = remote(view(near), from_core.at[0], sent.at[1], came.at[1], place.partner())
    first.start()
    yield
    second.start()
    yield
    first.wait_recv()
    add_into(held, view(2 * place.core + (1 - place.half)), from_core.at[1])
    third = remote(held, from_half, sent.at[2], came.at[2], place.across())
    third.start()
    yield
    second.wait_recv()
    third.wait_recv()
    add_into(out, view(place.group), from_core.at[0], from_half)
    first.wait_send()
    second.wait_send()
    third.wait_send()


def exchange_group_sems():
    return [pltpu.SemaphoreType.DMA((3,)), pltpu.SemaphoreType.DMA((4,)), pltpu.SemaphoreType.DMA]


def exchange_group(place, src, out, sent, came, own):
    mine = place.group
    copy = pltpu.make_async_copy(src.at[mine], out.at[mine], own)
    copy.start()
    core, half = place.core, place.half
    links = (
        (2 * (1 - core) + (1 - half), place.corner()),
        (2 * core + (1 - half), place.across()),
        (2 * (1 - core) + half, place.partner()),
    )
    copies = [
        remote(src.at[to], out.at[mine], sent.at[k], came.at[mine], device)
        for k, (to, device) in enumerate(links)
    ]
    for one in copies:
        one.start()
    yield
    for k, (peer, device) in enumerate(links):
        remote(src.at[peer], out.at[peer], sent.at[k], came.at[peer], device).wait_recv()
    for one in copies:
        one.wait_send()
    copy.wait()


def transfer(name, number, body, ins, outs, scratch, moved, out_spaces=None, in_spaces=None):
    spaces = out_spaces or [pl.ANY] * len(outs)
    in_spaces = in_spaces or [pltpu.VMEM] * len(ins)
    return pl.pallas_call(
        body,
        name=name,
        out_shape=outs,
        in_specs=[pl.BlockSpec(memory_space=space) for space in in_spaces],
        out_specs=[pl.BlockSpec(memory_space=space) for space in spaces],
        scratch_shapes=scratch,
        compiler_params=pltpu.CompilerParams(
            collective_id=number, has_side_effects=True, vmem_limit_bytes=VMEM_LIMIT
        ),
        cost_estimate=pl.CostEstimate(flops=0, bytes_accessed=moved * 40, transcendentals=0),
    )(*ins)


def shape(dims, dtype):
    return jax.ShapeDtypeStruct(tuple(dims), dtype)


def slabs(rows):
    return math.gcd(rows, 16)


def all_gather_blk(value, count, number):
    def body(src, out, *sems):
        place = Place(count)
        greet(place, blk=True)
        together(gather_blk(place, src, out, *sems))

    return transfer(
        f"gather{number}",
        number,
        body,
        [value],
        [shape((count,) + value.shape, value.dtype)],
        gather_blk_sems(count),
        value.size * 2 * count,
    )[0]


def reduce_scatter_blk(value, count, number):
    piece = value.shape[1:]

    def body(part, out, *scratch):
        place = Place(count)
        greet(place, blk=True)
        together(reduce_blk(place, part, out, *scratch))

    return transfer(
        f"reduce{number}",
        number,
        body,
        [value],
        [shape(piece, jnp.float32)],
        reduce_blk_scratch(count, piece, value.dtype),
        value.size * 2,
        [pltpu.VMEM],
    )[0]


class Taker:
    def __init__(self, refs):
        self.refs = list(refs)

    def __call__(self, amount):
        taken = self.refs[:amount]
        del self.refs[:amount]
        return taken


def gather_first(qkv, out_parts, tokens, gains, docs, down, count, number):
    names = 6

    def body(*refs):
        qkv_ref, out_ref, tok_ref, gain_ref, doc_ref, down_ref = refs[:names]
        qkv_all, out_mine, tok_all, gain_all, doc_all, down_all = refs[names : 2 * names]
        gain_mine = refs[2 * names]
        take = Taker(refs[2 * names + 1 :])
        place = Place(count)
        greet(place, blk=True, core=True, half=True, corner=True)

        def gain_task(near, far):
            yield from gather_blk(place, gain_ref, gain_mine, *near)
            yield from gather_group(place, gain_mine, gain_all, *far)

        def doc_task(sent, came, own):
            copy = pltpu.make_async_copy(doc_ref, doc_all.at[place.core], own)
            copy.start()
            send = remote(doc_ref, doc_all.at[place.core], sent, came, place.partner())
            send.start()
            yield
            remote(doc_ref, doc_all.at[1 - place.core], sent, came, place.partner()).wait_recv()
            send.wait_send()
            copy.wait()

        together(
            gain_task(take(3), take(3)),
            gather_blk(place, qkv_ref, qkv_all, *take(3)),
            doc_task(*take(3)),
            waiting(gather_group(place, tok_ref, tok_all, *take(3)), 2),
            waiting(exchange_group(place, out_ref, out_mine, *take(3)), 3),
            *(
                waiting(task, 2 + p, 4)
                for p, task in enumerate(
                    gather_group_rows(place, down_ref, down_all, ROW_PARTS, take)
                )
            ),
        )

    ins = [qkv, out_parts, tokens, gains, docs, down]
    return transfer(
        f"first{number}",
        number,
        body,
        ins,
        [
            shape((count,) + qkv.shape, qkv.dtype),
            shape(out_parts.shape, out_parts.dtype),
            shape((GROUPS,) + tokens.shape, tokens.dtype),
            shape((GROUPS, count) + gains.shape, gains.dtype),
            shape((2,) + docs.shape, docs.dtype),
            shape((GROUPS,) + down.shape, down.dtype),
        ],
        [pltpu.VMEM((count,) + gains.shape, gains.dtype)]
        + gather_blk_sems(count, 1)
        + gather_group_sems()
        + gather_blk_sems(count)
        + [pltpu.SemaphoreType.DMA] * 3
        + gather_group_sems()
        + exchange_group_sems()
        + gather_rows_scratch(down, ROW_PARTS),
        (qkv.size + out_parts.size) * 2 * count,
        None,
        [pltpu.VMEM] * 5 + [pl.ANY],
    )


def attend_step(count, g, here, key_half, key_at, q_ref, kv_ref, doc_ref, key_doc_ref, acc, tot):
    rows = q_ref.shape[1]
    sequence, half = g // 2, g % 2
    q2, position, doc = stacked_queries(g, half * count + here, q_ref, doc_ref)
    key_block = key_half * count + key_at
    at = pl.ds(pl.multiple_of((2 * sequence + key_half) * rows, rows), rows)
    kv = kv_ref.at[key_at, at]
    _, weights = attention_scores(
        q2, kv[:, :HEAD_DIM], position, doc, key_block, key_doc_ref[sequence, key_block], rows
    )
    tot[g] += jnp.sum(weights, axis=-1, keepdims=True)
    acc[g] += jnp.dot(
        weights.astype(jnp.bfloat16), kv[:, HEAD_DIM:], preferred_element_type=jnp.float32
    )


def stacked_queries(g, block, q_ref, doc_ref):
    rows = q_ref.shape[1]
    q2 = jnp.concatenate([q_ref[g, :, :HEAD_DIM], q_ref[g, :, HEAD_DIM:]], axis=0)
    inside = lax.broadcasted_iota(jnp.int32, (rows, 1), 0)
    position = block * rows + jnp.concatenate([inside, inside], axis=0)
    doc = jnp.concatenate([doc_ref[g], doc_ref[g]], axis=0)
    return q2, position, doc


def gather_attend(kv, out_mine, gate_up, queries, doc, key_doc, count, number):
    groups, out_rows, width = out_mine.shape
    rows = queries.shape[1]

    def body(*refs):
        kv_ref, out_ref, gate_up_ref, q_ref, doc_ref, key_doc_ref = refs[:6]
        kv_all, out_all, gate_up_all, attn_ref, full_ref, total_ref = refs[6:12]
        acc, tot = refs[12:14]
        take = Taker(refs[14:])
        place = Place(count)
        greet(place, blk=True, core=True, half=True)
        gathers = (
            GatherBlk(place, kv_ref, lambda i: kv_all.at[i], *take(3)),
            GatherBlk(place, out_ref, lambda i: out_all.at[:, i], *take(3)),
        )
        groups = gather_group_rows(place, gate_up_ref, gate_up_all, ROW_PARTS, take)
        for gather in gathers:
            gather.start()
        for task in groups:
            next(task)
        acc[...] = jnp.zeros_like(acc)
        tot[...] = jnp.zeros_like(tot)
        here, inner = place.here, place.inner

        def attend(k):
            def one(c, carry):
                key_at = place.near(k) * inner + c // 6
                sequence, kind = (c % 6) // 3, c % 3
                half = jnp.minimum(kind, 1)
                needed = jnp.where(kind == 1, key_at >= here, key_at <= here)

                @pl.when(needed)
                def _():
                    attend_step(
                        count,
                        2 * sequence + half,
                        here,
                        kind // 2,
                        key_at,
                        q_ref,
                        kv_all,
                        doc_ref,
                        key_doc_ref,
                        acc,
                        tot,
                    )

                return carry

            lax.fori_loop(0, inner * 6, one, 0)

        gathers[0].copy.wait()
        for k in range(place.outer):
            advance(gathers, k)
            gathers[0].beside_arrived(k)
            if 0 < k < place.outer - 1 and k <= 2:
                next(groups[k - 1])
            attend(k)

        def put(g, carry):
            total = tot[g]
            attended = acc[g] / total
            attended = jnp.concatenate([attended[:rows], attended[rows:]], axis=1)
            full_ref[g] = attended
            attn_ref[g] = attended.astype(jnp.bfloat16)
            total_ref[g] = total
            return carry

        lax.fori_loop(0, GROUPS, put, 0)
        next(groups[2])
        gathers[1].copy.wait()
        for k in range(place.outer):
            gathers[1].beside_arrived(k)
        for gather in gathers:
            gather.finish()
        together(*groups)

    return transfer(
        f"attend{number}",
        number,
        body,
        [kv, out_mine, gate_up, queries, doc, key_doc],
        [
            shape((count,) + kv.shape, kv.dtype),
            shape((groups, count, out_rows, width), out_mine.dtype),
            shape((GROUPS,) + gate_up.shape, gate_up.dtype),
            shape((GROUPS, rows, width), jnp.bfloat16),
            shape((GROUPS, rows, width), jnp.float32),
            shape((GROUPS, REPS * rows, 1), jnp.float32),
        ],
        [
            pltpu.VMEM((GROUPS, REPS * rows, HEAD_DIM), jnp.float32),
            pltpu.VMEM((GROUPS, REPS * rows, 1), jnp.float32),
        ]
        + gather_blk_sems(count)
        + gather_blk_sems(count)
        + gather_rows_scratch(gate_up, ROW_PARTS),
        (kv.size + out_mine.size) * 2 * count,
        [pltpu.VMEM, pl.ANY, pl.ANY, pltpu.VMEM, pltpu.VMEM, pltpu.VMEM],
        [pltpu.VMEM, pltpu.VMEM, pl.ANY, pltpu.VMEM, pltpu.VMEM, pltpu.VMEM],
    )


def attend_back_block(
    count, g, here, q_ref, kv_ref, doc_ref, key_doc_ref, grad_ref, full_ref, total_ref, dq_ref, key_acc
):
    rows = q_ref.shape[1]
    sequence, half = g // 2, g % 2
    block = half * count + here
    q2, position, doc = stacked_queries(g, block, q_ref, doc_ref)
    total = total_ref[g]
    grad = grad_ref[g].astype(jnp.float32)
    grad2 = jnp.concatenate([grad[:, :HEAD_DIM], grad[:, HEAD_DIM:]], axis=0)
    full2 = jnp.concatenate([full_ref[g, :, :HEAD_DIM], full_ref[g, :, HEAD_DIM:]], axis=0)
    total_grad = -jnp.sum(grad2 * full2, axis=-1, keepdims=True) / total
    sums_grad = (grad2 / total).astype(jnp.bfloat16)

    def one(key_block, acc):
        key_half = (key_block >= count).astype(jnp.int32)
        inner = key_block - key_half * count
        at = pl.ds(pl.multiple_of((2 * sequence + key_half) * rows, rows), rows)
        kv = kv_ref.at[inner, at]
        keys = kv[:, :HEAD_DIM]
        capped, weights = attention_scores(
            q2, keys, position, doc, key_block, key_doc_ref[sequence, key_block], rows
        )
        exp_grad = dot(sums_grad, kv[:, HEAD_DIM:], LAST)
        raw_grad = (
            weights * (exp_grad + total_grad) * (1.0 - capped * capped) * SCORE_SCALE
        ).astype(jnp.bfloat16)
        slot = inner * 2 + key_half
        key_acc[slot, :, :HEAD_DIM] += dot(raw_grad, q2, FIRST)
        key_acc[slot, :, HEAD_DIM:] += dot(weights.astype(jnp.bfloat16), sums_grad, FIRST)
        return acc + dot(raw_grad, keys, PLAIN)

    dq = lax.fori_loop(
        jnp.maximum(block - count, 0),
        block + 1,
        one,
        jnp.zeros((REPS * rows, HEAD_DIM), jnp.float32),
    )
    dq_ref[g] = jnp.concatenate([dq[:rows], dq[rows:]], axis=1).astype(jnp.bfloat16)


def attend_back_fits(count):
    return count == 8


def attend_back_reduce(
    queries, kv, doc, key_doc, grad, full, totals, out_part, gate_up_part, kv_piece, count, number
):
    out_piece = out_part.shape[:1] + out_part.shape[2:]
    gate_up_piece = gate_up_part.shape[1:]
    rows = queries.shape[1]
    steps = rows // kv_piece[1]
    bf16 = jnp.bfloat16

    def body(*refs):
        q_ref, kv_ref, doc_ref, key_doc_ref, grad_ref, full_ref, total_ref = refs[:7]
        out_ref, gate_up_ref = refs[7:9]
        dq_ref, dkv_sum, out_sum, gate_up_sum, dkv_part, key_acc = refs[9:15]
        take = Taker(refs[15:])
        place = Place(count)
        greet(place, blk=True, core=True, half=True)
        dkv = ReduceBlk(place, lambda i: dkv_part.at[i], dkv_sum, *take(REDUCE_REFS))
        out = ReduceBlk(place, lambda i: out_ref.at[:, i], out_sum, *take(REDUCE_REFS))
        folds = fold_rows(place, gate_up_ref, gate_up_sum, ROW_PARTS, take)
        out_events = out.events()

        def back(g):
            attend_back_block(
                count,
                g,
                place.here,
                q_ref,
                kv_ref,
                doc_ref,
                key_doc_ref,
                grad_ref,
                full_ref,
                total_ref,
                dq_ref,
                key_acc,
            )

        def clear(i, carry):
            key_acc[i] = jnp.zeros(key_acc.shape[1:], jnp.float32)
            return carry

        def put(sequence):
            def one(i, carry):
                for k in (0, 1):
                    value = key_acc[i * 2 + k].astype(bf16).reshape((steps,) + kv_piece[1:])
                    dkv_part[i, pl.ds((2 * sequence + k) * steps, steps)] = value
                return carry

            lax.fori_loop(0, count, one, 0)

        ends = jnp.logical_not(out.middle)

        turning = out.turning()

        def middle(*steps):
            @pl.when(out.middle)
            def _():
                for step in steps:
                    if isinstance(step, int):
                        turning[step]()
                    else:
                        out.pass_on(*step, True)

        def outside(*steps):
            @pl.when(ends)
            def _():
                for step in steps:
                    out.pass_on(*step, False)

        out.start()
        for fold in folds:
            next(fold)
        lax.fori_loop(0, 2 * count, clear, 0)
        back(0)
        next(folds[0])
        middle(0)
        back(1)
        put(0)
        middle(1, 2)
        outside((0, 0), (1, 0), (1, 1))
        next(folds[1])
        lax.fori_loop(0, 2 * count, clear, 0)
        back(2)
        outside((2, 0), (2, 1))
        middle((0, 0))
        back(3)
        put(1)
        middle((1, 0), (1, 1), (2, 0), (2, 1))
        dkv.start()
        dkv_events = dkv.events()
        order = [(folds, 2), (dkv_events, 0), (dkv_events, 1), (dkv_events, 2)]
        order += [(out_events, 8), (out_events, 9), (dkv_events, 3), (dkv_events, 4)]
        order += [(folds, 0), (dkv_events, 5), (dkv_events, 6), (folds, 1)]
        order += [(dkv_events, 7), (dkv_events, 8), (dkv_events, 9), (folds, 2)]
        for events, i in order:
            if events is folds:
                next(folds[i])
            else:
                events[i]()
        out.finish()
        dkv.finish()
        together(*folds)

    vmem = pltpu.VMEM
    return transfer(
        f"attend_back{number}",
        number,
        body,
        [queries, kv, doc, key_doc, grad, full, totals, out_part, gate_up_part],
        [
            shape(queries.shape, bf16),
            shape(kv_piece, bf16),
            shape(out_piece, bf16),
            shape(gate_up_piece, jnp.float32),
        ],
        [
            vmem((count,) + kv_piece, bf16),
            vmem((2 * count, rows, 2 * HEAD_DIM), jnp.float32),
        ]
        + reduce_blk_scratch(count, kv_piece, bf16)
        + reduce_blk_scratch(count, out_piece, bf16)
        + fold_rows_scratch(gate_up_piece, ROW_PARTS),
        (kv.size + out_part.size) * 2,
        [vmem, vmem, vmem, pl.ANY],
        [vmem] * 8 + [pl.ANY],
    )


def reduce_middle(dkv_part, out_part, gate_up_part, count, number):
    dkv_piece = dkv_part.shape[1:]
    out_piece = out_part.shape[:1] + out_part.shape[2:]

    gate_up_piece = gate_up_part.shape[1:]

    def body(dkv_ref, out_ref, gate_up_ref, dkv_sum, out_sum, gate_up_sum, *scratch):
        take = Taker(scratch)
        place = Place(count)
        greet(place, blk=True, core=True, half=True)
        together(
            reduce_blk(place, dkv_ref, dkv_sum, *take(REDUCE_REFS)),
            reduce_blk(place, lambda i: out_ref.at[:, i], out_sum, *take(REDUCE_REFS)),
            *(
                waiting(task, *rounds)
                for rounds, task in zip(
                    ((6, 5, 5), (8, 5, 3), (10, 6, 0)),
                    fold_rows(place, gate_up_ref, gate_up_sum, ROW_PARTS, take),
                )
            ),
        )

    return transfer(
        f"reduce{number}",
        number,
        body,
        [dkv_part, out_part, gate_up_part],
        [
            shape(dkv_piece, jnp.bfloat16),
            shape(out_piece, jnp.bfloat16),
            shape(gate_up_piece, jnp.float32),
        ],
        reduce_blk_scratch(count, dkv_piece, jnp.bfloat16)
        + reduce_blk_scratch(count, out_piece, jnp.bfloat16)
        + fold_rows_scratch(gate_up_piece, ROW_PARTS),
        (dkv_part.size + out_part.size) * 2,
        [pltpu.VMEM, pltpu.VMEM, pl.ANY],
        [pltpu.VMEM, pltpu.VMEM, pl.ANY],
    )


def reduce_last(qkv_part, norm_part, gain_part, out_sum, down_part, count, number):
    gain_piece = gain_part.shape[1:]
    qkv_piece, norm_piece = qkv_part.shape[1:], norm_part.shape[1:]

    def body(*refs):
        qkv_ref, norm_ref, gain_ref, out_ref, down_ref = refs[:5]
        qkv_sum, norm_sum, gain_sum, out_all, down_sum = refs[5:10]
        gain_mine = refs[10]
        take = Taker(refs[11:])
        place = Place(count)
        greet(place, blk=True, core=True, half=True, corner=True)

        def gain_task(near, far):
            yield from reduce_blk(place, gain_ref, gain_mine, *near)
            yield from reduce_group(place, gain_mine, gain_sum, *far)

        main = reduce_blk(place, qkv_ref, qkv_sum, *take(REDUCE_REFS))
        gain = gain_task(take(REDUCE_REFS), take(5))
        together(
            waiting(gain, 11),
            main,
            waiting(exchange_group(place, out_ref, out_all, *take(3)), 16),
            waiting(reduce_group(place, norm_ref, norm_sum, *take(5)), 0, 6, 9),
            *(
                waiting(task, *rounds)
                for rounds, task in zip(
                    ((7, 7, 2), (8, 8, 0), (9, 9, 0)),
                    fold_rows(place, down_ref, down_sum, ROW_PARTS, take),
                )
            ),
        )

    return transfer(
        f"last{number}",
        number,
        body,
        [qkv_part, norm_part, gain_part, out_sum, down_part],
        [
            shape(qkv_piece, jnp.float32),
            shape(norm_piece, jnp.float32),
            shape(gain_piece[1:], jnp.float32),
            shape(out_sum.shape, jnp.bfloat16),
            shape(down_part.shape[1:], jnp.float32),
        ],
        [pltpu.VMEM(gain_piece, jnp.float32)]
        + reduce_blk_scratch(count, qkv_piece, jnp.bfloat16)
        + reduce_blk_scratch(count, gain_piece, jnp.float32, 1)
        + reduce_group_scratch(gain_piece[1:], jnp.float32)
        + exchange_group_sems()
        + reduce_group_scratch(norm_piece, jnp.bfloat16)
        + fold_rows_scratch(down_part.shape[1:], ROW_PARTS),
        qkv_part.size * 2,
        [pltpu.VMEM] * 4 + [pl.ANY],
        [pltpu.VMEM] * 4 + [pl.ANY],
    )


GROUP_PARTS = 4


def all_gather_group(value, number):
    parts = GROUP_PARTS

    def body(src, out, *sems):
        place = Place(lax.axis_size("blk"))
        greet(place, core=True, half=True)
        together(*gather_group_rows(place, src, out, parts, Taker(sems), False))

    return transfer(
        f"group{number}",
        number,
        body,
        [value],
        [shape((GROUPS,) + value.shape, value.dtype)],
        gather_group_sems() * parts,
        value.size * 8,
    )[0]


def project_group(attn, weight, piece, number):
    width = weight.shape[0]
    parts = 3 if width % 768 == 0 else 1
    columns = width // parts
    bf16 = jnp.bfloat16

    def body(attn_ref, weight_ref, out, part, *scratch):
        take = Taker(scratch)
        place = Place(lax.axis_size("blk"))
        greet(place, core=True, half=True)

        def multiply(n, carry):
            at = pl.ds(pl.multiple_of(n * 256, 256), 256)
            left = attn_ref[...].reshape(-1, attn.shape[-1])
            value = dot(left, weight_ref[at], LAST).astype(bf16)
            part[:, :, :, at] = value.reshape((GROUPS,) + piece[:2] + (256,))
            return carry

        def task(p):
            at = pl.ds(p * columns, columns)
            return reduce_group(
                place, lambda g: part.at[g, :, :, at], out.at[:, :, at], *take(5)
            )

        tasks = [task(p) for p in range(parts)]
        for p in range(parts):
            lax.fori_loop(p * columns // 256, (p + 1) * columns // 256, multiply, 0)
            next(tasks[p])
            next(tasks[p])
        together(*tasks)

    return transfer(
        f"fold{number}",
        number,
        body,
        [attn, weight],
        [shape(piece, jnp.float32)],
        [pltpu.VMEM((GROUPS,) + piece, bf16)]
        + reduce_group_scratch(piece[:2] + (columns,), bf16) * parts,
        attn.size * 8,
        [pltpu.VMEM],
    )[0]


def dot(left, right, contract):
    return lax.dot_general(left, right, (contract, ((), ())), preferred_element_type=jnp.float32)


LAST = ((1,), (1,))
PLAIN = ((1,), (0,))
FIRST = ((0,), (0,))


LANES = 128
GELU_A = math.sqrt(2.0 / math.pi)
GELU_B = 0.044715


def feed_forward_fits(count, rows, width, hidden):
    inner = 4 if count >= 32 else 2
    outer = count // inner
    tile = rows * width * 2
    weights = 3 * hidden * width * 2
    kept = count * rows * 3 * hidden * 2
    total = weights + kept + tile * (3 * count + outer * (inner - 1) + 2 * outer + 3) + 9 * tile
    total += 6 * LANES * (count * rows + 3 * 256) * 2
    return total < 58 * 2**20 and hidden % (3 * LANES) == 0 and width % 256 == 0


def feed_forward_kernel(
    count,
    branch_ref,
    token_ref,
    cot_ref,
    gain_ref,
    gate_up_hbm,
    down_hbm,
    out_ref,
    middle_grad_ref,
    branch_grad_ref,
    gain_grad_ref,
    gate_up_grad_hbm,
    down_grad_hbm,
    w_gate_up,
    w_down,
    norm_all,
    grad_all,
    act,
    hidden,
    part,
    middle,
    norm_own,
    grad_own,
    total,
    turned,
    staged,
    beside,
    along,
    held,
    spare,
    w_sems,
    out_sems,
    *sems,
):
    place = Place(count)
    rows, width = norm_all.shape[1:]
    units = hidden.shape[1]
    chunks = units // LANES
    inner, outer = place.inner, place.outer
    slab = branch_ref.shape[1]
    steps = rows // slab
    columns = width // 256
    pair = inner * rows
    take = Taker(sems)

    def weight_copies(i):
        units_at = pl.ds(pl.multiple_of(i * LANES, LANES), LANES)
        return [
            pltpu.make_async_copy(
                gate_up_hbm.at[units_at, pl.ds(0, width)],
                w_gate_up.at[i, pl.ds(0, LANES)],
                w_sems.at[3 * i],
            ),
            pltpu.make_async_copy(
                gate_up_hbm.at[units_at, pl.ds(width, width)],
                w_gate_up.at[i, pl.ds(LANES, LANES)],
                w_sems.at[3 * i + 1],
            ),
            pltpu.make_async_copy(down_hbm.at[units_at], w_down.at[units_at], w_sems.at[3 * i + 2]),
        ]

    def start_weights(i, carry):
        for copy in weight_copies(i):
            copy.start()
        return carry

    def wait_weights(i, carry):
        for copy in weight_copies(i):
            copy.wait()
        return carry

    lax.fori_loop(0, chunks, start_weights, 0)

    def scale_of(values):
        return lax.rsqrt(jnp.mean(values * values, axis=-1, keepdims=True) + NORM_EPS)

    def slab_rows(i):
        return pl.ds(pl.multiple_of(i * slab, slab), slab)

    def before(i, carry):
        value = branch_ref[i]
        mid = token_ref[i].astype(jnp.float32) + value * scale_of(value) * gain_ref[1:2]
        middle[i] = mid
        norm_own[slab_rows(i)] = (mid * scale_of(mid) * gain_ref[2:3]).astype(jnp.bfloat16)
        return carry

    greet(place, blk=True, meanwhile=lambda: lax.fori_loop(0, steps, before, 0))

    def pair_rows(k):
        return pl.ds(pl.multiple_of(place.near_at(k) * pair, pair), pair)

    def pair_pieces(k):
        return pl.ds(place.near_at(k) * inner, inner)

    def column(n):
        return pl.ds(pl.multiple_of(n * 256, 256), 256)

    def put_part(k, n, value):
        split = value.astype(jnp.bfloat16).reshape((inner, steps, slab, 256))
        part[pair_pieces(k), :, :, column(n)] = split

    def receive(gather, k):
        def one(static):
            if static == 0:
                gather.copy.wait()
            advance([gather], static)
            gather.beside_arrived(static)

        for static in range(outer):
            pl.when(k == static)(lambda static=static: one(static))

    gather = GatherBlk(place, norm_own, lambda i: norm_all.at[i], *take(3))
    gather.start()
    lax.fori_loop(0, chunks, wait_weights, 0)
    def forward(k, carry):
        receive(gather, k)
        at = pair_rows(k)

        def up_chunk(j, carry):
            x = norm_all[pair_pieces(k)].reshape(pair, width)
            both = dot(x, w_gate_up[j], LAST)
            act[at, column(j)] = both.astype(jnp.bfloat16)
            gate, up = both[:, :LANES], both[:, LANES:]
            bent = 0.5 * gate * (1.0 + jnp.tanh(GELU_A * (gate + GELU_B * (gate * gate * gate))))
            hidden[at, pl.ds(pl.multiple_of(j * LANES, LANES), LANES)] = (bent * up).astype(
                jnp.bfloat16
            )
            return carry

        lax.fori_loop(0, chunks, up_chunk, 0)

        def down_chunk(n, carry):
            put_part(k, n, dot(hidden[at, :], w_down[:, column(n)], PLAIN))
            return carry

        lax.fori_loop(0, columns, down_chunk, 0)
        return carry

    lax.fori_loop(0, outer, forward, 0)
    gather.finish()
    reduce = ReduceBlk(place, lambda i: part.at[i], total, beside, along, held, spare, *take(6))
    reduce.start()
    for event in reduce.events():
        event()

    gain_grad_ref[...] = jnp.zeros_like(gain_grad_ref)

    def norm_back(value, gain, incoming):
        scale = scale_of(value)
        lifted = incoming * gain
        pull = jnp.mean(lifted * value, axis=-1, keepdims=True)
        gain_grad = jnp.sum(incoming * value * scale, axis=0, keepdims=True)
        return scale * lifted - value * (scale * scale * scale) * pull, gain_grad

    def between(i, carry):
        value, cot = total[i], cot_ref[i].astype(jnp.float32)
        gain = gain_ref[3:4]
        out_ref[i] = (middle[i] + value * scale_of(value) * gain).astype(jnp.bfloat16)
        grad, gain_grad = norm_back(value, gain, cot)
        gain_grad_ref[3:4] += gain_grad
        grad_own[slab_rows(i)] = grad.astype(jnp.bfloat16)
        return carry

    lax.fori_loop(0, steps, between, 0)
    reduce.finish()

    gather = GatherBlk(place, grad_own, lambda i: grad_all.at[i], *take(3))
    gather.start()
    def backward(k, carry):
        receive(gather, k)
        at = pair_rows(k)

        def back_chunk(j, carry):
            g = grad_all[pair_pieces(k)].reshape(pair, width)
            units_at = pl.ds(pl.multiple_of(j * LANES, LANES), LANES)
            grad = dot(g, w_down[units_at], LAST)
            both = act[at, column(j)].astype(jnp.float32)
            gate, up = both[:, :LANES], both[:, LANES:]
            bend = jnp.tanh(GELU_A * (gate + GELU_B * (gate * gate * gate)))
            bent = 0.5 * gate * (1.0 + bend)
            slope = 0.5 * (1.0 + bend) + (0.5 * GELU_A) * gate * (1.0 - bend * bend) * (
                1.0 + (3.0 * GELU_B) * gate * gate
            )
            pulled = jnp.concatenate([grad * up * slope, grad * bent], axis=1)
            act[at, column(j)] = pulled.astype(jnp.bfloat16)
            return carry

        lax.fori_loop(0, chunks, back_chunk, 0)

        def input_chunk(n, carry):
            w = w_gate_up[:, :, column(n)].reshape(2 * units, 256)
            put_part(k, n, dot(act[at, :], w, PLAIN))
            return carry

        lax.fori_loop(0, columns, input_chunk, 0)
        return carry

    lax.fori_loop(0, outer, backward, 0)
    gather.finish()
    reduce = ReduceBlk(place, lambda i: part.at[i], total, beside, along, held, spare, *take(6))
    reduce.start()

    tokens = count * rows
    slots = staged.shape[0]
    three = 3 * LANES

    def up_store(step):
        slot = lax.rem(step, slots)
        i, n = step // columns, lax.rem(step, columns)
        return [
            pltpu.make_async_copy(
                staged.at[slot, pl.ds((2 * q + h) * LANES, LANES)],
                gate_up_grad_hbm.at[
                    pl.ds(pl.multiple_of((3 * i + q) * LANES, LANES), LANES),
                    pl.ds(pl.multiple_of(h * width + n * 256, 256), 256),
                ],
                out_sems.at[slot, 2 * q + h],
            )
            for q in range(3)
            for h in (0, 1)
        ]

    def up_grad(step, carry):
        slot = lax.rem(step, slots)
        i, n = step // columns, lax.rem(step, columns)

        @pl.when(step >= slots)
        def _():
            for copy in up_store(step - slots):
                copy.wait()

        @pl.when(n == 0)
        def _():
            turned[...] = jnp.transpose(act[:, pl.ds(pl.multiple_of(2 * i * three, three), 2 * three)])

        x = norm_all[:, :, column(n)].reshape(tokens, 256)
        staged[slot] = dot(turned[...], x, PLAIN).astype(jnp.bfloat16)
        for copy in up_store(step):
            copy.start()
        return carry

    def down_store(step):
        slot = lax.rem(step, slots)
        i, n = step // columns, lax.rem(step, columns)
        return pltpu.make_async_copy(
            staged.at[slot, pl.ds(0, three)],
            down_grad_hbm.at[pl.ds(pl.multiple_of(i * three, three), three), column(n)],
            out_sems.at[slot, 6],
        )

    def down_grad(step, carry):
        slot = lax.rem(step, slots)
        i, n = step // columns, lax.rem(step, columns)

        @pl.when(step >= slots)
        def _():
            down_store(step - slots).wait()

        @pl.when(n == 0)
        def _():
            turned[pl.ds(0, three)] = jnp.transpose(
                hidden[:, pl.ds(pl.multiple_of(i * three, three), three)]
            )

        x = grad_all[:, :, column(n)].reshape(tokens, 256)
        staged[slot, pl.ds(0, three)] = dot(turned[pl.ds(0, three)], x, PLAIN).astype(jnp.bfloat16)
        down_store(step).start()
        return carry

    ups, downs = chunks // 3 * columns, units // three * columns
    events = reduce.events()
    early = len(events) - 3
    for k in range(early):
        lax.fori_loop(ups * k // early, ups * (k + 1) // early, up_grad, 0)
        events[k]()
    for step in range(max(0, ups - slots), ups):
        for copy in up_store(step):
            copy.wait()
    for k in range(3):
        lax.fori_loop(downs * k // 3, downs * (k + 1) // 3, down_grad, 0)
        events[early + k]()

    def after(i, carry):
        value, mid, cot = branch_ref[i], middle[i], cot_ref[i].astype(jnp.float32)
        grad, gain_grad = norm_back(mid, gain_ref[2:3], total[i])
        gain_grad_ref[2:3] += gain_grad
        middle_grad = cot + grad
        middle_grad_ref[i] = middle_grad
        grad, gain_grad = norm_back(value, gain_ref[1:2], middle_grad)
        gain_grad_ref[1:2] += gain_grad
        branch_grad_ref[i] = grad.astype(jnp.bfloat16)
        return carry

    lax.fori_loop(0, steps, after, 0)
    reduce.finish()
    for step in range(max(0, downs - slots), downs):
        down_store(step).wait()


def feed_forward(branch, tokens, cotangent, gains, gate_up_all, down_all, count, number):
    steps, slab, width = branch.shape
    rows = steps * slab
    units = down_all.shape[0]
    inner = 4 if count >= 32 else 2
    outer = count // inner
    piece = branch.shape
    bf16, f32 = jnp.bfloat16, jnp.float32
    vmem = pl.BlockSpec(memory_space=pltpu.VMEM)
    anywhere = pl.BlockSpec(memory_space=pl.ANY)
    slots = 3
    line_scratch = reduce_blk_scratch(count, piece, bf16)
    return pl.pallas_call(
        functools.partial(feed_forward_kernel, count),
        name="feed_forward",
        out_shape=[
            shape(piece, bf16),
            shape(piece, f32),
            shape(piece, bf16),
            shape((4, width), f32),
            shape(gate_up_all.shape, bf16),
            shape(down_all.shape, bf16),
        ],
        in_specs=[vmem] * 4 + [anywhere] * 2,
        out_specs=[vmem] * 4 + [anywhere] * 2,
        scratch_shapes=[
            pltpu.VMEM((units // LANES, 2 * LANES, width), bf16),
            pltpu.VMEM((units, width), bf16),
            pltpu.VMEM((count, rows, width), bf16),
            pltpu.VMEM((count, rows, width), bf16),
            pltpu.VMEM((count * rows, 2 * units), bf16),
            pltpu.VMEM((count * rows, units), bf16),
            pltpu.VMEM((count,) + piece, bf16),
            pltpu.VMEM(piece, f32),
            pltpu.VMEM((rows, width), bf16),
            pltpu.VMEM((rows, width), bf16),
            pltpu.VMEM(piece, f32),
            pltpu.VMEM((6 * LANES, count * rows), bf16),
            pltpu.VMEM((slots, 6 * LANES, 256), bf16),
        ]
        + line_scratch[:4]
        + [
            pltpu.SemaphoreType.DMA((3 * units // LANES,)),
            pltpu.SemaphoreType.DMA((slots, 7)),
        ]
        + gather_blk_sems(count)
        + line_scratch[4:]
        + gather_blk_sems(count)
        + line_scratch[4:],
        compiler_params=pltpu.CompilerParams(
            collective_id=number, has_side_effects=True, vmem_limit_bytes=67043328
        ),
        cost_estimate=pl.CostEstimate(
            flops=18 * count * rows * units * width,
            bytes_accessed=500 * 2**20,
            transcendentals=0,
        ),
    )(branch, tokens, cotangent, gains, gate_up_all, down_all)


def attention_scores(q2, k, query_pos, query_doc, key_block, key_doc, rows):
    raw = lax.dot_general(q2, k, (((1,), (1,)), ((), ())), preferred_element_type=jnp.float32)
    capped = jnp.tanh(raw * (SCORE_SCALE / SOFT_CAP))
    key_pos = key_block * rows + lax.broadcasted_iota(jnp.int32, (1, rows), 1)
    visible = (key_pos <= query_pos) & (key_doc == query_doc)
    return capped, jnp.where(visible, jnp.exp(SOFT_CAP * capped), 0.0)


def attention_query(q_ref, doc_ref, here, count, rows):
    half = pl.program_id(1)
    block = half * count + here
    q2 = jnp.concatenate([q_ref[0, :, :HEAD_DIM], q_ref[0, :, HEAD_DIM:]], axis=0)
    inside = lax.broadcasted_iota(jnp.int32, (rows, 1), 0)
    position = block * rows + jnp.concatenate([inside, inside], axis=0)
    doc = jnp.concatenate([doc_ref[0], doc_ref[0]], axis=0)
    return block, q2, position, doc


def attention_backward_kernel(
    count,
    here_ref,
    q_ref,
    kv_ref,
    doc_ref,
    key_doc_ref,
    grad_ref,
    full_ref,
    total_ref,
    dq_ref,
    dkv_ref,
    acc,
    key_acc,
):
    rows = q_ref.shape[1]
    half = pl.program_id(1)
    block, q2, position, doc = attention_query(q_ref, doc_ref, here_ref[0], count, rows)
    total = total_ref[0]
    grad = grad_ref[0].astype(jnp.float32)
    grad2 = jnp.concatenate([grad[:, :HEAD_DIM], grad[:, HEAD_DIM:]], axis=0)
    full2 = jnp.concatenate([full_ref[0, :, :HEAD_DIM], full_ref[0, :, HEAD_DIM:]], axis=0)
    total_grad = -jnp.sum(grad2 * full2, axis=-1, keepdims=True) / total
    sums_grad = (grad2 / total).astype(jnp.bfloat16)
    acc[...] = jnp.zeros_like(acc)

    @pl.when(half == 0)
    def _():
        def clear(i, carry):
            key_acc[i] = jnp.zeros(key_acc.shape[1:], jnp.float32)
            return carry

        lax.fori_loop(0, key_acc.shape[0], clear, 0)

    def one(key_block, carry):
        key_half = (key_block >= count).astype(jnp.int32)
        inner = key_block - key_half * count
        kv = kv_ref.at[inner, key_half]
        keys = kv[:, :HEAD_DIM]
        capped, weights = attention_scores(
            q2, keys, position, doc, key_block, key_doc_ref[0, key_block], rows
        )
        exp_grad = lax.dot_general(
            sums_grad, kv[:, HEAD_DIM:], (((1,), (1,)), ((), ())), preferred_element_type=jnp.float32
        )
        raw_grad = (
            weights * (exp_grad + total_grad) * (1.0 - capped * capped) * SCORE_SCALE
        ).astype(jnp.bfloat16)
        acc[...] += jnp.dot(raw_grad, keys, preferred_element_type=jnp.float32)
        over_rows = (((0,), (0,)), ((), ()))
        slot = inner * 2 + key_half
        key_acc[slot, :, :HEAD_DIM] += lax.dot_general(
            raw_grad, q2, over_rows, preferred_element_type=jnp.float32
        )
        key_acc[slot, :, HEAD_DIM:] += lax.dot_general(
            weights.astype(jnp.bfloat16), sums_grad, over_rows, preferred_element_type=jnp.float32
        )
        return carry

    lax.fori_loop(jnp.maximum(block - count, 0), block + 1, one, 0)
    dq = acc[...]
    dq_ref[0] = jnp.concatenate([dq[:rows], dq[rows:]], axis=1).astype(jnp.bfloat16)

    @pl.when(half == 1)
    def _():
        def put(i, carry):
            for k in (0, 1):
                dkv_ref[i, k] = key_acc[i * 2 + k].astype(jnp.bfloat16)
            return carry

        lax.fori_loop(0, count, put, 0)


def attention_specs(count, rows, width):
    query = pl.BlockSpec((1, rows, width), lambda s, h, here: (2 * s + h, 0, 0))
    keys = pl.BlockSpec((count, 2, rows, 2 * HEAD_DIM), lambda s, h, here: (0, s, 0, 0))
    doc = pl.BlockSpec((1, rows, 1), lambda s, h, here: (2 * s + h, 0, 0))
    key_doc = pl.BlockSpec((1, 2 * count, 1, rows), lambda s, h, here: (s, 0, 0, 0))
    total = pl.BlockSpec((1, REPS * rows, 1), lambda s, h, here: (2 * s + h, 0, 0))
    return query, keys, doc, key_doc, total


def attention_backward(here, q, kv, doc, key_doc, grad, full, totals):
    count, _, rows, _ = kv.shape
    width = REPS * HEAD_DIM
    query, keys, doc_spec, key_doc_spec, total = attention_specs(count, rows, width)
    return pl.pallas_call(
        functools.partial(attention_backward_kernel, count),
        name="attend_back",
        grid_spec=pltpu.PrefetchScalarGridSpec(
            num_scalar_prefetch=1,
            grid=(2, 2),
            in_specs=[query, keys, doc_spec, key_doc_spec, query, query, total],
            out_specs=[query, keys],
            scratch_shapes=[
                pltpu.VMEM((REPS * rows, HEAD_DIM), jnp.float32),
                pltpu.VMEM((2 * count, rows, 2 * HEAD_DIM), jnp.float32),
            ],
        ),
        out_shape=[shape((GROUPS, rows, width), jnp.bfloat16), shape(kv.shape, jnp.bfloat16)],
        compiler_params=pltpu.CompilerParams(vmem_limit_bytes=VMEM_LIMIT),
        cost_estimate=pl.CostEstimate(flops=2 * 10**9, bytes_accessed=80 * 2**20, transcendentals=0),
    )(here, q, kv, doc, key_doc, grad, full, totals)


def rms_scale(values, gain_row):
    return (
        values * lax.rsqrt(jnp.mean(values * values, axis=-1, keepdims=True) + NORM_EPS) * gain_row
    )


def gelu_tanh(values):
    return jax.nn.gelu(values, approximate=True)


def rope_tables(positions):
    half_width = HEAD_DIM // 2
    frequency = jnp.exp(
        jnp.arange(half_width, dtype=jnp.float32) * (-2.0 * math.log(ROPE_BASE) / HEAD_DIM)
    )
    angles = positions.astype(jnp.float32)[:, None] * frequency[None, :]
    cosine = jnp.concatenate([jnp.cos(angles), jnp.cos(angles)], axis=-1)
    sine = jnp.concatenate([jnp.sin(angles), jnp.sin(angles)], axis=-1)
    return cosine[:, None, :], sine[:, None, :]


def rotate(values, cosine, sine):
    half_width = HEAD_DIM // 2
    turned = jnp.concatenate([-values[..., half_width:], values[..., :half_width]], axis=-1)
    return values * cosine + turned * sine


def feed_forward_apart(
    branch_slabs, inputs, cotangent, gains, gate_up_all, down_all, count, piece
):
    rows, width = inputs.shape
    bf16 = jnp.bfloat16
    branch = branch_slabs.reshape(rows, width)
    middle = inputs + rms_scale(branch, gains[1])
    norm_three = rms_scale(middle, gains[2]).astype(bf16)
    gate_all = gate_up_all[:, :width]
    up_all = gate_up_all[:, width:]
    norm_all = all_gather_blk(norm_three, count, 4).reshape(count * rows, width)
    gate = dot(norm_all, gate_all, LAST)
    up = dot(norm_all, up_all, LAST)
    hidden = (gelu_tanh(gate) * up).astype(bf16)
    ffn_part = dot(hidden, down_all, PLAIN).astype(bf16)
    ffn_out = reduce_scatter_blk(ffn_part.reshape((count,) + piece), count, 5).reshape(rows, width)
    output = (middle + rms_scale(ffn_out, gains[3])).astype(bf16)[None]

    out_cotangent = cotangent[0].astype(jnp.float32)
    _, post_ffn_back = jax.vjp(rms_scale, ffn_out, gains[3])
    ffn_grad, gain_grad_four = post_ffn_back(out_cotangent)
    grad_all = all_gather_blk(ffn_grad.astype(bf16), count, 6).reshape(count * rows, width)
    activated, gelu_back = jax.vjp(gelu_tanh, gate)
    hidden_grad = dot(grad_all, down_all, LAST)
    gate_grad = gelu_back(hidden_grad * up)[0].astype(bf16)
    up_grad = (hidden_grad * activated).astype(bf16)
    norm_part = dot(gate_grad, gate_all, PLAIN) + dot(up_grad, up_all, PLAIN)
    norm_three_grad = reduce_scatter_blk(
        norm_part.astype(bf16).reshape((count,) + piece), count, 7
    ).reshape(rows, width)
    down_part = dot(hidden, grad_all, FIRST).astype(bf16)
    gate_up_part = jnp.concatenate(
        [dot(gate_grad, norm_all, FIRST), dot(up_grad, norm_all, FIRST)], axis=1
    ).astype(bf16)
    _, pre_ffn_back = jax.vjp(rms_scale, middle, gains[2])
    middle_part, gain_grad_three = pre_ffn_back(norm_three_grad)
    middle_grad = out_cotangent + middle_part
    _, post_attn_back = jax.vjp(rms_scale, branch, gains[1])
    branch_grad, gain_grad_two = post_attn_back(middle_grad)
    return (
        output,
        middle_grad,
        branch_grad.astype(bf16),
        gain_grad_two,
        gain_grad_three,
        gain_grad_four,
        gate_up_part,
        down_part,
    )


def shards(
    tokens, cotangent, segments, norm_gains, qkv_weight, out_weight, gate_up_weight, down_weight
):
    _, rows, width = tokens.shape
    count = lax.axis_size("blk")
    here = lax.axis_index("blk")
    mine = 2 * lax.axis_index("dp") + lax.axis_index("head")
    group_rows = GROUPS * rows
    head_width = REPS * HEAD_DIM
    bf16 = jnp.bfloat16
    slab = slabs(rows)
    piece = (rows // slab, slab, width)

    gain_rows = norm_gains.shape[0]
    gain_lanes = -(-gain_rows // 128) * 128
    gains_sent = jnp.pad(
        jnp.transpose(norm_gains).astype(jnp.float32), ((0, 4), (0, gain_lanes - gain_rows))
    )
    out_rows = out_weight.shape[0]
    out_sent = jnp.transpose(out_weight.reshape(out_rows, GROUPS, head_width), (1, 0, 2))
    qkv_rows = qkv_weight.shape[0]
    qkv_slab = slabs(qkv_rows)
    qkv_piece = (qkv_rows // qkv_slab, qkv_slab, width)
    qkv_all, out_mine, tokens_all, gains_all, docs_all, down_all = gather_first(
        qkv_weight,
        out_sent,
        tokens[0],
        gains_sent,
        segments.reshape(-1, 128),
        down_weight,
        count,
        1,
    )
    down_all = down_all.reshape(-1, width)
    gains = jnp.transpose(gains_all[:, :, :4, :gain_rows], (2, 0, 1, 3)).reshape(4, width)
    qkv_head = qkv_all.reshape(count * qkv_rows, width)
    docs = docs_all.reshape(2, 2, count, rows)
    key_doc = docs.reshape(2, 2 * count, 1, rows)
    own_doc = lax.dynamic_index_in_dim(docs, here, 2, keepdims=False).reshape(GROUPS, rows, 1)
    here_one = here.reshape(1)

    group_tokens = tokens_all.reshape(group_rows, width).astype(jnp.float32)
    norm_one = rms_scale(group_tokens, gains[0]).astype(bf16)
    proj = dot(norm_one, qkv_head, LAST)
    inside = jnp.arange(rows, dtype=jnp.int32)
    position = jnp.concatenate([here * rows + inside, (count + here) * rows + inside])
    cosine, sine = rope_tables(jnp.concatenate([position, position]))
    proj = proj.reshape(group_rows, REPS + 2, HEAD_DIM)
    turned = rotate(proj[:, : REPS + 1], cosine, sine)
    sent = jnp.concatenate([turned, proj[:, REPS + 1 :]], axis=1).astype(bf16)
    queries = sent[:, :REPS].reshape(GROUPS, rows, head_width)
    own_kv = sent[:, REPS:].reshape(group_rows, 2 * HEAD_DIM)
    kv_slab = slabs(group_rows)
    kv_piece = (group_rows // kv_slab, kv_slab, 2 * HEAD_DIM)
    kv, out_all, gate_up_all, attn, attended, totals = gather_attend(
        own_kv, out_mine, gate_up_weight, queries, own_doc, key_doc, count, 2
    )
    gate_up_all = gate_up_all.reshape(-1, 2 * width)
    out_head = out_all.reshape(width, head_width)
    attn = attn.reshape(group_rows, head_width)
    branch_slabs = project_group(attn.reshape(queries.shape), out_head, piece, 3)
    inputs = tokens[0].astype(jnp.float32)
    if feed_forward_fits(count, rows, width, down_all.shape[0]):
        output, middle_grad, branch_grad, gain_rest, gate_up_part, down_part = feed_forward(
            branch_slabs,
            tokens.reshape(piece),
            cotangent.reshape(piece),
            gains,
            gate_up_all,
            down_all,
            count,
            4,
        )
        output = output.reshape(tokens.shape)
        middle_grad = middle_grad.reshape(rows, width)
        branch_grad = branch_grad.reshape(rows, width)
        gain_grad_two, gain_grad_three, gain_grad_four = gain_rest[1], gain_rest[2], gain_rest[3]
    else:
        (
            output,
            middle_grad,
            branch_grad,
            gain_grad_two,
            gain_grad_three,
            gain_grad_four,
            gate_up_part,
            down_part,
        ) = feed_forward_apart(
            branch_slabs, inputs, cotangent, gains, gate_up_all, down_all, count, piece
        )
    branch_all = all_gather_group(branch_grad, 8).reshape(group_rows, width)
    attn_grad = dot(branch_all, out_head, PLAIN).astype(bf16).reshape(GROUPS, rows, head_width)
    out_part = dot(branch_all, attn, FIRST).astype(bf16)
    out_part = out_part.reshape(GROUPS, count, out_rows, head_width)
    gate_up_part = gate_up_part.reshape((GROUPS,) + gate_up_weight.shape)
    if attend_back_fits(count):
        dq, dkv, out_sum, gate_up_grad = attend_back_reduce(
            queries,
            kv,
            own_doc,
            key_doc,
            attn_grad,
            attended,
            totals,
            out_part,
            gate_up_part,
            kv_piece,
            count,
            9,
        )
    else:
        kv = kv.reshape(count, GROUPS, rows, 2 * HEAD_DIM)
        dq, dkv_part = attention_backward(
            here_one, queries, kv, own_doc, key_doc, attn_grad, attended, totals
        )
        dkv, out_sum, gate_up_grad = reduce_middle(
            dkv_part.reshape((count,) + kv_piece), out_part, gate_up_part, count, 9
        )
    sent_grad = jnp.concatenate(
        [
            dq.reshape(group_rows, REPS, HEAD_DIM),
            dkv.reshape(group_rows, 2, HEAD_DIM),
        ],
        axis=1,
    ).astype(jnp.float32)
    unturned = rotate(sent_grad[:, : REPS + 1], cosine, -sine)
    proj_grad = (
        jnp.concatenate([unturned, sent_grad[:, REPS + 1 :]], axis=1)
        .astype(bf16)
        .reshape(group_rows, (REPS + 2) * HEAD_DIM)
    )
    qkv_part = dot(proj_grad, norm_one, FIRST).astype(bf16)
    norm_one_part = dot(proj_grad, qkv_head, PLAIN)
    _, gain_back = jax.vjp(lambda gain: rms_scale(group_tokens, gain), gains[0])
    (gain_grad_one,) = gain_back(norm_one_part)
    gain_part = jnp.stack([gain_grad_one, gain_grad_two, gain_grad_three, gain_grad_four])
    gain_part = jnp.transpose(gain_part.reshape(4, GROUPS, count, gain_rows), (2, 1, 0, 3))
    gain_part = jnp.pad(gain_part, ((0, 0), (0, 0), (0, 4), (0, gain_lanes - gain_rows)))
    qkv_grad, norm_one_grad, gain_grad, out_grad, down_grad = reduce_last(
        qkv_part.reshape((count,) + qkv_piece),
        norm_one_part.astype(bf16).reshape((GROUPS,) + piece),
        gain_part[:, :, None],
        out_sum,
        down_part.reshape((GROUPS,) + down_weight.shape),
        count,
        10,
    )
    qkv_grad = qkv_grad.reshape(qkv_rows, width)
    out_grad = (
        jnp.transpose(out_grad, (1, 0, 2)).reshape(out_rows, GROUPS * head_width).astype(jnp.float32)
    )
    gain_grad = jnp.transpose(gain_grad.reshape(8, gain_lanes)[:4, :gain_rows])
    _, pre_attn_back = jax.vjp(lambda values: rms_scale(values, gains[0]), inputs)
    (input_part,) = pre_attn_back(norm_one_grad.reshape(rows, width))
    tokens_grad = (middle_grad + input_part).astype(bf16)[None]
    return (output, tokens_grad, gain_grad, qkv_grad, out_grad, gate_up_grad, down_grad)


def solution(mesh):
    whole = ("dp", "head", "blk")
    return jax.shard_map(
        shards,
        mesh=mesh,
        in_specs=(
            P("dp", ("head", "blk"), None),
            P("dp", ("head", "blk"), None),
            P("dp", None),
            P(whole, None),
            P(whole, None),
            P(whole, None),
            P(whole, None),
            P(whole, None),
        ),
        out_specs=(
            P("dp", ("head", "blk"), None),
            P("dp", ("head", "blk"), None),
            P(whole, None),
            P(whole, None),
            P(whole, None),
            P(whole, None),
            P(whole, None),
        ),
        check_vma=False,
    )
```
